32 devices in a mesh: fsdp: 2 (over x), context: 4 (over z), tensor: 4 (over y, core).
Axes of the slice: x: 2, y: 2, z: 4, core: 2. Of those that a mesh axis runs over, the one named last changes fastest.
Arguments:
- tokens: bfloat16 [4, 2048, 768], P('fsdp', 'context'), may hold values from -6 to 6
- cotangent: bfloat16 [4, 2048, 768], P('fsdp', 'context'), may hold values from -6 to 6
- query_key_value_weight: bfloat16 [768, 3, 768], P('fsdp', None, 'tensor'), may hold values from -0.21875 to 0.21875
- qv_bias: float32 [2, 768], P(None, 'tensor'), may hold values from -0.6 to 0.6
- attention_out_weight: bfloat16 [768, 768], P('tensor', 'fsdp'), may hold values from -2 to 2
- attention_out_bias: float32 [768], replicated, may hold values from -3 to 3
- gain_one: float32 [768], replicated, may hold values from 0.5 to 1.5
- shift_one: float32 [768], replicated, may hold values from -3 to 3
- up_projection_weight: bfloat16 [768, 3072], P('fsdp', 'tensor'), may hold values from -0.21875 to 0.21875
- input_ffn_bias: float32 [3072], P('tensor'), may hold values from -3 to 3
- down_projection_weight: bfloat16 [3072, 768], P('tensor', 'fsdp'), may hold values from -0.109375 to 0.109375
- output_ffn_bias: float32 [768], replicated, may hold values from -3 to 3
- gain_two: float32 [768], replicated, may hold values from 0.5 to 1.5
- shift_two: float32 [768], replicated, may hold values from -3 to 3
Outputs:
- output: bfloat16 [4, 2048, 768], P('fsdp', 'context')
- input_grad: bfloat16 [4, 2048, 768], P('fsdp', 'context')
- qkv_weight_grad: float32 [768, 3, 768], P('fsdp', None, 'tensor')
- qv_bias_grad: float32 [2, 768], P(None, 'tensor')
- out_weight_grad: float32 [768, 768], P('tensor', 'fsdp')
- out_bias_grad: float32 [768], replicated
- gain_one_grad: float32 [768], replicated
- shift_one_grad: float32 [768], replicated
- up_weight_grad: float32 [768, 3072], P('fsdp', 'tensor')
- up_bias_grad: float32 [3072], P('tensor')
- down_weight_grad: float32 [3072, 768], P('tensor', 'fsdp')
- down_bias_grad: float32 [768], replicated
- gain_two_grad: float32 [768], replicated
- shift_two_grad: float32 [768], replicated
The draws below stay inside these ranges and needn't reach their ends.
All inputs are finite; a program needn't handle non-finite values.
Results may differ from the reference program's by a relative error of at most 0.02.
Values may be sent and summed in bfloat16 or wider, within the bound.
No kernel may reach another device: no remote copies, remote signals or barrier semaphores. Data moves between devices by JAX's collectives and lax.ppermute only.
A program may use at most 128 MiB of HBM per device.

```python
import math
import jax
import jax.numpy as jnp
from jax import lax

D = 768
H = 12
HD = 64
FF = 3072
SEQ_LEN = 2048
SEQS = 4


def level_of(key, dims, split, smallest, high):
    factor_of, own = 1.0, jax.random.fold_in(key, 6)
    for position, blocks in split:
        heights = jnp.exp(jax.random.uniform(jax.random.fold_in(own, position), (blocks,), jnp.float32, smallest / len(split), high / len(split)))
        factor_of = factor_of * jnp.repeat(heights, dims[position] // blocks).reshape([-1 if axis == position else 1 for axis in range(len(dims))])
    return factor_of


def noise(own_key, shape, deviation, limit, cuts=(), held_as=jnp.bfloat16):
    factor_of = level_of(own_key, shape, cuts, -0.22, 0.18) if cuts else 1.0
    values = jax.random.normal(own_key, shape, jnp.float32) * deviation * factor_of
    return jnp.minimum(jnp.maximum(values, -limit), limit).astype(held_as)


def setup_inputs(seed: int = 0) -> dict:
    splits = jax.random.split(jax.random.key(seed), 15)
    tokens = noise(splits[0], (SEQS, SEQ_LEN, D), 1.0, 6.0, ((0, 2), (1, 4)))
    cotangent = noise(splits[1], (SEQS, SEQ_LEN, D), 1.0, 6.0, ((0, 2), (1, 4)))
    query_key_value_weight = noise(splits[2], (D, 3, D), D ** -0.5, 0.21875, ((0, 2), (2, 4)))
    qv_bias = noise(splits[3], (2, D), 0.1, 0.6, ((1, 4),), jnp.float32)
    attention_out_weight = noise(splits[4], (D, D), 8 ** -0.5, 2.0, ((0, 4), (1, 2)))
    attention_out_bias = noise(splits[5], (D,), 0.5, 3.0, (), jnp.float32)
    gain_one = jnp.clip(1.0 + 0.1 * jax.random.normal(splits[6], (D,), jnp.float32), 0.5, 1.5)
    shift_one = noise(splits[7], (D,), 0.5, 3.0, (), jnp.float32)
    up_projection_weight = noise(splits[8], (D, FF), D ** -0.5, 0.21875, ((0, 2), (1, 4)))
    input_ffn_bias = noise(splits[9], (FF,), 0.5, 3.0, ((0, 4),), jnp.float32)
    down_projection_weight = noise(splits[10], (FF, D), FF ** -0.5, 0.109375, ((0, 4), (1, 2)))
    output_ffn_bias = noise(splits[11], (D,), 0.5, 3.0, (), jnp.float32)
    gain_two = jnp.clip(1.0 + 0.1 * jax.random.normal(splits[12], (D,), jnp.float32), 0.5, 1.5)
    shift_two = noise(splits[13], (D,), 0.5, 3.0, (), jnp.float32)
    return dict(tokens=tokens, cotangent=cotangent, query_key_value_weight=query_key_value_weight, qv_bias=qv_bias, attention_out_weight=attention_out_weight, attention_out_bias=attention_out_bias, gain_one=gain_one, shift_one=shift_one, up_projection_weight=up_projection_weight, input_ffn_bias=input_ffn_bias, down_projection_weight=down_projection_weight, output_ffn_bias=output_ffn_bias, gain_two=gain_two, shift_two=shift_two)


@jax.custom_vjp
def lowered_input(v):
    return lax.optimization_barrier(v.astype(jnp.bfloat16)).astype(jnp.float32)

@jax.custom_vjp
def lowered_backward(v):
    return v

def low_keep(v):
    return (lowered_input(v), None)

def low_pass(kept, grad):
    return (grad,)

def back_keep(v):
    return (v, None)

def back_low(kept, grad):
    return (lowered_input(grad),)
lowered_input.defvjp(low_keep, low_pass)
lowered_backward.defvjp(back_keep, back_low)
epsilon = 1e-06

def layer_norm(hidden_in, norm_gain, norm_shift):
    centred = hidden_in - lax.optimization_barrier(jnp.mean(hidden_in, axis=-1, keepdims=True))
    inverse = lax.rsqrt(lax.optimization_barrier(jnp.mean(centred * centred, axis=-1, keepdims=True)) + epsilon)
    return centred * inverse * norm_gain + norm_shift

def attend_one(operands):
    query_seq, key_seq, value_seq = operands
    scores = lowered_backward(jnp.einsum('qhe,khe->hqk', query_seq, key_seq, precision=lax.Precision.HIGHEST) * (1.0 / math.sqrt(HD)))
    top_score = lax.optimization_barrier(jnp.max(scores, axis=-1, keepdims=True))
    expo_score = jnp.exp(scores - top_score)
    weights_soft = expo_score / lax.optimization_barrier(jnp.sum(expo_score, axis=-1, keepdims=True))
    return jnp.einsum('hqk,khe->qhe', lowered_input(weights_soft), value_seq, precision=lax.Precision.HIGHEST)

def forward_layer(input_token_group, query_key_value_weight, qv_bias, attention_out_weight, attention_out_bias, gain_one, shift_one, up_projection_weight, input_ffn_bias, down_projection_weight, output_ffn_bias, gain_two, shift_two):
    group_size = input_token_group.shape[0]
    bias_row_list = jnp.stack([qv_bias[0], jnp.zeros_like(qv_bias[0]), qv_bias[1]])
    query_key_value_result = jnp.einsum('tmf,fgp->tmgp', input_token_group, query_key_value_weight, precision=lax.Precision.HIGHEST) + bias_row_list
    query_key_value_result = lowered_input(lowered_backward(query_key_value_result))
    queries = query_key_value_result[:, :, 0].reshape(group_size, SEQ_LEN, H, HD)
    keys = query_key_value_result[:, :, 1].reshape(group_size, SEQ_LEN, H, HD)
    values = query_key_value_result[:, :, 2].reshape(group_size, SEQ_LEN, H, HD)
    mixed_output = lax.map(jax.checkpoint(attend_one), (queries, keys, values)).reshape(group_size, SEQ_LEN, D)
    mixed_output = lowered_input(lowered_backward(mixed_output))
    attention_block = lowered_backward(jnp.einsum('zhn,np->zhp', mixed_output, attention_out_weight, precision=lax.Precision.HIGHEST) + attention_out_bias)
    first_output_result = layer_norm(input_token_group + attention_block, gain_one, shift_one)
    preactivation = lowered_backward(jnp.einsum('yjp,pa->yja', lowered_input(first_output_result), up_projection_weight, precision=lax.Precision.HIGHEST) + input_ffn_bias)
    hidden_state = lowered_input(jax.nn.gelu(preactivation, approximate=False))
    feedforward_block = lowered_backward(jnp.einsum('mtv,ve->mte', hidden_state, down_projection_weight, precision=lax.Precision.HIGHEST) + output_ffn_bias)
    return layer_norm(first_output_result + feedforward_block, gain_two, shift_two)

def reference(tokens, cotangent, query_key_value_weight, qv_bias, attention_out_weight, attention_out_bias, gain_one, shift_one, up_projection_weight, input_ffn_bias, down_projection_weight, output_ffn_bias, gain_two, shift_two):
    params = tuple((member.astype(jnp.float32) for member in (query_key_value_weight, qv_bias, attention_out_weight, attention_out_bias, gain_one, shift_one, up_projection_weight, input_ffn_bias, down_projection_weight, output_ffn_bias, gain_two, shift_two)))
    group_size = math.gcd(SEQS, max(1, 4096 // SEQ_LEN))
    group_count = SEQS // group_size
    token_groups = tokens.astype(jnp.float32).reshape(group_count, group_size, SEQ_LEN, D)
    cot_groups = cotangent.astype(jnp.float32).reshape(group_count, group_size, SEQ_LEN, D)

    def one_group(running, operands):
        input_token_group, cot_group = operands
        result, pullback = jax.vjp(forward_layer, input_token_group, *params)
        grads = pullback(cot_group)
        updated = tuple((running_sum + new_term for running_sum, new_term in zip(running, grads[1:])))
        return (updated, (result.astype(jnp.bfloat16), grads[0].astype(jnp.bfloat16)))
    start = tuple((jnp.zeros_like(member) for member in params))
    totals, (outputs, grad_tokens) = lax.scan(one_group, start, (token_groups, cot_groups))
    output = outputs.reshape(SEQS, SEQ_LEN, D)
    input_grad = grad_tokens.reshape(SEQS, SEQ_LEN, D)
    return (output, input_grad, totals[0], totals[1], totals[2], totals[3], totals[4], totals[5], totals[6], totals[7], totals[8], totals[9], totals[10], totals[11])
```

```python
import functools
import math

import jax
import jax.numpy as jnp
from jax import lax
from jax.experimental import pallas as pl
from jax.experimental.pallas import tpu as pltpu
from jax.sharding import PartitionSpec as P

HD = 64
SCALE = 1.0 / math.sqrt(HD)
SCALE_LOG2 = SCALE * math.log2(math.e)
EPS = 1e-06
BF = jnp.bfloat16
F32 = jnp.float32
NT = (((1,), (1,)), ((), ()))
TN = (((0,), (0,)), ((), ()))
NN = (((1,), (0,)), ((), ()))


def mm(a, b, dims=NN):
    return lax.dot_general(a, b, dims, preferred_element_type=F32)


def attend_fwd_kernel(q_ref, k_ref, v_ref, o_ref, l_ref):
    outs, logs = [], []
    for h in range(q_ref.shape[1] // HD):
        cols = slice(h * HD, (h + 1) * HD)
        scores = mm(q_ref[:, cols], k_ref[:, cols], NT)
        top = jnp.max(scores, axis=1, keepdims=True)
        expo = jnp.exp2((scores - top) * SCALE_LOG2)
        total = jnp.sum(expo, axis=1, keepdims=True)
        outs.append(mm(expo.astype(BF), v_ref[:, cols]) / total)
        logs.append(top * SCALE_LOG2 + jnp.log2(total))
    o_ref[...] = jnp.concatenate(outs, axis=1).astype(BF)
    l_ref[...] = jnp.concatenate(logs, axis=1).T


def attend_fwd(q, k, v, block=256):
    nq, w = q.shape
    nk = k.shape[0]
    heads = w // HD
    q_spec = pl.BlockSpec((block, w), lambda i: (i, 0))
    k_spec = pl.BlockSpec((nk, w), lambda i: (0, 0))
    return pl.pallas_call(
        attend_fwd_kernel,
        grid=(nq // block,),
        in_specs=[q_spec, k_spec, k_spec],
        out_specs=[q_spec, pl.BlockSpec((heads, block), lambda i: (0, i))],
        out_shape=[
            jax.ShapeDtypeStruct((nq, w), BF),
            jax.ShapeDtypeStruct((heads, nq), F32),
        ],
        cost_estimate=pl.CostEstimate(
            flops=16 * nq * nk * w,
            bytes_accessed=2 * w * (2 * nq + 2 * nk),
            transcendentals=nq * nk * heads,
        ),
        name="attend_fwd",
    )(q, k, v)


def attend_bwd_kernel(q_ref, k_ref, v_ref, g_ref, l_ref, ik_ref, iv_ref, dq_ref, dk_ref, dv_ref):
    dqs, dks, dvs = [], [], []
    for h in range(q_ref.shape[1] // HD):
        cols = slice(h * HD, (h + 1) * HD)
        q, k, v, g = q_ref[:, cols], k_ref[:, cols], v_ref[:, cols], g_ref[:, cols]
        probs = jnp.exp2(mm(k, q, NT) * SCALE_LOG2 - l_ref[h : h + 1, :])
        prod = probs * mm(v, g, NT)
        inner = jnp.sum(prod, axis=0, keepdims=True)
        grad_scores = (prod - probs * inner).astype(BF)
        dvs.append(mm(probs.astype(BF), g))
        dks.append(mm(grad_scores, q))
        dqs.append(mm(k, grad_scores, TN))
    dq_ref[...] = (jnp.concatenate(dqs, axis=0) * SCALE).T.astype(BF)
    dk = jnp.concatenate(dks, axis=1) * SCALE
    dv = jnp.concatenate(dvs, axis=1)

    @pl.when(pl.program_id(0) == 0)
    def _():
        dk_ref[...] = ik_ref[...] + dk
        dv_ref[...] = iv_ref[...] + dv

    @pl.when(pl.program_id(0) > 0)
    def _():
        dk_ref[...] += dk
        dv_ref[...] += dv


def attend_bwd(q, k, v, g, logs, start_k, start_v, block=256):
    nq, w = q.shape
    nk = k.shape[0]
    heads = w // HD
    q_spec = pl.BlockSpec((block, w), lambda i: (i, 0))
    k_spec = pl.BlockSpec((nk, w), lambda i: (0, 0))
    return pl.pallas_call(
        attend_bwd_kernel,
        grid=(nq // block,),
        in_specs=[q_spec, k_spec, k_spec, q_spec]
        + [pl.BlockSpec((heads, block), lambda i: (0, i)), k_spec, k_spec],
        out_specs=[q_spec, k_spec, k_spec],
        out_shape=[
            jax.ShapeDtypeStruct((nq, w), BF),
            jax.ShapeDtypeStruct((nk, w), F32),
            jax.ShapeDtypeStruct((nk, w), F32),
        ],
        cost_estimate=pl.CostEstimate(
            flops=40 * nq * nk * w,
            bytes_accessed=2 * w * (3 * nq + 6 * nk),
            transcendentals=nq * nk * heads,
        ),
        name="attend_bwd",
    )(q, k, v, g, logs, start_k, start_v)


def swap(x, axis, size, mask):
    return lax.ppermute(x, axis, [(i, i ^ mask) for i in range(size)])


def pick(pair_first, pair_second, bit, axis):
    n = pair_first.shape[axis]
    ring = jnp.concatenate([pair_first, pair_second, pair_first], axis=axis)
    return lax.dynamic_slice_in_dim(ring, bit * n, 2 * n, axis)


def layer_norm(x, gain, shift):
    centred = x - jnp.mean(x, axis=-1, keepdims=True)
    inverse = lax.rsqrt(jnp.mean(centred * centred, axis=-1, keepdims=True) + EPS)
    normed = centred * inverse
    return normed * gain + shift, normed, inverse


def norm_back(g, normed, inverse):
    return inverse * (
        g
        - jnp.mean(g, axis=-1, keepdims=True)
        - normed * jnp.mean(g * normed, axis=-1, keepdims=True)
    )


def gelu_both(x):
    cdf = 0.5 * (1.0 + lax.erf(x * (1.0 / math.sqrt(2.0))))
    pdf = jnp.exp(-0.5 * x * x) * (1.0 / math.sqrt(2.0 * math.pi))
    return x * cdf, cdf + x * pdf


def body(sizes, *args):
    (
        tokens,
        cotangent,
        w_qkv,
        qv_bias,
        w_out,
        out_bias,
        gain_one,
        shift_one,
        w_up,
        up_bias,
        w_down,
        down_bias,
        gain_two,
        shift_two,
    ) = args
    n_f, n_c, n_t = sizes
    blocks, rows, width = tokens.shape
    wide = w_qkv.shape[2]
    half = rows // 2
    f = lax.axis_index("fsdp")
    z = lax.axis_index("context")
    core = lax.axis_index("tensor") % 2
    group = z // 2
    over_core = functools.partial(swap, axis="tensor", size=n_t, mask=1)
    over_y = functools.partial(swap, axis="tensor", size=n_t, mask=2)
    over_z1 = functools.partial(swap, axis="context", size=n_c, mask=1)
    over_z2 = functools.partial(swap, axis="context", size=n_c, mask=2)

    def gather_f(w, axis):
        if n_f != 2:
            return lax.all_gather(w, "fsdp", axis=axis, tiled=True)
        return pick(w, swap(w, "fsdp", n_f, 1), f, axis)

    both = jnp.stack([tokens, cotangent])
    mine = lax.dynamic_index_in_dim(both, group, 1, keepdims=False)
    give = lax.dynamic_index_in_dim(both, 1 - group, 1, keepdims=False)
    mine = pick(mine[:, :half], mine[:, half:], core, 1)
    give_half = lax.dynamic_slice_in_dim(give, core * half, half, 1)
    swapped_half = over_z2(give_half)
    tok_a, cot_a = mine[0], mine[1][:half]
    tok_b_half, cot_b = swapped_half[0], swapped_half[1]
    other_a_half = over_z1(tok_a[:half])
    other_b_half = over_z1(tok_b_half)
    fetched = jnp.stack([tok_b_half, other_a_half, other_b_half])
    from_core = over_core(fetched)
    tok_b = jnp.concatenate([fetched[0], from_core[0]])
    own = jnp.concatenate([tok_a, tok_b])
    other = jnp.concatenate([fetched[1], from_core[1], fetched[2], from_core[2]])

    qkv_w = gather_f(w_qkv.reshape(w_qkv.shape[0], 3 * wide), 0)
    out_w = gather_f(w_out, 1)
    up_w = gather_f(w_up, 0)
    down_w = gather_f(w_down, 1)
    out_chip = jnp.concatenate([out_w, over_core(out_w)])
    out_far = over_y(out_chip)

    bias_row = jnp.concatenate([qv_bias[0], jnp.zeros_like(qv_bias[0]), qv_bias[1]])
    qkv_own = (mm(own, qkv_w) + bias_row).astype(BF)
    kv_other = (mm(other, qkv_w[:, wide:]) + bias_row[wide:]).astype(BF)
    q = qkv_own[:, :wide]
    k = jnp.concatenate([qkv_own[:, wide : 2 * wide], kv_other[:, :wide]])
    v = jnp.concatenate([qkv_own[:, 2 * wide :], kv_other[:, wide:]])

    saved = []
    for c in range(2):
        q_c = q[c * rows : (c + 1) * rows]
        mixed, logs = attend_fwd(q_c, k, v)
        tok_own = (tok_a if c == 0 else tok_b)[:half]
        g = (cot_a if c == 0 else cot_b).astype(F32)
        near = jnp.concatenate([mixed[:half], over_core(mixed[half:])], axis=1)
        far = over_y(near)
        attn = mm(near, out_chip) + mm(far, out_far)
        y_one, norm_one, inv_one = layer_norm(
            tok_own.astype(F32) + (attn + out_bias), gain_one, shift_one
        )
        y_low = y_one.astype(BF)
        y_all = jnp.concatenate([y_low, over_core(y_low)])
        hidden, slope = gelu_both(mm(y_all, up_w) + up_bias)
        hidden = hidden.astype(BF)
        part = mm(hidden, down_w)
        near_sum = (part[:half] + over_core(part[half:].astype(BF)).astype(F32)).astype(BF)
        ffn = near_sum.astype(F32) + over_y(near_sum).astype(F32)
        result, norm_two, inv_two = layer_norm(y_one + (ffn + down_bias), gain_two, shift_two)
        out_c = result.astype(BF)
        g2_gain = jnp.sum(g * norm_two, axis=0)
        g2_shift = jnp.sum(g, axis=0)
        grad_second = norm_back(g * gain_two, norm_two, inv_two)
        grad_ffn = grad_second.astype(BF)
        d_down_bias = jnp.sum(grad_ffn.astype(F32), axis=0)
        grad_ffn_all = jnp.concatenate([grad_ffn, over_core(grad_ffn)])
        d_down = mm(hidden, grad_ffn_all, TN)
        grad_pre = (mm(grad_ffn_all, down_w, NT) * slope).astype(BF)
        d_up_bias = jnp.sum(grad_pre.astype(F32), axis=0)
        d_up = mm(y_all, grad_pre, TN)
        part = mm(grad_pre, up_w, NT)
        near_sum = (part[:half] + over_core(part[half:].astype(BF)).astype(F32)).astype(BF)
        grad_y = grad_second + (near_sum.astype(F32) + over_y(near_sum).astype(F32))
        g1_gain = jnp.sum(grad_y * norm_one, axis=0)
        g1_shift = jnp.sum(grad_y, axis=0)
        grad_first = norm_back(grad_y * gain_one, norm_one, inv_one)
        grad_attn = grad_first.astype(BF)
        d_out_bias = jnp.sum(grad_attn.astype(F32), axis=0)
        grad_attn_all = jnp.concatenate([grad_attn, over_core(grad_attn)])
        d_out = mm(mixed, grad_attn_all, TN)
        grad_mixed = mm(grad_attn_all, out_w, NT).astype(BF)
        saved.append(
            dict(
                q=q_c,
                logs=logs,
                grad_mixed=grad_mixed,
                out=out_c,
                grad_first=grad_first,
                d_down=d_down,
                d_up=d_up,
                d_out=d_out,
                sums=jnp.stack(
                    [d_out_bias, g1_gain, g1_shift, d_down_bias, g2_gain, g2_shift]
                ),
                d_up_bias=d_up_bias,
            )
        )
    first, second = saved

    def reduce_weight(total, axis):
        n = total.shape[axis] // n_f
        if n_f == 2:
            keep = lax.dynamic_slice_in_dim(total, f * n, n, axis)
            send = lax.dynamic_slice_in_dim(total, (1 - f) * n, n, axis)
            keep = keep + swap(send.astype(BF), "fsdp", n_f, 1).astype(F32)
        else:
            keep = lax.psum_scatter(total, "fsdp", scatter_dimension=axis, tiled=True)
        m = keep.shape[0] // 2
        low = z % 2
        near = lax.dynamic_slice_in_dim(keep, low * m, m, 0)
        near = near + over_z1(
            lax.dynamic_slice_in_dim(keep, (1 - low) * m, m, 0).astype(BF)
        ).astype(F32)
        m = m // 2
        quarter = lax.dynamic_slice_in_dim(near, group * m, m, 0)
        quarter = quarter + over_z2(
            lax.dynamic_slice_in_dim(near, (1 - group) * m, m, 0).astype(BF)
        ).astype(F32)
        quarter = quarter.astype(BF)
        near = pick(quarter, over_z2(quarter), group, 0)
        return pick(near, over_z1(near), low, 0).astype(F32)

    owned_down = reduce_weight(first["d_down"] + second["d_down"], 1)
    owned_up = reduce_weight(first["d_up"] + second["d_up"], 0)

    zero = jnp.zeros(k.shape, F32)
    dq_a, dk, dv = attend_bwd(first["q"], k, v, first["grad_mixed"], first["logs"], zero, zero)
    dq_b, dk, dv = attend_bwd(second["q"], k, v, second["grad_mixed"], second["logs"], dk, dv)
    dkv = jnp.concatenate([dk, dv], axis=1)
    dkv = dkv[: 2 * rows] + over_z1(dkv[2 * rows :].astype(BF)).astype(F32)
    dqkv = jnp.concatenate([jnp.concatenate([dq_a, dq_b]), dkv.astype(BF)], axis=1)
    column_sums = jnp.sum(dqkv.astype(F32), axis=0)
    d_qkv = mm(own, dqkv, TN)
    owned_out = reduce_weight(first["d_out"] + second["d_out"], 1)
    owned_qkv = reduce_weight(d_qkv, 0).reshape(w_qkv.shape)

    def give_back(mine_half, swapped_back):
        pair = jnp.stack([mine_half, swapped_back])
        whole = pick(pair, over_core(pair), core, 1)
        return pick(whole[:1], whole[1:], group, 0)

    output = give_back(first["out"], over_z2(second["out"]))
    grads = []
    for c, item in ((1, second), (0, first)):
        part = mm(dqkv[c * rows : (c + 1) * rows], qkv_w, NT)
        near_sum = (part[:half] + over_core(part[half:].astype(BF)).astype(F32)).astype(BF)
        total = near_sum.astype(F32) + over_y(near_sum).astype(F32)
        grads.append((item["grad_first"] + total).astype(BF))
    input_grad = give_back(grads[1], over_z2(grads[0]))

    six = first["sums"] + second["sums"]
    six = six + over_core(six)
    last = jnp.concatenate(
        [column_sums[:wide], column_sums[2 * wide :], jnp.zeros(width - 2 * wide, F32)]
    )
    small = jnp.concatenate([six, (first["d_up_bias"] + second["d_up_bias"])[None], last[None]])
    small = small + swap(small, "fsdp", n_f, 1) if n_f == 2 else lax.psum(small, "fsdp")
    small = small + over_z1(small)
    small = small + over_z2(small)
    return (
        output,
        input_grad,
        owned_qkv,
        small[7, : 2 * wide].reshape(2, wide),
        owned_out,
        small[0],
        small[1],
        small[2],
        owned_up,
        small[6],
        owned_down,
        small[3],
        small[4],
        small[5],
    )


def solution(mesh):
    sizes = tuple(mesh.shape[name] for name in ("fsdp", "context", "tensor"))
    specs = (
        P("fsdp", None, "tensor"),
        P(None, "tensor"),
        P("tensor", "fsdp"),
        P(),
        P(),
        P(),
        P("fsdp", "tensor"),
        P("tensor"),
        P("tensor", "fsdp"),
        P(),
        P(),
        P(),
    )
    rows = P("fsdp", "context", None)
    return jax.shard_map(
        functools.partial(body, sizes),
        mesh=mesh,
        in_specs=(rows, rows) + specs,
        out_specs=(rows, rows) + specs,
        check_vma=False,
    )
```

```python
import functools
import math

import jax
import jax.numpy as jnp
from jax import lax
from jax.experimental import pallas as pl
from jax.experimental.pallas import tpu as pltpu
from jax.sharding import PartitionSpec as P

HD = 64
SCALE = 1.0 / math.sqrt(HD)
SCALE_LOG2 = SCALE * math.log2(math.e)
EPS = 1e-06
BF = jnp.bfloat16
F32 = jnp.float32
NT = (((1,), (1,)), ((), ()))
TN = (((0,), (0,)), ((), ()))
NN = (((1,), (0,)), ((), ()))


def mm(a, b, dims=NN):
    return lax.dot_general(a, b, dims, preferred_element_type=F32)


def shaped(shape, dtype):
    return jax.ShapeDtypeStruct(shape, dtype)


def call(kernel, outs, *operands, name, limit=16, **extra):
    return pl.pallas_call(
        kernel,
        out_shape=list(outs),
        cost_estimate=pl.CostEstimate(flops=1, bytes_accessed=1, transcendentals=0),
        compiler_params=pltpu.CompilerParams(vmem_limit_bytes=limit << 20),
        name=name,
        **extra,
    )(*operands)


SMEM = pl.BlockSpec(memory_space=pltpu.SMEM)
VMEM = pl.BlockSpec(memory_space=pltpu.VMEM)


def scalar_call(kernel, outs, scalars, *operands, **kw):
    specs = [SMEM] + [VMEM] * len(operands)
    return call(kernel, outs, scalars, *operands, in_specs=specs, **kw)


def qkv_kernel(*refs):
    rows, (w_ref, b_ref, q_ref, k_ref, v_ref) = refs[:8], refs[8:]
    n = rows[0].shape[0]
    wide = q_ref.shape[1]
    for i, ref in enumerate(rows):
        here = slice(i * n, (i + 1) * n)
        skip = 0 if i < 4 else wide
        full = (mm(ref[...], w_ref[:, skip:]) + b_ref[:, skip:]).astype(BF)
        if i < 4:
            q_ref[here, :] = full[:, :wide]
        k_ref[here, :] = full[:, wide - skip : 2 * wide - skip]
        v_ref[here, :] = full[:, 2 * wide - skip :]


def attend_fwd_kernel(chunk, *refs):
    q_ref, k_ref, v_ref = refs[:3]
    o_ref, p_ref, f_ref, l_ref = refs[-4:]
    outs, logs = [], []
    for h in range(q_ref.shape[1] // HD):
        cols = slice(h * HD, (h + 1) * HD)
        scores = mm(q_ref[:, cols], k_ref[:, cols], NT)
        top = jnp.max(scores, axis=1, keepdims=True)
        expo = jnp.exp2((scores - top) * SCALE_LOG2)
        total = jnp.sum(expo, axis=1, keepdims=True)
        outs.append(mm(expo.astype(BF), v_ref[:, cols]) / total)
        logs.append(top * SCALE_LOG2 + jnp.log2(total))
    mixed = jnp.concatenate(outs, axis=1)
    f_ref[...] = mixed
    l_ref[...] = jnp.concatenate(logs, axis=1).T
    for step, ref in enumerate((o_ref, p_ref)):

        @pl.when(pl.program_id(0) == step)
        def _():
            ref[...] = mixed.astype(BF)


def attend_fwd(chunk, block, q, k, v, *before):
    nq, w = q.shape
    nk = k.shape[0]
    heads = w // HD
    q_spec = pl.BlockSpec((block, w), lambda i: (chunk * 2 + i, 0))
    l_spec = pl.BlockSpec((heads, block), lambda i: (0, chunk * 2 + i))
    o_spec = pl.BlockSpec((block, w), lambda i: (0, 0))
    k_spec = pl.BlockSpec((nk, w), lambda i: (0, 0))
    anywhere = pl.BlockSpec(memory_space=pl.ANY)
    return call(
        functools.partial(attend_fwd_kernel, chunk),
        [shaped((block, w), BF)] * 2 + [shaped((nq, w), F32), shaped((heads, nq), F32)],
        q,
        k,
        v,
        *before,
        name="attend_fwd",
        limit=24,
        grid=(2,),
        in_specs=[q_spec, k_spec, k_spec] + [anywhere] * len(before),
        out_specs=[o_spec, o_spec, q_spec, l_spec],
        input_output_aliases={3: 2, 4: 3} if before else {},
    )


def grad_mixed_kernel(*refs):
    gas, (w_ref, f_ref, g_ref, d_ref) = refs[:4], refs[4:]
    n = gas[0].shape[0]
    heads = w_ref.shape[0] // HD
    for i, ga in enumerate(gas):
        here = slice(i * n, (i + 1) * n)
        g = mm(ga[...], w_ref[...], NT).astype(BF)
        g_ref[here, :] = g
        prod = (g.astype(F32) * f_ref[here, :]).T
        d_ref[:, here] = jnp.concatenate(
            [jnp.sum(prod[h * HD : (h + 1) * HD], axis=0, keepdims=True) for h in range(heads)]
        )


def attend_bwd_kernel(heads, first, last, split, *refs):
    q_ref, k_ref, v_ref, g_ref, l_ref, d_ref = refs[:6]
    add_ref = refs[6] if not first else None
    dq_ref, outs, acc = refs[6 + (not first)], refs[7 + (not first) : -1], refs[-1]
    dqs, dks, dvs = [], [], []
    for h in heads:
        cols = slice(h * HD, (h + 1) * HD)
        q, k, v, g = q_ref[:, cols], k_ref[:, cols], v_ref[:, cols], g_ref[:, cols]
        probs = jnp.exp2(mm(k, q, NT) * SCALE_LOG2 - l_ref[h : h + 1, :])
        grad_scores = (probs * (mm(v, g, NT) - d_ref[h : h + 1, :])).astype(BF)
        dvs.append(mm(probs.astype(BF), g))
        dks.append(mm(grad_scores, q) * SCALE)
        dqs.append(mm(k, grad_scores, TN))
    dq = (dqs[0] if len(dqs) == 1 else jnp.concatenate(dqs, axis=0)).T
    if not first:
        dq = dq + add_ref[...]
    dq_ref[...] = (dq * SCALE).astype(BF) if last else dq
    dkv = jnp.concatenate(dks + dvs, axis=1)
    step = pl.program_id(0)

    @pl.when(step == 0)
    def _():
        acc[...] = dkv

    @pl.when(step > 0)
    def _():
        acc[...] += dkv

    @pl.when(step == pl.num_programs(0) - 1)
    def _():
        n = acc.shape[0] // len(outs)
        for i, ref in enumerate(outs):
            ref[...] = acc[i * n : (i + 1) * n].astype(BF)


def attend_bwd(heads, key_block, key_rows, split, q, k, v, g, logs, inner, *add, last=True, block=256):
    nq, w = q.shape
    n = len(heads) * HD
    q_spec = pl.BlockSpec((block, w), lambda i: (i, 0))
    k_spec = pl.BlockSpec((key_rows, w), lambda i: (key_block, 0))
    n_spec = pl.BlockSpec((block, n), lambda i: (i, 0))
    l_spec = pl.BlockSpec((logs.shape[0], block), lambda i: (0, i))
    whole = pl.BlockSpec((key_rows // split, 2 * n), lambda i: (0, 0))
    return call(
        functools.partial(attend_bwd_kernel, heads, not add, last, split),
        [shaped((nq, n), BF if last else F32)] + [shaped((key_rows // split, 2 * n), BF)] * split,
        q,
        k,
        v,
        g,
        logs,
        inner,
        *add,
        name="attend_bwd",
        limit=36,
        grid=(nq // block,),
        in_specs=[q_spec, k_spec, k_spec, q_spec, l_spec, l_spec] + [n_spec] * len(add),
        out_specs=[n_spec] + [whole] * split,
        scratch_shapes=[pltpu.VMEM((key_rows, 2 * n), F32)],
    )


def normed(x):
    centred = x - jnp.mean(x, axis=-1, keepdims=True)
    inverse = lax.rsqrt(jnp.mean(centred * centred, axis=-1, keepdims=True) + EPS)
    return centred * inverse, inverse


def norm_back(g, norm, inverse):
    return inverse * (
        g
        - jnp.mean(g, axis=-1, keepdims=True)
        - norm * jnp.mean(g * norm, axis=-1, keepdims=True)
    )


def down_rows(*terms):
    return jnp.concatenate([jnp.sum(t, axis=0, keepdims=True) for t in terms], axis=0)


def lanes(ref, index, size):
    return ref[:, pl.ds(pl.multiple_of(index * size, 128), size)]


def norm_one_kernel(m0, m1, m2, m3, w0, w1, w2, w3, t_ref, p_ref, y_ref, low_ref, n_ref, i_ref):
    near = mm(m0[...], w0[...]) + mm(m1[...], w1[...])
    far = mm(m2[...], w2[...]) + mm(m3[...], w3[...])
    norm, inverse = normed(t_ref[...].astype(F32) + ((near + far) + p_ref[0:1, :]))
    y = norm * p_ref[1:2, :] + p_ref[2:3, :]
    y_ref[...] = y
    low_ref[...] = y.astype(BF)
    n_ref[...] = norm
    i_ref[...] = inverse


def ffn_kernel(s_ref, y_ref, up_own, up_far, b_ref, down_own, down_far, h_ref, sl_ref, p_ref):
    f = s_ref[0]
    size = up_own.shape[0]
    x = mm(lanes(y_ref, f, size), up_own[...]) + mm(lanes(y_ref, 1 - f, size), up_far[...]) + b_ref[...]
    cdf = 0.5 * (1.0 + lax.erf(x * (1.0 / math.sqrt(2.0))))
    pdf = jnp.exp(-0.5 * x * x) * (1.0 / math.sqrt(2.0 * math.pi))
    sl_ref[...] = cdf + x * pdf
    hidden = (x * cdf).astype(BF)
    h_ref[...] = hidden
    for part, ref in ((f, down_own), (1 - f, down_far)):
        here = pl.ds(pl.multiple_of(part * size, 128), size)
        p_ref[:, here] = mm(hidden, ref[...]).astype(p_ref.dtype)


def norm_two_kernel(near, far, y_ref, g_ref, p_ref, o_ref, gs_ref, gf_ref, sums):
    ffn = near[...].astype(F32) + far[...].astype(F32)
    norm, inverse = normed(y_ref[...] + (ffn + p_ref[0:1, :]))
    o_ref[...] = (norm * p_ref[1:2, :] + p_ref[2:3, :]).astype(BF)
    g = g_ref[...].astype(F32)
    grad = norm_back(g * p_ref[1:2, :], norm, inverse)
    low = grad.astype(BF)
    gs_ref[...] = grad
    gf_ref[...] = low
    sums[...] = down_rows(low.astype(F32), g * norm, g)


def ffn_back_kernel(s_ref, g_ref, down_own, down_far, sl_ref, up_own, up_far, gp_ref, p_ref, sums):
    f = s_ref[0]
    size = up_own.shape[0]
    grad = mm(lanes(g_ref, f, size), down_own[...], NT) + mm(lanes(g_ref, 1 - f, size), down_far[...], NT)
    low = (grad * sl_ref[...]).astype(BF)
    gp_ref[...] = low
    sums[...] = down_rows(low.astype(F32))
    for part, ref in ((f, up_own), (1 - f, up_far)):
        here = pl.ds(pl.multiple_of(part * size, 128), size)
        p_ref[:, here] = mm(low, ref[...], NT).astype(p_ref.dtype)


def norm_one_back_kernel(gs_ref, near, far, n_ref, i_ref, p_ref, g_ref, low_ref, sums):
    grad_y = gs_ref[...] + (near[...].astype(F32) + far[...].astype(F32))
    norm = n_ref[...]
    grad = norm_back(grad_y * p_ref[1:2, :], norm, i_ref[...])
    low = grad.astype(BF)
    g_ref[...] = grad
    low_ref[...] = low
    sums[...] = down_rows(low.astype(F32), grad_y * norm, grad_y)


def input_part_kernel(first_row, dq1, dkv1, m1, dq2, dkv2, m2, w_ref, o_ref, p_ref, sums):
    n = o_ref.shape[0]
    w1, w2 = dq1.shape[1], dq2.shape[1]
    total = None
    for part, ref in enumerate((o_ref, p_ref)):
        here = slice(first_row + part * n, first_row + (part + 1) * n)
        low1 = (dkv1[here, :].astype(F32) + m1[here, :].astype(F32)).astype(BF)
        low2 = (dkv2[here, :].astype(F32) + m2[here, :].astype(F32)).astype(BF)
        grads = jnp.concatenate(
            [dq1[here, :], dq2[here, :], low1[:, :w1], low2[:, :w2], low1[:, w1:], low2[:, w2:]], axis=1
        )
        ref[...] = mm(grads, w_ref[...], NT).astype(ref.dtype)
        column = jnp.sum(grads.astype(F32), axis=0, keepdims=True)
        total = column if total is None else total + column
    sums[...] = total


def near_kernel(a_ref, b_ref, o_ref):
    o_ref[...] = (a_ref[...] + b_ref[...].astype(F32)).astype(BF)


def input_grad_kernel(g_ref, a_ref, b_ref, o_ref):
    o_ref[...] = (g_ref[...] + (a_ref[...].astype(F32) + b_ref[...].astype(F32))).astype(BF)


def place_kernel(s_ref, a, b, c, d, o_ref):
    n = a.shape[0]
    group, core = s_ref[2], s_ref[3]
    for block, half, ref in ((group, core, a), (group, 1 - core, b), (1 - group, core, c), (1 - group, 1 - core, d)):
        o_ref[block, pl.ds(pl.multiple_of(half * n, n), n), :] = ref[...]


def pack_kernel(a0, a1, b0, b1, u0, u1, u2, u3, o_ref):
    o_ref[0:3, :] = a0[...] + a1[...]
    o_ref[3:6, :] = b0[...] + b1[...]
    o_ref[6:7, :] = u0[...] + u1[...] + u2[...] + u3[...]
    o_ref[7:8, :] = jnp.zeros_like(u0)


def pack_two_kernel(own, moved, s0, s1, o_ref):
    wide = s0.shape[1] // 3
    o_ref[0:6, :] = own[0:6, :] + moved[0:6, :]
    o_ref[6:7, :] = own[6:7, :]
    cols = s0[...] + s1[...]
    rest = jnp.zeros((1, o_ref.shape[1] - 2 * wide), F32)
    o_ref[7:8, :] = jnp.concatenate([cols[:, :wide], cols[:, 2 * wide :], rest], axis=1)


def add_kernel(a, b, o_ref):
    o_ref[...] = a[...] + b[...]


def store_quarters(acc, ref, z, start=0):
    n = acc.shape[0] // 4
    for j in range(4):
        ref[j ^ z, start : start + n, :] = acc[j * n : (j + 1) * n].astype(ref.dtype)


def up_grad_kernel(s_ref, *refs):
    ys, gs, (keep, send) = refs[:4], refs[4:8], refs[8:]
    f, z = s_ref[0], s_ref[1]
    size = ys[0].shape[1] // 2
    for out, part in ((send, 1 - f), (keep, f)):
        acc = sum(mm(lanes(y, part, size), g[...], TN) for y, g in zip(ys, gs))
        store_quarters(acc, out, z)


def down_grad_kernel(s_ref, *refs):
    hs, gs, (keep, send) = refs[:4], refs[4:8], refs[8:]
    f, z = s_ref[0], s_ref[1]
    size = gs[0].shape[1] // 2
    for out, part in ((send, 1 - f), (keep, f)):
        acc = sum(mm(h[...], lanes(g, part, size), TN) for h, g in zip(hs, gs))
        store_quarters(acc, out, z)


def qkv_grad_kernel(with_out, s_ref, *refs):
    rows, (dq, own_ref, far_ref), more, (keep, send) = refs[:8], refs[8:11], refs[11:-2], refs[-2:]
    f, z = s_ref[0], s_ref[1]
    size = rows[0].shape[1] // 2
    n = rows[0].shape[0]
    m = dq.shape[1]
    for out, part in ((send, 1 - f), (keep, f)):
        acc = far = None
        for i in range(4):
            here = slice(i * n, (i + 1) * n)
            one = mm(lanes(rows[i], part, size), jnp.concatenate([dq[here, :], own_ref[here, :]], axis=1), TN)
            two = mm(lanes(rows[4 + i], part, size), far_ref[here, :], TN)
            acc = one if acc is None else acc + one
            far = two if far is None else far + two
        acc = jnp.concatenate([acc[:, :m], acc[:, m:] + far], axis=1)
        store_quarters(acc, out, z)
        if with_out:
            ms, gs = more[:4], more[4:]
            grad = sum(mm(a[...], lanes(g, part, size), TN) for a, g in zip(ms, gs))
            store_quarters(grad, out, z, acc.shape[0] // 4)


def first_step_kernel(keep, moved, a_ref, send):
    for i in range(2):
        a_ref[i] = keep[2 * i] + moved[2 * i].astype(F32)
        send[i] = (keep[2 * i + 1] + moved[2 * i + 1].astype(F32)).astype(BF)


def second_step_kernel(a, moved, a_ref, send):
    a_ref[...] = a[0] + moved[0].astype(F32)
    send[...] = (a[1] + moved[1].astype(F32)).astype(BF)


def fourth_step_kernel(a, moved, pair):
    pair[0] = a[...]
    pair[1] = moved[...]


def last_step_kernel(s_ref, pair, moved, *outs):
    z = s_ref[1]
    for j, (ref, i) in enumerate(((pair, 0), (moved, 0), (pair, 1), (moved, 1))):
        start = 0
        for out in outs:
            n = out.shape[1]
            out[j ^ z] = ref[i, start : start + n, :].astype(F32)
            start += n


def swap(x, axis, size, mask):
    return lax.ppermute(x, axis, [(i, i ^ mask) for i in range(size)])


def pick(first, second, bit, axis):
    n = first.shape[axis]
    ring = jnp.concatenate([first, second, first], axis=axis)
    return lax.dynamic_slice_in_dim(ring, bit * n, 2 * n, axis)


class Order:
    def __init__(self):
        self.done = None

    def __call__(self, fn, *operands):
        if self.done is not None:
            operands, _ = lax.optimization_barrier((operands, self.done))
        out = fn(*operands)
        self.done = out
        return out


class Reduction:
    def __init__(self, run, name, place, over_z1, over_z2, keep, moved, sizes):
        self.run, self.name, self.place = run, name, place
        self.z1, self.z2, self.sizes = over_z1, over_z2, sizes
        self.keep, self.moved, self.stage = keep, moved, 0

    def kernel(self, body, outs, *operands):
        name = f"{self.name}_{self.stage}"
        with jax.named_scope(name):
            return self.run(lambda *x: call(body, outs, *x, name=name), *operands)

    def step(self):
        self.stage += 1
        _, n, m = self.keep.shape
        with jax.named_scope(f"{self.name}_{self.stage}"):
            if self.stage == 1:
                outs = [shaped((2, n, m), F32), shaped((2, n, m), BF)]
                self.a, send = self.kernel(first_step_kernel, outs, self.keep, self.moved)
                self.moved = self.z1(send)
            elif self.stage == 2:
                outs = [shaped((n, m), F32), shaped((n, m), BF)]
                self.a, send = self.kernel(second_step_kernel, outs, self.a, self.moved)
                self.moved = self.z2(send)
            elif self.stage == 3:
                (self.a,) = self.kernel(near_kernel, [shaped((n, m), BF)], self.a, self.moved)
                self.moved = self.z2(self.a)
            elif self.stage == 4:
                (self.a,) = self.kernel(fourth_step_kernel, [shaped((2, n, m), BF)], self.a, self.moved)
                self.moved = self.z1(self.a)
            else:
                outs = [shaped((4, size, m), F32) for size in self.sizes]
                self.out = self.run(
                    lambda *x: scalar_call(last_step_kernel, outs, *x, name="owned"),
                    self.place,
                    self.a,
                    self.moved,
                )


def body(sizes, *args):
    (
        tokens,
        cotangent,
        w_qkv,
        qv_bias,
        w_out,
        out_bias,
        gain_one,
        shift_one,
        w_up,
        up_bias,
        w_down,
        down_bias,
        gain_two,
        shift_two,
    ) = args
    n_f, n_c, n_t = sizes
    _, rows, width = tokens.shape
    wide = w_qkv.shape[2]
    heads = wide // HD
    hidden_here = w_up.shape[1]
    half = rows // 2
    f = lax.axis_index("fsdp") if n_f == 2 else 0
    z = lax.axis_index("context")
    core = lax.axis_index("tensor") % 2
    group = z // 2
    over_core = functools.partial(swap, axis="tensor", size=n_t, mask=1)
    over_y = functools.partial(swap, axis="tensor", size=n_t, mask=2)
    over_both = functools.partial(swap, axis="tensor", size=n_t, mask=3)
    over_z1 = functools.partial(swap, axis="context", size=n_c, mask=1)
    over_z2 = functools.partial(swap, axis="context", size=n_c, mask=2)
    over_x = functools.partial(swap, axis="fsdp", size=n_f, mask=1)
    run = Order()

    def whole_f(w, axis):
        return lax.all_gather(w, "fsdp", axis=axis, tiled=True)

    def halves(w, axis):
        if n_f == 2:
            return w, over_x(w)
        w = whole_f(w, axis)
        return jnp.split(w, 2, axis=axis)

    def block_of(x, which, part):
        return lax.dynamic_slice(x, (which, part * half, 0), (1, half, width))[0]

    with jax.named_scope("arrive"):
        give = run(lambda t: block_of(t, 1 - group, core), tokens)
        b_own = over_z2(give)
        a_own = run(lambda t: block_of(t, group, core), tokens)
        oa_own = over_z1(a_own)
        (qkv_flat,) = run(lambda w: (w.reshape(w.shape[0], 3 * wide),), w_qkv)
        if n_f == 2:
            qkv_moved = over_x(qkv_flat)
        else:
            qkv_moved = whole_f(qkv_flat, 0)
        a_far, place, par_one, par_two, bias_row, up_row = run(
            lambda t, qb, ub, p1, p2: (
                block_of(t, group, 1 - core),
                jnp.stack([jnp.int32(f), z.astype(jnp.int32), group.astype(jnp.int32), core.astype(jnp.int32)]),
                jnp.stack(p1),
                jnp.stack(p2),
                jnp.concatenate([qb[0], jnp.zeros_like(qb[0]), qb[1]])[None],
                ub[None],
            ),
            tokens,
            qv_bias,
            up_bias,
            (out_bias, gain_one, shift_one),
            (down_bias, gain_two, shift_two),
        )
        qkv_w = run(lambda a, b: pick(a, b, f, 0) if n_f == 2 else b, qkv_flat, qkv_moved)
        w_out_later, _ = lax.optimization_barrier((w_out, qkv_w))
        out_moved = over_x(w_out_later) if n_f == 2 else whole_f(w_out_later, 1)
        out_w = run(lambda a, b: pick(a, b, f, 1) if n_f == 2 else b, w_out, out_moved)
        b_own, oa_own = run(lambda a, b: (a, b), b_own, oa_own)
        ob_own = over_z1(b_own)
        b_far, oa_far = over_core(b_own), over_core(oa_own)
        b_far, oa_far, out_later = run(lambda a, b, c: (a, b, c), b_far, oa_far, out_w)
        out_near, out_far, out_both = over_core(out_later), over_y(out_later), over_both(out_later)
        ob_own = run(lambda a: a, ob_own)
        ob_far = over_core(ob_own)
    own = [a_own, a_far, b_own, b_far]
    other = [oa_own, oa_far, ob_own, ob_far]
    total = 8 * half
    n_own = total // 2

    q, k, v = run(
        lambda *x: call(
            qkv_kernel,
            [shaped((n_own, wide), BF), shaped((total, wide), BF), shaped((total, wide), BF)],
            *x,
            name="qkv",
        ),
        *own,
        *other,
        qkv_w,
        bias_row,
    )
    w_up_later, w_down_later, _ = lax.optimization_barrier((w_up, w_down, q))
    with jax.named_scope("up_weight"):
        up_two = halves(w_up_later, 0)
    with jax.named_scope("down_weight"):
        down_two = halves(w_down_later, 1)

    mixed, pieces, shared = [], [], ()
    for c in range(2):
        with jax.named_scope(f"attend{c}"):
            mo, mp, *shared = run(lambda *x: attend_fwd(c, half, *x), q, k, v, *shared)
            mixed += [mo, mp]
            pieces.append((mo, over_core(mp), over_y(mo), over_both(mp)))
    mixed_f, logs = shared

    tok = (a_own, b_own)
    f_rows = shaped((half, width), F32)
    b_rows = shaped((half, width), BF)
    h_rows = shaped((half, hidden_here), BF)
    state = [dict(), dict()]

    def norm_one(c):
        with jax.named_scope(f"normone{c}"):
            s = state[c]
            outs = [f_rows, b_rows, f_rows, shaped((half, 1), F32)]
            s["y"], s["yo"], s["n1"], s["i1"] = run(
                lambda *x: call(norm_one_kernel, outs, *x, name="norm_one"),
                *pieces[c],
                out_w,
                out_near,
                out_far,
                out_both,
                tok[c],
                par_one,
            )
            s["yp"] = over_core(s["yo"])

    def feed(c, which, dtype):
        with jax.named_scope(f"feed{c}{which}"):
            s = state[c]
            outs = [h_rows, shaped((half, hidden_here), F32), shaped((half, width), dtype)]
            s["h" + which], s["s" + which], s["p" + which] = run(
                lambda *x: scalar_call(ffn_kernel, outs, *x, name="feed"),
                place,
                s["y" + which],
                *up_two,
                up_row,
                *down_two,
            )
            if which == "p":
                s["c2"] = over_core(s["pp"])

    def near_sum(c, name):
        with jax.named_scope(f"near{c}{name}"):
            s = state[c]
            (s["near" + name],) = run(
                lambda *x: call(near_kernel, [b_rows], *x, name="near"), s["po"], s["c" + name]
            )
            s["far" + name] = over_y(s["near" + name])

    def norm_two(c):
        with jax.named_scope(f"normtwo{c}"):
            s = state[c]
            outs = [b_rows, f_rows, b_rows, shaped((3, width), F32)]
            s["out"], s["gs"], s["gfo"], s["sum2"] = run(
                lambda *x: call(norm_two_kernel, outs, *x, name="norm_two"),
                s["near2"],
                s["far2"],
                s["y"],
                cot[c],
                par_two,
            )
            s["gfp"] = over_core(s["gfo"])

    def feed_back(c, which, dtype):
        with jax.named_scope(f"feedback{c}{which}"):
            s = state[c]
            outs = [h_rows, shaped((half, width), dtype), shaped((1, hidden_here), F32)]
            s["gp" + which], s["p" + which], s["sumu" + which] = run(
                lambda *x: scalar_call(ffn_back_kernel, outs, *x, name="feed_back"),
                place,
                s["gf" + which],
                *down_two,
                s["s" + which],
                *up_two,
            )
            if which == "p":
                s["c5"] = over_core(s["pp"])

    def norm_one_back(c):
        with jax.named_scope(f"normoneback{c}"):
            s = state[c]
            s["gfirst"], s["gao"], s["sum1"] = run(
                lambda *x: call(
                    norm_one_back_kernel,
                    [f_rows, b_rows, shaped((3, width), F32)],
                    *x,
                    name="norm_one_back",
                ),
                s["gs"],
                s["near5"],
                s["far5"],
                s["n1"],
                s["i1"],
                par_one,
            )
            s["gap"] = over_core(s["gao"])

    def weight_grad(kernel, operands, shape, name, parts):
        with jax.named_scope(name):
            keep, send = run(
                lambda *x: scalar_call(kernel, [shaped(shape, F32), shaped(shape, BF)], *x, name=name),
                place,
                *operands,
            )
            return Reduction(run, name, place, over_z1, over_z2, keep, over_x(send), parts)

    four = [(c, w) for c in range(2) for w in "op"]

    def pieces_of(name):
        return [state[c][name + w] for c, w in four]

    norm_one(0)
    with jax.named_scope("cotangent"):
        cot_in, _ = lax.optimization_barrier((cotangent, state[0]["y"]))
        cot_give, cot_a = run(
            lambda x: (block_of(x, 1 - group, core), block_of(x, group, core)), cot_in
        )
        cot = (cot_a, over_z2(cot_give))
    feed(0, "o", F32)
    feed(0, "p", BF)
    norm_one(1)
    near_sum(0, "2")
    feed(1, "o", F32)
    feed(1, "p", BF)
    near_sum(1, "2")
    norm_two(0)
    feed_back(0, "o", F32)
    feed_back(0, "p", BF)
    norm_two(1)
    near_sum(0, "5")
    feed_back(1, "o", F32)
    if n_f == 2:
        red_down = weight_grad(
            down_grad_kernel,
            pieces_of("h") + pieces_of("gf"),
            (4, hidden_here // 4, width // 2),
            "down_grad",
            [hidden_here // 4],
        )
    feed_back(1, "p", BF)
    near_sum(1, "5")
    if n_f == 2:
        red_up = weight_grad(
            up_grad_kernel,
            pieces_of("y") + pieces_of("gp"),
            (4, width // 8, hidden_here),
            "up_grad",
            [width // 8],
        )
    norm_one_back(0)
    norm_one_back(1)
    with jax.named_scope("smallpack"):
        (packed,) = run(
            lambda *x: call(pack_kernel, [shaped((8, width), F32)], *x, name="pack"),
            *[state[c][s] for s in ("sum1", "sum2") for c in range(2)],
            *pieces_of("sumu"),
        )
        packed_moved = over_core(packed)
    if n_f == 2:
        red_down.step()
    with jax.named_scope("outback"):
        out_b, _ = lax.optimization_barrier((state[1]["out"], packed))
        out_back = over_z2(out_b)
    grad_attn = pieces_of("ga")
    grad_mixed, inner = run(
        lambda *x: call(
            grad_mixed_kernel, [shaped((n_own, wide), BF), shaped((heads, n_own), F32)], *x, name="grad_mixed"
        ),
        *grad_attn,
        out_w,
        mixed_f,
    )

    early, late = tuple(range(heads - 1)), (heads - 1,)
    bwd_args = (q, k, v, grad_mixed, logs, inner)
    n_one, n_two = 3 * len(early) * HD, 3 * HD
    with jax.named_scope("back1"):
        dq1, own1, far1 = run(lambda *x: attend_bwd(early, 0, total, 2, *x), *bwd_args)
        moved1 = over_z1(far1)
    if n_f == 2:
        red_one = weight_grad(
            functools.partial(qkv_grad_kernel, True),
            own + other + [dq1, own1, far1] + mixed + grad_attn,
            (4, width // 8 + wide // 4, n_one),
            "one_grad",
            [width // 8, wide // 4],
        )
        red_down.step()
    with jax.named_scope("back2"):
        dq2, far2 = run(lambda *x: attend_bwd(late, 1, n_own, 1, *x, last=False), *bwd_args)
        moved2 = over_z1(far2)
    if n_f == 2:
        red_up.step()
    with jax.named_scope("back3"):
        dq2, own2 = run(lambda *x: attend_bwd(late, 0, n_own, 1, *x), *bwd_args, dq2)
    if n_f == 2:
        red_two = weight_grad(
            functools.partial(qkv_grad_kernel, False),
            own + other + [dq2, own2, far2],
            (4, width // 8, n_two),
            "two_grad",
            [width // 8],
        )

    item = [dict(), dict()]

    def input_part(c):
        with jax.named_scope(f"inputpart{c}"):
            s = item[c]
            outs = [f_rows, b_rows, shaped((1, 3 * wide), F32)]
            s["po"], pp, s["sums"] = run(
                lambda *x: call(
                    functools.partial(input_part_kernel, c * rows), outs, *x, name="input_part"
                ),
                dq1,
                own1,
                moved1,
                dq2,
                own2,
                moved2,
                qkv_w,
            )
            s["cp"] = over_core(pp)

    def input_near(c):
        with jax.named_scope(f"inputnear{c}"):
            s = item[c]
            (s["near"],) = run(
                lambda *x: call(near_kernel, [b_rows], *x, name="near"), s["po"], s["cp"]
            )
            s["far"] = over_y(s["near"])

    def input_last(c):
        with jax.named_scope(f"inputlast{c}"):
            s = item[c]
            (s["in"],) = run(
                lambda *x: call(input_grad_kernel, [b_rows], *x, name="input_grad"),
                state[c]["gfirst"],
                s["near"],
                s["far"],
            )

    def placed(a, b):
        return run(
            lambda *x: scalar_call(place_kernel, [shaped(tokens.shape, BF)], *x, name="place"),
            place,
            a,
            over_core(a),
            b,
            over_core(b),
        )[0]

    def add_small(x, moved):
        return run(lambda *x: call(add_kernel, [shaped(small.shape, F32)], *x, name="add"), x, moved)[0]

    input_part(1)
    input_part(0)
    input_near(1)
    input_near(0)
    with jax.named_scope("small"):
        (small,) = run(
            lambda *x: call(pack_two_kernel, [shaped((8, width), F32)], *x, name="pack_two"),
            packed,
            packed_moved,
            item[0]["sums"],
            item[1]["sums"],
        )
        small_moved = over_x(small) if n_f == 2 else lax.psum(small, "fsdp") - small
    if n_f == 2:
        red_down.step()
        red_one.step()
        red_two.step()
    with jax.named_scope("small"):
        small = add_small(small, small_moved)
        small_moved = over_z1(small)
    input_last(1)
    with jax.named_scope("inputback"):
        in_back = over_z2(item[1]["in"])
    if n_f == 2:
        red_down.step()
        red_up.step()
        red_one.step()
        red_two.step()
    with jax.named_scope("small"):
        small = add_small(small, small_moved)
        small_moved = over_z2(small)
    input_last(0)
    if n_f == 2:
        red_down.step()
        red_up.step()
        red_one.step()
        red_two.step()
    with jax.named_scope("small"):
        small = add_small(small, small_moved)
    if n_f == 2:
        red_up.step()
        red_one.step()
        red_two.step()
        red_up.step()
        red_one.step()
        red_two.step()
    with jax.named_scope("placeout"):
        output = placed(state[0]["out"], out_back)
    with jax.named_scope("placein"):
        input_grad = placed(item[0]["in"], in_back)

    with jax.named_scope("finish"):
        if n_f == 2:
            owned_up = red_up.out[0].reshape(w_up.shape)
            owned_down = red_down.out[0].reshape(w_down.shape)
            owned_out = red_one.out[1].reshape(w_out.shape)
            a = red_one.out[0].reshape(width // 2, 3, (heads - 1) * HD)
            b = red_two.out[0].reshape(width // 2, 3, HD)
            owned_qkv = jnp.concatenate([a, b], axis=2)
        else:

            def reduce_plain(left, right, axis):
                grad = mm(jnp.concatenate(left), jnp.concatenate(right), TN)
                keep = lax.psum_scatter(grad, "fsdp", scatter_dimension=axis, tiled=True)
                return lax.psum(keep, "context").astype(BF).astype(F32)

            zero = jnp.zeros((n_own, wide), BF)
            cut = len(early) * HD
            dk = [own1[:, :cut], own2[:, :HD], far1[:, :cut], far2[:, :HD]]
            dv = [own1[:, cut:], own2[:, HD:], far1[:, cut:], far2[:, HD:]]
            left = jnp.concatenate([dq1, dq2, *dk[:2], *dv[:2]], axis=1)
            right = jnp.concatenate([zero, *dk[2:], *dv[2:]], axis=1)
            owned_up = reduce_plain(pieces_of("y"), pieces_of("gp"), 0)
            owned_down = reduce_plain(pieces_of("h"), pieces_of("gf"), 1)
            owned_out = reduce_plain(mixed, grad_attn, 1)
            owned_qkv = reduce_plain(own + other, [left, right], 0).reshape(w_qkv.shape)
    return (
        output,
        input_grad,
        owned_qkv,
        small[7, : 2 * wide].reshape(2, wide),
        owned_out,
        small[0],
        small[1],
        small[2],
        owned_up,
        small[6],
        owned_down,
        small[3],
        small[4],
        small[5],
    )


def solution(mesh):
    sizes = tuple(mesh.shape[name] for name in ("fsdp", "context", "tensor"))
    specs = (
        P("fsdp", None, "tensor"),
        P(None, "tensor"),
        P("tensor", "fsdp"),
        P(),
        P(),
        P(),
        P("fsdp", "tensor"),
        P("tensor"),
        P("tensor", "fsdp"),
        P(),
        P(),
        P(),
    )
    rows = P("fsdp", "context", None)
    return jax.shard_map(
        functools.partial(body, sizes),
        mesh=mesh,
        in_specs=(rows, rows) + specs,
        out_specs=(rows, rows) + specs,
        check_vma=False,
    )
```

```python
import functools
import math

import jax
import jax.numpy as jnp
from jax import lax
from jax.experimental import pallas as pl
from jax.experimental.pallas import tpu as pltpu
from jax.sharding import PartitionSpec as P

HD = 64
SCALE = 1.0 / math.sqrt(HD)
SCALE_LOG2 = SCALE * math.log2(math.e)
EPS = 1e-06
BF = jnp.bfloat16
F32 = jnp.float32
NT = (((1,), (1,)), ((), ()))
TN = (((0,), (0,)), ((), ()))
NN = (((1,), (0,)), ((), ()))


def mm(a, b, dims=NN):
    return lax.dot_general(a, b, dims, preferred_element_type=F32)


def shaped(shape, dtype):
    return jax.ShapeDtypeStruct(shape, dtype)


def call(kernel, outs, *operands, name, limit=16, **extra):
    return pl.pallas_call(
        kernel,
        out_shape=list(outs),
        cost_estimate=pl.CostEstimate(flops=int(2e9), bytes_accessed=1, transcendentals=0),
        compiler_params=pltpu.CompilerParams(vmem_limit_bytes=limit << 20),
        name=name,
        **extra,
    )(*operands)


SMEM = pl.BlockSpec(memory_space=pltpu.SMEM)
VMEM = pl.BlockSpec(memory_space=pltpu.VMEM)


def scalar_call(kernel, outs, scalars, *operands, **kw):
    specs = [SMEM] + [VMEM] * len(operands)
    return call(kernel, outs, scalars, *operands, in_specs=specs, **kw)


def lanes(ref, index, size):
    return ref[:, pl.ds(pl.multiple_of(index * size, 128), size)]


def qkv_kernel(*refs):
    rows, (w_ref, b_ref, q_ref, k_ref, v_ref) = refs[:8], refs[8:]
    n = rows[0].shape[0]
    wide = q_ref.shape[1]
    for i, ref in enumerate(rows):
        here = slice(i * n, (i + 1) * n)
        skip = 0 if i < 4 else wide
        full = (mm(ref[...], w_ref[skip:, :], NT) + b_ref[:, skip:]).astype(BF)
        if i < 4:
            q_ref[here, :] = full[:, :wide]
        k_ref[here, :] = full[:, wide - skip : 2 * wide - skip]
        v_ref[here, :] = full[:, 2 * wide - skip :]


def attend_fwd_kernel(chunk, *refs):
    q_ref, k_ref, v_ref = refs[:3]
    o_ref, p_ref, f_ref, l_ref = refs[-4:]
    outs, logs = [], []
    for h in range(q_ref.shape[1] // HD):
        cols = slice(h * HD, (h + 1) * HD)
        scores = mm(q_ref[:, cols], k_ref[:, cols], NT)
        top = jnp.max(scores, axis=1, keepdims=True)
        expo = jnp.exp2((scores - top) * SCALE_LOG2)
        total = jnp.sum(expo, axis=1, keepdims=True)
        outs.append(mm(expo.astype(BF), v_ref[:, cols]) / total)
        logs.append(top * SCALE_LOG2 + jnp.log2(total))
    mixed = jnp.concatenate(outs, axis=1)
    f_ref[...] = mixed
    l_ref[...] = jnp.concatenate(logs, axis=1).T
    for step, ref in enumerate((o_ref, p_ref)):

        @pl.when(pl.program_id(0) == step)
        def _():
            ref[...] = mixed.astype(BF)


def attend_fwd(chunk, block, q, k, v, *before):
    nq, w = q.shape
    nk = k.shape[0]
    heads = w // HD
    q_spec = pl.BlockSpec((block, w), lambda i: (chunk * 2 + i, 0))
    l_spec = pl.BlockSpec((heads, block), lambda i: (0, chunk * 2 + i))
    o_spec = pl.BlockSpec((block, w), lambda i: (0, 0))
    k_spec = pl.BlockSpec((nk, w), lambda i: (0, 0))
    anywhere = pl.BlockSpec(memory_space=pl.ANY)
    return call(
        functools.partial(attend_fwd_kernel, chunk),
        [shaped((block, w), BF)] * 2 + [shaped((nq, w), F32), shaped((heads, nq), F32)],
        q,
        k,
        v,
        *before,
        name="attend_fwd",
        limit=24,
        grid=(2,),
        in_specs=[q_spec, k_spec, k_spec] + [anywhere] * len(before),
        out_specs=[o_spec, o_spec, q_spec, l_spec],
        input_output_aliases={3: 2, 4: 3} if before else {},
    )


def grad_mixed_kernel(*refs):
    gas, (w_ref, f_ref, g_ref, d_ref) = refs[:4], refs[4:]
    n = gas[0].shape[0]
    heads = w_ref.shape[0] // HD
    for i, ga in enumerate(gas):
        here = slice(i * n, (i + 1) * n)
        g = mm(ga[...], w_ref[...], NT).astype(BF)
        g_ref[here, :] = g
        prod = (g.astype(F32) * f_ref[here, :]).T
        d_ref[:, here] = jnp.concatenate(
            [jnp.sum(prod[h * HD : (h + 1) * HD], axis=0, keepdims=True) for h in range(heads)]
        )


def attend_bwd_kernel(heads, first, last, split, *refs):
    q_ref, k_ref, v_ref, g_ref, l_ref, d_ref = refs[:6]
    add_ref = refs[6] if not first else None
    dq_ref, outs, acc = refs[6 + (not first)], refs[7 + (not first) : -1], refs[-1]
    dqs, dks, dvs = [], [], []
    for h in heads:
        cols = slice(h * HD, (h + 1) * HD)
        q, k, v, g = q_ref[:, cols], k_ref[:, cols], v_ref[:, cols], g_ref[:, cols]
        probs = jnp.exp2(mm(k, q, NT) * SCALE_LOG2 - l_ref[h : h + 1, :])
        grad_scores = (probs * (mm(v, g, NT) - d_ref[h : h + 1, :])).astype(BF)
        dvs.append(mm(probs.astype(BF), g))
        dks.append(mm(grad_scores, q) * SCALE)
        dqs.append(mm(k, grad_scores, TN))
    dq = (dqs[0] if len(dqs) == 1 else jnp.concatenate(dqs, axis=0)).T
    if not first:
        dq = dq + add_ref[...]
    dq_ref[...] = (dq * SCALE).astype(BF) if last else dq
    dkv = jnp.concatenate(dks + dvs, axis=1)
    step = pl.program_id(0)

    @pl.when(step == 0)
    def _():
        acc[...] = dkv

    @pl.when(step > 0)
    def _():
        acc[...] += dkv

    @pl.when(step == pl.num_programs(0) - 1)
    def _():
        n = acc.shape[0] // len(outs)
        for i, ref in enumerate(outs):
            ref[...] = acc[i * n : (i + 1) * n].astype(BF)


def attend_bwd(heads, key_block, key_rows, split, q, k, v, g, logs, inner, *add, last=True, block=256):
    nq, w = q.shape
    n = len(heads) * HD
    q_spec = pl.BlockSpec((block, w), lambda i: (i, 0))
    k_spec = pl.BlockSpec((key_rows, w), lambda i: (key_block, 0))
    n_spec = pl.BlockSpec((block, n), lambda i: (i, 0))
    l_spec = pl.BlockSpec((logs.shape[0], block), lambda i: (0, i))
    whole = pl.BlockSpec((key_rows // split, 2 * n), lambda i: (0, 0))
    return call(
        functools.partial(attend_bwd_kernel, heads, not add, last, split),
        [shaped((nq, n), BF if last else F32)] + [shaped((key_rows // split, 2 * n), BF)] * split,
        q,
        k,
        v,
        g,
        logs,
        inner,
        *add,
        name="attend_bwd",
        limit=36,
        grid=(nq // block,),
        in_specs=[q_spec, k_spec, k_spec, q_spec, l_spec, l_spec] + [n_spec] * len(add),
        out_specs=[n_spec] + [whole] * split,
        scratch_shapes=[pltpu.VMEM((key_rows, 2 * n), F32)],
    )


def normed(x):
    centred = x - jnp.mean(x, axis=-1, keepdims=True)
    inverse = lax.rsqrt(jnp.mean(centred * centred, axis=-1, keepdims=True) + EPS)
    return centred * inverse, inverse


def norm_back(g, norm, inverse):
    return inverse * (
        g
        - jnp.mean(g, axis=-1, keepdims=True)
        - norm * jnp.mean(g * norm, axis=-1, keepdims=True)
    )


def down_rows(*terms):
    return jnp.concatenate([jnp.sum(t, axis=0, keepdims=True) for t in terms], axis=0)


def norm_one_kernel(m0, m1, m2, m3, w0, w1, w2, w3, t_ref, p_ref, y_ref, low_ref, n_ref, i_ref):
    near = mm(m0[...], w0[...]) + mm(m1[...], w1[...])
    far = mm(m2[...], w2[...]) + mm(m3[...], w3[...])
    norm, inverse = normed(t_ref[...].astype(F32) + ((near + far) + p_ref[0:1, :]))
    y = norm * p_ref[1:2, :] + p_ref[2:3, :]
    y_ref[...] = y
    low_ref[...] = y.astype(BF)
    n_ref[...] = norm
    i_ref[...] = inverse


def ffn_kernel(s_ref, y_ref, up_own, up_far, b_ref, down_own, down_far, h_ref, sl_ref, p_ref):
    f = s_ref[0]
    size = up_own.shape[0]
    x = mm(lanes(y_ref, f, size), up_own[...]) + mm(lanes(y_ref, 1 - f, size), up_far[...]) + b_ref[...]
    cdf = 0.5 * (1.0 + lax.erf(x * (1.0 / math.sqrt(2.0))))
    pdf = jnp.exp(-0.5 * x * x) * (1.0 / math.sqrt(2.0 * math.pi))
    sl_ref[...] = cdf + x * pdf
    hidden = (x * cdf).astype(BF)
    h_ref[...] = hidden
    for part, ref in ((f, down_own), (1 - f, down_far)):
        here = pl.ds(pl.multiple_of(part * size, 128), size)
        p_ref[:, here] = mm(hidden, ref[...]).astype(p_ref.dtype)


def norm_two_kernel(near, far, y_ref, g_ref, p_ref, o_ref, gs_ref, gf_ref, sums):
    ffn = near[...].astype(F32) + far[...].astype(F32)
    norm, inverse = normed(y_ref[...] + (ffn + p_ref[0:1, :]))
    o_ref[...] = (norm * p_ref[1:2, :] + p_ref[2:3, :]).astype(BF)
    g = g_ref[...].astype(F32)
    grad = norm_back(g * p_ref[1:2, :], norm, inverse)
    low = grad.astype(BF)
    gs_ref[...] = grad
    gf_ref[...] = low
    sums[...] = down_rows(low.astype(F32), g * norm, g)


def ffn_back_kernel(s_ref, g_ref, down_own, down_far, sl_ref, up_own, up_far, gp_ref, p_ref, sums):
    f = s_ref[0]
    size = up_own.shape[0]
    grad = mm(lanes(g_ref, f, size), down_own[...], NT) + mm(lanes(g_ref, 1 - f, size), down_far[...], NT)
    low = (grad * sl_ref[...]).astype(BF)
    gp_ref[...] = low
    sums[...] = down_rows(low.astype(F32))
    for part, ref in ((f, up_own), (1 - f, up_far)):
        here = pl.ds(pl.multiple_of(part * size, 128), size)
        p_ref[:, here] = mm(low, ref[...], NT).astype(p_ref.dtype)


def norm_one_back_kernel(gs_ref, near, far, n_ref, i_ref, p_ref, g_ref, low_ref, sums):
    grad_y = gs_ref[...] + (near[...].astype(F32) + far[...].astype(F32))
    norm = n_ref[...]
    grad = norm_back(grad_y * p_ref[1:2, :], norm, i_ref[...])
    low = grad.astype(BF)
    g_ref[...] = grad
    low_ref[...] = low
    sums[...] = down_rows(low.astype(F32), grad_y * norm, grad_y)


def input_part_kernel(first_row, dq1, dkv1, m1, dq2, dkv2, m2, w_ref, o_ref, p_ref):
    n = o_ref.shape[0]
    w1, w2 = dq1.shape[1], dq2.shape[1]
    for part, ref in enumerate((o_ref, p_ref)):
        here = slice(first_row + part * n, first_row + (part + 1) * n)
        low1 = (dkv1[here, :].astype(F32) + m1[here, :].astype(F32)).astype(BF)
        low2 = (dkv2[here, :].astype(F32) + m2[here, :].astype(F32)).astype(BF)
        grads = jnp.concatenate(
            [dq1[here, :], dq2[here, :], low1[:, :w1], low2[:, :w2], low1[:, w1:], low2[:, w2:]], axis=1
        )
        ref[...] = mm(grads, w_ref[...]).astype(ref.dtype)


def near_kernel(a_ref, b_ref, o_ref):
    o_ref[...] = (a_ref[...] + b_ref[...].astype(F32)).astype(BF)


def input_grad_kernel(g_ref, a_ref, b_ref, o_ref):
    o_ref[...] = (g_ref[...] + (a_ref[...].astype(F32) + b_ref[...].astype(F32))).astype(BF)


def place_kernel(s_ref, a, b, c, d, o_ref):
    n = a.shape[0]
    group, core = s_ref[2], s_ref[3]
    for block, half, ref in ((group, core, a), (group, 1 - core, b), (1 - group, core, c), (1 - group, 1 - core, d)):
        o_ref[block, pl.ds(pl.multiple_of(half * n, n), n), :] = ref[...]


def pack_kernel(a0, a1, b0, b1, u0, u1, u2, u3, o_ref):
    o_ref[0:3, :] = a0[...] + a1[...]
    o_ref[3:6, :] = b0[...] + b1[...]
    o_ref[6:7, :] = u0[...] + u1[...] + u2[...] + u3[...]
    o_ref[7:8, :] = jnp.zeros_like(u0)


EXTRA = 16


def put(ref, main, small):
    n = main.shape[0]
    ref[0:n, :] = main.astype(ref.dtype)
    if small is not None:
        high = small.astype(ref.dtype)
        ref[n : n + EXTRA, :] = high
        if ref.shape[0] > n + EXTRA:
            ref[n + EXTRA :, :] = (small - high.astype(F32)).astype(ref.dtype)


def get(ref, small):
    if not small:
        return ref[...].astype(F32), None
    parts = 1 if ref.dtype == F32 else 2
    n = ref.shape[0] - parts * EXTRA
    rest = ref[n : n + EXTRA, :].astype(F32)
    if parts == 2:
        rest = rest + ref[n + EXTRA :, :].astype(F32)
    return ref[0:n, :].astype(F32), rest


def up_grad_kernel(s_ref, *refs):
    ys, gs, (keep, send) = refs[:4], refs[4:8], refs[8:]
    f = s_ref[0]
    size = ys[0].shape[1] // 2
    for out, part in ((send, 1 - f), (keep, f)):
        put(out, sum(mm(lanes(y, part, size), g[...], TN) for y, g in zip(ys, gs)), None)


def down_grad_kernel(s_ref, *refs):
    hs, gs, (keep, send) = refs[:4], refs[4:8], refs[8:]
    f = s_ref[0]
    size = gs[0].shape[1] // 2
    for out, part in ((send, 1 - f), (keep, f)):
        put(out, sum(mm(h[...], lanes(g, part, size), TN) for h, g in zip(hs, gs)), None)


def qkv_grad_kernel(with_out, s_ref, *refs):
    rows, (dq, own_ref, far_ref), more, (keep, send) = refs[:8], refs[8:11], refs[11:-2], refs[-2:]
    f = s_ref[0]
    size = rows[0].shape[1] // 2
    n = rows[0].shape[0]
    m = dq.shape[1]
    own = jnp.concatenate([dq[...], own_ref[...]], axis=1)
    far = far_ref[...]
    far_sums = jnp.sum(far.astype(F32), axis=0, keepdims=True)
    sums = jnp.sum(own.astype(F32), axis=0, keepdims=True)
    sums = jnp.concatenate([sums[:, :m], sums[:, m:] + far_sums], axis=1)
    if sums.shape[1] < size:
        sums = jnp.concatenate([sums, jnp.zeros((1, size - sums.shape[1]), F32)], axis=1)
    small = [sums]
    if with_out:
        packed, moved = more[-2:]
        six = packed[0:6, :] + moved[0:6, :]
        ups = packed[6:7, :]
        small = [six[:, :size], ups[:, :size], six[:, size:], ups[:, size:], sums]
    small.append(jnp.zeros((EXTRA - sum(x.shape[0] for x in small), size), F32))
    small = jnp.concatenate(small, axis=0)
    for out, part in ((send, 1 - f), (keep, f)):
        one = two = None
        for i in range(4):
            here = slice(i * n, (i + 1) * n)
            a = mm(own[here], lanes(rows[i], part, size), TN)
            b = mm(far[here], lanes(rows[4 + i], part, size), TN)
            one = a if one is None else one + a
            two = b if two is None else two + b
        grad = [one[:m], one[m:] + two]
        if with_out:
            grad.append(sum(mm(a[...], lanes(g, part, size), TN) for a, g in zip(more[:4], more[4:8])))
        put(out, jnp.concatenate(grad, axis=0), small)


def sum_kernel(small, a_ref, b_ref, *outs):
    (a, c), (b, d) = get(a_ref, small), get(b_ref, small)
    for out in outs:
        put(out, a + b, c + d if small else None)


def chosen(s_ref, own, moved, small, write):
    @pl.when(s_ref[1] == 1)
    def _():
        write(*(x for pair in zip(*(get(r, small) for r in moved)) for x in pair))

    @pl.when(s_ref[1] != 1)
    def _():
        write(*(x for pair in zip(*(get(r, small) for r in own)) for x in pair))


def owned_kernel(s_ref, own, moved, out):
    def write(main, _):
        out[...] = main

    chosen(s_ref, [own], [moved], False, write)


def owned_qkv_kernel(s_ref, own1, own2, moved1, moved2, qkv, outw, sums, bias):
    def write(one, two, small1, small2):
        n = outw.shape[0]
        m1, m2 = (one.shape[0] - n) // 3, two.shape[0] // 3
        for j in range(3):
            qkv[j, 0:m1, :] = one[j * m1 : (j + 1) * m1]
            qkv[j, m1:, :] = two[j * m2 : (j + 1) * m2]
        outw[...] = one[3 * m1 :]
        sums[0:7, :] = jnp.concatenate([small1[0:7], small1[7:14]], axis=1)
        sums[7:8, :] = jnp.zeros_like(sums[7:8, :])
        for i, j in ((0, 0), (1, 2)):
            bias[i : i + 1, :] = jnp.concatenate(
                [small1[14:15, j * m1 : (j + 1) * m1], small2[0:1, j * m2 : (j + 1) * m2]], axis=1
            )

    chosen(s_ref, [own1, own2], [moved1, moved2], True, write)


def swap(x, axis, size, mask):
    return lax.ppermute(x, axis, [(i, i ^ mask) for i in range(size)])


def pick(first, second, bit, axis):
    n = first.shape[axis]
    ring = jnp.concatenate([first, second, first], axis=axis)
    return lax.dynamic_slice_in_dim(ring, bit * n, 2 * n, axis)


class Order:
    def __init__(self):
        self.done = None

    def __call__(self, fn, *operands):
        if self.done is not None:
            operands, _ = lax.optimization_barrier((operands, self.done))
        out = fn(*operands)
        self.done = out
        return out


class Reduction:
    def __init__(self, run, name, keep, moved, small):
        self.run, self.name, self.small = run, name, small
        self.own, self.moved, self.stage = keep, moved, 0
        self.shape = moved.shape

    def step(self):
        self.stage += 1
        pairs = [[(0, 1), (3, 2)], [(1, 2), (2, 1)], [(1, 0), (2, 3)]][self.stage - 1]
        outs = [shaped(self.shape, BF)]
        if self.stage == 1:
            outs = [shaped(self.own.shape, F32)] + outs
        name = f"{self.name}_{self.stage}"
        kernel = functools.partial(sum_kernel, self.small)
        with jax.named_scope(name):
            out = self.run(lambda *x: call(kernel, outs, *x, name=name), self.own, self.moved)
            self.own = out[0]
            self.moved = lax.ppermute(out[-1], "context", pairs)


def body(sizes, *args):
    (
        tokens,
        cotangent,
        w_qkv,
        qv_bias,
        w_out,
        out_bias,
        gain_one,
        shift_one,
        w_up,
        up_bias,
        w_down,
        down_bias,
        gain_two,
        shift_two,
    ) = args
    n_f, n_c, n_t = sizes
    _, rows, width = tokens.shape
    wide = w_qkv.shape[2]
    heads = wide // HD
    hidden_here = w_up.shape[1]
    half = rows // 2
    f = lax.axis_index("fsdp") if n_f == 2 else 0
    z = lax.axis_index("context")
    core = lax.axis_index("tensor") % 2
    group = z // 2
    over_core = functools.partial(swap, axis="tensor", size=n_t, mask=1)
    over_y = functools.partial(swap, axis="tensor", size=n_t, mask=2)
    over_both = functools.partial(swap, axis="tensor", size=n_t, mask=3)
    over_z1 = functools.partial(swap, axis="context", size=n_c, mask=1)
    over_z2 = functools.partial(swap, axis="context", size=n_c, mask=2)
    over_x = functools.partial(swap, axis="fsdp", size=n_f, mask=1)
    run = Order()

    def whole_f(w, axis):
        return lax.all_gather(w, "fsdp", axis=axis, tiled=True)

    def halves(w, axis):
        if n_f == 2:
            return w, over_x(w)
        w = whole_f(w, axis)
        return jnp.split(w, 2, axis=axis)

    def block_of(x, which, part):
        return lax.dynamic_slice(x, (which, part * half, 0), (1, half, width))[0]

    def touch(*x):
        return run(lambda *a: a, *x)

    def after(x, *others):
        return lax.optimization_barrier((x, others))[0]

    with jax.named_scope("arrive"):
        give = run(lambda t: block_of(t, 1 - group, core), tokens)
        b_own = over_z2(give)
        a_own = run(lambda t: block_of(t, group, core), tokens)
        oa_own = over_z1(a_own)
        qkv_t = w_qkv.transpose(1, 2, 0).reshape(3 * wide, -1)
        qkv_moved = over_x(qkv_t) if n_f == 2 else whole_f(qkv_t, 1)
        out_moved = over_x(w_out) if n_f == 2 else whole_f(w_out, 1)
        a_far, place, par_one, par_two, bias_row, up_row = run(
            lambda t, qb, ub, p1, p2: (
                block_of(t, group, 1 - core),
                jnp.stack(
                    [
                        jnp.int32(f),
                        jnp.where((z == 0) | (z == n_c - 1), 1, 0).astype(jnp.int32),
                        group.astype(jnp.int32),
                        core.astype(jnp.int32),
                    ]
                ),
                jnp.stack(p1),
                jnp.stack(p2),
                jnp.concatenate([qb[0], jnp.zeros_like(qb[0]), qb[1]])[None],
                ub[None],
            ),
            tokens,
            qv_bias,
            up_bias,
            (out_bias, gain_one, shift_one),
            (down_bias, gain_two, shift_two),
        )
        qkv_w = run(lambda a, b: pick(a, b, f, 1) if n_f == 2 else b, qkv_t, qkv_moved)
        out_w = run(lambda a, b: pick(a, b, f, 1) if n_f == 2 else b, w_out, out_moved)
        (b_own,) = touch(b_own)
        ob_own = over_z1(b_own)
        (oa_own,) = touch(oa_own)
        b_far, oa_far = over_core(b_own), over_core(oa_own)
        b_far, oa_far, out_later = touch(b_far, oa_far, out_w)
        out_near, out_far = over_core(out_later), over_y(out_later)
        up_two = halves(after(w_up, out_later), 0)
        out_near, out_far = touch(out_near, out_far)
        (ob_own,) = touch(ob_own)
        ob_far = over_core(ob_own)
    own = [a_own, a_far, b_own, b_far]
    other = [oa_own, oa_far, ob_own, ob_far]
    total = 8 * half
    n_own = total // 2

    q, k, v = run(
        lambda *x: call(
            qkv_kernel,
            [shaped((n_own, wide), BF), shaped((total, wide), BF), shaped((total, wide), BF)],
            *x,
            name="qkv",
        ),
        *own,
        *other,
        qkv_w,
        bias_row,
    )
    with jax.named_scope("cotangent"):
        cot_give, cot_a = run(
            lambda x: (block_of(x, 1 - group, core), block_of(x, group, core)), cotangent
        )
        cot_b = over_z2(cot_give)
    with jax.named_scope("down_weight"):
        down_two = halves(after(w_down, q), 1)
    with jax.named_scope("out_weight"):
        out_both = over_both(after(out_later, q))

    mixed, pieces, shared = [], [], ()
    for c in range(2):
        with jax.named_scope(f"attend{c}"):
            mo, mp, *shared = run(lambda *x: attend_fwd(c, half, *x), q, k, v, *shared)
            mixed += [mo, mp]
            if c == 0:
                up_two = touch(*up_two)
            else:
                (*pieces[0], out_both) = touch(*pieces[0], out_both)
            mo, mp = touch(mo, mp)
            pieces.append((mo, over_core(mp), over_y(mo), over_both(mp)))
    mixed_f, logs = shared
    tok = (a_own, b_own)
    f_rows = shaped((half, width), F32)
    b_rows = shaped((half, width), BF)
    h_rows = shaped((half, hidden_here), BF)
    state = [dict(), dict()]

    def norm_one(c):
        with jax.named_scope(f"normone{c}"):
            s = state[c]
            outs = [f_rows, b_rows, f_rows, shaped((half, 1), F32)]
            s["y"], s["yo"], s["n1"], s["i1"] = run(
                lambda *x: call(norm_one_kernel, outs, *x, name="norm_one"),
                *pieces[c],
                out_w,
                out_near,
                out_far,
                out_both,
                tok[c],
                par_one,
            )
            s["yp"] = over_core(s["yo"])

    def feed(c, which, dtype):
        with jax.named_scope(f"feed{c}{which}"):
            s = state[c]
            outs = [h_rows, shaped((half, hidden_here), F32), shaped((half, width), dtype)]
            s["h" + which], s["s" + which], s["p" + which] = run(
                lambda *x: scalar_call(ffn_kernel, outs, *x, name="feed"),
                place,
                s["y" + which],
                *up_two,
                up_row,
                *down_two,
            )
            if which == "p":
                s["c2"] = over_core(s["pp"])

    def near_sum(c, name):
        with jax.named_scope(f"near{c}{name}"):
            s = state[c]
            (s["near" + name],) = run(
                lambda *x: call(near_kernel, [b_rows], *x, name="near"), s["po"], s["c" + name]
            )
            s["far" + name] = over_y(s["near" + name])

    def norm_two(c):
        with jax.named_scope(f"normtwo{c}"):
            s = state[c]
            outs = [b_rows, f_rows, b_rows, shaped((3, width), F32)]
            s["out"], s["gs"], s["gfo"], s["sum2"] = run(
                lambda *x: call(norm_two_kernel, outs, *x, name="norm_two"),
                s["near2"],
                s["far2"],
                s["y"],
                cot[c],
                par_two,
            )
            s["gfp"] = over_core(s["gfo"])

    def feed_back(c, which, dtype):
        with jax.named_scope(f"feedback{c}{which}"):
            s = state[c]
            outs = [h_rows, shaped((half, width), dtype), shaped((1, hidden_here), F32)]
            s["gp" + which], s["p" + which], s["sumu" + which] = run(
                lambda *x: scalar_call(ffn_back_kernel, outs, *x, name="feed_back"),
                place,
                s["gf" + which],
                *down_two,
                s["s" + which],
                *up_two,
            )
            if which == "p":
                s["c5"] = over_core(s["pp"])

    def norm_one_back(c):
        with jax.named_scope(f"normoneback{c}"):
            s = state[c]
            s["gfirst"], s["gao"], s["sum1"] = run(
                lambda *x: call(
                    norm_one_back_kernel,
                    [f_rows, b_rows, shaped((3, width), F32)],
                    *x,
                    name="norm_one_back",
                ),
                s["gs"],
                s["near5"],
                s["far5"],
                s["n1"],
                s["i1"],
                par_one,
            )
            s["gap"] = over_core(s["gao"])

    def weight_grad(kernel, operands, rows, cols, name, small=False):
        with jax.named_scope(name):
            outs = [
                shaped((rows + small * EXTRA, cols), F32),
                shaped((rows + small * 2 * EXTRA, cols), BF),
            ]
            keep, send = run(lambda *x: scalar_call(kernel, outs, *x, name=name), place, *operands)
            return Reduction(run, name, keep, over_x(send), small)

    def owned(red, name):
        with jax.named_scope(name):
            return run(
                lambda *x: scalar_call(owned_kernel, [shaped(red.shape, F32)], *x, name=name),
                place,
                red.own,
                red.moved,
            )[0]

    four = [(c, w) for c in range(2) for w in "op"]

    def pieces_of(name):
        return [state[c][name + w] for c, w in four]

    norm_one(0)
    feed(0, "o", F32)
    norm_one(1)
    feed(0, "p", BF)
    (cot_b,) = touch(cot_b)
    cot = (cot_a, cot_b)
    feed(1, "p", BF)
    near_sum(0, "2")
    feed(1, "o", F32)
    near_sum(1, "2")
    norm_two(0)
    feed_back(0, "o", F32)
    feed_back(0, "p", BF)
    norm_two(1)
    with jax.named_scope("outback"):
        out_back = over_z2(state[1]["out"])
    near_sum(0, "5")
    feed_back(1, "o", F32)
    feed_back(1, "p", BF)
    if n_f == 2:
        red_down = weight_grad(
            down_grad_kernel, pieces_of("h") + pieces_of("gf"), hidden_here, width // 2, "down_grad"
        )
    norm_one_back(0)
    near_sum(1, "5")
    if n_f == 2:
        red_up = weight_grad(
            up_grad_kernel, pieces_of("y") + pieces_of("gp"), width // 2, hidden_here, "up_grad"
        )
    (out_back,) = touch(out_back)
    norm_one_back(1)
    with jax.named_scope("smallpack"):
        (packed,) = run(
            lambda *x: call(pack_kernel, [shaped((8, width), F32)], *x, name="pack"),
            *[state[c][s] for s in ("sum1", "sum2") for c in range(2)],
            *pieces_of("sumu"),
        )
        packed_moved = over_core(packed)
    def placed(blocks):
        return run(
            lambda *x: scalar_call(place_kernel, [shaped(tokens.shape, BF)], *x, name="place"),
            place,
            *blocks,
        )[0]

    def both_halves(a, b):
        return a, over_core(a), b, over_core(b)

    if n_f == 2:
        red_down.step()
    with jax.named_scope("placeout"):
        out_blocks = both_halves(after(state[0]["out"], out_back), out_back)
    grad_attn = pieces_of("ga")
    grad_mixed, inner = run(
        lambda *x: call(
            grad_mixed_kernel, [shaped((n_own, wide), BF), shaped((heads, n_own), F32)], *x, name="grad_mixed"
        ),
        *grad_attn,
        out_w,
        mixed_f,
    )
    (*out_blocks, packed_moved) = touch(*out_blocks, packed_moved)

    early, late = tuple(range(heads - 1)), (heads - 1,)
    bwd_args = (q, k, v, grad_mixed, logs, inner)
    n_one, n_two = 3 * len(early) * HD, 3 * HD
    with jax.named_scope("back1"):
        dq1, own1, far1 = run(lambda *x: attend_bwd(early, 0, total, 2, *x), *bwd_args)
    if n_f == 2:
        red_up.step()
        red_down.step()
    with jax.named_scope("back1"):
        moved1 = over_z1(after(far1, run.done))
    with jax.named_scope("back2"):
        dq2, far2 = run(lambda *x: attend_bwd(late, 1, n_own, 1, *x, last=False), *bwd_args)
        moved2 = over_z1(far2)
    with jax.named_scope("back3"):
        dq2, own2 = run(lambda *x: attend_bwd(late, 0, n_own, 1, *x), *bwd_args, dq2)
    if n_f == 2:
        red_one = weight_grad(
            functools.partial(qkv_grad_kernel, True),
            own + other + [dq1, own1, far1] + mixed + grad_attn + [packed, packed_moved],
            n_one + wide,
            width // 2,
            "one_grad",
            True,
        )
    with jax.named_scope("placeout"):
        output = placed(out_blocks)
    if n_f == 2:
        red_down.step()
        red_up.step()
        (moved1,) = touch(moved1)
        red_two = weight_grad(
            functools.partial(qkv_grad_kernel, False),
            own + other + [dq2, own2, far2],
            n_two,
            width // 2,
            "two_grad",
            True,
        )
        red_one.step()

    item = [dict(), dict()]

    def input_part(c):
        with jax.named_scope(f"inputpart{c}"):
            s = item[c]
            s["po"], pp = run(
                lambda *x: call(
                    functools.partial(input_part_kernel, c * rows), [f_rows, b_rows], *x, name="input_part"
                ),
                dq1,
                own1,
                moved1,
                dq2,
                own2,
                moved2,
                qkv_w,
            )
            s["cp"] = over_core(pp)

    def input_near(c):
        with jax.named_scope(f"inputnear{c}"):
            s = item[c]
            (s["near"],) = run(
                lambda *x: call(near_kernel, [b_rows], *x, name="near"), s["po"], s["cp"]
            )
            s["far"] = over_y(s["near"])

    def input_last(c):
        with jax.named_scope(f"inputlast{c}"):
            s = item[c]
            (s["in"],) = run(
                lambda *x: call(input_grad_kernel, [b_rows], *x, name="input_grad"),
                state[c]["gfirst"],
                s["near"],
                s["far"],
            )

    input_part(1)
    input_part(0)
    input_near(1)
    if n_f == 2:
        red_up.step()
        owned_down = owned(red_down, "owned_down")
    input_near(0)
    if n_f == 2:
        red_two.step()
    input_last(1)
    with jax.named_scope("inputback"):
        in_back = over_z2(item[1]["in"])
    if n_f == 2:
        red_one.step()
    input_last(0)
    if n_f == 2:
        red_two.step()
        owned_up = owned(red_up, "owned_up")
        red_one.step()
        red_two.step()
    (in_back,) = touch(in_back)
    with jax.named_scope("placein"):
        in_blocks = both_halves(after(item[0]["in"], in_back), in_back)
    with jax.named_scope("finish"):
        if n_f == 2:
            qkv_grad, owned_out, small, bias_grad = run(
                lambda *x: scalar_call(
                    owned_qkv_kernel,
                    [
                        shaped((3, wide, width // 2), F32),
                        shaped((wide, width // 2), F32),
                        shaped((8, width), F32),
                        shaped((2, wide), F32),
                    ],
                    *x,
                    name="owned_qkv",
                ),
                place,
                red_one.own,
                red_two.own,
                red_one.moved,
                red_two.moved,
            )
            owned_qkv = qkv_grad.transpose(2, 0, 1)
        else:

            def reduce_plain(left, right, axis):
                grad = mm(jnp.concatenate(left), jnp.concatenate(right), TN)
                keep = lax.psum_scatter(grad, "fsdp", scatter_dimension=axis, tiled=True)
                return lax.psum(keep, "context").astype(BF).astype(F32)

            zero = jnp.zeros((n_own, wide), BF)
            cut = len(early) * HD
            dk = [own1[:, :cut], own2[:, :HD], far1[:, :cut], far2[:, :HD]]
            dv = [own1[:, cut:], own2[:, HD:], far1[:, cut:], far2[:, HD:]]
            left = jnp.concatenate([dq1, dq2, *dk[:2], *dv[:2]], axis=1)
            right = jnp.concatenate([zero, *dk[2:], *dv[2:]], axis=1)
            owned_up = reduce_plain(pieces_of("y"), pieces_of("gp"), 0)
            owned_down = reduce_plain(pieces_of("h"), pieces_of("gf"), 1)
            owned_out = reduce_plain(mixed, grad_attn, 1)
            owned_qkv = reduce_plain(own + other, [left, right], 0).reshape(w_qkv.shape)
            column_sums = jnp.sum((left.astype(F32) + right.astype(F32)), axis=0)
            bias_grad = jnp.stack([column_sums[:wide], column_sums[2 * wide :]])
            small = jnp.concatenate([packed[:6] + packed_moved[:6], packed[6:]])
            small, bias_grad = lax.psum((small, bias_grad), ("fsdp", "context"))
    with jax.named_scope("placein"):
        input_grad = placed(in_blocks)
    return (
        output,
        input_grad,
        owned_qkv,
        bias_grad,
        owned_out,
        small[0],
        small[1],
        small[2],
        owned_up,
        small[6],
        owned_down,
        small[3],
        small[4],
        small[5],
    )


def solution(mesh):
    sizes = tuple(mesh.shape[name] for name in ("fsdp", "context", "tensor"))
    specs = (
        P("fsdp", None, "tensor"),
        P(None, "tensor"),
        P("tensor", "fsdp"),
        P(),
        P(),
        P(),
        P("fsdp", "tensor"),
        P("tensor"),
        P("tensor", "fsdp"),
        P(),
        P(),
        P(),
    )
    rows = P("fsdp", "context", None)
    return jax.shard_map(
        functools.partial(body, sizes),
        mesh=mesh,
        in_specs=(rows, rows) + specs,
        out_specs=(rows, rows) + specs,
        check_vma=False,
    )
```

```python
import functools
import math

import jax
import jax.numpy as jnp
from jax import lax
from jax.experimental import pallas as pl
from jax.experimental.pallas import tpu as pltpu
from jax.sharding import PartitionSpec as P

HD = 64
SCALE = 1.0 / math.sqrt(HD)
SCALE_LOG2 = SCALE * math.log2(math.e)
EPS = 1e-06
BF = jnp.bfloat16
F32 = jnp.float32
NT = (((1,), (1,)), ((), ()))
TN = (((0,), (0,)), ((), ()))
NN = (((1,), (0,)), ((), ()))


def mm(a, b, dims=NN):
    return lax.dot_general(a, b, dims, preferred_element_type=F32)


def shaped(shape, dtype):
    return jax.ShapeDtypeStruct(shape, dtype)


def call(kernel, outs, *operands, name, limit=16, **extra):
    return pl.pallas_call(
        kernel,
        out_shape=list(outs),
        cost_estimate=pl.CostEstimate(flops=int(3e10), bytes_accessed=1, transcendentals=0),
        compiler_params=pltpu.CompilerParams(vmem_limit_bytes=limit << 20),
        name=name,
        **extra,
    )(*operands)


SMEM = pl.BlockSpec(memory_space=pltpu.SMEM)
VMEM = pl.BlockSpec(memory_space=pltpu.VMEM)


def scalar_call(kernel, outs, scalars, *operands, **kw):
    specs = [SMEM] + [VMEM] * len(operands)
    return call(kernel, outs, scalars, *operands, in_specs=specs, **kw)


def lanes(ref, index, size):
    return ref[:, pl.ds(pl.multiple_of(index * size, 128), size)]


def qkv_kernel(*refs):
    rows, (w_ref, b_ref, q_ref, k_ref, v_ref) = refs[:8], refs[8:]
    n = rows[0].shape[0]
    wide = q_ref.shape[1]
    for i, ref in enumerate(rows):
        here = slice(i * n, (i + 1) * n)
        skip = 0 if i < 4 else wide
        full = (mm(ref[...], w_ref[skip:, :], NT) + b_ref[:, skip:]).astype(BF)
        if i < 4:
            q_ref[here, :] = full[:, :wide]
        k_ref[here, :] = full[:, wide - skip : 2 * wide - skip]
        v_ref[here, :] = full[:, 2 * wide - skip :]


def attend_fwd_kernel(chunk, *refs):
    q_ref, k_ref, v_ref = refs[:3]
    o_ref, p_ref, f_ref, l_ref = refs[-4:]
    outs, logs = [], []
    for h in range(q_ref.shape[1] // HD):
        cols = slice(h * HD, (h + 1) * HD)
        scores = mm(q_ref[:, cols], k_ref[:, cols], NT)
        top = jnp.max(scores, axis=1, keepdims=True)
        expo = jnp.exp2((scores - top) * SCALE_LOG2)
        total = jnp.sum(expo, axis=1, keepdims=True)
        outs.append(mm(expo.astype(BF), v_ref[:, cols]) / total)
        logs.append(top * SCALE_LOG2 + jnp.log2(total))
    mixed = jnp.concatenate(outs, axis=1)
    f_ref[...] = mixed
    l_ref[...] = jnp.concatenate(logs, axis=1).T
    for step, ref in enumerate((o_ref, p_ref)):

        @pl.when(pl.program_id(0) == step)
        def _():
            ref[...] = mixed.astype(BF)


def attend_fwd(chunk, block, q, k, v, *before):
    nq, w = q.shape
    nk = k.shape[0]
    heads = w // HD
    q_spec = pl.BlockSpec((block, w), lambda i: (chunk * 2 + i, 0))
    l_spec = pl.BlockSpec((heads, block), lambda i: (0, chunk * 2 + i))
    o_spec = pl.BlockSpec((block, w), lambda i: (0, 0))
    k_spec = pl.BlockSpec((nk, w), lambda i: (0, 0))
    anywhere = pl.BlockSpec(memory_space=pl.ANY)
    return call(
        functools.partial(attend_fwd_kernel, chunk),
        [shaped((block, w), BF)] * 2 + [shaped((nq, w), F32), shaped((heads, nq), F32)],
        q,
        k,
        v,
        *before,
        name="attend_fwd",
        limit=24,
        grid=(2,),
        in_specs=[q_spec, k_spec, k_spec] + [anywhere] * len(before),
        out_specs=[o_spec, o_spec, q_spec, l_spec],
        input_output_aliases={3: 2, 4: 3} if before else {},
    )


def grad_mixed_kernel(*refs):
    gas, (w_ref, f_ref, g_ref, d_ref) = refs[:4], refs[4:]
    n = gas[0].shape[0]
    heads = w_ref.shape[0] // HD
    for i, ga in enumerate(gas):
        here = slice(i * n, (i + 1) * n)
        g = mm(ga[...], w_ref[...], NT).astype(BF)
        g_ref[here, :] = g
        prod = (g.astype(F32) * f_ref[here, :]).T
        d_ref[:, here] = jnp.concatenate(
            [jnp.sum(prod[h * HD : (h + 1) * HD], axis=0, keepdims=True) for h in range(heads)]
        )


def attend_bwd_kernel(heads, first, last, split, *refs):
    q_ref, k_ref, v_ref, g_ref, l_ref, d_ref = refs[:6]
    add_ref = refs[6] if not first else None
    dq_ref, outs, acc = refs[6 + (not first)], refs[7 + (not first) : -1], refs[-1]
    dqs, dks, dvs = [], [], []
    for h in heads:
        cols = slice(h * HD, (h + 1) * HD)
        q, k, v, g = q_ref[:, cols], k_ref[:, cols], v_ref[:, cols], g_ref[:, cols]
        probs = jnp.exp2(mm(k, q, NT) * SCALE_LOG2 - l_ref[h : h + 1, :])
        grad_scores = (probs * (mm(v, g, NT) - d_ref[h : h + 1, :])).astype(BF)
        dvs.append(mm(probs.astype(BF), g))
        dks.append(mm(grad_scores, q) * SCALE)
        dqs.append(mm(k, grad_scores, TN))
    dq = (dqs[0] if len(dqs) == 1 else jnp.concatenate(dqs, axis=0)).T
    if not first:
        dq = dq + add_ref[...]
    dq_ref[...] = (dq * SCALE).astype(BF) if last else dq
    dkv = jnp.concatenate(dks + dvs, axis=1)
    step = pl.program_id(0)

    @pl.when(step == 0)
    def _():
        acc[...] = dkv

    @pl.when(step > 0)
    def _():
        acc[...] += dkv

    @pl.when(step == pl.num_programs(0) - 1)
    def _():
        n = acc.shape[0] // len(outs)
        for i, ref in enumerate(outs):
            ref[...] = acc[i * n : (i + 1) * n].astype(BF)


def attend_bwd(heads, key_block, key_rows, split, q, k, v, g, logs, inner, *add, last=True, block=256):
    nq, w = q.shape
    n = len(heads) * HD
    q_spec = pl.BlockSpec((block, w), lambda i: (i, 0))
    k_spec = pl.BlockSpec((key_rows, w), lambda i: (key_block, 0))
    n_spec = pl.BlockSpec((block, n), lambda i: (i, 0))
    l_spec = pl.BlockSpec((logs.shape[0], block), lambda i: (0, i))
    whole = pl.BlockSpec((key_rows // split, 2 * n), lambda i: (0, 0))
    return call(
        functools.partial(attend_bwd_kernel, heads, not add, last, split),
        [shaped((nq, n), BF if last else F32)] + [shaped((key_rows // split, 2 * n), BF)] * split,
        q,
        k,
        v,
        g,
        logs,
        inner,
        *add,
        name="attend_bwd",
        limit=36,
        grid=(nq // block,),
        in_specs=[q_spec, k_spec, k_spec, q_spec, l_spec, l_spec] + [n_spec] * len(add),
        out_specs=[n_spec] + [whole] * split,
        scratch_shapes=[pltpu.VMEM((key_rows, 2 * n), F32)],
    )


def normed(x):
    centred = x - jnp.mean(x, axis=-1, keepdims=True)
    inverse = lax.rsqrt(jnp.mean(centred * centred, axis=-1, keepdims=True) + EPS)
    return centred * inverse, inverse


def norm_back(g, norm, inverse):
    return inverse * (
        g
        - jnp.mean(g, axis=-1, keepdims=True)
        - norm * jnp.mean(g * norm, axis=-1, keepdims=True)
    )


def down_rows(*terms):
    return jnp.concatenate([jnp.sum(t, axis=0, keepdims=True) for t in terms], axis=0)


def norm_one_kernel(m0, m1, m2, m3, w0, w1, w2, w3, t_ref, p_ref, y_ref, low_ref, n_ref, i_ref):
    near = mm(m0[...], w0[...]) + mm(m1[...], w1[...])
    far = mm(m2[...], w2[...]) + mm(m3[...], w3[...])
    norm, inverse = normed(t_ref[...].astype(F32) + ((near + far) + p_ref[0:1, :]))
    y = norm * p_ref[1:2, :] + p_ref[2:3, :]
    y_ref[...] = y
    low_ref[...] = y.astype(BF)
    n_ref[...] = norm
    i_ref[...] = inverse


def ffn_kernel(s_ref, y_ref, up_own, up_far, b_ref, down_own, down_far, h_ref, sl_ref, p_ref):
    f = s_ref[0]
    size = up_own.shape[0]
    x = mm(lanes(y_ref, f, size), up_own[...]) + mm(lanes(y_ref, 1 - f, size), up_far[...]) + b_ref[...]
    cdf = 0.5 * (1.0 + lax.erf(x * (1.0 / math.sqrt(2.0))))
    pdf = jnp.exp(-0.5 * x * x) * (1.0 / math.sqrt(2.0 * math.pi))
    sl_ref[...] = cdf + x * pdf
    hidden = (x * cdf).astype(BF)
    h_ref[...] = hidden
    for part, ref in ((f, down_own), (1 - f, down_far)):
        here = pl.ds(pl.multiple_of(part * size, 128), size)
        p_ref[:, here] = mm(hidden, ref[...]).astype(p_ref.dtype)


def norm_two_kernel(near, far, y_ref, g_ref, p_ref, o_ref, gs_ref, gf_ref, sums):
    ffn = near[...].astype(F32) + far[...].astype(F32)
    norm, inverse = normed(y_ref[...] + (ffn + p_ref[0:1, :]))
    o_ref[...] = (norm * p_ref[1:2, :] + p_ref[2:3, :]).astype(BF)
    g = g_ref[...].astype(F32)
    grad = norm_back(g * p_ref[1:2, :], norm, inverse)
    low = grad.astype(BF)
    gs_ref[...] = grad
    gf_ref[...] = low
    sums[...] = down_rows(low.astype(F32), g * norm, g)


def ffn_back_kernel(s_ref, g_ref, down_own, down_far, sl_ref, up_own, up_far, gp_ref, p_ref, sums):
    f = s_ref[0]
    size = up_own.shape[0]
    grad = mm(lanes(g_ref, f, size), down_own[...], NT) + mm(lanes(g_ref, 1 - f, size), down_far[...], NT)
    low = (grad * sl_ref[...]).astype(BF)
    gp_ref[...] = low
    sums[...] = down_rows(low.astype(F32))
    for part, ref in ((f, up_own), (1 - f, up_far)):
        here = pl.ds(pl.multiple_of(part * size, 128), size)
        p_ref[:, here] = mm(low, ref[...], NT).astype(p_ref.dtype)


def norm_one_back_kernel(gs_ref, near, far, n_ref, i_ref, p_ref, g_ref, low_ref, sums):
    grad_y = gs_ref[...] + (near[...].astype(F32) + far[...].astype(F32))
    norm = n_ref[...]
    grad = norm_back(grad_y * p_ref[1:2, :], norm, i_ref[...])
    low = grad.astype(BF)
    g_ref[...] = grad
    low_ref[...] = low
    sums[...] = down_rows(low.astype(F32), grad_y * norm, grad_y)


def input_part_kernel(first_row, dq1, dkv1, m1, dq2, dkv2, m2, w_ref, o_ref, p_ref):
    n = o_ref.shape[0]
    w1, w2 = dq1.shape[1], dq2.shape[1]
    for part, ref in enumerate((o_ref, p_ref)):
        here = slice(first_row + part * n, first_row + (part + 1) * n)
        low1 = (dkv1[here, :].astype(F32) + m1[here, :].astype(F32)).astype(BF)
        low2 = (dkv2[here, :].astype(F32) + m2[here, :].astype(F32)).astype(BF)
        grads = jnp.concatenate(
            [dq1[here, :], dq2[here, :], low1[:, :w1], low2[:, :w2], low1[:, w1:], low2[:, w2:]], axis=1
        )
        ref[...] = mm(grads, w_ref[...]).astype(ref.dtype)


def near_kernel(a_ref, b_ref, o_ref):
    o_ref[...] = (a_ref[...] + b_ref[...].astype(F32)).astype(BF)


def input_grad_kernel(g_ref, a_ref, b_ref, o_ref):
    o_ref[...] = (g_ref[...] + (a_ref[...].astype(F32) + b_ref[...].astype(F32))).astype(BF)


def place_kernel(s_ref, a, b, c, d, o_ref):
    n = a.shape[0]
    group, core = s_ref[2], s_ref[3]
    for block, half, ref in ((group, core, a), (group, 1 - core, b), (1 - group, core, c), (1 - group, 1 - core, d)):
        o_ref[block, pl.ds(pl.multiple_of(half * n, n), n), :] = ref[...]


def pack_kernel(a0, a1, b0, b1, u0, u1, u2, u3, o_ref):
    o_ref[0:3, :] = a0[...] + a1[...]
    o_ref[3:6, :] = b0[...] + b1[...]
    o_ref[6:7, :] = u0[...] + u1[...] + u2[...] + u3[...]
    o_ref[7:8, :] = jnp.zeros_like(u0)


EXTRA = 16


def put(ref, main, small):
    n = main.shape[0]
    ref[0:n, :] = main.astype(ref.dtype)
    if small is not None:
        high = small.astype(ref.dtype)
        ref[n : n + EXTRA, :] = high
        if ref.shape[0] > n + EXTRA:
            ref[n + EXTRA :, :] = (small - high.astype(F32)).astype(ref.dtype)


def get(ref, small):
    if not small:
        return ref[...].astype(F32), None
    parts = 1 if ref.dtype == F32 else 2
    n = ref.shape[0] - parts * EXTRA
    rest = ref[n : n + EXTRA, :].astype(F32)
    if parts == 2:
        rest = rest + ref[n + EXTRA :, :].astype(F32)
    return ref[0:n, :].astype(F32), rest


def up_grad_kernel(s_ref, *refs):
    ys, gs, (keep, send) = refs[:4], refs[4:8], refs[8:]
    f = s_ref[0]
    size = ys[0].shape[1] // 2
    for out, part in ((send, 1 - f), (keep, f)):
        put(out, sum(mm(lanes(y, part, size), g[...], TN) for y, g in zip(ys, gs)), None)


def down_grad_kernel(s_ref, *refs):
    hs, gs, (keep, send) = refs[:4], refs[4:8], refs[8:]
    f = s_ref[0]
    size = gs[0].shape[1] // 2
    for out, part in ((send, 1 - f), (keep, f)):
        put(out, sum(mm(h[...], lanes(g, part, size), TN) for h, g in zip(hs, gs)), None)


def qkv_grad_kernel(with_out, s_ref, *refs):
    rows, (dq, own_ref, far_ref), more, (keep, send) = refs[:8], refs[8:11], refs[11:-2], refs[-2:]
    f = s_ref[0]
    size = rows[0].shape[1] // 2
    n = rows[0].shape[0]
    m = dq.shape[1]
    own = jnp.concatenate([dq[...], own_ref[...]], axis=1)
    far = far_ref[...]
    far_sums = jnp.sum(far.astype(F32), axis=0, keepdims=True)
    sums = jnp.sum(own.astype(F32), axis=0, keepdims=True)
    sums = jnp.concatenate([sums[:, :m], sums[:, m:] + far_sums], axis=1)
    if sums.shape[1] < size:
        sums = jnp.concatenate([sums, jnp.zeros((1, size - sums.shape[1]), F32)], axis=1)
    small = [sums]
    if with_out:
        packed, moved = more[-2:]
        six = packed[0:6, :] + moved[0:6, :]
        ups = packed[6:7, :]
        small = [six[:, :size], ups[:, :size], six[:, size:], ups[:, size:], sums]
    small.append(jnp.zeros((EXTRA - sum(x.shape[0] for x in small), size), F32))
    small = jnp.concatenate(small, axis=0)
    for out, part in ((send, 1 - f), (keep, f)):
        one = two = None
        for i in range(4):
            here = slice(i * n, (i + 1) * n)
            a = mm(own[here], lanes(rows[i], part, size), TN)
            b = mm(far[here], lanes(rows[4 + i], part, size), TN)
            one = a if one is None else one + a
            two = b if two is None else two + b
        grad = [one[:m], one[m:] + two]
        if with_out:
            grad.append(sum(mm(a[...], lanes(g, part, size), TN) for a, g in zip(more[:4], more[4:8])))
        put(out, jnp.concatenate(grad, axis=0), small)


def sum_kernel(small, a_ref, b_ref, *outs):
    (a, c), (b, d) = get(a_ref, small), get(b_ref, small)
    for out in outs:
        put(out, a + b, c + d if small else None)


def chosen(s_ref, own, moved, small, write):
    @pl.when(s_ref[1] == 1)
    def _():
        write(*(x for pair in zip(*(get(r, small) for r in moved)) for x in pair))

    @pl.when(s_ref[1] != 1)
    def _():
        write(*(x for pair in zip(*(get(r, small) for r in own)) for x in pair))


def owned_kernel(s_ref, own, moved, out):
    def write(main, _):
        out[...] = main

    chosen(s_ref, [own], [moved], False, write)


def owned_qkv_kernel(s_ref, own1, own2, moved1, moved2, qkv, outw, sums, bias):
    def write(one, two, small1, small2):
        n = outw.shape[0]
        m1, m2 = (one.shape[0] - n) // 3, two.shape[0] // 3
        for j in range(3):
            qkv[j, 0:m1, :] = one[j * m1 : (j + 1) * m1]
            qkv[j, m1:, :] = two[j * m2 : (j + 1) * m2]
        outw[...] = one[3 * m1 :]
        sums[0:7, :] = jnp.concatenate([small1[0:7], small1[7:14]], axis=1)
        sums[7:8, :] = jnp.zeros_like(sums[7:8, :])
        for i, j in ((0, 0), (1, 2)):
            bias[i : i + 1, :] = jnp.concatenate(
                [small1[14:15, j * m1 : (j + 1) * m1], small2[0:1, j * m2 : (j + 1) * m2]], axis=1
            )

    chosen(s_ref, [own1, own2], [moved1, moved2], True, write)


def swap(x, axis, size, mask):
    return lax.ppermute(x, axis, [(i, i ^ mask) for i in range(size)])


def pick(first, second, bit, axis):
    n = first.shape[axis]
    ring = jnp.concatenate([first, second, first], axis=axis)
    return lax.dynamic_slice_in_dim(ring, bit * n, 2 * n, axis)


class Order:
    def __init__(self):
        self.done = None

    def __call__(self, fn, *operands):
        if self.done is not None:
            operands, _ = lax.optimization_barrier((operands, self.done))
        out = fn(*operands)
        self.done = out
        return out


class Reduction:
    def __init__(self, run, name, keep, moved, small):
        self.run, self.name, self.small = run, name, small
        self.own, self.moved, self.stage = keep, moved, 0
        self.shape = moved.shape

    def step(self):
        self.stage += 1
        pairs = [[(0, 1), (3, 2)], [(1, 2), (2, 1)], [(1, 0), (2, 3)]][self.stage - 1]
        outs = [shaped(self.shape, BF)]
        if self.stage == 1:
            outs = [shaped(self.own.shape, F32)] + outs
        name = f"{self.name}_{self.stage}"
        kernel = functools.partial(sum_kernel, self.small)
        with jax.named_scope(name):
            out = self.run(lambda *x: call(kernel, outs, *x, name=name), self.own, self.moved)
            self.own = out[0]
            self.moved = lax.ppermute(out[-1], "context", pairs)


def body(sizes, *args):
    (
        tokens,
        cotangent,
        w_qkv,
        qv_bias,
        w_out,
        out_bias,
        gain_one,
        shift_one,
        w_up,
        up_bias,
        w_down,
        down_bias,
        gain_two,
        shift_two,
    ) = args
    n_f, n_c, n_t = sizes
    _, rows, width = tokens.shape
    wide = w_qkv.shape[2]
    heads = wide // HD
    hidden_here = w_up.shape[1]
    half = rows // 2
    f = lax.axis_index("fsdp") if n_f == 2 else 0
    z = lax.axis_index("context")
    core = lax.axis_index("tensor") % 2
    group = z // 2
    over_core = functools.partial(swap, axis="tensor", size=n_t, mask=1)
    over_y = functools.partial(swap, axis="tensor", size=n_t, mask=2)
    over_both = functools.partial(swap, axis="tensor", size=n_t, mask=3)
    over_z1 = functools.partial(swap, axis="context", size=n_c, mask=1)
    over_z2 = functools.partial(swap, axis="context", size=n_c, mask=2)
    over_x = functools.partial(swap, axis="fsdp", size=n_f, mask=1)
    run = Order()

    def whole_f(w, axis):
        return lax.all_gather(w, "fsdp", axis=axis, tiled=True)

    def halves(w, axis):
        if n_f == 2:
            return w, over_x(w)
        w = whole_f(w, axis)
        return jnp.split(w, 2, axis=axis)

    def block_of(x, which, part):
        return lax.dynamic_slice(x, (which, part * half, 0), (1, half, width))[0]

    def touch(*x):
        return run(lambda *a: a, *x)

    def after(x, *others):
        return lax.optimization_barrier((x, others))[0]

    with jax.named_scope("arrive"):
        give = run(lambda t: block_of(t, 1 - group, core), tokens)
        b_own = over_z2(give)
        a_own = run(lambda t: block_of(t, group, core), tokens)
        oa_own = over_z1(a_own)
        qkv_t = w_qkv.transpose(1, 2, 0).reshape(3 * wide, -1)
        qkv_moved = over_x(qkv_t) if n_f == 2 else whole_f(qkv_t, 1)
        out_moved = over_x(w_out) if n_f == 2 else whole_f(w_out, 1)
        a_far, place, par_one, par_two, bias_row, up_row = run(
            lambda t, qb, ub, p1, p2: (
                block_of(t, group, 1 - core),
                jnp.stack(
                    [
                        jnp.int32(f),
                        jnp.where((z == 0) | (z == n_c - 1), 1, 0).astype(jnp.int32),
                        group.astype(jnp.int32),
                        core.astype(jnp.int32),
                    ]
                ),
                jnp.stack(p1),
                jnp.stack(p2),
                jnp.concatenate([qb[0], jnp.zeros_like(qb[0]), qb[1]])[None],
                ub[None],
            ),
            tokens,
            qv_bias,
            up_bias,
            (out_bias, gain_one, shift_one),
            (down_bias, gain_two, shift_two),
        )
        qkv_w = run(lambda a, b: pick(a, b, f, 1) if n_f == 2 else b, qkv_t, qkv_moved)
        out_w = run(lambda a, b: pick(a, b, f, 1) if n_f == 2 else b, w_out, out_moved)
        (b_own,) = touch(b_own)
        ob_own = over_z1(b_own)
        (oa_own,) = touch(oa_own)
        b_far, oa_far = over_core(b_own), over_core(oa_own)
        b_far, oa_far, out_later = touch(b_far, oa_far, out_w)
        out_near, out_far = over_core(out_later), over_y(out_later)
        up_two = halves(after(w_up, out_later), 0)
        out_near, out_far = touch(out_near, out_far)
        (ob_own,) = touch(ob_own)
        ob_far = over_core(ob_own)
    own = [a_own, a_far, b_own, b_far]
    other = [oa_own, oa_far, ob_own, ob_far]
    total = 8 * half
    n_own = total // 2

    q, k, v = run(
        lambda *x: call(
            qkv_kernel,
            [shaped((n_own, wide), BF), shaped((total, wide), BF), shaped((total, wide), BF)],
            *x,
            name="qkv",
        ),
        *own,
        *other,
        qkv_w,
        bias_row,
    )
    with jax.named_scope("cotangent"):
        cot_give, cot_a = run(
            lambda x: (block_of(x, 1 - group, core), block_of(x, group, core)), cotangent
        )
        cot_b = over_z2(cot_give)
    with jax.named_scope("down_weight"):
        down_two = halves(after(w_down, q), 1)
    with jax.named_scope("out_weight"):
        out_both = over_both(after(out_later, q))

    mixed, pieces, shared = [], [], ()
    for c in range(2):
        with jax.named_scope(f"attend{c}"):
            mo, mp, *shared = run(lambda *x: attend_fwd(c, half, *x), q, k, v, *shared)
            mixed += [mo, mp]
            if c == 0:
                (*up_two, out_both) = touch(*up_two, out_both)
            else:
                (*pieces[0], cot_b) = touch(*pieces[0], cot_b)
            mo, mp = touch(mo, mp)
            pieces.append((mo, over_core(mp), over_y(mo), over_both(mp)))
    mixed_f, logs = shared
    tok = (a_own, b_own)
    f_rows = shaped((half, width), F32)
    b_rows = shaped((half, width), BF)
    h_rows = shaped((half, hidden_here), BF)
    state = [dict(), dict()]

    def norm_one(c):
        with jax.named_scope(f"normone{c}"):
            s = state[c]
            outs = [f_rows, b_rows, f_rows, shaped((half, 1), F32)]
            s["y"], s["yo"], s["n1"], s["i1"] = run(
                lambda *x: call(norm_one_kernel, outs, *x, name="norm_one"),
                *pieces[c],
                out_w,
                out_near,
                out_far,
                out_both,
                tok[c],
                par_one,
            )
            s["yp"] = over_core(s["yo"])

    def feed(c, which, dtype):
        with jax.named_scope(f"feed{c}{which}"):
            s = state[c]
            outs = [h_rows, shaped((half, hidden_here), F32), shaped((half, width), dtype)]
            s["h" + which], s["s" + which], s["p" + which] = run(
                lambda *x: scalar_call(ffn_kernel, outs, *x, name="feed"),
                place,
                s["y" + which],
                *up_two,
                up_row,
                *down_two,
            )
            if which == "p":
                s["c2"] = over_core(s["pp"])

    def near_sum(c, name):
        with jax.named_scope(f"near{c}{name}"):
            s = state[c]
            (s["near" + name],) = run(
                lambda *x: call(near_kernel, [b_rows], *x, name="near"), s["po"], s["c" + name]
            )
            s["far" + name] = over_y(s["near" + name])

    def norm_two(c):
        with jax.named_scope(f"normtwo{c}"):
            s = state[c]
            outs = [b_rows, f_rows, b_rows, shaped((3, width), F32)]
            s["out"], s["gs"], s["gfo"], s["sum2"] = run(
                lambda *x: call(norm_two_kernel, outs, *x, name="norm_two"),
                s["near2"],
                s["far2"],
                s["y"],
                cot[c],
                par_two,
            )
            s["gfp"] = over_core(s["gfo"])

    def feed_back(c, which, dtype):
        with jax.named_scope(f"feedback{c}{which}"):
            s = state[c]
            outs = [h_rows, shaped((half, width), dtype), shaped((1, hidden_here), F32)]
            s["gp" + which], s["p" + which], s["sumu" + which] = run(
                lambda *x: scalar_call(ffn_back_kernel, outs, *x, name="feed_back"),
                place,
                s["gf" + which],
                *down_two,
                s["s" + which],
                *up_two,
            )
            if which == "p":
                s["c5"] = over_core(s["pp"])

    def norm_one_back(c):
        with jax.named_scope(f"normoneback{c}"):
            s = state[c]
            s["gfirst"], s["gao"], s["sum1"] = run(
                lambda *x: call(
                    norm_one_back_kernel,
                    [f_rows, b_rows, shaped((3, width), F32)],
                    *x,
                    name="norm_one_back",
                ),
                s["gs"],
                s["near5"],
                s["far5"],
                s["n1"],
                s["i1"],
                par_one,
            )
            s["gap"] = over_core(s["gao"])

    def weight_grad(kernel, operands, rows, cols, name, small=False):
        with jax.named_scope(name):
            outs = [
                shaped((rows + small * EXTRA, cols), F32),
                shaped((rows + small * 2 * EXTRA, cols), BF),
            ]
            keep, send = run(lambda *x: scalar_call(kernel, outs, *x, name=name), place, *operands)
            return Reduction(run, name, keep, over_x(send), small)

    def owned(red, name):
        with jax.named_scope(name):
            return run(
                lambda *x: scalar_call(owned_kernel, [shaped(red.shape, F32)], *x, name=name),
                place,
                red.own,
                red.moved,
            )[0]

    four = [(c, w) for c in range(2) for w in "op"]

    def pieces_of(name):
        return [state[c][name + w] for c, w in four]

    cot = (cot_a, cot_b)
    norm_one(0)
    feed(0, "o", F32)
    norm_one(1)
    feed(0, "p", BF)
    feed(1, "p", BF)
    near_sum(0, "2")
    feed(1, "o", F32)
    near_sum(1, "2")
    norm_two(0)
    feed_back(0, "o", F32)
    feed_back(0, "p", BF)
    norm_two(1)
    with jax.named_scope("outback"):
        out_back = over_z2(state[1]["out"])
    near_sum(0, "5")
    feed_back(1, "o", F32)
    feed_back(1, "p", BF)
    if n_f == 2:
        red_down = weight_grad(
            down_grad_kernel, pieces_of("h") + pieces_of("gf"), hidden_here, width // 2, "down_grad"
        )
    near_sum(1, "5")
    norm_one_back(0)
    if n_f == 2:
        red_up = weight_grad(
            up_grad_kernel, pieces_of("y") + pieces_of("gp"), width // 2, hidden_here, "up_grad"
        )
    norm_one_back(1)
    (out_back,) = touch(out_back)
    with jax.named_scope("smallpack"):
        (packed,) = run(
            lambda *x: call(pack_kernel, [shaped((8, width), F32)], *x, name="pack"),
            *[state[c][s] for s in ("sum1", "sum2") for c in range(2)],
            *pieces_of("sumu"),
        )
        packed_moved = over_core(packed)
    def placed(blocks):
        return run(
            lambda *x: scalar_call(place_kernel, [shaped(tokens.shape, BF)], *x, name="place"),
            place,
            *blocks,
        )[0]

    def both_halves(a, b):
        return a, over_core(a), b, over_core(b)

    if n_f == 2:
        red_down.step()
    with jax.named_scope("placeout"):
        out_blocks = both_halves(after(state[0]["out"], out_back), out_back)
    grad_attn = pieces_of("ga")
    grad_mixed, inner = run(
        lambda *x: call(
            grad_mixed_kernel, [shaped((n_own, wide), BF), shaped((heads, n_own), F32)], *x, name="grad_mixed"
        ),
        *grad_attn,
        out_w,
        mixed_f,
    )
    (*out_blocks, packed_moved) = touch(*out_blocks, packed_moved)

    early, late = tuple(range(heads - 1)), (heads - 1,)
    bwd_args = (q, k, v, grad_mixed, logs, inner)
    n_one, n_two = 3 * len(early) * HD, 3 * HD
    with jax.named_scope("back1"):
        dq1, own1, far1 = run(lambda *x: attend_bwd(early, 0, total, 2, *x), *bwd_args)
    if n_f == 2:
        red_up.step()
        red_down.step()
    with jax.named_scope("back1"):
        moved1 = over_z1(after(far1, run.done))
    with jax.named_scope("back2"):
        dq2, far2 = run(lambda *x: attend_bwd(late, 1, n_own, 1, *x, last=False), *bwd_args)
        moved2 = over_z1(far2)
    with jax.named_scope("back3"):
        dq2, own2 = run(lambda *x: attend_bwd(late, 0, n_own, 1, *x), *bwd_args, dq2)
    if n_f == 2:
        red_one = weight_grad(
            functools.partial(qkv_grad_kernel, True),
            own + other + [dq1, own1, far1] + mixed + grad_attn + [packed, packed_moved],
            n_one + wide,
            width // 2,
            "one_grad",
            True,
        )
    with jax.named_scope("placeout"):
        output = placed(out_blocks)
    if n_f == 2:
        red_down.step()
        red_up.step()
        red_two = weight_grad(
            functools.partial(qkv_grad_kernel, False),
            own + other + [dq2, own2, far2],
            n_two,
            width // 2,
            "two_grad",
            True,
        )
        red_one.step()
        (moved1,) = touch(moved1)

    item = [dict(), dict()]

    def input_part(c):
        with jax.named_scope(f"inputpart{c}"):
            s = item[c]
            s["po"], pp = run(
                lambda *x: call(
                    functools.partial(input_part_kernel, c * rows), [f_rows, b_rows], *x, name="input_part"
                ),
                dq1,
                own1,
                moved1,
                dq2,
                own2,
                moved2,
                qkv_w,
            )
            s["cp"] = over_core(pp)

    def input_near(c):
        with jax.named_scope(f"inputnear{c}"):
            s = item[c]
            (s["near"],) = run(
                lambda *x: call(near_kernel, [b_rows], *x, name="near"), s["po"], s["cp"]
            )
            s["far"] = over_y(s["near"])

    def input_last(c):
        with jax.named_scope(f"inputlast{c}"):
            s = item[c]
            (s["in"],) = run(
                lambda *x: call(input_grad_kernel, [b_rows], *x, name="input_grad"),
                state[c]["gfirst"],
                s["near"],
                s["far"],
            )

    input_part(1)
    input_part(0)
    if n_f == 2:
        (red_down.moved,) = touch(red_down.moved)
    input_near(1)
    input_near(0)
    if n_f == 2:
        red_up.step()
        owned_down = owned(red_down, "owned_down")
        red_two.step()
        red_one.step()
    input_last(1)
    with jax.named_scope("inputback"):
        in_back = over_z2(item[1]["in"])
    if n_f == 2:
        red_two.step()
    input_last(0)
    with jax.named_scope("placein"):
        in_far = over_core(item[0]["in"])
    if n_f == 2:
        owned_up = owned(red_up, "owned_up")
        red_one.step()
        red_two.step()
    (in_back,) = touch(in_back)
    with jax.named_scope("placein"):
        in_blocks = [item[0]["in"], in_far, in_back, over_core(in_back)]
    with jax.named_scope("finish"):
        if n_f == 2:
            qkv_grad, owned_out, small, bias_grad = run(
                lambda *x: scalar_call(
                    owned_qkv_kernel,
                    [
                        shaped((3, wide, width // 2), F32),
                        shaped((wide, width // 2), F32),
                        shaped((8, width), F32),
                        shaped((2, wide), F32),
                    ],
                    *x,
                    name="owned_qkv",
                ),
                place,
                red_one.own,
                red_two.own,
                red_one.moved,
                red_two.moved,
            )
            owned_qkv = qkv_grad.transpose(2, 0, 1)
        else:

            def reduce_plain(left, right, axis):
                grad = mm(jnp.concatenate(left), jnp.concatenate(right), TN)
                keep = lax.psum_scatter(grad, "fsdp", scatter_dimension=axis, tiled=True)
                return lax.psum(keep, "context").astype(BF).astype(F32)

            zero = jnp.zeros((n_own, wide), BF)
            cut = len(early) * HD
            dk = [own1[:, :cut], own2[:, :HD], far1[:, :cut], far2[:, :HD]]
            dv = [own1[:, cut:], own2[:, HD:], far1[:, cut:], far2[:, HD:]]
            left = jnp.concatenate([dq1, dq2, *dk[:2], *dv[:2]], axis=1)
            right = jnp.concatenate([zero, *dk[2:], *dv[2:]], axis=1)
            owned_up = reduce_plain(pieces_of("y"), pieces_of("gp"), 0)
            owned_down = reduce_plain(pieces_of("h"), pieces_of("gf"), 1)
            owned_out = reduce_plain(mixed, grad_attn, 1)
            owned_qkv = reduce_plain(own + other, [left, right], 0).reshape(w_qkv.shape)
            column_sums = jnp.sum((left.astype(F32) + right.astype(F32)), axis=0)
            bias_grad = jnp.stack([column_sums[:wide], column_sums[2 * wide :]])
            small = jnp.concatenate([packed[:6] + packed_moved[:6], packed[6:]])
            small, bias_grad = lax.psum((small, bias_grad), ("fsdp", "context"))
    with jax.named_scope("placein"):
        input_grad = placed(in_blocks)
    return (
        output,
        input_grad,
        owned_qkv,
        bias_grad,
        owned_out,
        small[0],
        small[1],
        small[2],
        owned_up,
        small[6],
        owned_down,
        small[3],
        small[4],
        small[5],
    )


def solution(mesh):
    sizes = tuple(mesh.shape[name] for name in ("fsdp", "context", "tensor"))
    specs = (
        P("fsdp", None, "tensor"),
        P(None, "tensor"),
        P("tensor", "fsdp"),
        P(),
        P(),
        P(),
        P("fsdp", "tensor"),
        P("tensor"),
        P("tensor", "fsdp"),
        P(),
        P(),
        P(),
    )
    rows = P("fsdp", "context", None)
    return jax.shard_map(
        functools.partial(body, sizes),
        mesh=mesh,
        in_specs=(rows, rows) + specs,
        out_specs=(rows, rows) + specs,
        check_vma=False,
    )
```

```python
import functools
import math

import jax
import jax.numpy as jnp
from jax import lax
from jax.experimental import pallas as pl
from jax.experimental.pallas import tpu as pltpu
from jax.sharding import PartitionSpec as P

HD = 64
SCALE = 1.0 / math.sqrt(HD)
SCALE_LOG2 = SCALE * math.log2(math.e)
EPS = 1e-06
BF = jnp.bfloat16
F32 = jnp.float32
NT = (((1,), (1,)), ((), ()))
TN = (((0,), (0,)), ((), ()))
NN = (((1,), (0,)), ((), ()))


def mm(a, b, dims=NN):
    return lax.dot_general(a, b, dims, preferred_element_type=F32)


def shaped(shape, dtype):
    return jax.ShapeDtypeStruct(shape, dtype)


def call(kernel, outs, *operands, name, limit=16, **extra):
    return pl.pallas_call(
        kernel,
        out_shape=list(outs),
        cost_estimate=pl.CostEstimate(flops=int(5e9), bytes_accessed=1, transcendentals=0),
        compiler_params=pltpu.CompilerParams(vmem_limit_bytes=limit << 20),
        name=name,
        **extra,
    )(*operands)


SMEM = pl.BlockSpec(memory_space=pltpu.SMEM)
VMEM = pl.BlockSpec(memory_space=pltpu.VMEM)


def scalar_call(kernel, outs, scalars, *operands, **kw):
    specs = [SMEM] + [VMEM] * len(operands)
    return call(kernel, outs, scalars, *operands, in_specs=specs, **kw)


def lanes(ref, index, size):
    return ref[:, pl.ds(pl.multiple_of(index * size, 128), size)]


def qkv_kernel(*refs):
    rows, (w_ref, b_ref, q_ref, k_ref, v_ref) = refs[:8], refs[8:]
    n = rows[0].shape[0]
    wide = q_ref.shape[1]
    for i, ref in enumerate(rows):
        here = slice(i * n, (i + 1) * n)
        skip = 0 if i < 4 else wide
        full = (mm(ref[...], w_ref[skip:, :], NT) + b_ref[:, skip:]).astype(BF)
        if i < 4:
            q_ref[here, :] = full[:, :wide]
        k_ref[here, :] = full[:, wide - skip : 2 * wide - skip]
        v_ref[here, :] = full[:, 2 * wide - skip :]


def attend_fwd_kernel(chunk, *refs):
    q_ref, k_ref, v_ref = refs[:3]
    o_ref, p_ref, f_ref, l_ref = refs[-4:]
    outs, logs = [], []
    for h in range(q_ref.shape[1] // HD):
        cols = slice(h * HD, (h + 1) * HD)
        scores = mm(q_ref[:, cols], k_ref[:, cols], NT)
        top = jnp.max(scores, axis=1, keepdims=True)
        expo = jnp.exp2((scores - top) * SCALE_LOG2)
        total = jnp.sum(expo, axis=1, keepdims=True)
        outs.append(mm(expo.astype(BF), v_ref[:, cols]) / total)
        logs.append(top * SCALE_LOG2 + jnp.log2(total))
    mixed = jnp.concatenate(outs, axis=1)
    f_ref[...] = mixed
    l_ref[...] = jnp.concatenate(logs, axis=1).T
    for step, ref in enumerate((o_ref, p_ref)):

        @pl.when(pl.program_id(0) == step)
        def _():
            ref[...] = mixed.astype(BF)


def attend_fwd(chunk, block, q, k, v, *before):
    nq, w = q.shape
    nk = k.shape[0]
    heads = w // HD
    q_spec = pl.BlockSpec((block, w), lambda i: (chunk * 2 + i, 0))
    l_spec = pl.BlockSpec((heads, block), lambda i: (0, chunk * 2 + i))
    o_spec = pl.BlockSpec((block, w), lambda i: (0, 0))
    k_spec = pl.BlockSpec((nk, w), lambda i: (0, 0))
    anywhere = pl.BlockSpec(memory_space=pl.ANY)
    return call(
        functools.partial(attend_fwd_kernel, chunk),
        [shaped((block, w), BF)] * 2 + [shaped((nq, w), F32), shaped((heads, nq), F32)],
        q,
        k,
        v,
        *before,
        name="attend_fwd",
        limit=24,
        grid=(2,),
        in_specs=[q_spec, k_spec, k_spec] + [anywhere] * len(before),
        out_specs=[o_spec, o_spec, q_spec, l_spec],
        input_output_aliases={3: 2, 4: 3} if before else {},
    )


def grad_mixed_kernel(*refs):
    gas, (w_ref, f_ref, g_ref, d_ref) = refs[:4], refs[4:]
    n = gas[0].shape[0]
    heads = w_ref.shape[0] // HD
    for i, ga in enumerate(gas):
        here = slice(i * n, (i + 1) * n)
        g = mm(ga[...], w_ref[...], NT).astype(BF)
        g_ref[here, :] = g
        prod = (g.astype(F32) * f_ref[here, :]).T
        d_ref[:, here] = jnp.concatenate(
            [jnp.sum(prod[h * HD : (h + 1) * HD], axis=0, keepdims=True) for h in range(heads)]
        )


def attend_bwd_kernel(heads, first, last, split, *refs):
    q_ref, k_ref, v_ref, g_ref, l_ref, d_ref = refs[:6]
    add_ref = refs[6] if not first else None
    dq_ref, outs, acc = refs[6 + (not first)], refs[7 + (not first) : -1], refs[-1]
    dqs, dks, dvs = [], [], []
    for h in heads:
        cols = slice(h * HD, (h + 1) * HD)
        q, k, v, g = q_ref[:, cols], k_ref[:, cols], v_ref[:, cols], g_ref[:, cols]
        probs = jnp.exp2(mm(k, q, NT) * SCALE_LOG2 - l_ref[h : h + 1, :])
        grad_scores = (probs * (mm(v, g, NT) - d_ref[h : h + 1, :])).astype(BF)
        dvs.append(mm(probs.astype(BF), g))
        dks.append(mm(grad_scores, q) * SCALE)
        dqs.append(mm(k, grad_scores, TN))
    dq = (dqs[0] if len(dqs) == 1 else jnp.concatenate(dqs, axis=0)).T
    if not first:
        dq = dq + add_ref[...]
    dq_ref[...] = (dq * SCALE).astype(BF) if last else dq
    dkv = jnp.concatenate(dks + dvs, axis=1)
    step = pl.program_id(0)

    @pl.when(step == 0)
    def _():
        acc[...] = dkv

    @pl.when(step > 0)
    def _():
        acc[...] += dkv

    @pl.when(step == pl.num_programs(0) - 1)
    def _():
        n = acc.shape[0] // len(outs)
        for i, ref in enumerate(outs):
            ref[...] = acc[i * n : (i + 1) * n].astype(BF)


def attend_bwd(heads, key_block, key_rows, split, q, k, v, g, logs, inner, *add, last=True, block=256):
    nq, w = q.shape
    n = len(heads) * HD
    q_spec = pl.BlockSpec((block, w), lambda i: (i, 0))
    k_spec = pl.BlockSpec((key_rows, w), lambda i: (key_block, 0))
    n_spec = pl.BlockSpec((block, n), lambda i: (i, 0))
    l_spec = pl.BlockSpec((logs.shape[0], block), lambda i: (0, i))
    whole = pl.BlockSpec((key_rows // split, 2 * n), lambda i: (0, 0))
    return call(
        functools.partial(attend_bwd_kernel, heads, not add, last, split),
        [shaped((nq, n), BF if last else F32)] + [shaped((key_rows // split, 2 * n), BF)] * split,
        q,
        k,
        v,
        g,
        logs,
        inner,
        *add,
        name="attend_bwd",
        limit=36,
        grid=(nq // block,),
        in_specs=[q_spec, k_spec, k_spec, q_spec, l_spec, l_spec] + [n_spec] * len(add),
        out_specs=[n_spec] + [whole] * split,
        scratch_shapes=[pltpu.VMEM((key_rows, 2 * n), F32)],
    )


def normed(x):
    centred = x - jnp.mean(x, axis=-1, keepdims=True)
    inverse = lax.rsqrt(jnp.mean(centred * centred, axis=-1, keepdims=True) + EPS)
    return centred * inverse, inverse


def norm_back(g, norm, inverse):
    return inverse * (
        g
        - jnp.mean(g, axis=-1, keepdims=True)
        - norm * jnp.mean(g * norm, axis=-1, keepdims=True)
    )


def down_rows(*terms):
    return jnp.concatenate([jnp.sum(t, axis=0, keepdims=True) for t in terms], axis=0)


def norm_one_kernel(m0, m1, m2, m3, w0, w1, w2, w3, t_ref, p_ref, y_ref, low_ref, n_ref, i_ref):
    near = mm(m0[...], w0[...]) + mm(m1[...], w1[...])
    far = mm(m2[...], w2[...]) + mm(m3[...], w3[...])
    norm, inverse = normed(t_ref[...].astype(F32) + ((near + far) + p_ref[0:1, :]))
    y = norm * p_ref[1:2, :] + p_ref[2:3, :]
    y_ref[...] = y
    low_ref[...] = y.astype(BF)
    n_ref[...] = norm
    i_ref[...] = inverse


def ffn_kernel(s_ref, y_ref, up_own, up_far, b_ref, down_own, down_far, h_ref, sl_ref, p_ref):
    f = s_ref[0]
    size = up_own.shape[0]
    x = mm(lanes(y_ref, f, size), up_own[...]) + mm(lanes(y_ref, 1 - f, size), up_far[...]) + b_ref[...]
    cdf = 0.5 * (1.0 + lax.erf(x * (1.0 / math.sqrt(2.0))))
    pdf = jnp.exp(-0.5 * x * x) * (1.0 / math.sqrt(2.0 * math.pi))
    sl_ref[...] = cdf + x * pdf
    hidden = (x * cdf).astype(BF)
    h_ref[...] = hidden
    for part, ref in ((f, down_own), (1 - f, down_far)):
        here = pl.ds(pl.multiple_of(part * size, 128), size)
        p_ref[:, here] = mm(hidden, ref[...]).astype(p_ref.dtype)


def norm_two_kernel(near, far, y_ref, g_ref, p_ref, o_ref, gs_ref, gf_ref, sums):
    ffn = near[...].astype(F32) + far[...].astype(F32)
    norm, inverse = normed(y_ref[...] + (ffn + p_ref[0:1, :]))
    o_ref[...] = (norm * p_ref[1:2, :] + p_ref[2:3, :]).astype(BF)
    g = g_ref[...].astype(F32)
    grad = norm_back(g * p_ref[1:2, :], norm, inverse)
    low = grad.astype(BF)
    gs_ref[...] = grad
    gf_ref[...] = low
    sums[...] = down_rows(low.astype(F32), g * norm, g)


def ffn_back_kernel(s_ref, g_ref, down_own, down_far, sl_ref, up_own, up_far, gp_ref, p_ref, sums):
    f = s_ref[0]
    size = up_own.shape[0]
    grad = mm(lanes(g_ref, f, size), down_own[...], NT) + mm(lanes(g_ref, 1 - f, size), down_far[...], NT)
    low = (grad * sl_ref[...]).astype(BF)
    gp_ref[...] = low
    sums[...] = down_rows(low.astype(F32))
    for part, ref in ((f, up_own), (1 - f, up_far)):
        here = pl.ds(pl.multiple_of(part * size, 128), size)
        p_ref[:, here] = mm(low, ref[...], NT).astype(p_ref.dtype)


def norm_one_back_kernel(gs_ref, near, far, n_ref, i_ref, p_ref, g_ref, low_ref, sums):
    grad_y = gs_ref[...] + (near[...].astype(F32) + far[...].astype(F32))
    norm = n_ref[...]
    grad = norm_back(grad_y * p_ref[1:2, :], norm, i_ref[...])
    low = grad.astype(BF)
    g_ref[...] = grad
    low_ref[...] = low
    sums[...] = down_rows(low.astype(F32), grad_y * norm, grad_y)


def input_part_kernel(first_row, dq1, dkv1, m1, dq2, dkv2, m2, w_ref, o_ref, p_ref):
    n = o_ref.shape[0]
    w1, w2 = dq1.shape[1], dq2.shape[1]
    for part, ref in enumerate((o_ref, p_ref)):
        here = slice(first_row + part * n, first_row + (part + 1) * n)
        low1 = (dkv1[here, :].astype(F32) + m1[here, :].astype(F32)).astype(BF)
        low2 = (dkv2[here, :].astype(F32) + m2[here, :].astype(F32)).astype(BF)
        grads = jnp.concatenate(
            [dq1[here, :], dq2[here, :], low1[:, :w1], low2[:, :w2], low1[:, w1:], low2[:, w2:]], axis=1
        )
        ref[...] = mm(grads, w_ref[...]).astype(ref.dtype)


def near_kernel(a_ref, b_ref, o_ref):
    o_ref[...] = (a_ref[...] + b_ref[...].astype(F32)).astype(BF)


def input_grad_kernel(g_ref, a_ref, b_ref, o_ref):
    o_ref[...] = (g_ref[...] + (a_ref[...].astype(F32) + b_ref[...].astype(F32))).astype(BF)


def place_kernel(s_ref, a, b, c, d, o_ref):
    n = a.shape[0]
    group, core = s_ref[2], s_ref[3]
    for block, half, ref in ((group, core, a), (group, 1 - core, b), (1 - group, core, c), (1 - group, 1 - core, d)):
        o_ref[block, pl.ds(pl.multiple_of(half * n, n), n), :] = ref[...]


def pack_kernel(a0, a1, b0, b1, u0, u1, u2, u3, o_ref):
    o_ref[0:3, :] = a0[...] + a1[...]
    o_ref[3:6, :] = b0[...] + b1[...]
    o_ref[6:7, :] = u0[...] + u1[...] + u2[...] + u3[...]
    o_ref[7:8, :] = jnp.zeros_like(u0)


EXTRA = 16


def two_parts(x):
    high = x.astype(BF).astype(F32)
    return high + (x - high).astype(BF).astype(F32)


def put(ref, main, small):
    n = main.shape[0]
    ref[0:n, :] = main.astype(ref.dtype)
    if small is not None:
        high = small.astype(ref.dtype)
        ref[n : n + EXTRA, :] = high
        if ref.shape[0] > n + EXTRA:
            ref[n + EXTRA :, :] = (small - high.astype(F32)).astype(ref.dtype)


def get(ref, small):
    if not small:
        return ref[...].astype(F32), None
    parts = 1 if ref.dtype == F32 else 2
    n = ref.shape[0] - parts * EXTRA
    rest = ref[n : n + EXTRA, :].astype(F32)
    if parts == 2:
        rest = rest + ref[n + EXTRA :, :].astype(F32)
    return ref[0:n, :].astype(F32), rest


def up_grad_kernel(s_ref, *refs):
    ys, gs, (keep, send) = refs[:4], refs[4:8], refs[8:]
    f = s_ref[0]
    size = ys[0].shape[1] // 2
    for out, part in ((send, 1 - f), (keep, f)):
        put(out, sum(mm(lanes(y, part, size), g[...], TN) for y, g in zip(ys, gs)), None)


def down_grad_kernel(s_ref, *refs):
    hs, gs, (keep, send) = refs[:4], refs[4:8], refs[8:]
    f = s_ref[0]
    size = gs[0].shape[1] // 2
    for out, part in ((send, 1 - f), (keep, f)):
        put(out, sum(mm(h[...], lanes(g, part, size), TN) for h, g in zip(hs, gs)), None)


def qkv_grad_kernel(with_out, s_ref, *refs):
    rows, (dq, own_ref, far_ref), more, (keep, send) = refs[:8], refs[8:11], refs[11:-2], refs[-2:]
    f = s_ref[0]
    size = rows[0].shape[1] // 2
    n = rows[0].shape[0]
    m = dq.shape[1]
    own = jnp.concatenate([dq[...], own_ref[...]], axis=1)
    far = far_ref[...]
    far_sums = jnp.sum(far.astype(F32), axis=0, keepdims=True)
    sums = jnp.sum(own.astype(F32), axis=0, keepdims=True)
    sums = jnp.concatenate([sums[:, :m], sums[:, m:] + far_sums], axis=1)
    if sums.shape[1] < size:
        sums = jnp.concatenate([sums, jnp.zeros((1, size - sums.shape[1]), F32)], axis=1)
    small = [sums]
    if with_out:
        packed, moved = more[-2:]
        six = packed[0:6, :] + moved[0:6, :]
        ups = packed[6:7, :]
        small = [six[:, :size], ups[:, :size], six[:, size:], ups[:, size:], sums]
    small.append(jnp.zeros((EXTRA - sum(x.shape[0] for x in small), size), F32))
    small = two_parts(jnp.concatenate(small, axis=0))
    for out, part in ((send, 1 - f), (keep, f)):
        one = two = None
        for i in range(4):
            here = slice(i * n, (i + 1) * n)
            a = mm(own[here], lanes(rows[i], part, size), TN)
            b = mm(far[here], lanes(rows[4 + i], part, size), TN)
            one = a if one is None else one + a
            two = b if two is None else two + b
        grad = [one[:m], one[m:] + two]
        if with_out:
            grad.append(sum(mm(a[...], lanes(g, part, size), TN) for a, g in zip(more[:4], more[4:8])))
        put(out, jnp.concatenate(grad, axis=0), small)


def half_of(main, which):
    n = main.shape[0] // 2
    return jnp.where(which == 0, main[:n], main[n:])


def first_sum_kernel(small, s_ref, keep, moved, own, send):
    (a, c), (b, d) = get(keep, small), get(moved, small)
    total = a + b
    rest = two_parts(c + d) if small else None
    put(own, half_of(total, s_ref[1]), rest)
    put(send, half_of(total, 1 - s_ref[1]), rest)


def sum_kernel(small, a_ref, b_ref, out):
    (a, c), (b, d) = get(a_ref, small), get(b_ref, small)
    put(out, a + b, c + d if small else None)


def joined(s_ref, own, moved):
    first = s_ref[1] == 0
    return jnp.concatenate([jnp.where(first, own, moved), jnp.where(first, moved, own)], axis=0)


def owned_kernel(s_ref, own, moved, out):
    out[...] = joined(s_ref, get(own, False)[0], get(moved, False)[0])


def owned_qkv_kernel(s_ref, own1, own2, moved1, moved2, qkv, outw, sums, bias):
    (one, small1), (two, small2) = get(own1, True), get(own2, True)
    one = joined(s_ref, one, get(moved1, True)[0])
    two = joined(s_ref, two, get(moved2, True)[0])
    n = outw.shape[0]
    m1, m2 = (one.shape[0] - n) // 3, two.shape[0] // 3
    for j in range(3):
        qkv[j, 0:m1, :] = one[j * m1 : (j + 1) * m1]
        qkv[j, m1:, :] = two[j * m2 : (j + 1) * m2]
    outw[...] = one[3 * m1 :]
    sums[0:7, :] = jnp.concatenate([small1[0:7], small1[7:14]], axis=1)
    sums[7:8, :] = jnp.zeros_like(sums[7:8, :])
    for i, j in ((0, 0), (1, 2)):
        bias[i : i + 1, :] = jnp.concatenate(
            [small1[14:15, j * m1 : (j + 1) * m1], small2[0:1, j * m2 : (j + 1) * m2]], axis=1
        )


def swap(x, axis, size, mask):
    return lax.ppermute(x, axis, [(i, i ^ mask) for i in range(size)])


def pick(first, second, bit, axis):
    n = first.shape[axis]
    ring = jnp.concatenate([first, second, first], axis=axis)
    return lax.dynamic_slice_in_dim(ring, bit * n, 2 * n, axis)


class Order:
    def __init__(self):
        self.done = None

    def __call__(self, fn, *operands):
        if self.done is not None:
            operands, _ = lax.optimization_barrier((operands, self.done))
        out = fn(*operands)
        self.done = out
        return out


class Reduction:
    def __init__(self, run, name, place, keep, moved, small, over_z1, over_z2):
        self.run, self.name, self.place, self.small = run, name, place, small
        self.own, self.moved, self.stage = keep, moved, 0
        self.over = [over_z1, over_z2, over_z1]
        self.rows, self.cols = keep.shape[0] - small * EXTRA, keep.shape[1]

    def step(self):
        self.stage += 1
        low = shaped((self.rows // 2 + self.small * 2 * EXTRA, self.cols), BF)
        wide = shaped((self.rows // 2 + self.small * EXTRA, self.cols), F32)
        name = f"{self.name}_{self.stage}"
        with jax.named_scope(name):
            if self.stage == 1:
                kernel = functools.partial(first_sum_kernel, self.small)
                fn = lambda *x: scalar_call(kernel, [wide, low], *x, name=name)
                self.own, send = self.run(fn, self.place, self.own, self.moved)
            else:
                kernel = functools.partial(sum_kernel, self.small)
                fn = lambda *x: call(kernel, [low], *x, name=name)
                (self.own,) = self.run(fn, self.own, self.moved)
                send = self.own
            self.moved = self.over[self.stage - 1](send)


def body(sizes, *args):
    (
        tokens,
        cotangent,
        w_qkv,
        qv_bias,
        w_out,
        out_bias,
        gain_one,
        shift_one,
        w_up,
        up_bias,
        w_down,
        down_bias,
        gain_two,
        shift_two,
    ) = args
    n_f, n_c, n_t = sizes
    _, rows, width = tokens.shape
    wide = w_qkv.shape[2]
    heads = wide // HD
    hidden_here = w_up.shape[1]
    half = rows // 2
    f = lax.axis_index("fsdp") if n_f == 2 else 0
    z = lax.axis_index("context")
    core = lax.axis_index("tensor") % 2
    group = z // 2
    over_core = functools.partial(swap, axis="tensor", size=n_t, mask=1)
    over_y = functools.partial(swap, axis="tensor", size=n_t, mask=2)
    over_both = functools.partial(swap, axis="tensor", size=n_t, mask=3)
    over_z1 = functools.partial(swap, axis="context", size=n_c, mask=1)
    over_z2 = functools.partial(swap, axis="context", size=n_c, mask=2)
    over_x = functools.partial(swap, axis="fsdp", size=n_f, mask=1)
    run = Order()

    def whole_f(w, axis):
        return lax.all_gather(w, "fsdp", axis=axis, tiled=True)

    def halves(w, axis):
        if n_f == 2:
            return w, over_x(w)
        w = whole_f(w, axis)
        return jnp.split(w, 2, axis=axis)

    def block_of(x, which, part):
        return lax.dynamic_slice(x, (which, part * half, 0), (1, half, width))[0]

    def touch(*x):
        return run(lambda *a: a, *x)

    def after(x, *others):
        return lax.optimization_barrier((x, others))[0]

    with jax.named_scope("arrive"):
        give = run(lambda t: block_of(t, 1 - group, core), tokens)
        b_own = over_z2(give)
        a_own = run(lambda t: block_of(t, group, core), tokens)
        oa_own = over_z1(a_own)
        qkv_t = w_qkv.transpose(1, 2, 0).reshape(3 * wide, -1)
        qkv_moved = over_x(qkv_t) if n_f == 2 else whole_f(qkv_t, 1)
        out_moved = over_x(w_out) if n_f == 2 else whole_f(w_out, 1)
        a_far, place, par_one, par_two, bias_row, up_row = run(
            lambda t, qb, ub, p1, p2: (
                block_of(t, group, 1 - core),
                jnp.stack(
                    [
                        jnp.int32(f),
                        (z % 2).astype(jnp.int32),
                        group.astype(jnp.int32),
                        core.astype(jnp.int32),
                    ]
                ),
                jnp.stack(p1),
                jnp.stack(p2),
                jnp.concatenate([qb[0], jnp.zeros_like(qb[0]), qb[1]])[None],
                ub[None],
            ),
            tokens,
            qv_bias,
            up_bias,
            (out_bias, gain_one, shift_one),
            (down_bias, gain_two, shift_two),
        )
        qkv_w = run(lambda a, b: pick(a, b, f, 1) if n_f == 2 else b, qkv_t, qkv_moved)
        out_w = run(lambda a, b: pick(a, b, f, 1) if n_f == 2 else b, w_out, out_moved)
        (b_own,) = touch(b_own)
        ob_own = over_z1(b_own)
        (oa_own,) = touch(oa_own)
        b_far, oa_far = over_core(b_own), over_core(oa_own)
        b_far, oa_far, out_later = touch(b_far, oa_far, out_w)
        out_near, out_far = over_core(out_later), over_y(out_later)
        up_two = halves(after(w_up, out_later), 0)
        out_near, out_far = touch(out_near, out_far)
        (ob_own,) = touch(ob_own)
        ob_far = over_core(ob_own)
    own = [a_own, a_far, b_own, b_far]
    other = [oa_own, oa_far, ob_own, ob_far]
    total = 8 * half
    n_own = total // 2

    q, k, v = run(
        lambda *x: call(
            qkv_kernel,
            [shaped((n_own, wide), BF), shaped((total, wide), BF), shaped((total, wide), BF)],
            *x,
            name="qkv",
        ),
        *own,
        *other,
        qkv_w,
        bias_row,
    )
    with jax.named_scope("cotangent"):
        cot_give, cot_a = run(
            lambda x: (block_of(x, 1 - group, core), block_of(x, group, core)), cotangent
        )
        cot_b = over_z2(cot_give)
    with jax.named_scope("down_weight"):
        down_two = halves(after(w_down, q), 1)
    with jax.named_scope("out_weight"):
        out_both = over_both(after(out_later, q))

    mixed, pieces, shared = [], [], ()
    for c in range(2):
        with jax.named_scope(f"attend{c}"):
            mo, mp, *shared = run(lambda *x: attend_fwd(c, half, *x), q, k, v, *shared)
            mixed += [mo, mp]
            if c == 0:
                (*up_two, out_both) = touch(*up_two, out_both)
            else:
                (*pieces[0], cot_b) = touch(*pieces[0], cot_b)
            mo, mp = touch(mo, mp)
            pieces.append((mo, over_core(mp), over_y(mo), over_both(mp)))
    mixed_f, logs = shared
    tok = (a_own, b_own)
    f_rows = shaped((half, width), F32)
    b_rows = shaped((half, width), BF)
    h_rows = shaped((half, hidden_here), BF)
    state = [dict(), dict()]

    def norm_one(c):
        with jax.named_scope(f"normone{c}"):
            s = state[c]
            outs = [f_rows, b_rows, f_rows, shaped((half, 1), F32)]
            s["y"], s["yo"], s["n1"], s["i1"] = run(
                lambda *x: call(norm_one_kernel, outs, *x, name="norm_one"),
                *pieces[c],
                out_w,
                out_near,
                out_far,
                out_both,
                tok[c],
                par_one,
            )
            s["yp"] = over_core(s["yo"])

    def feed(c, which, dtype):
        with jax.named_scope(f"feed{c}{which}"):
            s = state[c]
            outs = [h_rows, shaped((half, hidden_here), F32), shaped((half, width), dtype)]
            s["h" + which], s["s" + which], s["p" + which] = run(
                lambda *x: scalar_call(ffn_kernel, outs, *x, name="feed"),
                place,
                s["y" + which],
                *up_two,
                up_row,
                *down_two,
            )
            if which == "p":
                s["c2"] = over_core(s["pp"])

    def near_sum(c, name):
        with jax.named_scope(f"near{c}{name}"):
            s = state[c]
            (s["near" + name],) = run(
                lambda *x: call(near_kernel, [b_rows], *x, name="near"), s["po"], s["c" + name]
            )
            s["far" + name] = over_y(s["near" + name])

    def norm_two(c):
        with jax.named_scope(f"normtwo{c}"):
            s = state[c]
            outs = [b_rows, f_rows, b_rows, shaped((3, width), F32)]
            s["out"], s["gs"], s["gfo"], s["sum2"] = run(
                lambda *x: call(norm_two_kernel, outs, *x, name="norm_two"),
                s["near2"],
                s["far2"],
                s["y"],
                cot[c],
                par_two,
            )
            s["gfp"] = over_core(s["gfo"])

    def feed_back(c, which, dtype):
        with jax.named_scope(f"feedback{c}{which}"):
            s = state[c]
            outs = [h_rows, shaped((half, width), dtype), shaped((1, hidden_here), F32)]
            s["gp" + which], s["p" + which], s["sumu" + which] = run(
                lambda *x: scalar_call(ffn_back_kernel, outs, *x, name="feed_back"),
                place,
                s["gf" + which],
                *down_two,
                s["s" + which],
                *up_two,
            )
            if which == "p":
                s["c5"] = over_core(s["pp"])

    def norm_one_back(c):
        with jax.named_scope(f"normoneback{c}"):
            s = state[c]
            s["gfirst"], s["gao"], s["sum1"] = run(
                lambda *x: call(
                    norm_one_back_kernel,
                    [f_rows, b_rows, shaped((3, width), F32)],
                    *x,
                    name="norm_one_back",
                ),
                s["gs"],
                s["near5"],
                s["far5"],
                s["n1"],
                s["i1"],
                par_one,
            )
            s["gap"] = over_core(s["gao"])

    def weight_grad(kernel, operands, rows, cols, name, small=False):
        with jax.named_scope(name):
            outs = [
                shaped((rows + small * EXTRA, cols), F32),
                shaped((rows + small * 2 * EXTRA, cols), BF),
            ]
            keep, send = run(lambda *x: scalar_call(kernel, outs, *x, name=name), place, *operands)
            return Reduction(run, name, place, keep, over_x(send), small, over_z1, over_z2)

    def owned(red, name):
        with jax.named_scope(name):
            return run(
                lambda *x: scalar_call(owned_kernel, [shaped((red.rows, red.cols), F32)], *x, name=name),
                place,
                red.own,
                red.moved,
            )[0]

    four = [(c, w) for c in range(2) for w in "op"]

    def pieces_of(name):
        return [state[c][name + w] for c, w in four]

    cot = (cot_a, cot_b)
    norm_one(0)
    feed(0, "o", F32)
    norm_one(1)
    feed(0, "p", BF)
    feed(1, "p", BF)
    near_sum(0, "2")
    feed(1, "o", F32)
    near_sum(1, "2")
    norm_two(0)
    feed_back(0, "o", F32)
    feed_back(0, "p", BF)
    norm_two(1)
    with jax.named_scope("outback"):
        out_back = over_z2(state[1]["out"])
    near_sum(0, "5")
    feed_back(1, "o", F32)
    feed_back(1, "p", BF)
    if n_f == 2:
        red_down = weight_grad(
            down_grad_kernel, pieces_of("h") + pieces_of("gf"), hidden_here, width // 2, "down_grad"
        )
    near_sum(1, "5")
    norm_one_back(0)
    if n_f == 2:
        red_up = weight_grad(
            up_grad_kernel, pieces_of("y") + pieces_of("gp"), width // 2, hidden_here, "up_grad"
        )
    norm_one_back(1)
    (out_back,) = touch(out_back)
    with jax.named_scope("smallpack"):
        (packed,) = run(
            lambda *x: call(pack_kernel, [shaped((8, width), F32)], *x, name="pack"),
            *[state[c][s] for s in ("sum1", "sum2") for c in range(2)],
            *pieces_of("sumu"),
        )
        packed_moved = over_core(packed)
    def placed(blocks):
        return run(
            lambda *x: scalar_call(place_kernel, [shaped(tokens.shape, BF)], *x, name="place"),
            place,
            *blocks,
        )[0]

    def both_halves(a, b):
        return a, over_core(a), b, over_core(b)

    if n_f == 2:
        red_down.step()
    with jax.named_scope("placeout"):
        out_blocks = both_halves(after(state[0]["out"], out_back), out_back)
    grad_attn = pieces_of("ga")
    grad_mixed, inner = run(
        lambda *x: call(
            grad_mixed_kernel, [shaped((n_own, wide), BF), shaped((heads, n_own), F32)], *x, name="grad_mixed"
        ),
        *grad_attn,
        out_w,
        mixed_f,
    )
    (*out_blocks, packed_moved) = touch(*out_blocks, packed_moved)

    early, late = tuple(range(heads - 1)), (heads - 1,)
    bwd_args = (q, k, v, grad_mixed, logs, inner)
    n_one, n_two = 3 * len(early) * HD, 3 * HD
    with jax.named_scope("back1"):
        dq1, own1, far1 = run(lambda *x: attend_bwd(early, 0, total, 2, *x), *bwd_args)
    if n_f == 2:
        red_up.step()
        red_down.step()
    with jax.named_scope("back1"):
        moved1 = over_z1(after(far1, run.done))
    with jax.named_scope("back2"):
        dq2, far2 = run(lambda *x: attend_bwd(late, 1, n_own, 1, *x, last=False), *bwd_args)
        moved2 = over_z1(far2)
    with jax.named_scope("back3"):
        dq2, own2 = run(lambda *x: attend_bwd(late, 0, n_own, 1, *x), *bwd_args, dq2)
    if n_f == 2:
        red_one = weight_grad(
            functools.partial(qkv_grad_kernel, True),
            own + other + [dq1, own1, far1] + mixed + grad_attn + [packed, packed_moved],
            n_one + wide,
            width // 2,
            "one_grad",
            True,
        )
    with jax.named_scope("placeout"):
        output = placed(out_blocks)
    if n_f == 2:
        red_down.step()
        red_up.step()
        red_two = weight_grad(
            functools.partial(qkv_grad_kernel, False),
            own + other + [dq2, own2, far2],
            n_two,
            width // 2,
            "two_grad",
            True,
        )
        red_one.step()
        (moved1,) = touch(moved1)

    item = [dict(), dict()]

    def input_part(c):
        with jax.named_scope(f"inputpart{c}"):
            s = item[c]
            s["po"], pp = run(
                lambda *x: call(
                    functools.partial(input_part_kernel, c * rows), [f_rows, b_rows], *x, name="input_part"
                ),
                dq1,
                own1,
                moved1,
                dq2,
                own2,
                moved2,
                qkv_w,
            )
            s["cp"] = over_core(pp)

    def input_near(c):
        with jax.named_scope(f"inputnear{c}"):
            s = item[c]
            (s["near"],) = run(
                lambda *x: call(near_kernel, [b_rows], *x, name="near"), s["po"], s["cp"]
            )
            s["far"] = over_y(s["near"])

    def input_last(c):
        with jax.named_scope(f"inputlast{c}"):
            s = item[c]
            (s["in"],) = run(
                lambda *x: call(input_grad_kernel, [b_rows], *x, name="input_grad"),
                state[c]["gfirst"],
                s["near"],
                s["far"],
            )

    input_part(1)
    input_part(0)
    if n_f == 2:
        (red_down.moved,) = touch(red_down.moved)
    input_near(1)
    input_near(0)
    if n_f == 2:
        red_up.step()
        owned_down = owned(red_down, "owned_down")
        red_two.step()
        red_one.step()
    input_last(1)
    with jax.named_scope("inputback"):
        in_back = over_z2(item[1]["in"])
    if n_f == 2:
        red_two.step()
    input_last(0)
    with jax.named_scope("placein"):
        in_far = over_core(item[0]["in"])
    if n_f == 2:
        owned_up = owned(red_up, "owned_up")
        red_one.step()
        red_two.step()
    (in_back,) = touch(in_back)
    with jax.named_scope("placein"):
        in_blocks = [item[0]["in"], in_far, in_back, over_core(in_back)]
    with jax.named_scope("finish"):
        if n_f == 2:
            qkv_grad, owned_out, small, bias_grad = run(
                lambda *x: scalar_call(
                    owned_qkv_kernel,
                    [
                        shaped((3, wide, width // 2), F32),
                        shaped((wide, width // 2), F32),
                        shaped((8, width), F32),
                        shaped((2, wide), F32),
                    ],
                    *x,
                    name="owned_qkv",
                ),
                place,
                red_one.own,
                red_two.own,
                red_one.moved,
                red_two.moved,
            )
            owned_qkv = qkv_grad.transpose(2, 0, 1)
        else:

            def reduce_plain(left, right, axis):
                grad = mm(jnp.concatenate(left), jnp.concatenate(right), TN)
                keep = lax.psum_scatter(grad, "fsdp", scatter_dimension=axis, tiled=True)
                return lax.psum(keep, "context").astype(BF).astype(F32)

            zero = jnp.zeros((n_own, wide), BF)
            cut = len(early) * HD
            dk = [own1[:, :cut], own2[:, :HD], far1[:, :cut], far2[:, :HD]]
            dv = [own1[:, cut:], own2[:, HD:], far1[:, cut:], far2[:, HD:]]
            left = jnp.concatenate([dq1, dq2, *dk[:2], *dv[:2]], axis=1)
            right = jnp.concatenate([zero, *dk[2:], *dv[2:]], axis=1)
            owned_up = reduce_plain(pieces_of("y"), pieces_of("gp"), 0)
            owned_down = reduce_plain(pieces_of("h"), pieces_of("gf"), 1)
            owned_out = reduce_plain(mixed, grad_attn, 1)
            owned_qkv = reduce_plain(own + other, [left, right], 0).reshape(w_qkv.shape)
            column_sums = jnp.sum((left.astype(F32) + right.astype(F32)), axis=0)
            bias_grad = jnp.stack([column_sums[:wide], column_sums[2 * wide :]])
            small = jnp.concatenate([packed[:6] + packed_moved[:6], packed[6:]])
            small, bias_grad = lax.psum((small, bias_grad), ("fsdp", "context"))
    with jax.named_scope("placein"):
        input_grad = placed(in_blocks)
    return (
        output,
        input_grad,
        owned_qkv,
        bias_grad,
        owned_out,
        small[0],
        small[1],
        small[2],
        owned_up,
        small[6],
        owned_down,
        small[3],
        small[4],
        small[5],
    )


def solution(mesh):
    sizes = tuple(mesh.shape[name] for name in ("fsdp", "context", "tensor"))
    specs = (
        P("fsdp", None, "tensor"),
        P(None, "tensor"),
        P("tensor", "fsdp"),
        P(),
        P(),
        P(),
        P("fsdp", "tensor"),
        P("tensor"),
        P("tensor", "fsdp"),
        P(),
        P(),
        P(),
    )
    rows = P("fsdp", "context", None)
    return jax.shard_map(
        functools.partial(body, sizes),
        mesh=mesh,
        in_specs=(rows, rows) + specs,
        out_specs=(rows, rows) + specs,
        check_vma=False,
    )
```

```python
import functools
import math

import jax
import jax.numpy as jnp
from jax import lax
from jax.experimental import pallas as pl
from jax.experimental.pallas import tpu as pltpu
from jax.sharding import PartitionSpec as P

HD = 64
SCALE = 1.0 / math.sqrt(HD)
SCALE_LOG2 = SCALE * math.log2(math.e)
EPS = 1e-06
BF = jnp.bfloat16
F32 = jnp.float32
NT = (((1,), (1,)), ((), ()))
TN = (((0,), (0,)), ((), ()))
NN = (((1,), (0,)), ((), ()))


def mm(a, b, dims=NN):
    return lax.dot_general(a, b, dims, preferred_element_type=F32)


def shaped(shape, dtype):
    return jax.ShapeDtypeStruct(shape, dtype)


def call(kernel, outs, *operands, name, limit=16, **extra):
    return pl.pallas_call(
        kernel,
        out_shape=list(outs),
        cost_estimate=pl.CostEstimate(flops=int(5e9), bytes_accessed=1, transcendentals=0),
        compiler_params=pltpu.CompilerParams(vmem_limit_bytes=limit << 20),
        name=name,
        **extra,
    )(*operands)


SMEM = pl.BlockSpec(memory_space=pltpu.SMEM)
VMEM = pl.BlockSpec(memory_space=pltpu.VMEM)


def scalar_call(kernel, outs, scalars, *operands, **kw):
    specs = [SMEM] + [VMEM] * len(operands)
    return call(kernel, outs, scalars, *operands, in_specs=specs, **kw)


def lanes(ref, index, size):
    return ref[:, pl.ds(pl.multiple_of(index * size, 128), size)]


def qkv_kernel(*refs):
    rows, (w_ref, b_ref, q_ref, k_ref, v_ref) = refs[:8], refs[8:]
    n = rows[0].shape[0]
    wide = q_ref.shape[1]
    for i, ref in enumerate(rows):
        here = slice(i * n, (i + 1) * n)
        skip = 0 if i < 4 else wide
        full = (mm(ref[...], w_ref[skip:, :], NT) + b_ref[:, skip:]).astype(BF)
        if i < 4:
            q_ref[here, :] = full[:, :wide]
        k_ref[here, :] = full[:, wide - skip : 2 * wide - skip]
        v_ref[here, :] = full[:, 2 * wide - skip :]


def attend_fwd_kernel(chunk, *refs):
    q_ref, k_ref, v_ref = refs[:3]
    o_ref, p_ref, f_ref, l_ref = refs[-4:]
    outs, logs = [], []
    for h in range(q_ref.shape[1] // HD):
        cols = slice(h * HD, (h + 1) * HD)
        scores = mm(q_ref[:, cols], k_ref[:, cols], NT)
        top = jnp.max(scores, axis=1, keepdims=True)
        expo = jnp.exp2((scores - top) * SCALE_LOG2)
        total = jnp.sum(expo, axis=1, keepdims=True)
        outs.append(mm(expo.astype(BF), v_ref[:, cols]) / total)
        logs.append(top * SCALE_LOG2 + jnp.log2(total))
    mixed = jnp.concatenate(outs, axis=1)
    f_ref[...] = mixed
    l_ref[...] = jnp.concatenate(logs, axis=1).T
    for step, ref in enumerate((o_ref, p_ref)):

        @pl.when(pl.program_id(0) == step)
        def _():
            ref[...] = mixed.astype(BF)


def attend_fwd(chunk, block, q, k, v, *before):
    nq, w = q.shape
    nk = k.shape[0]
    heads = w // HD
    q_spec = pl.BlockSpec((block, w), lambda i: (chunk * 2 + i, 0))
    l_spec = pl.BlockSpec((heads, block), lambda i: (0, chunk * 2 + i))
    o_spec = pl.BlockSpec((block, w), lambda i: (0, 0))
    k_spec = pl.BlockSpec((nk, w), lambda i: (0, 0))
    anywhere = pl.BlockSpec(memory_space=pl.ANY)
    return call(
        functools.partial(attend_fwd_kernel, chunk),
        [shaped((block, w), BF)] * 2 + [shaped((nq, w), F32), shaped((heads, nq), F32)],
        q,
        k,
        v,
        *before,
        name="attend_fwd",
        limit=24,
        grid=(2,),
        in_specs=[q_spec, k_spec, k_spec] + [anywhere] * len(before),
        out_specs=[o_spec, o_spec, q_spec, l_spec],
        input_output_aliases={3: 2, 4: 3} if before else {},
    )


def grad_mixed_kernel(*refs):
    gas, (w_ref, f_ref, g_ref, d_ref) = refs[:4], refs[4:]
    n = gas[0].shape[0]
    heads = w_ref.shape[0] // HD
    for i, ga in enumerate(gas):
        here = slice(i * n, (i + 1) * n)
        g = mm(ga[...], w_ref[...], NT).astype(BF)
        g_ref[here, :] = g
        prod = (g.astype(F32) * f_ref[here, :]).T
        d_ref[:, here] = jnp.concatenate(
            [jnp.sum(prod[h * HD : (h + 1) * HD], axis=0, keepdims=True) for h in range(heads)]
        )


def attend_bwd_kernel(heads, first, last, split, *refs):
    q_ref, k_ref, v_ref, g_ref, l_ref, d_ref = refs[:6]
    add_ref = refs[6] if not first else None
    dq_ref, outs, acc = refs[6 + (not first)], refs[7 + (not first) : -1], refs[-1]
    dqs, dks, dvs = [], [], []
    for h in heads:
        cols = slice(h * HD, (h + 1) * HD)
        q, k, v, g = q_ref[:, cols], k_ref[:, cols], v_ref[:, cols], g_ref[:, cols]
        probs = jnp.exp2(mm(k, q, NT) * SCALE_LOG2 - l_ref[h : h + 1, :])
        grad_scores = (probs * (mm(v, g, NT) - d_ref[h : h + 1, :])).astype(BF)
        dvs.append(mm(probs.astype(BF), g))
        dks.append(mm(grad_scores, q) * SCALE)
        dqs.append(mm(k, grad_scores, TN))
    dq = (dqs[0] if len(dqs) == 1 else jnp.concatenate(dqs, axis=0)).T
    if not first:
        dq = dq + add_ref[...]
    dq_ref[...] = (dq * SCALE).astype(BF) if last else dq
    dkv = jnp.concatenate(dks + dvs, axis=1)
    step = pl.program_id(0)

    @pl.when(step == 0)
    def _():
        acc[...] = dkv

    @pl.when(step > 0)
    def _():
        acc[...] += dkv

    @pl.when(step == pl.num_programs(0) - 1)
    def _():
        n = acc.shape[0] // len(outs)
        for i, ref in enumerate(outs):
            ref[...] = acc[i * n : (i + 1) * n].astype(BF)


def attend_bwd(heads, key_block, key_rows, split, q, k, v, g, logs, inner, *add, last=True, block=256):
    nq, w = q.shape
    n = len(heads) * HD
    q_spec = pl.BlockSpec((block, w), lambda i: (i, 0))
    k_spec = pl.BlockSpec((key_rows, w), lambda i: (key_block, 0))
    n_spec = pl.BlockSpec((block, n), lambda i: (i, 0))
    l_spec = pl.BlockSpec((logs.shape[0], block), lambda i: (0, i))
    whole = pl.BlockSpec((key_rows // split, 2 * n), lambda i: (0, 0))
    return call(
        functools.partial(attend_bwd_kernel, heads, not add, last, split),
        [shaped((nq, n), BF if last else F32)] + [shaped((key_rows // split, 2 * n), BF)] * split,
        q,
        k,
        v,
        g,
        logs,
        inner,
        *add,
        name="attend_bwd",
        limit=36,
        grid=(nq // block,),
        in_specs=[q_spec, k_spec, k_spec, q_spec, l_spec, l_spec] + [n_spec] * len(add),
        out_specs=[n_spec] + [whole] * split,
        scratch_shapes=[pltpu.VMEM((key_rows, 2 * n), F32)],
    )


def normed(x):
    centred = x - jnp.mean(x, axis=-1, keepdims=True)
    inverse = lax.rsqrt(jnp.mean(centred * centred, axis=-1, keepdims=True) + EPS)
    return centred * inverse, inverse


def norm_back(g, norm, inverse):
    return inverse * (
        g
        - jnp.mean(g, axis=-1, keepdims=True)
        - norm * jnp.mean(g * norm, axis=-1, keepdims=True)
    )


def down_rows(*terms):
    return jnp.concatenate([jnp.sum(t, axis=0, keepdims=True) for t in terms], axis=0)


def norm_one_kernel(m0, m1, m2, m3, w0, w1, w2, w3, t_ref, p_ref, y_ref, low_ref, n_ref, i_ref):
    near = mm(m0[...], w0[...]) + mm(m1[...], w1[...])
    far = mm(m2[...], w2[...]) + mm(m3[...], w3[...])
    norm, inverse = normed(t_ref[...].astype(F32) + ((near + far) + p_ref[0:1, :]))
    y = norm * p_ref[1:2, :] + p_ref[2:3, :]
    y_ref[...] = y
    low_ref[...] = y.astype(BF)
    n_ref[...] = norm
    i_ref[...] = inverse


def ffn_kernel(s_ref, y_ref, up_own, up_far, b_ref, down_own, down_far, h_ref, sl_ref, p_ref):
    f = s_ref[0]
    size = up_own.shape[0]
    x = mm(lanes(y_ref, f, size), up_own[...]) + mm(lanes(y_ref, 1 - f, size), up_far[...]) + b_ref[...]
    cdf = 0.5 * (1.0 + lax.erf(x * (1.0 / math.sqrt(2.0))))
    pdf = jnp.exp(-0.5 * x * x) * (1.0 / math.sqrt(2.0 * math.pi))
    sl_ref[...] = cdf + x * pdf
    hidden = (x * cdf).astype(BF)
    h_ref[...] = hidden
    for part, ref in ((f, down_own), (1 - f, down_far)):
        here = pl.ds(pl.multiple_of(part * size, 128), size)
        p_ref[:, here] = mm(hidden, ref[...]).astype(p_ref.dtype)


def norm_two_kernel(near, far, y_ref, g_ref, p_ref, o_ref, gs_ref, gf_ref, sums):
    ffn = near[...].astype(F32) + far[...].astype(F32)
    norm, inverse = normed(y_ref[...] + (ffn + p_ref[0:1, :]))
    o_ref[...] = (norm * p_ref[1:2, :] + p_ref[2:3, :]).astype(BF)
    g = g_ref[...].astype(F32)
    grad = norm_back(g * p_ref[1:2, :], norm, inverse)
    low = grad.astype(BF)
    gs_ref[...] = grad
    gf_ref[...] = low
    sums[...] = down_rows(low.astype(F32), g * norm, g)


def ffn_back_kernel(s_ref, g_ref, down_own, down_far, sl_ref, up_own, up_far, gp_ref, p_ref, sums):
    f = s_ref[0]
    size = up_own.shape[0]
    grad = mm(lanes(g_ref, f, size), down_own[...], NT) + mm(lanes(g_ref, 1 - f, size), down_far[...], NT)
    low = (grad * sl_ref[...]).astype(BF)
    gp_ref[...] = low
    sums[...] = down_rows(low.astype(F32))
    for part, ref in ((f, up_own), (1 - f, up_far)):
        here = pl.ds(pl.multiple_of(part * size, 128), size)
        p_ref[:, here] = mm(low, ref[...], NT).astype(p_ref.dtype)


def norm_one_back_kernel(gs_ref, near, far, n_ref, i_ref, p_ref, g_ref, low_ref, sums):
    grad_y = gs_ref[...] + (near[...].astype(F32) + far[...].astype(F32))
    norm = n_ref[...]
    grad = norm_back(grad_y * p_ref[1:2, :], norm, i_ref[...])
    low = grad.astype(BF)
    g_ref[...] = grad
    low_ref[...] = low
    sums[...] = down_rows(low.astype(F32), grad_y * norm, grad_y)


def input_part_kernel(first_row, dq1, dkv1, m1, dq2, dkv2, m2, w_ref, o_ref, p_ref):
    n = o_ref.shape[0]
    w1, w2 = dq1.shape[1], dq2.shape[1]
    for part, ref in enumerate((o_ref, p_ref)):
        here = slice(first_row + part * n, first_row + (part + 1) * n)
        low1 = (dkv1[here, :].astype(F32) + m1[here, :].astype(F32)).astype(BF)
        low2 = (dkv2[here, :].astype(F32) + m2[here, :].astype(F32)).astype(BF)
        grads = jnp.concatenate(
            [dq1[here, :], dq2[here, :], low1[:, :w1], low2[:, :w2], low1[:, w1:], low2[:, w2:]], axis=1
        )
        ref[...] = mm(grads, w_ref[...]).astype(ref.dtype)


def near_kernel(a_ref, b_ref, o_ref):
    o_ref[...] = (a_ref[...] + b_ref[...].astype(F32)).astype(BF)


def input_grad_kernel(g_ref, a_ref, b_ref, o_ref):
    o_ref[...] = (g_ref[...] + (a_ref[...].astype(F32) + b_ref[...].astype(F32))).astype(BF)


def place_kernel(s_ref, a, b, c, d, o_ref):
    n = a.shape[0]
    group, core = s_ref[2], s_ref[3]
    for block, half, ref in ((group, core, a), (group, 1 - core, b), (1 - group, core, c), (1 - group, 1 - core, d)):
        o_ref[block, pl.ds(pl.multiple_of(half * n, n), n), :] = ref[...]


def pack_kernel(a0, a1, b0, b1, u0, u1, u2, u3, o_ref):
    o_ref[0:3, :] = a0[...] + a1[...]
    o_ref[3:6, :] = b0[...] + b1[...]
    o_ref[6:7, :] = u0[...] + u1[...] + u2[...] + u3[...]
    o_ref[7:8, :] = jnp.zeros_like(u0)


EXTRA = 16


def two_parts(x):
    high = x.astype(BF).astype(F32)
    return high + (x - high).astype(BF).astype(F32)


def put(ref, main, small):
    n = main.shape[0]
    ref[0:n, :] = main.astype(ref.dtype)
    if small is not None:
        high = small.astype(ref.dtype)
        ref[n : n + EXTRA, :] = high
        if ref.shape[0] > n + EXTRA:
            ref[n + EXTRA :, :] = (small - high.astype(F32)).astype(ref.dtype)


def get(ref, small):
    if not small:
        return ref[...].astype(F32), None
    parts = 1 if ref.dtype == F32 else 2
    n = ref.shape[0] - parts * EXTRA
    rest = ref[n : n + EXTRA, :].astype(F32)
    if parts == 2:
        rest = rest + ref[n + EXTRA :, :].astype(F32)
    return ref[0:n, :].astype(F32), rest


def up_grad_kernel(s_ref, *refs):
    ys, gs, (keep, send) = refs[:4], refs[4:8], refs[8:]
    f = s_ref[0]
    size = ys[0].shape[1] // 2
    for out, part in ((send, 1 - f), (keep, f)):
        put(out, sum(mm(lanes(y, part, size), g[...], TN) for y, g in zip(ys, gs)), None)


def down_grad_kernel(s_ref, *refs):
    hs, gs, (keep, send) = refs[:4], refs[4:8], refs[8:]
    f = s_ref[0]
    size = gs[0].shape[1] // 2
    for out, part in ((send, 1 - f), (keep, f)):
        put(out, sum(mm(h[...], lanes(g, part, size), TN) for h, g in zip(hs, gs)), None)


def qkv_grad_kernel(with_out, s_ref, *refs):
    rows, (dq, own_ref, far_ref), more, (keep, send) = refs[:8], refs[8:11], refs[11:-2], refs[-2:]
    f = s_ref[0]
    size = rows[0].shape[1] // 2
    n = rows[0].shape[0]
    m = dq.shape[1]
    own = jnp.concatenate([dq[...], own_ref[...]], axis=1)
    far = far_ref[...]
    far_sums = jnp.sum(far.astype(F32), axis=0, keepdims=True)
    sums = jnp.sum(own.astype(F32), axis=0, keepdims=True)
    sums = jnp.concatenate([sums[:, :m], sums[:, m:] + far_sums], axis=1)
    if sums.shape[1] < size:
        sums = jnp.concatenate([sums, jnp.zeros((1, size - sums.shape[1]), F32)], axis=1)
    small = [sums]
    if with_out:
        packed, moved = more[-2:]
        six = packed[0:6, :] + moved[0:6, :]
        ups = packed[6:7, :]
        small = [six[:, :size], ups[:, :size], six[:, size:], ups[:, size:], sums]
    small.append(jnp.zeros((EXTRA - sum(x.shape[0] for x in small), size), F32))
    small = two_parts(jnp.concatenate(small, axis=0))
    for out, part in ((send, 1 - f), (keep, f)):
        one = two = None
        for i in range(4):
            here = slice(i * n, (i + 1) * n)
            a = mm(own[here], lanes(rows[i], part, size), TN)
            b = mm(far[here], lanes(rows[4 + i], part, size), TN)
            one = a if one is None else one + a
            two = b if two is None else two + b
        grad = [one[:m], one[m:] + two]
        if with_out:
            grad.append(sum(mm(a[...], lanes(g, part, size), TN) for a, g in zip(more[:4], more[4:8])))
        put(out, jnp.concatenate(grad, axis=0), small)


def half_of(main, which):
    n = main.shape[0] // 2
    return jnp.where(which == 0, main[:n], main[n:])


def first_sum_kernel(small, s_ref, keep, moved, own, send):
    (a, c), (b, d) = get(keep, small), get(moved, small)
    total = a + b
    rest = two_parts(c + d) if small else None
    put(own, half_of(total, s_ref[1]), rest)
    put(send, half_of(total, 1 - s_ref[1]), rest)


def sum_kernel(small, a_ref, b_ref, out):
    (a, c), (b, d) = get(a_ref, small), get(b_ref, small)
    put(out, a + b, c + d if small else None)


def joined(s_ref, own, moved):
    first = s_ref[1] == 0
    return jnp.concatenate([jnp.where(first, own, moved), jnp.where(first, moved, own)], axis=0)


def owned_kernel(s_ref, own, moved, out):
    out[...] = joined(s_ref, get(own, False)[0], get(moved, False)[0])


def owned_qkv_kernel(s_ref, own1, own2, moved1, moved2, qkv, outw, sums, bias):
    (one, small1), (two, small2) = get(own1, True), get(own2, True)
    one = joined(s_ref, one, get(moved1, True)[0])
    two = joined(s_ref, two, get(moved2, True)[0])
    n = outw.shape[0]
    m1, m2 = (one.shape[0] - n) // 3, two.shape[0] // 3
    for j in range(3):
        qkv[j, 0:m1, :] = one[j * m1 : (j + 1) * m1]
        qkv[j, m1:, :] = two[j * m2 : (j + 1) * m2]
    outw[...] = one[3 * m1 :]
    sums[0:7, :] = jnp.concatenate([small1[0:7], small1[7:14]], axis=1)
    sums[7:8, :] = jnp.zeros_like(sums[7:8, :])
    for i, j in ((0, 0), (1, 2)):
        bias[i : i + 1, :] = jnp.concatenate(
            [small1[14:15, j * m1 : (j + 1) * m1], small2[0:1, j * m2 : (j + 1) * m2]], axis=1
        )


def swap(x, axis, size, mask):
    return lax.ppermute(x, axis, [(i, i ^ mask) for i in range(size)])


def pick(first, second, bit, axis):
    n = first.shape[axis]
    ring = jnp.concatenate([first, second, first], axis=axis)
    return lax.dynamic_slice_in_dim(ring, bit * n, 2 * n, axis)


class Order:
    def __init__(self):
        self.done = None

    def __call__(self, fn, *operands):
        if self.done is not None:
            operands, _ = lax.optimization_barrier((operands, self.done))
        out = fn(*operands)
        self.done = out
        return out


class Reduction:
    def __init__(self, run, name, place, keep, moved, small, over_z1, over_z2):
        self.run, self.name, self.place, self.small = run, name, place, small
        self.own, self.moved, self.stage = keep, moved, 0
        self.over = [over_z1, over_z2, over_z1]
        self.rows, self.cols = keep.shape[0] - small * EXTRA, keep.shape[1]

    def step(self):
        self.stage += 1
        low = shaped((self.rows // 2 + self.small * 2 * EXTRA, self.cols), BF)
        wide = shaped((self.rows // 2 + self.small * EXTRA, self.cols), F32)
        name = f"{self.name}_{self.stage}"
        with jax.named_scope(name):
            if self.stage == 1:
                kernel = functools.partial(first_sum_kernel, self.small)
                fn = lambda *x: scalar_call(kernel, [wide, low], *x, name=name)
                self.own, send = self.run(fn, self.place, self.own, self.moved)
            else:
                kernel = functools.partial(sum_kernel, self.small)
                fn = lambda *x: call(kernel, [low], *x, name=name)
                (self.own,) = self.run(fn, self.own, self.moved)
                send = self.own
            self.moved = self.over[self.stage - 1](send)


def body(sizes, *args):
    (
        tokens,
        cotangent,
        w_qkv,
        qv_bias,
        w_out,
        out_bias,
        gain_one,
        shift_one,
        w_up,
        up_bias,
        w_down,
        down_bias,
        gain_two,
        shift_two,
    ) = args
    n_f, n_c, n_t = sizes
    _, rows, width = tokens.shape
    wide = w_qkv.shape[2]
    heads = wide // HD
    hidden_here = w_up.shape[1]
    half = rows // 2
    f = lax.axis_index("fsdp") if n_f == 2 else 0
    z = lax.axis_index("context")
    core = lax.axis_index("tensor") % 2
    group = z // 2
    over_core = functools.partial(swap, axis="tensor", size=n_t, mask=1)
    over_y = functools.partial(swap, axis="tensor", size=n_t, mask=2)
    over_both = functools.partial(swap, axis="tensor", size=n_t, mask=3)
    over_z1 = functools.partial(swap, axis="context", size=n_c, mask=1)
    over_z2 = functools.partial(swap, axis="context", size=n_c, mask=2)
    over_x = functools.partial(swap, axis="fsdp", size=n_f, mask=1)
    run = Order()

    def whole_f(w, axis):
        return lax.all_gather(w, "fsdp", axis=axis, tiled=True)

    def halves(w, axis):
        if n_f == 2:
            return w, over_x(w)
        w = whole_f(w, axis)
        return jnp.split(w, 2, axis=axis)

    def block_of(x, which, part):
        return lax.dynamic_slice(x, (which, part * half, 0), (1, half, width))[0]

    def touch(*x):
        return run(lambda *a: a, *x)

    def after(x, *others):
        return lax.optimization_barrier((x, others))[0]

    with jax.named_scope("arrive"):
        give = run(lambda t: block_of(t, 1 - group, core), tokens)
        b_own = over_z2(give)
        a_own = run(lambda t: block_of(t, group, core), tokens)
        oa_own = over_z1(a_own)
        qkv_t = w_qkv.transpose(1, 2, 0).reshape(3 * wide, -1)
        qkv_moved = over_x(qkv_t) if n_f == 2 else whole_f(qkv_t, 1)
        out_moved = over_x(w_out) if n_f == 2 else whole_f(w_out, 1)
        cot_give, cot_a, a_far, place, par_one, par_two, bias_row, up_row = run(
            lambda g, t, qb, ub, p1, p2: (
                block_of(g, 1 - group, core),
                block_of(g, group, core),
                block_of(t, group, 1 - core),
                jnp.stack(
                    [
                        jnp.int32(f),
                        (z % 2).astype(jnp.int32),
                        group.astype(jnp.int32),
                        core.astype(jnp.int32),
                    ]
                ),
                jnp.stack(p1),
                jnp.stack(p2),
                jnp.concatenate([qb[0], jnp.zeros_like(qb[0]), qb[1]])[None],
                ub[None],
            ),
            cotangent,
            tokens,
            qv_bias,
            up_bias,
            (out_bias, gain_one, shift_one),
            (down_bias, gain_two, shift_two),
        )
        qkv_w = run(lambda a, b: pick(a, b, f, 1) if n_f == 2 else b, qkv_t, qkv_moved)
        out_w = run(lambda a, b: pick(a, b, f, 1) if n_f == 2 else b, w_out, out_moved)
        (b_own,) = touch(b_own)
        ob_own = over_z1(b_own)
        (oa_own,) = touch(oa_own)
        b_far, oa_far = over_core(b_own), over_core(oa_own)
        b_far, oa_far, out_later = touch(b_far, oa_far, out_w)
        out_near, out_far = over_core(out_later), over_y(out_later)
        up_two = halves(after(w_up, out_later), 0)
        out_near, out_far = touch(out_near, out_far)
        (ob_own,) = touch(ob_own)
        ob_far = over_core(ob_own)
    with jax.named_scope("cotangent"):
        cot_b = over_z2(after(cot_give, ob_own))
    own = [a_own, a_far, b_own, b_far]
    other = [oa_own, oa_far, ob_own, ob_far]
    total = 8 * half
    n_own = total // 2

    q, k, v = run(
        lambda *x: call(
            qkv_kernel,
            [shaped((n_own, wide), BF), shaped((total, wide), BF), shaped((total, wide), BF)],
            *x,
            name="qkv",
        ),
        *own,
        *other,
        qkv_w,
        bias_row,
    )
    with jax.named_scope("down_weight"):
        down_two = halves(after(w_down, q), 1)
    with jax.named_scope("out_weight"):
        out_both = over_both(after(out_later, q))

    mixed, pieces, shared = [], [], ()
    for c in range(2):
        with jax.named_scope(f"attend{c}"):
            mo, mp, *shared = run(lambda *x: attend_fwd(c, half, *x), q, k, v, *shared)
            mixed += [mo, mp]
            if c == 0:
                (*up_two, out_both) = touch(*up_two, out_both)
            else:
                (*pieces[0], cot_b) = touch(*pieces[0], cot_b)
            mo, mp = touch(mo, mp)
            pieces.append((mo, over_core(mp), over_y(mo), over_both(mp)))
    mixed_f, logs = shared
    tok = (a_own, b_own)
    f_rows = shaped((half, width), F32)
    b_rows = shaped((half, width), BF)
    h_rows = shaped((half, hidden_here), BF)
    state = [dict(), dict()]

    def norm_one(c):
        with jax.named_scope(f"normone{c}"):
            s = state[c]
            outs = [f_rows, b_rows, f_rows, shaped((half, 1), F32)]
            s["y"], s["yo"], s["n1"], s["i1"] = run(
                lambda *x: call(norm_one_kernel, outs, *x, name="norm_one"),
                *pieces[c],
                out_w,
                out_near,
                out_far,
                out_both,
                tok[c],
                par_one,
            )
            s["yp"] = over_core(s["yo"])

    def feed(c, which, dtype):
        with jax.named_scope(f"feed{c}{which}"):
            s = state[c]
            outs = [h_rows, shaped((half, hidden_here), F32), shaped((half, width), dtype)]
            s["h" + which], s["s" + which], s["p" + which] = run(
                lambda *x: scalar_call(ffn_kernel, outs, *x, name="feed"),
                place,
                s["y" + which],
                *up_two,
                up_row,
                *down_two,
            )
            if which == "p":
                s["c2"] = over_core(s["pp"])

    def near_sum(c, name):
        with jax.named_scope(f"near{c}{name}"):
            s = state[c]
            (s["near" + name],) = run(
                lambda *x: call(near_kernel, [b_rows], *x, name="near"), s["po"], s["c" + name]
            )
            s["far" + name] = over_y(s["near" + name])

    def norm_two(c):
        with jax.named_scope(f"normtwo{c}"):
            s = state[c]
            outs = [b_rows, f_rows, b_rows, shaped((3, width), F32)]
            s["out"], s["gs"], s["gfo"], s["sum2"] = run(
                lambda *x: call(norm_two_kernel, outs, *x, name="norm_two"),
                s["near2"],
                s["far2"],
                s["y"],
                cot[c],
                par_two,
            )
            s["gfp"] = over_core(s["gfo"])

    def feed_back(c, which, dtype):
        with jax.named_scope(f"feedback{c}{which}"):
            s = state[c]
            outs = [h_rows, shaped((half, width), dtype), shaped((1, hidden_here), F32)]
            s["gp" + which], s["p" + which], s["sumu" + which] = run(
                lambda *x: scalar_call(ffn_back_kernel, outs, *x, name="feed_back"),
                place,
                s["gf" + which],
                *down_two,
                s["s" + which],
                *up_two,
            )
            if which == "p":
                s["c5"] = over_core(s["pp"])

    def norm_one_back(c):
        with jax.named_scope(f"normoneback{c}"):
            s = state[c]
            s["gfirst"], s["gao"], s["sum1"] = run(
                lambda *x: call(
                    norm_one_back_kernel,
                    [f_rows, b_rows, shaped((3, width), F32)],
                    *x,
                    name="norm_one_back",
                ),
                s["gs"],
                s["near5"],
                s["far5"],
                s["n1"],
                s["i1"],
                par_one,
            )
            s["gap"] = over_core(s["gao"])

    def weight_grad(kernel, operands, rows, cols, name, small=False):
        with jax.named_scope(name):
            outs = [
                shaped((rows + small * EXTRA, cols), F32),
                shaped((rows + small * 2 * EXTRA, cols), BF),
            ]
            keep, send = run(lambda *x: scalar_call(kernel, outs, *x, name=name), place, *operands)
            return Reduction(run, name, place, keep, over_x(send), small, over_z1, over_z2)

    def owned(red, name):
        with jax.named_scope(name):
            return run(
                lambda *x: scalar_call(owned_kernel, [shaped((red.rows, red.cols), F32)], *x, name=name),
                place,
                red.own,
                red.moved,
            )[0]

    four = [(c, w) for c in range(2) for w in "op"]

    def pieces_of(name):
        return [state[c][name + w] for c, w in four]

    cot = (cot_a, cot_b)
    norm_one(0)
    feed(0, "o", F32)
    norm_one(1)
    feed(0, "p", BF)
    feed(1, "p", BF)
    near_sum(0, "2")
    feed(1, "o", F32)
    near_sum(1, "2")
    norm_two(0)
    feed_back(0, "o", F32)
    feed_back(0, "p", BF)
    norm_two(1)
    with jax.named_scope("outback"):
        out_back = over_z2(state[1]["out"])
    near_sum(0, "5")
    feed_back(1, "o", F32)
    feed_back(1, "p", BF)
    if n_f == 2:
        red_down = weight_grad(
            down_grad_kernel, pieces_of("h") + pieces_of("gf"), hidden_here, width // 2, "down_grad"
        )
    near_sum(1, "5")
    norm_one_back(0)
    if n_f == 2:
        red_up = weight_grad(
            up_grad_kernel, pieces_of("y") + pieces_of("gp"), width // 2, hidden_here, "up_grad"
        )
    norm_one_back(1)
    (out_back,) = touch(out_back)
    with jax.named_scope("smallpack"):
        (packed,) = run(
            lambda *x: call(pack_kernel, [shaped((8, width), F32)], *x, name="pack"),
            *[state[c][s] for s in ("sum1", "sum2") for c in range(2)],
            *pieces_of("sumu"),
        )
        packed_moved = over_core(packed)
    def placed(blocks):
        return run(
            lambda *x: scalar_call(place_kernel, [shaped(tokens.shape, BF)], *x, name="place"),
            place,
            *blocks,
        )[0]

    def both_halves(a, b):
        return a, over_core(a), b, over_core(b)

    if n_f == 2:
        red_down.step()
    with jax.named_scope("placeout"):
        out_blocks = both_halves(after(state[0]["out"], out_back), out_back)
    grad_attn = pieces_of("ga")
    grad_mixed, inner = run(
        lambda *x: call(
            grad_mixed_kernel, [shaped((n_own, wide), BF), shaped((heads, n_own), F32)], *x, name="grad_mixed"
        ),
        *grad_attn,
        out_w,
        mixed_f,
    )
    (*out_blocks, packed_moved) = touch(*out_blocks, packed_moved)

    early, late = tuple(range(heads - 1)), (heads - 1,)
    bwd_args = (q, k, v, grad_mixed, logs, inner)
    n_one, n_two = 3 * len(early) * HD, 3 * HD
    with jax.named_scope("back1"):
        dq1, own1, far1 = run(lambda *x: attend_bwd(early, 0, total, 2, *x), *bwd_args)
    if n_f == 2:
        red_down.step()
    with jax.named_scope("back1"):
        moved1 = over_z1(after(far1, run.done))
    with jax.named_scope("back2"):
        dq2, far2 = run(lambda *x: attend_bwd(late, 1, n_own, 1, *x, last=False), *bwd_args)
        moved2 = over_z1(far2)
    if n_f == 2:
        red_up.step()
    with jax.named_scope("back3"):
        dq2, own2 = run(lambda *x: attend_bwd(late, 0, n_own, 1, *x), *bwd_args, dq2)
    if n_f == 2:
        red_one = weight_grad(
            functools.partial(qkv_grad_kernel, True),
            own + other + [dq1, own1, far1] + mixed + grad_attn + [packed, packed_moved],
            n_one + wide,
            width // 2,
            "one_grad",
            True,
        )
    with jax.named_scope("placeout"):
        output = placed(out_blocks)
    (moved1,) = touch(moved1)
    if n_f == 2:
        red_two = weight_grad(
            functools.partial(qkv_grad_kernel, False),
            own + other + [dq2, own2, far2],
            n_two,
            width // 2,
            "two_grad",
            True,
        )
        red_down.step()

    item = [dict(), dict()]

    def input_part(c):
        with jax.named_scope(f"inputpart{c}"):
            s = item[c]
            s["po"], pp = run(
                lambda *x: call(
                    functools.partial(input_part_kernel, c * rows), [f_rows, b_rows], *x, name="input_part"
                ),
                dq1,
                own1,
                moved1,
                dq2,
                own2,
                moved2,
                qkv_w,
            )
            s["cp"] = over_core(pp)

    def input_near(c):
        with jax.named_scope(f"inputnear{c}"):
            s = item[c]
            (s["near"],) = run(
                lambda *x: call(near_kernel, [b_rows], *x, name="near"), s["po"], s["cp"]
            )
            s["far"] = over_y(s["near"])

    def input_last(c):
        with jax.named_scope(f"inputlast{c}"):
            s = item[c]
            (s["in"],) = run(
                lambda *x: call(input_grad_kernel, [b_rows], *x, name="input_grad"),
                state[c]["gfirst"],
                s["near"],
                s["far"],
            )

    input_part(1)
    if n_f == 2:
        red_up.step()
    input_near(1)
    if n_f == 2:
        red_one.step()
        red_two.step()
        (red_down.moved,) = touch(red_down.moved)
    input_part(0)
    input_last(1)
    with jax.named_scope("inputback"):
        in_back = over_z2(item[1]["in"])
    if n_f == 2:
        red_one.step()
    input_near(0)
    if n_f == 2:
        owned_down = owned(red_down, "owned_down")
        red_up.step()
        red_two.step()
    input_last(0)
    with jax.named_scope("placein"):
        in_far = over_core(item[0]["in"])
    if n_f == 2:
        owned_up = owned(red_up, "owned_up")
        red_one.step()
        red_two.step()
    (in_back,) = touch(in_back)
    with jax.named_scope("placein"):
        in_blocks = [item[0]["in"], in_far, in_back, over_core(in_back)]
    with jax.named_scope("finish"):
        if n_f == 2:
            qkv_grad, owned_out, small, bias_grad = run(
                lambda *x: scalar_call(
                    owned_qkv_kernel,
                    [
                        shaped((3, wide, width // 2), F32),
                        shaped((wide, width // 2), F32),
                        shaped((8, width), F32),
                        shaped((2, wide), F32),
                    ],
                    *x,
                    name="owned_qkv",
                ),
                place,
                red_one.own,
                red_two.own,
                red_one.moved,
                red_two.moved,
            )
            owned_qkv = qkv_grad.transpose(2, 0, 1)
        else:

            def reduce_plain(left, right, axis):
                grad = mm(jnp.concatenate(left), jnp.concatenate(right), TN)
                keep = lax.psum_scatter(grad, "fsdp", scatter_dimension=axis, tiled=True)
                return lax.psum(keep, "context").astype(BF).astype(F32)

            zero = jnp.zeros((n_own, wide), BF)
            cut = len(early) * HD
            dk = [own1[:, :cut], own2[:, :HD], far1[:, :cut], far2[:, :HD]]
            dv = [own1[:, cut:], own2[:, HD:], far1[:, cut:], far2[:, HD:]]
            left = jnp.concatenate([dq1, dq2, *dk[:2], *dv[:2]], axis=1)
            right = jnp.concatenate([zero, *dk[2:], *dv[2:]], axis=1)
            owned_up = reduce_plain(pieces_of("y"), pieces_of("gp"), 0)
            owned_down = reduce_plain(pieces_of("h"), pieces_of("gf"), 1)
            owned_out = reduce_plain(mixed, grad_attn, 1)
            owned_qkv = reduce_plain(own + other, [left, right], 0).reshape(w_qkv.shape)
            column_sums = jnp.sum((left.astype(F32) + right.astype(F32)), axis=0)
            bias_grad = jnp.stack([column_sums[:wide], column_sums[2 * wide :]])
            small = jnp.concatenate([packed[:6] + packed_moved[:6], packed[6:]])
            small, bias_grad = lax.psum((small, bias_grad), ("fsdp", "context"))
    with jax.named_scope("placein"):
        input_grad = placed(in_blocks)
    return (
        output,
        input_grad,
        owned_qkv,
        bias_grad,
        owned_out,
        small[0],
        small[1],
        small[2],
        owned_up,
        small[6],
        owned_down,
        small[3],
        small[4],
        small[5],
    )


def solution(mesh):
    sizes = tuple(mesh.shape[name] for name in ("fsdp", "context", "tensor"))
    specs = (
        P("fsdp", None, "tensor"),
        P(None, "tensor"),
        P("tensor", "fsdp"),
        P(),
        P(),
        P(),
        P("fsdp", "tensor"),
        P("tensor"),
        P("tensor", "fsdp"),
        P(),
        P(),
        P(),
    )
    rows = P("fsdp", "context", None)
    return jax.shard_map(
        functools.partial(body, sizes),
        mesh=mesh,
        in_specs=(rows, rows) + specs,
        out_specs=(rows, rows) + specs,
        check_vma=False,
    )
```

```python
import functools
import math

import jax
import jax.numpy as jnp
from jax import lax
from jax.experimental import pallas as pl
from jax.experimental.pallas import tpu as pltpu
from jax.sharding import PartitionSpec as P

HD = 64
SCALE = 1.0 / math.sqrt(HD)
SCALE_LOG2 = SCALE * math.log2(math.e)
EPS = 1e-06
BF = jnp.bfloat16
F32 = jnp.float32
NT = (((1,), (1,)), ((), ()))
TN = (((0,), (0,)), ((), ()))
NN = (((1,), (0,)), ((), ()))


def mm(a, b, dims=NN):
    return lax.dot_general(a, b, dims, preferred_element_type=F32)


def shaped(shape, dtype):
    return jax.ShapeDtypeStruct(shape, dtype)


def call(kernel, outs, *operands, name, limit=16, **extra):
    return pl.pallas_call(
        kernel,
        out_shape=list(outs),
        cost_estimate=pl.CostEstimate(flops=int(5e9), bytes_accessed=1, transcendentals=0),
        compiler_params=pltpu.CompilerParams(vmem_limit_bytes=limit << 20),
        name=name,
        **extra,
    )(*operands)


SMEM = pl.BlockSpec(memory_space=pltpu.SMEM)
VMEM = pl.BlockSpec(memory_space=pltpu.VMEM)


def scalar_call(kernel, outs, scalars, *operands, **kw):
    specs = [SMEM] + [VMEM] * len(operands)
    return call(kernel, outs, scalars, *operands, in_specs=specs, **kw)


def lanes(ref, index, size):
    return ref[:, pl.ds(pl.multiple_of(index * size, 128), size)]


def qkv_kernel(*refs):
    rows, (w_ref, b_ref, q_ref, k_ref, v_ref) = refs[:7], refs[7:]
    n = rows[0].shape[0]
    wide = q_ref.shape[1]
    for i, ref in enumerate(rows):
        here = slice(i * n, (i + 1) * n)
        skip = 0 if i < 4 else wide
        full = (mm(ref[...], w_ref[skip:, :], NT) + b_ref[:, skip:]).astype(BF)
        if i < 4:
            q_ref[here, :] = full[:, :wide]
        k_ref[here, :] = full[:, wide - skip : 2 * wide - skip]
        v_ref[here, :] = full[:, 2 * wide - skip :]


def last_kv_kernel(x_ref, w_ref, b_ref, *refs):
    k_ref, v_ref = refs[-2:]
    wide = k_ref.shape[1]
    full = (mm(x_ref[...], w_ref[wide:, :], NT) + b_ref[:, wide:]).astype(BF)
    k_ref[...] = full[:, :wide]
    v_ref[...] = full[:, wide:]


def attend_fwd_kernel(chunk, *refs):
    q_ref, k_ref, v_ref = refs[:3]
    o_ref, p_ref, f_ref, l_ref = refs[-4:]
    outs, logs = [], []
    for h in range(q_ref.shape[1] // HD):
        cols = slice(h * HD, (h + 1) * HD)
        scores = mm(q_ref[:, cols], k_ref[:, cols], NT)
        top = jnp.max(scores, axis=1, keepdims=True)
        expo = jnp.exp2((scores - top) * SCALE_LOG2)
        total = jnp.sum(expo, axis=1, keepdims=True)
        outs.append(mm(expo.astype(BF), v_ref[:, cols]) / total)
        logs.append(top * SCALE_LOG2 + jnp.log2(total))
    mixed = jnp.concatenate(outs, axis=1)
    f_ref[...] = mixed
    l_ref[...] = jnp.concatenate(logs, axis=1).T
    for step, ref in enumerate((o_ref, p_ref)):

        @pl.when(pl.program_id(0) == step)
        def _():
            ref[...] = mixed.astype(BF)


def attend_fwd(chunk, block, q, k, v, *before):
    nq, w = q.shape
    nk = k.shape[0]
    heads = w // HD
    q_spec = pl.BlockSpec((block, w), lambda i: (chunk * 2 + i, 0))
    l_spec = pl.BlockSpec((heads, block), lambda i: (0, chunk * 2 + i))
    o_spec = pl.BlockSpec((block, w), lambda i: (0, 0))
    k_spec = pl.BlockSpec((nk, w), lambda i: (0, 0))
    anywhere = pl.BlockSpec(memory_space=pl.ANY)
    return call(
        functools.partial(attend_fwd_kernel, chunk),
        [shaped((block, w), BF)] * 2 + [shaped((nq, w), F32), shaped((heads, nq), F32)],
        q,
        k,
        v,
        *before,
        name="attend_fwd",
        limit=24,
        grid=(2,),
        in_specs=[q_spec, k_spec, k_spec] + [anywhere] * len(before),
        out_specs=[o_spec, o_spec, q_spec, l_spec],
        input_output_aliases={3: 2, 4: 3} if before else {},
    )


def grad_mixed_kernel(*refs):
    gas, (w_ref, f_ref, g_ref, d_ref) = refs[:4], refs[4:]
    n = gas[0].shape[0]
    heads = w_ref.shape[0] // HD
    for i, ga in enumerate(gas):
        here = slice(i * n, (i + 1) * n)
        g = mm(ga[...], w_ref[...], NT).astype(BF)
        g_ref[here, :] = g
        prod = (g.astype(F32) * f_ref[here, :]).T
        d_ref[:, here] = jnp.concatenate(
            [jnp.sum(prod[h * HD : (h + 1) * HD], axis=0, keepdims=True) for h in range(heads)]
        )


def attend_bwd_kernel(heads, first, last, split, *refs):
    q_ref, k_ref, v_ref, g_ref, l_ref, d_ref = refs[:6]
    add_ref = refs[6] if not first else None
    dq_ref, outs, acc = refs[6 + (not first)], refs[7 + (not first) : -1], refs[-1]
    dqs, dks, dvs = [], [], []
    for h in heads:
        cols = slice(h * HD, (h + 1) * HD)
        q, k, v, g = q_ref[:, cols], k_ref[:, cols], v_ref[:, cols], g_ref[:, cols]
        probs = jnp.exp2(mm(k, q, NT) * SCALE_LOG2 - l_ref[h : h + 1, :])
        grad_scores = (probs * (mm(v, g, NT) - d_ref[h : h + 1, :])).astype(BF)
        dvs.append(mm(probs.astype(BF), g))
        dks.append(mm(grad_scores, q) * SCALE)
        dqs.append(mm(k, grad_scores, TN))
    dq = (dqs[0] if len(dqs) == 1 else jnp.concatenate(dqs, axis=0)).T
    if not first:
        dq = dq + add_ref[...]
    dq_ref[...] = (dq * SCALE).astype(BF) if last else dq
    dkv = jnp.concatenate(dks + dvs, axis=1)
    step = pl.program_id(0)

    @pl.when(step == 0)
    def _():
        acc[...] = dkv

    @pl.when(step > 0)
    def _():
        acc[...] += dkv

    @pl.when(step == pl.num_programs(0) - 1)
    def _():
        n = acc.shape[0] // len(outs)
        for i, ref in enumerate(outs):
            ref[...] = acc[i * n : (i + 1) * n].astype(BF)


def attend_bwd(heads, key_block, key_rows, split, q, k, v, g, logs, inner, *add, last=True, block=256):
    nq, w = q.shape
    n = len(heads) * HD
    q_spec = pl.BlockSpec((block, w), lambda i: (i, 0))
    k_spec = pl.BlockSpec((key_rows, w), lambda i: (key_block, 0))
    n_spec = pl.BlockSpec((block, n), lambda i: (i, 0))
    l_spec = pl.BlockSpec((logs.shape[0], block), lambda i: (0, i))
    whole = pl.BlockSpec((key_rows // split, 2 * n), lambda i: (0, 0))
    return call(
        functools.partial(attend_bwd_kernel, heads, not add, last, split),
        [shaped((nq, n), BF if last else F32)] + [shaped((key_rows // split, 2 * n), BF)] * split,
        q,
        k,
        v,
        g,
        logs,
        inner,
        *add,
        name="attend_bwd",
        limit=36,
        grid=(nq // block,),
        in_specs=[q_spec, k_spec, k_spec, q_spec, l_spec, l_spec] + [n_spec] * len(add),
        out_specs=[n_spec] + [whole] * split,
        scratch_shapes=[pltpu.VMEM((key_rows, 2 * n), F32)],
    )


def normed(x):
    centred = x - jnp.mean(x, axis=-1, keepdims=True)
    inverse = lax.rsqrt(jnp.mean(centred * centred, axis=-1, keepdims=True) + EPS)
    return centred * inverse, inverse


def norm_back(g, norm, inverse):
    return inverse * (
        g
        - jnp.mean(g, axis=-1, keepdims=True)
        - norm * jnp.mean(g * norm, axis=-1, keepdims=True)
    )


def down_rows(*terms):
    return jnp.concatenate([jnp.sum(t, axis=0, keepdims=True) for t in terms], axis=0)


def norm_one_kernel(m0, m1, m2, m3, w0, w1, w2, w3, t_ref, p_ref, y_ref, low_ref, n_ref, i_ref):
    near = mm(m0[...], w0[...]) + mm(m1[...], w1[...])
    far = mm(m2[...], w2[...]) + mm(m3[...], w3[...])
    norm, inverse = normed(t_ref[...].astype(F32) + ((near + far) + p_ref[0:1, :]))
    y = norm * p_ref[1:2, :] + p_ref[2:3, :]
    y_ref[...] = y
    low_ref[...] = y.astype(BF)
    n_ref[...] = norm
    i_ref[...] = inverse


def ffn_kernel(s_ref, y_ref, up_own, up_far, b_ref, down_own, down_far, h_ref, sl_ref, p_ref):
    f = s_ref[0]
    size = up_own.shape[0]
    x = mm(lanes(y_ref, f, size), up_own[...]) + mm(lanes(y_ref, 1 - f, size), up_far[...]) + b_ref[...]
    cdf = 0.5 * (1.0 + lax.erf(x * (1.0 / math.sqrt(2.0))))
    pdf = jnp.exp(-0.5 * x * x) * (1.0 / math.sqrt(2.0 * math.pi))
    sl_ref[...] = cdf + x * pdf
    hidden = (x * cdf).astype(BF)
    h_ref[...] = hidden
    for part, ref in ((f, down_own), (1 - f, down_far)):
        here = pl.ds(pl.multiple_of(part * size, 128), size)
        p_ref[:, here] = mm(hidden, ref[...]).astype(p_ref.dtype)


def norm_two_kernel(near, far, y_ref, g_ref, p_ref, o_ref, gs_ref, gf_ref, sums):
    ffn = near[...].astype(F32) + far[...].astype(F32)
    norm, inverse = normed(y_ref[...] + (ffn + p_ref[0:1, :]))
    o_ref[...] = (norm * p_ref[1:2, :] + p_ref[2:3, :]).astype(BF)
    g = g_ref[...].astype(F32)
    grad = norm_back(g * p_ref[1:2, :], norm, inverse)
    low = grad.astype(BF)
    gs_ref[...] = grad
    gf_ref[...] = low
    sums[...] = down_rows(low.astype(F32), g * norm, g)


def ffn_back_kernel(s_ref, g_ref, down_own, down_far, sl_ref, up_own, up_far, gp_ref, p_ref, sums):
    f = s_ref[0]
    size = up_own.shape[0]
    grad = mm(lanes(g_ref, f, size), down_own[...], NT) + mm(lanes(g_ref, 1 - f, size), down_far[...], NT)
    low = (grad * sl_ref[...]).astype(BF)
    gp_ref[...] = low
    sums[...] = down_rows(low.astype(F32))
    for part, ref in ((f, up_own), (1 - f, up_far)):
        here = pl.ds(pl.multiple_of(part * size, 128), size)
        p_ref[:, here] = mm(low, ref[...], NT).astype(p_ref.dtype)


def norm_one_back_kernel(gs_ref, near, far, n_ref, i_ref, p_ref, g_ref, low_ref, sums):
    grad_y = gs_ref[...] + (near[...].astype(F32) + far[...].astype(F32))
    norm = n_ref[...]
    grad = norm_back(grad_y * p_ref[1:2, :], norm, i_ref[...])
    low = grad.astype(BF)
    g_ref[...] = grad
    low_ref[...] = low
    sums[...] = down_rows(low.astype(F32), grad_y * norm, grad_y)


def input_part_kernel(first_row, dq1, dkv1, m1, dq2, dkv2, m2, w_ref, o_ref, p_ref):
    n = o_ref.shape[0]
    w1, w2 = dq1.shape[1], dq2.shape[1]
    for part, ref in enumerate((o_ref, p_ref)):
        here = slice(first_row + part * n, first_row + (part + 1) * n)
        low1 = (dkv1[here, :].astype(F32) + m1[here, :].astype(F32)).astype(BF)
        low2 = (dkv2[here, :].astype(F32) + m2[here, :].astype(F32)).astype(BF)
        grads = jnp.concatenate(
            [dq1[here, :], dq2[here, :], low1[:, :w1], low2[:, :w2], low1[:, w1:], low2[:, w2:]], axis=1
        )
        ref[...] = mm(grads, w_ref[...]).astype(ref.dtype)


def near_kernel(a_ref, b_ref, o_ref):
    o_ref[...] = (a_ref[...] + b_ref[...].astype(F32)).astype(BF)


def input_grad_kernel(g_ref, a_ref, b_ref, o_ref):
    o_ref[...] = (g_ref[...] + (a_ref[...].astype(F32) + b_ref[...].astype(F32))).astype(BF)


def place_kernel(s_ref, a, b, c, d, o_ref):
    n = a.shape[0]
    group, core = s_ref[2], s_ref[3]
    for block, half, ref in ((group, core, a), (group, 1 - core, b), (1 - group, core, c), (1 - group, 1 - core, d)):
        o_ref[block, pl.ds(pl.multiple_of(half * n, n), n), :] = ref[...]


def pack_kernel(a0, a1, b0, b1, u0, u1, u2, u3, o_ref):
    o_ref[0:3, :] = a0[...] + a1[...]
    o_ref[3:6, :] = b0[...] + b1[...]
    o_ref[6:7, :] = u0[...] + u1[...] + u2[...] + u3[...]
    o_ref[7:8, :] = jnp.zeros_like(u0)


EXTRA = 16


def two_parts(x):
    high = x.astype(BF).astype(F32)
    return high + (x - high).astype(BF).astype(F32)


def put(ref, main, small):
    n = main.shape[0]
    ref[0:n, :] = main.astype(ref.dtype)
    if small is not None:
        high = small.astype(ref.dtype)
        ref[n : n + EXTRA, :] = high
        if ref.shape[0] > n + EXTRA:
            ref[n + EXTRA :, :] = (small - high.astype(F32)).astype(ref.dtype)


def get(ref, small):
    if not small:
        return ref[...].astype(F32), None
    parts = 1 if ref.dtype == F32 else 2
    n = ref.shape[0] - parts * EXTRA
    rest = ref[n : n + EXTRA, :].astype(F32)
    if parts == 2:
        rest = rest + ref[n + EXTRA :, :].astype(F32)
    return ref[0:n, :].astype(F32), rest


def up_grad_kernel(s_ref, *refs):
    ys, gs, (keep, send) = refs[:4], refs[4:8], refs[8:]
    f = s_ref[0]
    size = ys[0].shape[1] // 2
    for out, part in ((send, 1 - f), (keep, f)):
        put(out, sum(mm(lanes(y, part, size), g[...], TN) for y, g in zip(ys, gs)), None)


def down_grad_kernel(s_ref, *refs):
    hs, gs, (keep, send) = refs[:4], refs[4:8], refs[8:]
    f = s_ref[0]
    size = gs[0].shape[1] // 2
    for out, part in ((send, 1 - f), (keep, f)):
        put(out, sum(mm(h[...], lanes(g, part, size), TN) for h, g in zip(hs, gs)), None)


def qkv_grad_kernel(with_out, s_ref, *refs):
    rows, (dq, own_ref, far_ref), more, (keep, send) = refs[:8], refs[8:11], refs[11:-2], refs[-2:]
    f = s_ref[0]
    size = rows[0].shape[1] // 2
    n = rows[0].shape[0]
    m = dq.shape[1]
    own = jnp.concatenate([dq[...], own_ref[...]], axis=1)
    far = far_ref[...]
    far_sums = jnp.sum(far.astype(F32), axis=0, keepdims=True)
    sums = jnp.sum(own.astype(F32), axis=0, keepdims=True)
    sums = jnp.concatenate([sums[:, :m], sums[:, m:] + far_sums], axis=1)
    if sums.shape[1] < size:
        sums = jnp.concatenate([sums, jnp.zeros((1, size - sums.shape[1]), F32)], axis=1)
    small = [sums]
    if with_out:
        packed, moved = more[-2:]
        six = packed[0:6, :] + moved[0:6, :]
        ups = packed[6:7, :]
        small = [six[:, :size], ups[:, :size], six[:, size:], ups[:, size:], sums]
    small.append(jnp.zeros((EXTRA - sum(x.shape[0] for x in small), size), F32))
    small = two_parts(jnp.concatenate(small, axis=0))
    for out, part in ((send, 1 - f), (keep, f)):
        one = two = None
        for i in range(4):
            here = slice(i * n, (i + 1) * n)
            a = mm(own[here], lanes(rows[i], part, size), TN)
            b = mm(far[here], lanes(rows[4 + i], part, size), TN)
            one = a if one is None else one + a
            two = b if two is None else two + b
        grad = [one[:m], one[m:] + two]
        if with_out:
            grad.append(sum(mm(a[...], lanes(g, part, size), TN) for a, g in zip(more[:4], more[4:8])))
        put(out, jnp.concatenate(grad, axis=0), small)


def half_of(main, which):
    n = main.shape[0] // 2
    return jnp.where(which == 0, main[:n], main[n:])


def first_sum_kernel(small, s_ref, keep, moved, own, send):
    (a, c), (b, d) = get(keep, small), get(moved, small)
    total = a + b
    rest = two_parts(c + d) if small else None
    put(own, half_of(total, s_ref[1]), rest)
    put(send, half_of(total, 1 - s_ref[1]), rest)


def sum_kernel(small, a_ref, b_ref, out):
    (a, c), (b, d) = get(a_ref, small), get(b_ref, small)
    put(out, a + b, c + d if small else None)


def joined(s_ref, own, moved):
    first = s_ref[1] == 0
    return jnp.concatenate([jnp.where(first, own, moved), jnp.where(first, moved, own)], axis=0)


def owned_kernel(s_ref, own, moved, out):
    out[...] = joined(s_ref, get(own, False)[0], get(moved, False)[0])


def owned_qkv_kernel(s_ref, own1, own2, moved1, moved2, qkv, outw, sums, bias):
    (one, small1), (two, small2) = get(own1, True), get(own2, True)
    one = joined(s_ref, one, get(moved1, True)[0])
    two = joined(s_ref, two, get(moved2, True)[0])
    n = outw.shape[0]
    m1, m2 = (one.shape[0] - n) // 3, two.shape[0] // 3
    for j in range(3):
        qkv[j, 0:m1, :] = one[j * m1 : (j + 1) * m1]
        qkv[j, m1:, :] = two[j * m2 : (j + 1) * m2]
    outw[...] = one[3 * m1 :]
    sums[0:7, :] = jnp.concatenate([small1[0:7], small1[7:14]], axis=1)
    sums[7:8, :] = jnp.zeros_like(sums[7:8, :])
    for i, j in ((0, 0), (1, 2)):
        bias[i : i + 1, :] = jnp.concatenate(
            [small1[14:15, j * m1 : (j + 1) * m1], small2[0:1, j * m2 : (j + 1) * m2]], axis=1
        )


def swap(x, axis, size, mask):
    return lax.ppermute(x, axis, [(i, i ^ mask) for i in range(size)])


def pick(first, second, bit, axis):
    n = first.shape[axis]
    ring = jnp.concatenate([first, second, first], axis=axis)
    return lax.dynamic_slice_in_dim(ring, bit * n, 2 * n, axis)


class Order:
    def __init__(self):
        self.done = None

    def __call__(self, fn, *operands):
        if self.done is not None:
            operands, _ = lax.optimization_barrier((operands, self.done))
        out = fn(*operands)
        self.done = out
        return out


class Reduction:
    def __init__(self, run, name, place, keep, moved, small, over_z1, over_z2):
        self.run, self.name, self.place, self.small = run, name, place, small
        self.own, self.moved, self.stage = keep, moved, 0
        self.over = [over_z1, over_z2, over_z1]
        self.rows, self.cols = keep.shape[0] - small * EXTRA, keep.shape[1]

    def step(self):
        self.stage += 1
        low = shaped((self.rows // 2 + self.small * 2 * EXTRA, self.cols), BF)
        wide = shaped((self.rows // 2 + self.small * EXTRA, self.cols), F32)
        name = f"{self.name}_{self.stage}"
        with jax.named_scope(name):
            if self.stage == 1:
                kernel = functools.partial(first_sum_kernel, self.small)
                fn = lambda *x: scalar_call(kernel, [wide, low], *x, name=name)
                self.own, send = self.run(fn, self.place, self.own, self.moved)
            else:
                kernel = functools.partial(sum_kernel, self.small)
                fn = lambda *x: call(kernel, [low], *x, name=name)
                (self.own,) = self.run(fn, self.own, self.moved)
                send = self.own
            self.moved = self.over[self.stage - 1](send)


def body(sizes, *args):
    (
        tokens,
        cotangent,
        w_qkv,
        qv_bias,
        w_out,
        out_bias,
        gain_one,
        shift_one,
        w_up,
        up_bias,
        w_down,
        down_bias,
        gain_two,
        shift_two,
    ) = args
    n_f, n_c, n_t = sizes
    _, rows, width = tokens.shape
    wide = w_qkv.shape[2]
    heads = wide // HD
    hidden_here = w_up.shape[1]
    half = rows // 2
    f = lax.axis_index("fsdp") if n_f == 2 else 0
    z = lax.axis_index("context")
    core = lax.axis_index("tensor") % 2
    group = z // 2
    over_core = functools.partial(swap, axis="tensor", size=n_t, mask=1)
    over_y = functools.partial(swap, axis="tensor", size=n_t, mask=2)
    over_both = functools.partial(swap, axis="tensor", size=n_t, mask=3)
    over_z1 = functools.partial(swap, axis="context", size=n_c, mask=1)
    over_z2 = functools.partial(swap, axis="context", size=n_c, mask=2)
    over_x = functools.partial(swap, axis="fsdp", size=n_f, mask=1)
    run = Order()

    def whole_f(w, axis):
        return lax.all_gather(w, "fsdp", axis=axis, tiled=True)

    def halves(w, axis):
        if n_f == 2:
            return w, over_x(w)
        w = whole_f(w, axis)
        return jnp.split(w, 2, axis=axis)

    def block_of(x, which, part):
        return lax.dynamic_slice(x, (which, part * half, 0), (1, half, width))[0]

    def touch(*x):
        return run(lambda *a: a, *x)

    def after(x, *others):
        return lax.optimization_barrier((x, others))[0]

    with jax.named_scope("arrive"):
        give = run(lambda t: block_of(t, 1 - group, core), tokens)
        b_own = over_z2(give)
        a_own = run(lambda t: block_of(t, group, core), tokens)
        oa_own = over_z1(a_own)
        qkv_t = after(w_qkv.transpose(1, 2, 0).reshape(3 * wide, -1), a_own)
        qkv_moved = over_x(qkv_t) if n_f == 2 else whole_f(qkv_t, 1)
        w_out_later = after(w_out, a_own)
        out_moved = over_x(w_out_later) if n_f == 2 else whole_f(w_out_later, 1)
        cot_give, cot_a, a_far, place, par_one, par_two, bias_row, up_row = run(
            lambda g, t, qb, ub, p1, p2: (
                block_of(g, 1 - group, core),
                block_of(g, group, core),
                block_of(t, group, 1 - core),
                jnp.stack(
                    [
                        jnp.int32(f),
                        (z % 2).astype(jnp.int32),
                        group.astype(jnp.int32),
                        core.astype(jnp.int32),
                    ]
                ),
                jnp.stack(p1),
                jnp.stack(p2),
                jnp.concatenate([qb[0], jnp.zeros_like(qb[0]), qb[1]])[None],
                ub[None],
            ),
            cotangent,
            tokens,
            qv_bias,
            up_bias,
            (out_bias, gain_one, shift_one),
            (down_bias, gain_two, shift_two),
        )
        qkv_w = run(lambda a, b: pick(a, b, f, 1) if n_f == 2 else b, qkv_t, qkv_moved)
        out_w = run(lambda a, b: pick(a, b, f, 1) if n_f == 2 else b, w_out, out_moved)
        (b_own,) = touch(b_own)
        ob_own = over_z1(b_own)
        (oa_own,) = touch(oa_own)
        b_far, oa_far = over_core(b_own), over_core(oa_own)
        b_far, oa_far, out_later = touch(b_far, oa_far, out_w)
        out_near, out_far = over_core(out_later), over_y(out_later)
        up_two = halves(after(w_up, out_later), 0)
        out_near, out_far = touch(out_near, out_far)
        (ob_own,) = touch(ob_own)
        ob_far = over_core(ob_own)
    with jax.named_scope("cotangent"):
        cot_b = over_z2(after(cot_give, ob_own))
    own = [a_own, a_far, b_own, b_far]
    other = [oa_own, oa_far, ob_own, ob_far]
    total = 8 * half
    n_own = total // 2

    q, k, v = run(
        lambda *x: call(
            qkv_kernel,
            [shaped((n_own, wide), BF), shaped((total, wide), BF), shaped((total, wide), BF)],
            *x,
            name="qkv",
        ),
        *own,
        *other[:3],
        qkv_w,
        bias_row,
    )
    row_spec = pl.BlockSpec((half, wide), lambda i: (7, 0))
    k, v = run(
        lambda *x: call(
            last_kv_kernel,
            [shaped((total, wide), BF), shaped((total, wide), BF)],
            *x,
            name="last_kv",
            grid=(1,),
            in_specs=[pl.BlockSpec(a.shape, lambda i: (0, 0)) for a in x[:3]]
            + [pl.BlockSpec(memory_space=pl.ANY)] * 2,
            out_specs=[row_spec, row_spec],
            input_output_aliases={3: 0, 4: 1},
        ),
        ob_far,
        qkv_w,
        bias_row,
        k,
        v,
    )
    with jax.named_scope("down_weight"):
        down_two = halves(after(w_down, q), 1)
    with jax.named_scope("out_weight"):
        out_both = over_both(after(out_later, q))

    mixed, pieces, shared = [], [], ()
    for c in range(2):
        with jax.named_scope(f"attend{c}"):
            mo, mp, *shared = run(lambda *x: attend_fwd(c, half, *x), q, k, v, *shared)
            mixed += [mo, mp]
            if c == 0:
                (*up_two, out_both) = touch(*up_two, out_both)
            else:
                (*pieces[0], cot_b) = touch(*pieces[0], cot_b)
            mo, mp = touch(mo, mp)
            pieces.append((mo, over_core(mp), over_y(mo), over_both(mp)))
    mixed_f, logs = shared
    tok = (a_own, b_own)
    f_rows = shaped((half, width), F32)
    b_rows = shaped((half, width), BF)
    h_rows = shaped((half, hidden_here), BF)
    state = [dict(), dict()]

    def norm_one(c):
        with jax.named_scope(f"normone{c}"):
            s = state[c]
            outs = [f_rows, b_rows, f_rows, shaped((half, 1), F32)]
            s["y"], s["yo"], s["n1"], s["i1"] = run(
                lambda *x: call(norm_one_kernel, outs, *x, name="norm_one"),
                *pieces[c],
                out_w,
                out_near,
                out_far,
                out_both,
                tok[c],
                par_one,
            )
            s["yp"] = over_core(s["yo"])

    def feed(c, which, dtype):
        with jax.named_scope(f"feed{c}{which}"):
            s = state[c]
            outs = [h_rows, shaped((half, hidden_here), F32), shaped((half, width), dtype)]
            s["h" + which], s["s" + which], s["p" + which] = run(
                lambda *x: scalar_call(ffn_kernel, outs, *x, name="feed"),
                place,
                s["y" + which],
                *up_two,
                up_row,
                *down_two,
            )
            if which == "p":
                s["c2"] = over_core(s["pp"])

    def near_sum(c, name):
        with jax.named_scope(f"near{c}{name}"):
            s = state[c]
            (s["near" + name],) = run(
                lambda *x: call(near_kernel, [b_rows], *x, name="near"), s["po"], s["c" + name]
            )
            s["far" + name] = over_y(s["near" + name])

    def norm_two(c):
        with jax.named_scope(f"normtwo{c}"):
            s = state[c]
            outs = [b_rows, f_rows, b_rows, shaped((3, width), F32)]
            s["out"], s["gs"], s["gfo"], s["sum2"] = run(
                lambda *x: call(norm_two_kernel, outs, *x, name="norm_two"),
                s["near2"],
                s["far2"],
                s["y"],
                cot[c],
                par_two,
            )
            s["gfp"] = over_core(s["gfo"])

    def feed_back(c, which, dtype):
        with jax.named_scope(f"feedback{c}{which}"):
            s = state[c]
            outs = [h_rows, shaped((half, width), dtype), shaped((1, hidden_here), F32)]
            s["gp" + which], s["p" + which], s["sumu" + which] = run(
                lambda *x: scalar_call(ffn_back_kernel, outs, *x, name="feed_back"),
                place,
                s["gf" + which],
                *down_two,
                s["s" + which],
                *up_two,
            )
            if which == "p":
                s["c5"] = over_core(s["pp"])

    def norm_one_back(c):
        with jax.named_scope(f"normoneback{c}"):
            s = state[c]
            s["gfirst"], s["gao"], s["sum1"] = run(
                lambda *x: call(
                    norm_one_back_kernel,
                    [f_rows, b_rows, shaped((3, width), F32)],
                    *x,
                    name="norm_one_back",
                ),
                s["gs"],
                s["near5"],
                s["far5"],
                s["n1"],
                s["i1"],
                par_one,
            )
            s["gap"] = over_core(s["gao"])

    def weight_grad(kernel, operands, rows, cols, name, small=False):
        with jax.named_scope(name):
            outs = [
                shaped((rows + small * EXTRA, cols), F32),
                shaped((rows + small * 2 * EXTRA, cols), BF),
            ]
            keep, send = run(lambda *x: scalar_call(kernel, outs, *x, name=name), place, *operands)
            return Reduction(run, name, place, keep, over_x(send), small, over_z1, over_z2)

    def owned(red, name):
        with jax.named_scope(name):
            return run(
                lambda *x: scalar_call(owned_kernel, [shaped((red.rows, red.cols), F32)], *x, name=name),
                place,
                red.own,
                red.moved,
            )[0]

    four = [(c, w) for c in range(2) for w in "op"]

    def pieces_of(name):
        return [state[c][name + w] for c, w in four]

    cot = (cot_a, cot_b)
    norm_one(0)
    feed(0, "o", F32)
    norm_one(1)
    feed(0, "p", BF)
    feed(1, "p", BF)
    near_sum(0, "2")
    feed(1, "o", F32)
    near_sum(1, "2")
    norm_two(0)
    feed_back(0, "o", F32)
    feed_back(0, "p", BF)
    norm_two(1)
    with jax.named_scope("outback"):
        out_back = over_z2(state[1]["out"])
    near_sum(0, "5")
    feed_back(1, "o", F32)
    feed_back(1, "p", BF)
    if n_f == 2:
        red_down = weight_grad(
            down_grad_kernel, pieces_of("h") + pieces_of("gf"), hidden_here, width // 2, "down_grad"
        )
    near_sum(1, "5")
    norm_one_back(0)
    if n_f == 2:
        red_up = weight_grad(
            up_grad_kernel, pieces_of("y") + pieces_of("gp"), width // 2, hidden_here, "up_grad"
        )
    norm_one_back(1)
    (out_back,) = touch(out_back)
    with jax.named_scope("smallpack"):
        (packed,) = run(
            lambda *x: call(pack_kernel, [shaped((8, width), F32)], *x, name="pack"),
            *[state[c][s] for s in ("sum1", "sum2") for c in range(2)],
            *pieces_of("sumu"),
        )
        packed_moved = over_core(packed)
    def placed(blocks):
        return run(
            lambda *x: scalar_call(place_kernel, [shaped(tokens.shape, BF)], *x, name="place"),
            place,
            *blocks,
        )[0]

    def both_halves(a, b):
        return a, over_core(a), b, over_core(b)

    if n_f == 2:
        red_down.step()
    with jax.named_scope("placeout"):
        out_blocks = both_halves(after(state[0]["out"], out_back), out_back)
    grad_attn = pieces_of("ga")
    grad_mixed, inner = run(
        lambda *x: call(
            grad_mixed_kernel, [shaped((n_own, wide), BF), shaped((heads, n_own), F32)], *x, name="grad_mixed"
        ),
        *grad_attn,
        out_w,
        mixed_f,
    )
    (*out_blocks, packed_moved) = touch(*out_blocks, packed_moved)

    early, late = tuple(range(heads - 1)), (heads - 1,)
    bwd_args = (q, k, v, grad_mixed, logs, inner)
    n_one, n_two = 3 * len(early) * HD, 3 * HD
    with jax.named_scope("back1"):
        dq1, own1, far1 = run(lambda *x: attend_bwd(early, 0, total, 2, *x), *bwd_args)
    with jax.named_scope("back1"):
        moved1 = over_z1(far1)
    with jax.named_scope("back2"):
        dq2, far2 = run(lambda *x: attend_bwd(late, 1, n_own, 1, *x, last=False), *bwd_args)
        moved2 = over_z1(far2)
    if n_f == 2:
        red_down.step()
    with jax.named_scope("back3"):
        dq2, own2 = run(lambda *x: attend_bwd(late, 0, n_own, 1, *x), *bwd_args, dq2)
    if n_f == 2:
        red_up.step()
        red_one = weight_grad(
            functools.partial(qkv_grad_kernel, True),
            own + other + [dq1, own1, far1] + mixed + grad_attn + [packed, packed_moved],
            n_one + wide,
            width // 2,
            "one_grad",
            True,
        )
    (moved1,) = touch(moved1)
    if n_f == 2:
        red_two = weight_grad(
            functools.partial(qkv_grad_kernel, False),
            own + other + [dq2, own2, far2],
            n_two,
            width // 2,
            "two_grad",
            True,
        )

    item = [dict(), dict()]

    def input_part(c):
        with jax.named_scope(f"inputpart{c}"):
            s = item[c]
            s["po"], pp = run(
                lambda *x: call(
                    functools.partial(input_part_kernel, c * rows), [f_rows, b_rows], *x, name="input_part"
                ),
                dq1,
                own1,
                moved1,
                dq2,
                own2,
                moved2,
                qkv_w,
            )
            s["cp"] = over_core(pp)

    def input_near(c):
        with jax.named_scope(f"inputnear{c}"):
            s = item[c]
            (s["near"],) = run(
                lambda *x: call(near_kernel, [b_rows], *x, name="near"), s["po"], s["cp"]
            )
            s["far"] = over_y(s["near"])

    def input_last(c):
        with jax.named_scope(f"inputlast{c}"):
            s = item[c]
            (s["in"],) = run(
                lambda *x: call(input_grad_kernel, [b_rows], *x, name="input_grad"),
                state[c]["gfirst"],
                s["near"],
                s["far"],
            )

    input_part(1)
    with jax.named_scope("placeout"):
        output = placed(out_blocks)
    input_near(1)
    if n_f == 2:
        red_down.step()
        red_up.step()
        red_one.step()
    input_last(1)
    with jax.named_scope("inputback"):
        in_back = over_z2(item[1]["in"])
    if n_f == 2:
        red_two.step()
        (red_down.moved,) = touch(red_down.moved)
    input_part(0)
    if n_f == 2:
        owned_down = owned(red_down, "owned_down")
    input_near(0)
    if n_f == 2:
        red_one.step()
        red_up.step()
        red_two.step()
    input_last(0)
    with jax.named_scope("placein"):
        in_far = over_core(item[0]["in"])
    if n_f == 2:
        owned_up = owned(red_up, "owned_up")
        red_one.step()
        red_two.step()
    (in_back,) = touch(in_back)
    with jax.named_scope("placein"):
        in_blocks = [item[0]["in"], in_far, in_back, over_core(in_back)]
    with jax.named_scope("finish"):
        if n_f == 2:
            qkv_grad, owned_out, small, bias_grad = run(
                lambda *x: scalar_call(
                    owned_qkv_kernel,
                    [
                        shaped((3, wide, width // 2), F32),
                        shaped((wide, width // 2), F32),
                        shaped((8, width), F32),
                        shaped((2, wide), F32),
                    ],
                    *x,
                    name="owned_qkv",
                ),
                place,
                red_one.own,
                red_two.own,
                red_one.moved,
                red_two.moved,
            )
            owned_qkv = qkv_grad.transpose(2, 0, 1)
        else:

            def reduce_plain(left, right, axis):
                grad = mm(jnp.concatenate(left), jnp.concatenate(right), TN)
                keep = lax.psum_scatter(grad, "fsdp", scatter_dimension=axis, tiled=True)
                return lax.psum(keep, "context").astype(BF).astype(F32)

            zero = jnp.zeros((n_own, wide), BF)
            cut = len(early) * HD
            dk = [own1[:, :cut], own2[:, :HD], far1[:, :cut], far2[:, :HD]]
            dv = [own1[:, cut:], own2[:, HD:], far1[:, cut:], far2[:, HD:]]
            left = jnp.concatenate([dq1, dq2, *dk[:2], *dv[:2]], axis=1)
            right = jnp.concatenate([zero, *dk[2:], *dv[2:]], axis=1)
            owned_up = reduce_plain(pieces_of("y"), pieces_of("gp"), 0)
            owned_down = reduce_plain(pieces_of("h"), pieces_of("gf"), 1)
            owned_out = reduce_plain(mixed, grad_attn, 1)
            owned_qkv = reduce_plain(own + other, [left, right], 0).reshape(w_qkv.shape)
            column_sums = jnp.sum((left.astype(F32) + right.astype(F32)), axis=0)
            bias_grad = jnp.stack([column_sums[:wide], column_sums[2 * wide :]])
            small = jnp.concatenate([packed[:6] + packed_moved[:6], packed[6:]])
            small, bias_grad = lax.psum((small, bias_grad), ("fsdp", "context"))
    with jax.named_scope("placein"):
        input_grad = placed(in_blocks)
    return (
        output,
        input_grad,
        owned_qkv,
        bias_grad,
        owned_out,
        small[0],
        small[1],
        small[2],
        owned_up,
        small[6],
        owned_down,
        small[3],
        small[4],
        small[5],
    )


def solution(mesh):
    sizes = tuple(mesh.shape[name] for name in ("fsdp", "context", "tensor"))
    specs = (
        P("fsdp", None, "tensor"),
        P(None, "tensor"),
        P("tensor", "fsdp"),
        P(),
        P(),
        P(),
        P("fsdp", "tensor"),
        P("tensor"),
        P("tensor", "fsdp"),
        P(),
        P(),
        P(),
    )
    rows = P("fsdp", "context", None)
    return jax.shard_map(
        functools.partial(body, sizes),
        mesh=mesh,
        in_specs=(rows, rows) + specs,
        out_specs=(rows, rows) + specs,
        check_vma=False,
    )
```

```python
import functools
import math

import jax
import jax.numpy as jnp
from jax import lax
from jax.experimental import pallas as pl
from jax.experimental.pallas import tpu as pltpu
from jax.sharding import PartitionSpec as P

HD = 64
SCALE = 1.0 / math.sqrt(HD)
SCALE_LOG2 = SCALE * math.log2(math.e)
EPS = 1e-06
BF = jnp.bfloat16
F32 = jnp.float32
NT = (((1,), (1,)), ((), ()))
TN = (((0,), (0,)), ((), ()))
NN = (((1,), (0,)), ((), ()))


def mm(a, b, dims=NN):
    return lax.dot_general(a, b, dims, preferred_element_type=F32)


def shaped(shape, dtype):
    return jax.ShapeDtypeStruct(shape, dtype)


def call(kernel, outs, *operands, name, limit=16, **extra):
    return pl.pallas_call(
        kernel,
        out_shape=list(outs),
        cost_estimate=pl.CostEstimate(flops=int(5e9), bytes_accessed=1, transcendentals=0),
        compiler_params=pltpu.CompilerParams(vmem_limit_bytes=limit << 20),
        name=name,
        **extra,
    )(*operands)


SMEM = pl.BlockSpec(memory_space=pltpu.SMEM)
VMEM = pl.BlockSpec(memory_space=pltpu.VMEM)


def scalar_call(kernel, outs, scalars, *operands, **kw):
    specs = [SMEM] + [VMEM] * len(operands)
    return call(kernel, outs, scalars, *operands, in_specs=specs, **kw)


def lanes(ref, index, size):
    return ref[:, pl.ds(pl.multiple_of(index * size, 128), size)]


def qkv_kernel(*refs):
    rows, (w_ref, b_ref, q_ref, k_ref, v_ref) = refs[:7], refs[7:]
    n = rows[0].shape[0]
    wide = q_ref.shape[1]
    for i, ref in enumerate(rows):
        here = slice(i * n, (i + 1) * n)
        skip = 0 if i < 4 else wide
        full = (mm(ref[...], w_ref[skip:, :], NT) + b_ref[:, skip:]).astype(BF)
        if i < 4:
            q_ref[here, :] = full[:, :wide]
        k_ref[here, :] = full[:, wide - skip : 2 * wide - skip]
        v_ref[here, :] = full[:, 2 * wide - skip :]


def last_kv_kernel(x_ref, w_ref, b_ref, *refs):
    k_ref, v_ref = refs[-2:]
    wide = k_ref.shape[1]
    full = (mm(x_ref[...], w_ref[wide:, :], NT) + b_ref[:, wide:]).astype(BF)
    k_ref[...] = full[:, :wide]
    v_ref[...] = full[:, wide:]


def attend_fwd_kernel(chunk, *refs):
    q_ref, k_ref, v_ref = refs[:3]
    o_ref, p_ref, f_ref, l_ref = refs[-4:]
    outs, logs = [], []
    for h in range(q_ref.shape[1] // HD):
        cols = slice(h * HD, (h + 1) * HD)
        scores = mm(q_ref[:, cols], k_ref[:, cols], NT)
        top = jnp.max(scores, axis=1, keepdims=True)
        expo = jnp.exp2((scores - top) * SCALE_LOG2)
        total = jnp.sum(expo, axis=1, keepdims=True)
        outs.append(mm(expo.astype(BF), v_ref[:, cols]) / total)
        logs.append(top * SCALE_LOG2 + jnp.log2(total))
    mixed = jnp.concatenate(outs, axis=1)
    f_ref[...] = mixed
    l_ref[...] = jnp.concatenate(logs, axis=1).T
    for step, ref in enumerate((o_ref, p_ref)):

        @pl.when(pl.program_id(0) == step)
        def _():
            ref[...] = mixed.astype(BF)


def attend_fwd(chunk, block, q, k, v, *before):
    nq, w = q.shape
    nk = k.shape[0]
    heads = w // HD
    q_spec = pl.BlockSpec((block, w), lambda i: (chunk * 2 + i, 0))
    l_spec = pl.BlockSpec((heads, block), lambda i: (0, chunk * 2 + i))
    o_spec = pl.BlockSpec((block, w), lambda i: (0, 0))
    k_spec = pl.BlockSpec((nk, w), lambda i: (0, 0))
    anywhere = pl.BlockSpec(memory_space=pl.ANY)
    return call(
        functools.partial(attend_fwd_kernel, chunk),
        [shaped((block, w), BF)] * 2 + [shaped((nq, w), F32), shaped((heads, nq), F32)],
        q,
        k,
        v,
        *before,
        name="attend_fwd",
        limit=24,
        grid=(2,),
        in_specs=[q_spec, k_spec, k_spec] + [anywhere] * len(before),
        out_specs=[o_spec, o_spec, q_spec, l_spec],
        input_output_aliases={3: 2, 4: 3} if before else {},
    )


def grad_mixed_kernel(*refs):
    gas, (w_ref, f_ref, g_ref, d_ref) = refs[:4], refs[4:]
    n = gas[0].shape[0]
    heads = w_ref.shape[0] // HD
    for i, ga in enumerate(gas):
        here = slice(i * n, (i + 1) * n)
        g = mm(ga[...], w_ref[...], NT).astype(BF)
        g_ref[here, :] = g
        prod = (g.astype(F32) * f_ref[here, :]).T
        d_ref[:, here] = jnp.concatenate(
            [jnp.sum(prod[h * HD : (h + 1) * HD], axis=0, keepdims=True) for h in range(heads)]
        )


def attend_bwd_kernel(heads, first, last, split, *refs):
    q_ref, k_ref, v_ref, g_ref, l_ref, d_ref = refs[:6]
    add_ref = refs[6] if not first else None
    dq_ref, outs, acc = refs[6 + (not first)], refs[7 + (not first) : -1], refs[-1]
    dqs, dks, dvs = [], [], []
    for h in heads:
        cols = slice(h * HD, (h + 1) * HD)
        q, k, v, g = q_ref[:, cols], k_ref[:, cols], v_ref[:, cols], g_ref[:, cols]
        probs = jnp.exp2(mm(k, q, NT) * SCALE_LOG2 - l_ref[h : h + 1, :])
        grad_scores = (probs * (mm(v, g, NT) - d_ref[h : h + 1, :])).astype(BF)
        dvs.append(mm(probs.astype(BF), g))
        dks.append(mm(grad_scores, q) * SCALE)
        dqs.append(mm(k, grad_scores, TN))
    dq = (dqs[0] if len(dqs) == 1 else jnp.concatenate(dqs, axis=0)).T
    if not first:
        dq = dq + add_ref[...]
    dq_ref[...] = (dq * SCALE).astype(BF) if last else dq
    dkv = jnp.concatenate(dks + dvs, axis=1)
    step = pl.program_id(0)

    @pl.when(step == 0)
    def _():
        acc[...] = dkv

    @pl.when(step > 0)
    def _():
        acc[...] += dkv

    @pl.when(step == pl.num_programs(0) - 1)
    def _():
        n = acc.shape[0] // len(outs)
        for i, ref in enumerate(outs):
            ref[...] = acc[i * n : (i + 1) * n].astype(BF)


def attend_bwd(heads, key_block, key_rows, split, q, k, v, g, logs, inner, *add, last=True, block=256):
    nq, w = q.shape
    n = len(heads) * HD
    q_spec = pl.BlockSpec((block, w), lambda i: (i, 0))
    k_spec = pl.BlockSpec((key_rows, w), lambda i: (key_block, 0))
    n_spec = pl.BlockSpec((block, n), lambda i: (i, 0))
    l_spec = pl.BlockSpec((logs.shape[0], block), lambda i: (0, i))
    whole = pl.BlockSpec((key_rows // split, 2 * n), lambda i: (0, 0))
    return call(
        functools.partial(attend_bwd_kernel, heads, not add, last, split),
        [shaped((nq, n), BF if last else F32)] + [shaped((key_rows // split, 2 * n), BF)] * split,
        q,
        k,
        v,
        g,
        logs,
        inner,
        *add,
        name="attend_bwd",
        limit=36,
        grid=(nq // block,),
        in_specs=[q_spec, k_spec, k_spec, q_spec, l_spec, l_spec] + [n_spec] * len(add),
        out_specs=[n_spec] + [whole] * split,
        scratch_shapes=[pltpu.VMEM((key_rows, 2 * n), F32)],
    )


def normed(x):
    centred = x - jnp.mean(x, axis=-1, keepdims=True)
    inverse = lax.rsqrt(jnp.mean(centred * centred, axis=-1, keepdims=True) + EPS)
    return centred * inverse, inverse


def norm_back(g, norm, inverse):
    return inverse * (
        g
        - jnp.mean(g, axis=-1, keepdims=True)
        - norm * jnp.mean(g * norm, axis=-1, keepdims=True)
    )


def down_rows(*terms):
    return jnp.concatenate([jnp.sum(t, axis=0, keepdims=True) for t in terms], axis=0)


def norm_one_kernel(m0, m1, m2, m3, w0, w1, w2, w3, t_ref, p_ref, y_ref, low_ref, n_ref, i_ref):
    near = mm(m0[...], w0[...]) + mm(m1[...], w1[...])
    far = mm(m2[...], w2[...]) + mm(m3[...], w3[...])
    norm, inverse = normed(t_ref[...].astype(F32) + ((near + far) + p_ref[0:1, :]))
    y = norm * p_ref[1:2, :] + p_ref[2:3, :]
    y_ref[...] = y
    low_ref[...] = y.astype(BF)
    n_ref[...] = norm
    i_ref[...] = inverse


def ffn_kernel(s_ref, y_ref, up_own, up_far, b_ref, down_own, down_far, h_ref, sl_ref, p_ref):
    f = s_ref[0]
    size = up_own.shape[0]
    x = mm(lanes(y_ref, f, size), up_own[...]) + mm(lanes(y_ref, 1 - f, size), up_far[...]) + b_ref[...]
    cdf = 0.5 * (1.0 + lax.erf(x * (1.0 / math.sqrt(2.0))))
    pdf = jnp.exp(-0.5 * x * x) * (1.0 / math.sqrt(2.0 * math.pi))
    sl_ref[...] = cdf + x * pdf
    hidden = (x * cdf).astype(BF)
    h_ref[...] = hidden
    for part, ref in ((f, down_own), (1 - f, down_far)):
        here = pl.ds(pl.multiple_of(part * size, 128), size)
        p_ref[:, here] = mm(hidden, ref[...]).astype(p_ref.dtype)


def norm_two_kernel(near, far, y_ref, g_ref, p_ref, o_ref, gs_ref, gf_ref, sums):
    ffn = near[...].astype(F32) + far[...].astype(F32)
    norm, inverse = normed(y_ref[...] + (ffn + p_ref[0:1, :]))
    o_ref[...] = (norm * p_ref[1:2, :] + p_ref[2:3, :]).astype(BF)
    g = g_ref[...].astype(F32)
    grad = norm_back(g * p_ref[1:2, :], norm, inverse)
    low = grad.astype(BF)
    gs_ref[...] = grad
    gf_ref[...] = low
    sums[...] = down_rows(low.astype(F32), g * norm, g)


def ffn_back_kernel(s_ref, g_ref, down_own, down_far, sl_ref, up_own, up_far, gp_ref, p_ref, sums):
    f = s_ref[0]
    size = up_own.shape[0]
    grad = mm(lanes(g_ref, f, size), down_own[...], NT) + mm(lanes(g_ref, 1 - f, size), down_far[...], NT)
    low = (grad * sl_ref[...]).astype(BF)
    gp_ref[...] = low
    sums[...] = down_rows(low.astype(F32))
    for part, ref in ((f, up_own), (1 - f, up_far)):
        here = pl.ds(pl.multiple_of(part * size, 128), size)
        p_ref[:, here] = mm(low, ref[...], NT).astype(p_ref.dtype)


def norm_one_back_kernel(gs_ref, near, far, n_ref, i_ref, p_ref, g_ref, low_ref, sums):
    grad_y = gs_ref[...] + (near[...].astype(F32) + far[...].astype(F32))
    norm = n_ref[...]
    grad = norm_back(grad_y * p_ref[1:2, :], norm, i_ref[...])
    low = grad.astype(BF)
    g_ref[...] = grad
    low_ref[...] = low
    sums[...] = down_rows(low.astype(F32), grad_y * norm, grad_y)


def by_kind(parts):
    return [x[:, :HD] for x in parts] + [x[:, HD:] for x in parts]


def input_part_kernel(first_row, *refs):
    w_ref, o_ref, p_ref = refs[-3:]
    heads = (len(refs) - 3) // 3
    dqs, dkvs, moved = (refs[i * heads : (i + 1) * heads] for i in range(3))
    n = o_ref.shape[0]
    for part, ref in enumerate((o_ref, p_ref)):
        here = slice(first_row + part * n, first_row + (part + 1) * n)
        lows = [(a[here, :].astype(F32) + b[here, :].astype(F32)).astype(BF) for a, b in zip(dkvs, moved)]
        grads = jnp.concatenate([d[here, :] for d in dqs] + by_kind(lows), axis=1)
        ref[...] = mm(grads, w_ref[...]).astype(ref.dtype)


def near_kernel(a_ref, b_ref, o_ref):
    o_ref[...] = (a_ref[...] + b_ref[...].astype(F32)).astype(BF)


def input_grad_kernel(g_ref, a_ref, b_ref, o_ref):
    o_ref[...] = (g_ref[...] + (a_ref[...].astype(F32) + b_ref[...].astype(F32))).astype(BF)


def place_kernel(s_ref, a, b, c, d, o_ref):
    n = a.shape[0]
    group, core = s_ref[2], s_ref[3]
    for block, half, ref in ((group, core, a), (group, 1 - core, b), (1 - group, core, c), (1 - group, 1 - core, d)):
        o_ref[block, pl.ds(pl.multiple_of(half * n, n), n), :] = ref[...]


def pack_kernel(a0, a1, b0, b1, u0, u1, u2, u3, o_ref):
    o_ref[0:3, :] = a0[...] + a1[...]
    o_ref[3:6, :] = b0[...] + b1[...]
    o_ref[6:7, :] = u0[...] + u1[...] + u2[...] + u3[...]
    o_ref[7:8, :] = jnp.zeros_like(u0)


EXTRA = 16


def two_parts(x):
    high = x.astype(BF).astype(F32)
    return high + (x - high).astype(BF).astype(F32)


def put(ref, main, small):
    n = main.shape[0]
    ref[0:n, :] = main.astype(ref.dtype)
    if small is not None:
        high = small.astype(ref.dtype)
        ref[n : n + EXTRA, :] = high
        if ref.shape[0] > n + EXTRA:
            ref[n + EXTRA :, :] = (small - high.astype(F32)).astype(ref.dtype)


def get(ref, small):
    if not small:
        return ref[...].astype(F32), None
    parts = 1 if ref.dtype == F32 else 2
    n = ref.shape[0] - parts * EXTRA
    rest = ref[n : n + EXTRA, :].astype(F32)
    if parts == 2:
        rest = rest + ref[n + EXTRA :, :].astype(F32)
    return ref[0:n, :].astype(F32), rest


def up_grad_kernel(s_ref, *refs):
    ys, gs, (keep, send) = refs[:4], refs[4:8], refs[8:]
    f = s_ref[0]
    size = ys[0].shape[1] // 2
    for out, part in ((send, 1 - f), (keep, f)):
        put(out, sum(mm(lanes(y, part, size), g[...], TN) for y, g in zip(ys, gs)), None)


def down_grad_kernel(s_ref, *refs):
    hs, gs, (keep, send) = refs[:4], refs[4:8], refs[8:]
    f = s_ref[0]
    size = gs[0].shape[1] // 2
    for out, part in ((send, 1 - f), (keep, f)):
        put(out, sum(mm(h[...], lanes(g, part, size), TN) for h, g in zip(hs, gs)), None)


def qkv_grad_kernel(heads, with_out, s_ref, *refs):
    rows, more, (keep, send) = refs[:8], refs[8 + 3 * heads : -2], refs[-2:]
    dqs, owns, fars = (refs[8 + i * heads : 8 + (i + 1) * heads] for i in range(3))
    f = s_ref[0]
    size = rows[0].shape[1] // 2
    n = rows[0].shape[0]
    m = heads * HD
    own = jnp.concatenate([d[...] for d in dqs] + by_kind([x[...] for x in owns]), axis=1)
    far = jnp.concatenate(by_kind([x[...] for x in fars]), axis=1)
    far_sums = jnp.sum(far.astype(F32), axis=0, keepdims=True)
    sums = jnp.sum(own.astype(F32), axis=0, keepdims=True)
    sums = jnp.concatenate([sums[:, :m], sums[:, m:] + far_sums], axis=1)
    if sums.shape[1] < size:
        sums = jnp.concatenate([sums, jnp.zeros((1, size - sums.shape[1]), F32)], axis=1)
    small = [sums]
    if with_out:
        packed, moved = more[-2:]
        six = packed[0:6, :] + moved[0:6, :]
        ups = packed[6:7, :]
        small = [six[:, :size], ups[:, :size], six[:, size:], ups[:, size:], sums]
    small.append(jnp.zeros((EXTRA - sum(x.shape[0] for x in small), size), F32))
    small = two_parts(jnp.concatenate(small, axis=0))
    for out, part in ((send, 1 - f), (keep, f)):
        one = two = None
        for i in range(4):
            here = slice(i * n, (i + 1) * n)
            a = mm(own[here], lanes(rows[i], part, size), TN)
            b = mm(far[here], lanes(rows[4 + i], part, size), TN)
            one = a if one is None else one + a
            two = b if two is None else two + b
        grad = [one[:m], one[m:] + two]
        if with_out:
            grad.append(sum(mm(a[...], lanes(g, part, size), TN) for a, g in zip(more[:4], more[4:8])))
        put(out, jnp.concatenate(grad, axis=0), small)


def half_of(main, which):
    n = main.shape[0] // 2
    return jnp.where(which == 0, main[:n], main[n:])


def first_sum_kernel(small, s_ref, keep, moved, own, send):
    (a, c), (b, d) = get(keep, small), get(moved, small)
    total = a + b
    rest = two_parts(c + d) if small else None
    put(own, half_of(total, s_ref[1]), rest)
    put(send, half_of(total, 1 - s_ref[1]), rest)


def sum_kernel(small, a_ref, b_ref, out):
    (a, c), (b, d) = get(a_ref, small), get(b_ref, small)
    put(out, a + b, c + d if small else None)


def joined(s_ref, own, moved):
    first = s_ref[1] == 0
    return jnp.concatenate([jnp.where(first, own, moved), jnp.where(first, moved, own)], axis=0)


def owned_kernel(s_ref, own, moved, out):
    out[...] = joined(s_ref, get(own, False)[0], get(moved, False)[0])


def owned_qkv_kernel(s_ref, own1, own2, moved1, moved2, qkv, outw, sums, bias):
    (one, small1), (two, small2) = get(own1, True), get(own2, True)
    one = joined(s_ref, one, get(moved1, True)[0])
    two = joined(s_ref, two, get(moved2, True)[0])
    n = outw.shape[0]
    m1, m2 = (one.shape[0] - n) // 3, two.shape[0] // 3
    for j in range(3):
        qkv[j, 0:m1, :] = one[j * m1 : (j + 1) * m1]
        qkv[j, m1:, :] = two[j * m2 : (j + 1) * m2]
    outw[...] = one[3 * m1 :]
    sums[0:7, :] = jnp.concatenate([small1[0:7], small1[7:14]], axis=1)
    sums[7:8, :] = jnp.zeros_like(sums[7:8, :])
    for i, j in ((0, 0), (1, 2)):
        bias[i : i + 1, :] = jnp.concatenate(
            [small1[14:15, j * m1 : (j + 1) * m1], small2[0:1, j * m2 : (j + 1) * m2]], axis=1
        )


def swap(x, axis, size, mask):
    return lax.ppermute(x, axis, [(i, i ^ mask) for i in range(size)])


def pick(first, second, bit, axis):
    n = first.shape[axis]
    ring = jnp.concatenate([first, second, first], axis=axis)
    return lax.dynamic_slice_in_dim(ring, bit * n, 2 * n, axis)


class Order:
    def __init__(self):
        self.done = None

    def __call__(self, fn, *operands):
        if self.done is not None:
            operands, _ = lax.optimization_barrier((operands, self.done))
        out = fn(*operands)
        self.done = out
        return out


class Reduction:
    def __init__(self, run, name, place, keep, moved, small, over_z1, over_z2):
        self.run, self.name, self.place, self.small = run, name, place, small
        self.own, self.moved, self.stage = keep, moved, 0
        self.over = [over_z1, over_z2, over_z1]
        self.rows, self.cols = keep.shape[0] - small * EXTRA, keep.shape[1]

    def step(self):
        self.stage += 1
        low = shaped((self.rows // 2 + self.small * 2 * EXTRA, self.cols), BF)
        wide = shaped((self.rows // 2 + self.small * EXTRA, self.cols), F32)
        name = f"{self.name}_{self.stage}"
        with jax.named_scope(name):
            if self.stage == 1:
                kernel = functools.partial(first_sum_kernel, self.small)
                fn = lambda *x: scalar_call(kernel, [wide, low], *x, name=name)
                self.own, send = self.run(fn, self.place, self.own, self.moved)
            else:
                kernel = functools.partial(sum_kernel, self.small)
                fn = lambda *x: call(kernel, [low], *x, name=name)
                (self.own,) = self.run(fn, self.own, self.moved)
                send = self.own
            self.moved = self.over[self.stage - 1](send)


def body(sizes, *args):
    (
        tokens,
        cotangent,
        w_qkv,
        qv_bias,
        w_out,
        out_bias,
        gain_one,
        shift_one,
        w_up,
        up_bias,
        w_down,
        down_bias,
        gain_two,
        shift_two,
    ) = args
    n_f, n_c, n_t = sizes
    _, rows, width = tokens.shape
    wide = w_qkv.shape[2]
    heads = wide // HD
    hidden_here = w_up.shape[1]
    half = rows // 2
    f = lax.axis_index("fsdp") if n_f == 2 else 0
    z = lax.axis_index("context")
    core = lax.axis_index("tensor") % 2
    group = z // 2
    over_core = functools.partial(swap, axis="tensor", size=n_t, mask=1)
    over_y = functools.partial(swap, axis="tensor", size=n_t, mask=2)
    over_both = functools.partial(swap, axis="tensor", size=n_t, mask=3)
    over_z1 = functools.partial(swap, axis="context", size=n_c, mask=1)
    over_z2 = functools.partial(swap, axis="context", size=n_c, mask=2)
    over_x = functools.partial(swap, axis="fsdp", size=n_f, mask=1)
    run = Order()

    def whole_f(w, axis):
        return lax.all_gather(w, "fsdp", axis=axis, tiled=True)

    def halves(w, axis):
        if n_f == 2:
            return w, over_x(w)
        w = whole_f(w, axis)
        return jnp.split(w, 2, axis=axis)

    def block_of(x, which, part):
        return lax.dynamic_slice(x, (which, part * half, 0), (1, half, width))[0]

    def touch(*x):
        return run(lambda *a: a, *x)

    def after(x, *others):
        return lax.optimization_barrier((x, others))[0]

    with jax.named_scope("arrive"):
        give = run(lambda t: block_of(t, 1 - group, core), tokens)
        b_own = over_z2(give)
        a_own = run(lambda t: block_of(t, group, core), tokens)
        oa_own = over_z1(a_own)
        qkv_t = after(w_qkv.transpose(1, 2, 0).reshape(3 * wide, -1), a_own)
        qkv_moved = over_x(qkv_t) if n_f == 2 else whole_f(qkv_t, 1)
        w_out_later = after(w_out, a_own)
        out_moved = over_x(w_out_later) if n_f == 2 else whole_f(w_out_later, 1)
        cot_give, cot_a, a_far, place, par_one, par_two, bias_row, up_row = run(
            lambda g, t, qb, ub, p1, p2: (
                block_of(g, 1 - group, core),
                block_of(g, group, core),
                block_of(t, group, 1 - core),
                jnp.stack(
                    [
                        jnp.int32(f),
                        (z % 2).astype(jnp.int32),
                        group.astype(jnp.int32),
                        core.astype(jnp.int32),
                    ]
                ),
                jnp.stack(p1),
                jnp.stack(p2),
                jnp.concatenate([qb[0], jnp.zeros_like(qb[0]), qb[1]])[None],
                ub[None],
            ),
            cotangent,
            tokens,
            qv_bias,
            up_bias,
            (out_bias, gain_one, shift_one),
            (down_bias, gain_two, shift_two),
        )
        qkv_w = run(lambda a, b: pick(a, b, f, 1) if n_f == 2 else b, qkv_t, qkv_moved)
        out_w = run(lambda a, b: pick(a, b, f, 1) if n_f == 2 else b, w_out, out_moved)
        (b_own,) = touch(b_own)
        ob_own = over_z1(b_own)
        (oa_own,) = touch(oa_own)
        b_far, oa_far = over_core(b_own), over_core(oa_own)
        b_far, oa_far, out_later = touch(b_far, oa_far, out_w)
        out_near, out_far = over_core(out_later), over_y(out_later)
        up_two = halves(after(w_up, out_later), 0)
        out_near, out_far = touch(out_near, out_far)
        (ob_own,) = touch(ob_own)
        ob_far = over_core(ob_own)
    with jax.named_scope("cotangent"):
        cot_b = over_z2(after(cot_give, ob_own))
    own = [a_own, a_far, b_own, b_far]
    other = [oa_own, oa_far, ob_own, ob_far]
    total = 8 * half
    n_own = total // 2

    q, k, v = run(
        lambda *x: call(
            qkv_kernel,
            [shaped((n_own, wide), BF), shaped((total, wide), BF), shaped((total, wide), BF)],
            *x,
            name="qkv",
        ),
        *own,
        *other[:3],
        qkv_w,
        bias_row,
    )
    row_spec = pl.BlockSpec((half, wide), lambda i: (7, 0))
    k, v = run(
        lambda *x: call(
            last_kv_kernel,
            [shaped((total, wide), BF), shaped((total, wide), BF)],
            *x,
            name="last_kv",
            grid=(1,),
            in_specs=[pl.BlockSpec(a.shape, lambda i: (0, 0)) for a in x[:3]]
            + [pl.BlockSpec(memory_space=pl.ANY)] * 2,
            out_specs=[row_spec, row_spec],
            input_output_aliases={3: 0, 4: 1},
        ),
        ob_far,
        qkv_w,
        bias_row,
        k,
        v,
    )
    with jax.named_scope("down_weight"):
        down_two = halves(after(w_down, q), 1)
    with jax.named_scope("out_weight"):
        out_both = over_both(after(out_later, q))

    mixed, pieces, shared = [], [], ()
    for c in range(2):
        with jax.named_scope(f"attend{c}"):
            mo, mp, *shared = run(lambda *x: attend_fwd(c, half, *x), q, k, v, *shared)
            mixed += [mo, mp]
            if c == 0:
                (*up_two, out_both) = touch(*up_two, out_both)
            else:
                (*pieces[0], cot_b) = touch(*pieces[0], cot_b)
            mo, mp = touch(mo, mp)
            pieces.append((mo, over_core(mp), over_y(mo), over_both(mp)))
    mixed_f, logs = shared
    tok = (a_own, b_own)
    f_rows = shaped((half, width), F32)
    b_rows = shaped((half, width), BF)
    h_rows = shaped((half, hidden_here), BF)
    state = [dict(), dict()]

    def norm_one(c):
        with jax.named_scope(f"normone{c}"):
            s = state[c]
            outs = [f_rows, b_rows, f_rows, shaped((half, 1), F32)]
            s["y"], s["yo"], s["n1"], s["i1"] = run(
                lambda *x: call(norm_one_kernel, outs, *x, name="norm_one"),
                *pieces[c],
                out_w,
                out_near,
                out_far,
                out_both,
                tok[c],
                par_one,
            )
            s["yp"] = over_core(s["yo"])

    def feed(c, which, dtype):
        with jax.named_scope(f"feed{c}{which}"):
            s = state[c]
            outs = [h_rows, shaped((half, hidden_here), F32), shaped((half, width), dtype)]
            s["h" + which], s["s" + which], s["p" + which] = run(
                lambda *x: scalar_call(ffn_kernel, outs, *x, name="feed"),
                place,
                s["y" + which],
                *up_two,
                up_row,
                *down_two,
            )
            if which == "p":
                s["c2"] = over_core(s["pp"])

    def near_sum(c, name):
        with jax.named_scope(f"near{c}{name}"):
            s = state[c]
            (s["near" + name],) = run(
                lambda *x: call(near_kernel, [b_rows], *x, name="near"), s["po"], s["c" + name]
            )
            s["far" + name] = over_y(s["near" + name])

    def norm_two(c):
        with jax.named_scope(f"normtwo{c}"):
            s = state[c]
            outs = [b_rows, f_rows, b_rows, shaped((3, width), F32)]
            s["out"], s["gs"], s["gfo"], s["sum2"] = run(
                lambda *x: call(norm_two_kernel, outs, *x, name="norm_two"),
                s["near2"],
                s["far2"],
                s["y"],
                cot[c],
                par_two,
            )
            s["gfp"] = over_core(s["gfo"])

    def feed_back(c, which, dtype):
        with jax.named_scope(f"feedback{c}{which}"):
            s = state[c]
            outs = [h_rows, shaped((half, width), dtype), shaped((1, hidden_here), F32)]
            s["gp" + which], s["p" + which], s["sumu" + which] = run(
                lambda *x: scalar_call(ffn_back_kernel, outs, *x, name="feed_back"),
                place,
                s["gf" + which],
                *down_two,
                s["s" + which],
                *up_two,
            )
            if which == "p":
                s["c5"] = over_core(s["pp"])

    def norm_one_back(c):
        with jax.named_scope(f"normoneback{c}"):
            s = state[c]
            s["gfirst"], s["gao"], s["sum1"] = run(
                lambda *x: call(
                    norm_one_back_kernel,
                    [f_rows, b_rows, shaped((3, width), F32)],
                    *x,
                    name="norm_one_back",
                ),
                s["gs"],
                s["near5"],
                s["far5"],
                s["n1"],
                s["i1"],
                par_one,
            )
            s["gap"] = over_core(s["gao"])

    def weight_grad(kernel, operands, rows, cols, name, small=False):
        with jax.named_scope(name):
            outs = [
                shaped((rows + small * EXTRA, cols), F32),
                shaped((rows + small * 2 * EXTRA, cols), BF),
            ]
            keep, send = run(lambda *x: scalar_call(kernel, outs, *x, name=name), place, *operands)
            return Reduction(run, name, place, keep, over_x(send), small, over_z1, over_z2)

    def owned(red, name):
        with jax.named_scope(name):
            return run(
                lambda *x: scalar_call(owned_kernel, [shaped((red.rows, red.cols), F32)], *x, name=name),
                place,
                red.own,
                red.moved,
            )[0]

    four = [(c, w) for c in range(2) for w in "op"]

    def pieces_of(name):
        return [state[c][name + w] for c, w in four]

    cot = (cot_a, cot_b)
    norm_one(0)
    feed(0, "o", F32)
    norm_one(1)
    feed(0, "p", BF)
    feed(1, "p", BF)
    near_sum(0, "2")
    feed(1, "o", F32)
    near_sum(1, "2")
    norm_two(0)
    feed_back(0, "o", F32)
    feed_back(0, "p", BF)
    norm_two(1)
    with jax.named_scope("outback"):
        out_back = over_z2(state[1]["out"])
    near_sum(0, "5")
    feed_back(1, "o", F32)
    feed_back(1, "p", BF)
    if n_f == 2:
        red_down = weight_grad(
            down_grad_kernel, pieces_of("h") + pieces_of("gf"), hidden_here, width // 2, "down_grad"
        )
    near_sum(1, "5")
    norm_one_back(0)
    if n_f == 2:
        red_up = weight_grad(
            up_grad_kernel, pieces_of("y") + pieces_of("gp"), width // 2, hidden_here, "up_grad"
        )
    norm_one_back(1)
    (out_back,) = touch(out_back)
    with jax.named_scope("smallpack"):
        (packed,) = run(
            lambda *x: call(pack_kernel, [shaped((8, width), F32)], *x, name="pack"),
            *[state[c][s] for s in ("sum1", "sum2") for c in range(2)],
            *pieces_of("sumu"),
        )
        packed_moved = over_core(packed)
    def placed(blocks):
        return run(
            lambda *x: scalar_call(place_kernel, [shaped(tokens.shape, BF)], *x, name="place"),
            place,
            *blocks,
        )[0]

    def both_halves(a, b):
        return a, over_core(a), b, over_core(b)

    if n_f == 2:
        red_down.step()
    with jax.named_scope("placeout"):
        out_blocks = both_halves(after(state[0]["out"], out_back), out_back)
    grad_attn = pieces_of("ga")
    grad_mixed, inner = run(
        lambda *x: call(
            grad_mixed_kernel, [shaped((n_own, wide), BF), shaped((heads, n_own), F32)], *x, name="grad_mixed"
        ),
        *grad_attn,
        out_w,
        mixed_f,
    )
    (*out_blocks, packed_moved) = touch(*out_blocks, packed_moved)

    early, late = tuple(range(heads - 1)), (heads - 1,)
    bwd_args = (q, k, v, grad_mixed, logs, inner)
    n_one, n_two = 3 * len(early) * HD, 3 * HD
    dqs, owns, fars, moved = [], [], [], []
    for h in early:
        with jax.named_scope(f"back{h}"):
            dq, mine, far = run(lambda *x: attend_bwd((h,), 0, total, 2, *x), *bwd_args)
            dqs.append(dq)
            owns.append(mine)
            fars.append(far)
            moved.append(over_z1(far))
        if n_f == 2 and h == 0:
            red_down.step()
            red_up.step()
    with jax.named_scope("backfar"):
        dq, far = run(lambda *x: attend_bwd(late, 1, n_own, 1, *x, last=False), *bwd_args)
        fars.append(far)
        moved.append(over_z1(far))
    with jax.named_scope("backown"):
        dq, mine = run(lambda *x: attend_bwd(late, 0, n_own, 1, *x), *bwd_args, dq)
        dqs.append(dq)
        owns.append(mine)
    if n_f == 2:
        red_up.step()
    (moved[0],) = touch(moved[0])
    if n_f == 2:
        red_one = weight_grad(
            functools.partial(qkv_grad_kernel, len(early), True),
            own + other + dqs[:-1] + owns[:-1] + fars[:-1] + mixed + grad_attn + [packed, packed_moved],
            n_one + wide,
            width // 2,
            "one_grad",
            True,
        )
        red_down.step()
    moved[1:-1] = touch(*moved[1:-1])
    if n_f == 2:
        red_two = weight_grad(
            functools.partial(qkv_grad_kernel, 1, False),
            own + other + dqs[-1:] + owns[-1:] + fars[-1:],
            n_two,
            width // 2,
            "two_grad",
            True,
        )

    item = [dict(), dict()]

    def input_part(c):
        with jax.named_scope(f"inputpart{c}"):
            s = item[c]
            s["po"], pp = run(
                lambda *x: call(
                    functools.partial(input_part_kernel, c * rows), [f_rows, b_rows], *x, name="input_part"
                ),
                *dqs,
                *owns,
                *moved,
                qkv_w,
            )
            s["cp"] = over_core(pp)

    def input_near(c):
        with jax.named_scope(f"inputnear{c}"):
            s = item[c]
            (s["near"],) = run(
                lambda *x: call(near_kernel, [b_rows], *x, name="near"), s["po"], s["cp"]
            )
            s["far"] = over_y(s["near"])

    def input_last(c):
        with jax.named_scope(f"inputlast{c}"):
            s = item[c]
            (s["in"],) = run(
                lambda *x: call(input_grad_kernel, [b_rows], *x, name="input_grad"),
                state[c]["gfirst"],
                s["near"],
                s["far"],
            )

    input_part(1)
    with jax.named_scope("placeout"):
        output = placed(out_blocks)
    input_near(1)
    if n_f == 2:
        red_up.step()
        red_one.step()
    input_last(1)
    with jax.named_scope("inputback"):
        in_back = over_z2(item[1]["in"])
    if n_f == 2:
        red_two.step()
        (red_down.moved,) = touch(red_down.moved)
    input_part(0)
    if n_f == 2:
        owned_down = owned(red_down, "owned_down")
    input_near(0)
    if n_f == 2:
        red_one.step()
        owned_up = owned(red_up, "owned_up")
        red_two.step()
    input_last(0)
    with jax.named_scope("placein"):
        in_far = over_core(item[0]["in"])
    if n_f == 2:
        red_one.step()
        red_two.step()
    (in_back,) = touch(in_back)
    with jax.named_scope("placein"):
        in_blocks = [item[0]["in"], in_far, in_back, over_core(in_back)]
    with jax.named_scope("finish"):
        if n_f == 2:
            qkv_grad, owned_out, small, bias_grad = run(
                lambda *x: scalar_call(
                    owned_qkv_kernel,
                    [
                        shaped((3, wide, width // 2), F32),
                        shaped((wide, width // 2), F32),
                        shaped((8, width), F32),
                        shaped((2, wide), F32),
                    ],
                    *x,
                    name="owned_qkv",
                ),
                place,
                red_one.own,
                red_two.own,
                red_one.moved,
                red_two.moved,
            )
            owned_qkv = qkv_grad.transpose(2, 0, 1)
        else:

            def reduce_plain(left, right, axis):
                grad = mm(jnp.concatenate(left), jnp.concatenate(right), TN)
                keep = lax.psum_scatter(grad, "fsdp", scatter_dimension=axis, tiled=True)
                return lax.psum(keep, "context").astype(BF).astype(F32)

            zero = jnp.zeros((n_own, wide), BF)
            left = jnp.concatenate(dqs + by_kind(owns), axis=1)
            right = jnp.concatenate([zero] + by_kind(fars), axis=1)
            owned_up = reduce_plain(pieces_of("y"), pieces_of("gp"), 0)
            owned_down = reduce_plain(pieces_of("h"), pieces_of("gf"), 1)
            owned_out = reduce_plain(mixed, grad_attn, 1)
            owned_qkv = reduce_plain(own + other, [left, right], 0).reshape(w_qkv.shape)
            column_sums = jnp.sum((left.astype(F32) + right.astype(F32)), axis=0)
            bias_grad = jnp.stack([column_sums[:wide], column_sums[2 * wide :]])
            small = jnp.concatenate([packed[:6] + packed_moved[:6], packed[6:]])
            small, bias_grad = lax.psum((small, bias_grad), ("fsdp", "context"))
    with jax.named_scope("placein"):
        input_grad = placed(in_blocks)
    return (
        output,
        input_grad,
        owned_qkv,
        bias_grad,
        owned_out,
        small[0],
        small[1],
        small[2],
        owned_up,
        small[6],
        owned_down,
        small[3],
        small[4],
        small[5],
    )


def solution(mesh):
    sizes = tuple(mesh.shape[name] for name in ("fsdp", "context", "tensor"))
    specs = (
        P("fsdp", None, "tensor"),
        P(None, "tensor"),
        P("tensor", "fsdp"),
        P(),
        P(),
        P(),
        P("fsdp", "tensor"),
        P("tensor"),
        P("tensor", "fsdp"),
        P(),
        P(),
        P(),
    )
    rows = P("fsdp", "context", None)
    return jax.shard_map(
        functools.partial(body, sizes),
        mesh=mesh,
        in_specs=(rows, rows) + specs,
        out_specs=(rows, rows) + specs,
        check_vma=False,
    )
```

```python
import functools
import math

import jax
import jax.numpy as jnp
from jax import lax
from jax.experimental import pallas as pl
from jax.experimental.pallas import tpu as pltpu
from jax.sharding import PartitionSpec as P

HD = 64
SCALE = 1.0 / math.sqrt(HD)
SCALE_LOG2 = SCALE * math.log2(math.e)
EPS = 1e-06
BF = jnp.bfloat16
F32 = jnp.float32
NT = (((1,), (1,)), ((), ()))
TN = (((0,), (0,)), ((), ()))
NN = (((1,), (0,)), ((), ()))


def mm(a, b, dims=NN):
    return lax.dot_general(a, b, dims, preferred_element_type=F32)


def shaped(shape, dtype):
    return jax.ShapeDtypeStruct(shape, dtype)


def call(kernel, outs, *operands, name, limit=16, **extra):
    return pl.pallas_call(
        kernel,
        out_shape=list(outs),
        cost_estimate=pl.CostEstimate(flops=int(5e9), bytes_accessed=1, transcendentals=0),
        compiler_params=pltpu.CompilerParams(vmem_limit_bytes=limit << 20),
        name=name,
        **extra,
    )(*operands)


SMEM = pl.BlockSpec(memory_space=pltpu.SMEM)
VMEM = pl.BlockSpec(memory_space=pltpu.VMEM)


def scalar_call(kernel, outs, scalars, *operands, **kw):
    specs = [SMEM] + [VMEM] * len(operands)
    return call(kernel, outs, scalars, *operands, in_specs=specs, **kw)


def lanes(ref, index, size):
    return ref[:, pl.ds(pl.multiple_of(index * size, 128), size)]


def qkv_kernel(*refs):
    rows, (w_ref, b_ref, q_ref, k_ref, v_ref) = refs[:7], refs[7:]
    n = rows[0].shape[0]
    wide = q_ref.shape[1]
    for i, ref in enumerate(rows):
        here = slice(i * n, (i + 1) * n)
        skip = 0 if i < 4 else wide
        full = (mm(ref[...], w_ref[skip:, :], NT) + b_ref[:, skip:]).astype(BF)
        if i < 4:
            q_ref[here, :] = full[:, :wide]
        k_ref[here, :] = full[:, wide - skip : 2 * wide - skip]
        v_ref[here, :] = full[:, 2 * wide - skip :]


def last_kv_kernel(x_ref, w_ref, b_ref, *refs):
    k_ref, v_ref = refs[-2:]
    wide = k_ref.shape[1]
    full = (mm(x_ref[...], w_ref[wide:, :], NT) + b_ref[:, wide:]).astype(BF)
    k_ref[...] = full[:, :wide]
    v_ref[...] = full[:, wide:]


def attend_fwd_kernel(chunk, *refs):
    q_ref, k_ref, v_ref = refs[:3]
    o_ref, p_ref, f_ref, l_ref = refs[-4:]
    outs, logs = [], []
    for h in range(q_ref.shape[1] // HD):
        cols = slice(h * HD, (h + 1) * HD)
        scores = mm(q_ref[:, cols], k_ref[:, cols], NT)
        top = jnp.max(scores, axis=1, keepdims=True)
        expo = jnp.exp2((scores - top) * SCALE_LOG2)
        total = jnp.sum(expo, axis=1, keepdims=True)
        outs.append(mm(expo.astype(BF), v_ref[:, cols]) / total)
        logs.append(top * SCALE_LOG2 + jnp.log2(total))
    mixed = jnp.concatenate(outs, axis=1)
    f_ref[...] = mixed
    l_ref[...] = jnp.concatenate(logs, axis=1).T
    for step, ref in enumerate((o_ref, p_ref)):

        @pl.when(pl.program_id(0) == step)
        def _():
            ref[...] = mixed.astype(BF)


def attend_fwd(chunk, block, q, k, v, *before):
    nq, w = q.shape
    nk = k.shape[0]
    heads = w // HD
    q_spec = pl.BlockSpec((block, w), lambda i: (chunk * 2 + i, 0))
    l_spec = pl.BlockSpec((heads, block), lambda i: (0, chunk * 2 + i))
    o_spec = pl.BlockSpec((block, w), lambda i: (0, 0))
    k_spec = pl.BlockSpec((nk, w), lambda i: (0, 0))
    anywhere = pl.BlockSpec(memory_space=pl.ANY)
    return call(
        functools.partial(attend_fwd_kernel, chunk),
        [shaped((block, w), BF)] * 2 + [shaped((nq, w), F32), shaped((heads, nq), F32)],
        q,
        k,
        v,
        *before,
        name="attend_fwd",
        limit=24,
        grid=(2,),
        in_specs=[q_spec, k_spec, k_spec] + [anywhere] * len(before),
        out_specs=[o_spec, o_spec, q_spec, l_spec],
        input_output_aliases={3: 2, 4: 3} if before else {},
    )


def grad_mixed_kernel(*refs):
    gas, (w_ref, f_ref, g_ref, d_ref) = refs[:4], refs[4:]
    n = gas[0].shape[0]
    heads = w_ref.shape[0] // HD
    for i, ga in enumerate(gas):
        here = slice(i * n, (i + 1) * n)
        g = mm(ga[...], w_ref[...], NT).astype(BF)
        g_ref[here, :] = g
        prod = (g.astype(F32) * f_ref[here, :]).T
        d_ref[:, here] = jnp.concatenate(
            [jnp.sum(prod[h * HD : (h + 1) * HD], axis=0, keepdims=True) for h in range(heads)]
        )


def attend_bwd_kernel(heads, first, last, split, *refs):
    q_ref, k_ref, v_ref, g_ref, l_ref, d_ref = refs[:6]
    add_ref = refs[6] if not first else None
    dq_ref, outs, acc = refs[6 + (not first)], refs[7 + (not first) : -1], refs[-1]
    dqs, dks, dvs = [], [], []
    for h in heads:
        cols = slice(h * HD, (h + 1) * HD)
        q, k, v, g = q_ref[:, cols], k_ref[:, cols], v_ref[:, cols], g_ref[:, cols]
        probs = jnp.exp2(mm(k, q, NT) * SCALE_LOG2 - l_ref[h : h + 1, :])
        grad_scores = (probs * (mm(v, g, NT) - d_ref[h : h + 1, :])).astype(BF)
        dvs.append(mm(probs.astype(BF), g))
        dks.append(mm(grad_scores, q) * SCALE)
        dqs.append(mm(k, grad_scores, TN))
    dq = (dqs[0] if len(dqs) == 1 else jnp.concatenate(dqs, axis=0)).T
    if not first:
        dq = dq + add_ref[...]
    dq_ref[...] = (dq * SCALE).astype(BF) if last else dq
    dkv = jnp.concatenate(dks + dvs, axis=1)
    step = pl.program_id(0)

    @pl.when(step == 0)
    def _():
        acc[...] = dkv

    @pl.when(step > 0)
    def _():
        acc[...] += dkv

    @pl.when(step == pl.num_programs(0) - 1)
    def _():
        n = acc.shape[0] // len(outs)
        for i, ref in enumerate(outs):
            ref[...] = acc[i * n : (i + 1) * n].astype(BF)


def attend_bwd(heads, key_block, key_rows, split, q, k, v, g, logs, inner, *add, last=True, block=256):
    nq, w = q.shape
    n = len(heads) * HD
    q_spec = pl.BlockSpec((block, w), lambda i: (i, 0))
    k_spec = pl.BlockSpec((key_rows, w), lambda i: (key_block, 0))
    n_spec = pl.BlockSpec((block, n), lambda i: (i, 0))
    l_spec = pl.BlockSpec((logs.shape[0], block), lambda i: (0, i))
    whole = pl.BlockSpec((key_rows // split, 2 * n), lambda i: (0, 0))
    return call(
        functools.partial(attend_bwd_kernel, heads, not add, last, split),
        [shaped((nq, n), BF if last else F32)] + [shaped((key_rows // split, 2 * n), BF)] * split,
        q,
        k,
        v,
        g,
        logs,
        inner,
        *add,
        name="attend_bwd",
        limit=36,
        grid=(nq // block,),
        in_specs=[q_spec, k_spec, k_spec, q_spec, l_spec, l_spec] + [n_spec] * len(add),
        out_specs=[n_spec] + [whole] * split,
        scratch_shapes=[pltpu.VMEM((key_rows, 2 * n), F32)],
    )


def normed(x):
    centred = x - jnp.mean(x, axis=-1, keepdims=True)
    inverse = lax.rsqrt(jnp.mean(centred * centred, axis=-1, keepdims=True) + EPS)
    return centred * inverse, inverse


def norm_back(g, norm, inverse):
    return inverse * (
        g
        - jnp.mean(g, axis=-1, keepdims=True)
        - norm * jnp.mean(g * norm, axis=-1, keepdims=True)
    )


def down_rows(*terms):
    return jnp.concatenate([jnp.sum(t, axis=0, keepdims=True) for t in terms], axis=0)


def norm_one_kernel(m0, m1, m2, m3, w0, w1, w2, w3, t_ref, p_ref, y_ref, low_ref, n_ref, i_ref):
    near = mm(m0[...], w0[...]) + mm(m1[...], w1[...])
    far = mm(m2[...], w2[...]) + mm(m3[...], w3[...])
    norm, inverse = normed(t_ref[...].astype(F32) + ((near + far) + p_ref[0:1, :]))
    y = norm * p_ref[1:2, :] + p_ref[2:3, :]
    y_ref[...] = y
    low_ref[...] = y.astype(BF)
    n_ref[...] = norm
    i_ref[...] = inverse


def ffn_kernel(s_ref, y_ref, up_own, up_far, b_ref, down_own, down_far, h_ref, sl_ref, p_ref):
    f = s_ref[0]
    size = up_own.shape[0]
    x = mm(lanes(y_ref, f, size), up_own[...]) + mm(lanes(y_ref, 1 - f, size), up_far[...]) + b_ref[...]
    cdf = 0.5 * (1.0 + lax.erf(x * (1.0 / math.sqrt(2.0))))
    pdf = jnp.exp(-0.5 * x * x) * (1.0 / math.sqrt(2.0 * math.pi))
    sl_ref[...] = cdf + x * pdf
    hidden = (x * cdf).astype(BF)
    h_ref[...] = hidden
    for part, ref in ((f, down_own), (1 - f, down_far)):
        here = pl.ds(pl.multiple_of(part * size, 128), size)
        p_ref[:, here] = mm(hidden, ref[...]).astype(p_ref.dtype)


def norm_two_kernel(near, far, y_ref, g_ref, p_ref, o_ref, gs_ref, gf_ref, sums):
    ffn = near[...].astype(F32) + far[...].astype(F32)
    norm, inverse = normed(y_ref[...] + (ffn + p_ref[0:1, :]))
    o_ref[...] = (norm * p_ref[1:2, :] + p_ref[2:3, :]).astype(BF)
    g = g_ref[...].astype(F32)
    grad = norm_back(g * p_ref[1:2, :], norm, inverse)
    low = grad.astype(BF)
    gs_ref[...] = grad
    gf_ref[...] = low
    sums[...] = down_rows(low.astype(F32), g * norm, g)


def ffn_back_kernel(s_ref, g_ref, down_own, down_far, sl_ref, up_own, up_far, gp_ref, p_ref, sums):
    f = s_ref[0]
    size = up_own.shape[0]
    grad = mm(lanes(g_ref, f, size), down_own[...], NT) + mm(lanes(g_ref, 1 - f, size), down_far[...], NT)
    low = (grad * sl_ref[...]).astype(BF)
    gp_ref[...] = low
    sums[...] = down_rows(low.astype(F32))
    for part, ref in ((f, up_own), (1 - f, up_far)):
        here = pl.ds(pl.multiple_of(part * size, 128), size)
        p_ref[:, here] = mm(low, ref[...], NT).astype(p_ref.dtype)


def norm_one_back_kernel(gs_ref, near, far, n_ref, i_ref, p_ref, g_ref, low_ref, sums):
    grad_y = gs_ref[...] + (near[...].astype(F32) + far[...].astype(F32))
    norm = n_ref[...]
    grad = norm_back(grad_y * p_ref[1:2, :], norm, i_ref[...])
    low = grad.astype(BF)
    g_ref[...] = grad
    low_ref[...] = low
    sums[...] = down_rows(low.astype(F32), grad_y * norm, grad_y)


def by_kind(parts):
    return [x[:, :HD] for x in parts] + [x[:, HD:] for x in parts]


def input_part_kernel(first_row, *refs):
    w_ref, o_ref, p_ref = refs[-3:]
    heads = (len(refs) - 3) // 3
    dqs, dkvs, moved = (refs[i * heads : (i + 1) * heads] for i in range(3))
    n = o_ref.shape[0]
    for part, ref in enumerate((o_ref, p_ref)):
        here = slice(first_row + part * n, first_row + (part + 1) * n)
        lows = [(a[here, :].astype(F32) + b[here, :].astype(F32)).astype(BF) for a, b in zip(dkvs, moved)]
        grads = jnp.concatenate([d[here, :] for d in dqs] + by_kind(lows), axis=1)
        ref[...] = mm(grads, w_ref[...]).astype(ref.dtype)


def near_kernel(a_ref, b_ref, o_ref):
    o_ref[...] = (a_ref[...] + b_ref[...].astype(F32)).astype(BF)


def input_grad_kernel(g_ref, a_ref, b_ref, o_ref):
    o_ref[...] = (g_ref[...] + (a_ref[...].astype(F32) + b_ref[...].astype(F32))).astype(BF)


def place_kernel(s_ref, a, b, c, d, o_ref):
    n = a.shape[0]
    group, core = s_ref[2], s_ref[3]
    for block, half, ref in ((group, core, a), (group, 1 - core, b), (1 - group, core, c), (1 - group, 1 - core, d)):
        o_ref[block, pl.ds(pl.multiple_of(half * n, n), n), :] = ref[...]


def pack_kernel(a0, a1, b0, b1, u0, u1, u2, u3, o_ref):
    o_ref[0:3, :] = a0[...] + a1[...]
    o_ref[3:6, :] = b0[...] + b1[...]
    o_ref[6:7, :] = u0[...] + u1[...] + u2[...] + u3[...]
    o_ref[7:8, :] = jnp.zeros_like(u0)


EXTRA = 16


def two_parts(x):
    high = x.astype(BF).astype(F32)
    return high + (x - high).astype(BF).astype(F32)


def put(ref, main, small):
    n = main.shape[0]
    ref[0:n, :] = main.astype(ref.dtype)
    if small is not None:
        high = small.astype(ref.dtype)
        ref[n : n + EXTRA, :] = high
        if ref.shape[0] > n + EXTRA:
            ref[n + EXTRA :, :] = (small - high.astype(F32)).astype(ref.dtype)


def get(ref, small):
    if not small:
        return ref[...].astype(F32), None
    parts = 1 if ref.dtype == F32 else 2
    n = ref.shape[0] - parts * EXTRA
    rest = ref[n : n + EXTRA, :].astype(F32)
    if parts == 2:
        rest = rest + ref[n + EXTRA :, :].astype(F32)
    return ref[0:n, :].astype(F32), rest


def up_grad_kernel(s_ref, *refs):
    ys, gs, (keep, send) = refs[:4], refs[4:8], refs[8:]
    f = s_ref[0]
    size = ys[0].shape[1] // 2
    for out, part in ((send, 1 - f), (keep, f)):
        put(out, sum(mm(lanes(y, part, size), g[...], TN) for y, g in zip(ys, gs)), None)


def down_grad_kernel(s_ref, *refs):
    hs, gs, (keep, send) = refs[:4], refs[4:8], refs[8:]
    f = s_ref[0]
    size = gs[0].shape[1] // 2
    for out, part in ((send, 1 - f), (keep, f)):
        put(out, sum(mm(h[...], lanes(g, part, size), TN) for h, g in zip(hs, gs)), None)


def qkv_grad_kernel(heads, with_out, s_ref, *refs):
    rows, more, (keep, send) = refs[:8], refs[8 + 3 * heads : -2], refs[-2:]
    dqs, owns, fars = (refs[8 + i * heads : 8 + (i + 1) * heads] for i in range(3))
    f = s_ref[0]
    size = rows[0].shape[1] // 2
    n = rows[0].shape[0]
    m = heads * HD
    own = jnp.concatenate([d[...] for d in dqs] + by_kind([x[...] for x in owns]), axis=1)
    far = jnp.concatenate(by_kind([x[...] for x in fars]), axis=1)
    far_sums = jnp.sum(far.astype(F32), axis=0, keepdims=True)
    sums = jnp.sum(own.astype(F32), axis=0, keepdims=True)
    sums = jnp.concatenate([sums[:, :m], sums[:, m:] + far_sums], axis=1)
    if sums.shape[1] < size:
        sums = jnp.concatenate([sums, jnp.zeros((1, size - sums.shape[1]), F32)], axis=1)
    small = [sums]
    if with_out:
        packed, moved = more[-2:]
        six = packed[0:6, :] + moved[0:6, :]
        ups = packed[6:7, :]
        small = [six[:, :size], ups[:, :size], six[:, size:], ups[:, size:], sums]
    small.append(jnp.zeros((EXTRA - sum(x.shape[0] for x in small), size), F32))
    small = two_parts(jnp.concatenate(small, axis=0))
    for out, part in ((send, 1 - f), (keep, f)):
        one = two = None
        for i in range(4):
            here = slice(i * n, (i + 1) * n)
            a = mm(own[here], lanes(rows[i], part, size), TN)
            b = mm(far[here], lanes(rows[4 + i], part, size), TN)
            one = a if one is None else one + a
            two = b if two is None else two + b
        grad = [one[:m], one[m:] + two]
        if with_out:
            grad.append(sum(mm(a[...], lanes(g, part, size), TN) for a, g in zip(more[:4], more[4:8])))
        put(out, jnp.concatenate(grad, axis=0), small)


def half_of(main, which):
    n = main.shape[0] // 2
    return jnp.where(which == 0, main[:n], main[n:])


def first_sum_kernel(small, s_ref, keep, moved, own, send):
    (a, c), (b, d) = get(keep, small), get(moved, small)
    total = a + b
    rest = two_parts(c + d) if small else None
    put(own, half_of(total, s_ref[1]), rest)
    put(send, half_of(total, 1 - s_ref[1]), rest)


def sum_kernel(small, a_ref, b_ref, out):
    (a, c), (b, d) = get(a_ref, small), get(b_ref, small)
    put(out, a + b, c + d if small else None)


def joined(s_ref, own, moved):
    first = s_ref[1] == 0
    return jnp.concatenate([jnp.where(first, own, moved), jnp.where(first, moved, own)], axis=0)


def owned_kernel(s_ref, own, moved, out):
    out[...] = joined(s_ref, get(own, False)[0], get(moved, False)[0])


def owned_qkv_kernel(s_ref, own1, own2, moved1, moved2, qkv, outw, sums, bias):
    (one, small1), (two, small2) = get(own1, True), get(own2, True)
    one = joined(s_ref, one, get(moved1, True)[0])
    two = joined(s_ref, two, get(moved2, True)[0])
    n = outw.shape[0]
    m1, m2 = (one.shape[0] - n) // 3, two.shape[0] // 3
    for j in range(3):
        qkv[j, 0:m1, :] = one[j * m1 : (j + 1) * m1]
        qkv[j, m1:, :] = two[j * m2 : (j + 1) * m2]
    outw[...] = one[3 * m1 :]
    sums[0:7, :] = jnp.concatenate([small1[0:7], small1[7:14]], axis=1)
    sums[7:8, :] = jnp.zeros_like(sums[7:8, :])
    for i, j in ((0, 0), (1, 2)):
        bias[i : i + 1, :] = jnp.concatenate(
            [small1[14:15, j * m1 : (j + 1) * m1], small2[0:1, j * m2 : (j + 1) * m2]], axis=1
        )


def swap(x, axis, size, mask):
    return lax.ppermute(x, axis, [(i, i ^ mask) for i in range(size)])


def pick(first, second, bit, axis):
    n = first.shape[axis]
    ring = jnp.concatenate([first, second, first], axis=axis)
    return lax.dynamic_slice_in_dim(ring, bit * n, 2 * n, axis)


class Order:
    def __init__(self):
        self.done = None

    def __call__(self, fn, *operands):
        if self.done is not None:
            operands, _ = lax.optimization_barrier((operands, self.done))
        out = fn(*operands)
        self.done = out
        return out


class Reduction:
    def __init__(self, run, name, place, keep, moved, small, over_z1, over_z2):
        self.run, self.name, self.place, self.small = run, name, place, small
        self.own, self.moved, self.stage = keep, moved, 0
        self.over = [over_z1, over_z2, over_z1]
        self.rows, self.cols = keep.shape[0] - small * EXTRA, keep.shape[1]

    def step(self):
        self.stage += 1
        low = shaped((self.rows // 2 + self.small * 2 * EXTRA, self.cols), BF)
        wide = shaped((self.rows // 2 + self.small * EXTRA, self.cols), F32)
        name = f"{self.name}_{self.stage}"
        with jax.named_scope(name):
            if self.stage == 1:
                kernel = functools.partial(first_sum_kernel, self.small)
                fn = lambda *x: scalar_call(kernel, [wide, low], *x, name=name)
                self.own, send = self.run(fn, self.place, self.own, self.moved)
            else:
                kernel = functools.partial(sum_kernel, self.small)
                fn = lambda *x: call(kernel, [low], *x, name=name)
                (self.own,) = self.run(fn, self.own, self.moved)
                send = self.own
            self.moved = self.over[self.stage - 1](send)


def body(sizes, *args):
    (
        tokens,
        cotangent,
        w_qkv,
        qv_bias,
        w_out,
        out_bias,
        gain_one,
        shift_one,
        w_up,
        up_bias,
        w_down,
        down_bias,
        gain_two,
        shift_two,
    ) = args
    n_f, n_c, n_t = sizes
    _, rows, width = tokens.shape
    wide = w_qkv.shape[2]
    heads = wide // HD
    hidden_here = w_up.shape[1]
    half = rows // 2
    f = lax.axis_index("fsdp") if n_f == 2 else 0
    z = lax.axis_index("context")
    core = lax.axis_index("tensor") % 2
    group = z // 2
    over_core = functools.partial(swap, axis="tensor", size=n_t, mask=1)
    over_y = functools.partial(swap, axis="tensor", size=n_t, mask=2)
    over_both = functools.partial(swap, axis="tensor", size=n_t, mask=3)
    over_z1 = functools.partial(swap, axis="context", size=n_c, mask=1)
    over_z2 = functools.partial(swap, axis="context", size=n_c, mask=2)
    over_x = functools.partial(swap, axis="fsdp", size=n_f, mask=1)
    run = Order()

    def whole_f(w, axis):
        return lax.all_gather(w, "fsdp", axis=axis, tiled=True)

    def halves(w, axis):
        if n_f == 2:
            return w, over_x(w)
        w = whole_f(w, axis)
        return jnp.split(w, 2, axis=axis)

    def block_of(x, which, part):
        return lax.dynamic_slice(x, (which, part * half, 0), (1, half, width))[0]

    def touch(*x):
        return run(lambda *a: a, *x)

    def after(x, *others):
        return lax.optimization_barrier((x, others))[0]

    with jax.named_scope("arrive"):
        give = run(lambda t: block_of(t, 1 - group, core), tokens)
        b_own = over_z2(give)
        a_own = run(lambda t: block_of(t, group, core), tokens)
        oa_own = over_z1(a_own)
        qkv_t = after(w_qkv.transpose(1, 2, 0).reshape(3 * wide, -1), a_own)
        qkv_moved = over_x(qkv_t) if n_f == 2 else whole_f(qkv_t, 1)
        w_out_later = after(w_out, a_own)
        out_moved = over_x(w_out_later) if n_f == 2 else whole_f(w_out_later, 1)
        cot_give, cot_a, a_far, place, par_one, par_two, bias_row, up_row = run(
            lambda g, t, qb, ub, p1, p2: (
                block_of(g, 1 - group, core),
                block_of(g, group, core),
                block_of(t, group, 1 - core),
                jnp.stack(
                    [
                        jnp.int32(f),
                        (z % 2).astype(jnp.int32),
                        group.astype(jnp.int32),
                        core.astype(jnp.int32),
                    ]
                ),
                jnp.stack(p1),
                jnp.stack(p2),
                jnp.concatenate([qb[0], jnp.zeros_like(qb[0]), qb[1]])[None],
                ub[None],
            ),
            cotangent,
            tokens,
            qv_bias,
            up_bias,
            (out_bias, gain_one, shift_one),
            (down_bias, gain_two, shift_two),
        )
        qkv_w = run(lambda a, b: pick(a, b, f, 1) if n_f == 2 else b, qkv_t, qkv_moved)
        out_w = run(lambda a, b: pick(a, b, f, 1) if n_f == 2 else b, w_out, out_moved)
        (b_own,) = touch(b_own)
        ob_own = over_z1(b_own)
        (oa_own,) = touch(oa_own)
        b_far, oa_far = over_core(b_own), over_core(oa_own)
        b_far, oa_far, out_later = touch(b_far, oa_far, out_w)
        out_near, out_far = over_core(out_later), over_y(out_later)
        up_two = halves(after(w_up, out_later), 0)
        out_near, out_far = touch(out_near, out_far)
        (ob_own,) = touch(ob_own)
        ob_far = over_core(ob_own)
    with jax.named_scope("cotangent"):
        cot_b = over_z2(after(cot_give, ob_own))
    own = [a_own, a_far, b_own, b_far]
    other = [oa_own, oa_far, ob_own, ob_far]
    total = 8 * half
    n_own = total // 2

    q, k, v = run(
        lambda *x: call(
            qkv_kernel,
            [shaped((n_own, wide), BF), shaped((total, wide), BF), shaped((total, wide), BF)],
            *x,
            name="qkv",
        ),
        *own,
        *other[:3],
        qkv_w,
        bias_row,
    )
    row_spec = pl.BlockSpec((half, wide), lambda i: (7, 0))
    k, v = run(
        lambda *x: call(
            last_kv_kernel,
            [shaped((total, wide), BF), shaped((total, wide), BF)],
            *x,
            name="last_kv",
            grid=(1,),
            in_specs=[pl.BlockSpec(a.shape, lambda i: (0, 0)) for a in x[:3]]
            + [pl.BlockSpec(memory_space=pl.ANY)] * 2,
            out_specs=[row_spec, row_spec],
            input_output_aliases={3: 0, 4: 1},
        ),
        ob_far,
        qkv_w,
        bias_row,
        k,
        v,
    )
    with jax.named_scope("down_weight"):
        down_two = halves(after(w_down, q), 1)
    with jax.named_scope("out_weight"):
        out_both = over_both(after(out_later, q))

    mixed, pieces, shared = [], [], ()
    for c in range(2):
        with jax.named_scope(f"attend{c}"):
            mo, mp, *shared = run(lambda *x: attend_fwd(c, half, *x), q, k, v, *shared)
            mixed += [mo, mp]
            if c == 0:
                (*up_two, out_both) = touch(*up_two, out_both)
            else:
                (*pieces[0], cot_b) = touch(*pieces[0], cot_b)
            mo, mp = touch(mo, mp)
            pieces.append((mo, over_core(mp), over_y(mo), over_both(mp)))
    mixed_f, logs = shared
    tok = (a_own, b_own)
    f_rows = shaped((half, width), F32)
    b_rows = shaped((half, width), BF)
    h_rows = shaped((half, hidden_here), BF)
    state = [dict(), dict()]

    def norm_one(c):
        with jax.named_scope(f"normone{c}"):
            s = state[c]
            outs = [f_rows, b_rows, f_rows, shaped((half, 1), F32)]
            s["y"], s["yo"], s["n1"], s["i1"] = run(
                lambda *x: call(norm_one_kernel, outs, *x, name="norm_one"),
                *pieces[c],
                out_w,
                out_near,
                out_far,
                out_both,
                tok[c],
                par_one,
            )
            s["yp"] = over_core(s["yo"])

    def feed(c, which, dtype):
        with jax.named_scope(f"feed{c}{which}"):
            s = state[c]
            outs = [h_rows, shaped((half, hidden_here), F32), shaped((half, width), dtype)]
            s["h" + which], s["s" + which], s["p" + which] = run(
                lambda *x: scalar_call(ffn_kernel, outs, *x, name="feed"),
                place,
                s["y" + which],
                *up_two,
                up_row,
                *down_two,
            )
            if which == "p":
                s["c2"] = over_core(s["pp"])

    def near_sum(c, name):
        with jax.named_scope(f"near{c}{name}"):
            s = state[c]
            (s["near" + name],) = run(
                lambda *x: call(near_kernel, [b_rows], *x, name="near"), s["po"], s["c" + name]
            )
            s["far" + name] = over_y(s["near" + name])

    def norm_two(c):
        with jax.named_scope(f"normtwo{c}"):
            s = state[c]
            outs = [b_rows, f_rows, b_rows, shaped((3, width), F32)]
            s["out"], s["gs"], s["gfo"], s["sum2"] = run(
                lambda *x: call(norm_two_kernel, outs, *x, name="norm_two"),
                s["near2"],
                s["far2"],
                s["y"],
                cot[c],
                par_two,
            )
            s["gfp"] = over_core(s["gfo"])

    def feed_back(c, which, dtype):
        with jax.named_scope(f"feedback{c}{which}"):
            s = state[c]
            outs = [h_rows, shaped((half, width), dtype), shaped((1, hidden_here), F32)]
            s["gp" + which], s["p" + which], s["sumu" + which] = run(
                lambda *x: scalar_call(ffn_back_kernel, outs, *x, name="feed_back"),
                place,
                s["gf" + which],
                *down_two,
                s["s" + which],
                *up_two,
            )
            if which == "p":
                s["c5"] = over_core(s["pp"])

    def norm_one_back(c):
        with jax.named_scope(f"normoneback{c}"):
            s = state[c]
            s["gfirst"], s["gao"], s["sum1"] = run(
                lambda *x: call(
                    norm_one_back_kernel,
                    [f_rows, b_rows, shaped((3, width), F32)],
                    *x,
                    name="norm_one_back",
                ),
                s["gs"],
                s["near5"],
                s["far5"],
                s["n1"],
                s["i1"],
                par_one,
            )
            s["gap"] = over_core(s["gao"])

    def weight_grad(kernel, operands, rows, cols, name, small=False):
        with jax.named_scope(name):
            outs = [
                shaped((rows + small * EXTRA, cols), F32),
                shaped((rows + small * 2 * EXTRA, cols), BF),
            ]
            keep, send = run(lambda *x: scalar_call(kernel, outs, *x, name=name), place, *operands)
            return Reduction(run, name, place, keep, over_x(send), small, over_z1, over_z2)

    def owned(red, name):
        with jax.named_scope(name):
            return run(
                lambda *x: scalar_call(owned_kernel, [shaped((red.rows, red.cols), F32)], *x, name=name),
                place,
                red.own,
                red.moved,
            )[0]

    four = [(c, w) for c in range(2) for w in "op"]

    def pieces_of(name):
        return [state[c][name + w] for c, w in four]

    cot = (cot_a, cot_b)
    norm_one(0)
    feed(0, "o", F32)
    norm_one(1)
    feed(0, "p", BF)
    feed(1, "p", BF)
    near_sum(0, "2")
    feed(1, "o", F32)
    near_sum(1, "2")
    norm_two(0)
    feed_back(0, "o", F32)
    feed_back(0, "p", BF)
    norm_two(1)
    with jax.named_scope("outback"):
        out_back = over_z2(state[1]["out"])
    near_sum(0, "5")
    feed_back(1, "o", F32)
    feed_back(1, "p", BF)
    if n_f == 2:
        red_down = weight_grad(
            down_grad_kernel, pieces_of("h") + pieces_of("gf"), hidden_here, width // 2, "down_grad"
        )
    near_sum(1, "5")
    norm_one_back(0)
    if n_f == 2:
        red_up = weight_grad(
            up_grad_kernel, pieces_of("y") + pieces_of("gp"), width // 2, hidden_here, "up_grad"
        )
    norm_one_back(1)
    (out_back,) = touch(out_back)
    with jax.named_scope("smallpack"):
        (packed,) = run(
            lambda *x: call(pack_kernel, [shaped((8, width), F32)], *x, name="pack"),
            *[state[c][s] for s in ("sum1", "sum2") for c in range(2)],
            *pieces_of("sumu"),
        )
        packed_moved = over_core(packed)
    def placed(blocks):
        return run(
            lambda *x: scalar_call(place_kernel, [shaped(tokens.shape, BF)], *x, name="place"),
            place,
            *blocks,
        )[0]

    def both_halves(a, b):
        return a, over_core(a), b, over_core(b)

    if n_f == 2:
        red_down.step()
    with jax.named_scope("placeout"):
        out_blocks = both_halves(after(state[0]["out"], out_back), out_back)
    grad_attn = pieces_of("ga")
    grad_mixed, inner = run(
        lambda *x: call(
            grad_mixed_kernel, [shaped((n_own, wide), BF), shaped((heads, n_own), F32)], *x, name="grad_mixed"
        ),
        *grad_attn,
        out_w,
        mixed_f,
    )
    (*out_blocks, packed_moved) = touch(*out_blocks, packed_moved)

    early, late = tuple(range(heads - 1)), (heads - 1,)
    bwd_args = (q, k, v, grad_mixed, logs, inner)
    n_one, n_two = 3 * len(early) * HD, 3 * HD
    dqs, owns, fars, moved = [], [], [], []
    for h in early:
        with jax.named_scope(f"back{h}"):
            dq, mine, far = run(lambda *x: attend_bwd((h,), 0, total, 2, *x), *bwd_args)
            dqs.append(dq)
            owns.append(mine)
            fars.append(far)
            moved.append(over_z1(far))
        if n_f == 2 and h == 0:
            red_down.step()
    with jax.named_scope("backfar"):
        dq, far = run(lambda *x: attend_bwd(late, 1, n_own, 1, *x, last=False), *bwd_args)
        fars.append(far)
        moved.append(over_z1(far))
    with jax.named_scope("backown"):
        dq, mine = run(lambda *x: attend_bwd(late, 0, n_own, 1, *x), *bwd_args, dq)
        dqs.append(dq)
        owns.append(mine)
    if n_f == 2:
        red_up.step()
    (moved[0],) = touch(moved[0])
    if n_f == 2:
        red_one = weight_grad(
            functools.partial(qkv_grad_kernel, len(early), True),
            own + other + dqs[:-1] + owns[:-1] + fars[:-1] + mixed + grad_attn + [packed, packed_moved],
            n_one + wide,
            width // 2,
            "one_grad",
            True,
        )
    moved[1:-1] = touch(*moved[1:-1])
    if n_f == 2:
        red_two = weight_grad(
            functools.partial(qkv_grad_kernel, 1, False),
            own + other + dqs[-1:] + owns[-1:] + fars[-1:],
            n_two,
            width // 2,
            "two_grad",
            True,
        )

    item = [dict(), dict()]

    def input_part(c):
        with jax.named_scope(f"inputpart{c}"):
            s = item[c]
            s["po"], pp = run(
                lambda *x: call(
                    functools.partial(input_part_kernel, c * rows), [f_rows, b_rows], *x, name="input_part"
                ),
                *dqs,
                *owns,
                *moved,
                qkv_w,
            )
            s["cp"] = over_core(pp)

    def input_near(c):
        with jax.named_scope(f"inputnear{c}"):
            s = item[c]
            (s["near"],) = run(
                lambda *x: call(near_kernel, [b_rows], *x, name="near"), s["po"], s["cp"]
            )
            s["far"] = over_y(s["near"])

    def input_last(c):
        with jax.named_scope(f"inputlast{c}"):
            s = item[c]
            (s["in"],) = run(
                lambda *x: call(input_grad_kernel, [b_rows], *x, name="input_grad"),
                state[c]["gfirst"],
                s["near"],
                s["far"],
            )

    input_part(1)
    with jax.named_scope("placeout"):
        output = placed(out_blocks)
    input_near(1)
    if n_f == 2:
        red_down.step()
        red_up.step()
        red_one.step()
    input_last(1)
    with jax.named_scope("inputback"):
        in_back = over_z2(item[1]["in"])
    if n_f == 2:
        red_two.step()
        (red_down.moved,) = touch(red_down.moved)
    input_part(0)
    if n_f == 2:
        owned_down = owned(red_down, "owned_down")
    input_near(0)
    if n_f == 2:
        red_one.step()
        red_up.step()
        red_two.step()
    input_last(0)
    with jax.named_scope("placein"):
        in_far = over_core(item[0]["in"])
    if n_f == 2:
        owned_up = owned(red_up, "owned_up")
        red_one.step()
        red_two.step()
    (in_back,) = touch(in_back)
    with jax.named_scope("placein"):
        in_blocks = [item[0]["in"], in_far, in_back, over_core(in_back)]
    with jax.named_scope("finish"):
        if n_f == 2:
            qkv_grad, owned_out, small, bias_grad = run(
                lambda *x: scalar_call(
                    owned_qkv_kernel,
                    [
                        shaped((3, wide, width // 2), F32),
                        shaped((wide, width // 2), F32),
                        shaped((8, width), F32),
                        shaped((2, wide), F32),
                    ],
                    *x,
                    name="owned_qkv",
                ),
                place,
                red_one.own,
                red_two.own,
                red_one.moved,
                red_two.moved,
            )
            owned_qkv = qkv_grad.transpose(2, 0, 1)
        else:

            def reduce_plain(left, right, axis):
                grad = mm(jnp.concatenate(left), jnp.concatenate(right), TN)
                keep = lax.psum_scatter(grad, "fsdp", scatter_dimension=axis, tiled=True)
                return lax.psum(keep, "context").astype(BF).astype(F32)

            zero = jnp.zeros((n_own, wide), BF)
            left = jnp.concatenate(dqs + by_kind(owns), axis=1)
            right = jnp.concatenate([zero] + by_kind(fars), axis=1)
            owned_up = reduce_plain(pieces_of("y"), pieces_of("gp"), 0)
            owned_down = reduce_plain(pieces_of("h"), pieces_of("gf"), 1)
            owned_out = reduce_plain(mixed, grad_attn, 1)
            owned_qkv = reduce_plain(own + other, [left, right], 0).reshape(w_qkv.shape)
            column_sums = jnp.sum((left.astype(F32) + right.astype(F32)), axis=0)
            bias_grad = jnp.stack([column_sums[:wide], column_sums[2 * wide :]])
            small = jnp.concatenate([packed[:6] + packed_moved[:6], packed[6:]])
            small, bias_grad = lax.psum((small, bias_grad), ("fsdp", "context"))
    with jax.named_scope("placein"):
        input_grad = placed(in_blocks)
    return (
        output,
        input_grad,
        owned_qkv,
        bias_grad,
        owned_out,
        small[0],
        small[1],
        small[2],
        owned_up,
        small[6],
        owned_down,
        small[3],
        small[4],
        small[5],
    )


def solution(mesh):
    sizes = tuple(mesh.shape[name] for name in ("fsdp", "context", "tensor"))
    specs = (
        P("fsdp", None, "tensor"),
        P(None, "tensor"),
        P("tensor", "fsdp"),
        P(),
        P(),
        P(),
        P("fsdp", "tensor"),
        P("tensor"),
        P("tensor", "fsdp"),
        P(),
        P(),
        P(),
    )
    rows = P("fsdp", "context", None)
    return jax.shard_map(
        functools.partial(body, sizes),
        mesh=mesh,
        in_specs=(rows, rows) + specs,
        out_specs=(rows, rows) + specs,
        check_vma=False,
    )
```

```python
import functools
import math

import jax
import jax.numpy as jnp
from jax import lax
from jax.experimental import pallas as pl
from jax.experimental.pallas import tpu as pltpu
from jax.sharding import PartitionSpec as P

HD = 64
SCALE = 1.0 / math.sqrt(HD)
SCALE_LOG2 = SCALE * math.log2(math.e)
EPS = 1e-06
BF = jnp.bfloat16
F32 = jnp.float32
NT = (((1,), (1,)), ((), ()))
TN = (((0,), (0,)), ((), ()))
NN = (((1,), (0,)), ((), ()))


def mm(a, b, dims=NN):
    return lax.dot_general(a, b, dims, preferred_element_type=F32)


def shaped(shape, dtype):
    return jax.ShapeDtypeStruct(shape, dtype)


def call(kernel, outs, *operands, name, limit=16, **extra):
    return pl.pallas_call(
        kernel,
        out_shape=list(outs),
        cost_estimate=pl.CostEstimate(flops=int(5e9), bytes_accessed=1, transcendentals=0),
        compiler_params=pltpu.CompilerParams(vmem_limit_bytes=limit << 20),
        name=name,
        **extra,
    )(*operands)


SMEM = pl.BlockSpec(memory_space=pltpu.SMEM)
VMEM = pl.BlockSpec(memory_space=pltpu.VMEM)


def scalar_call(kernel, outs, scalars, *operands, **kw):
    specs = [SMEM] + [VMEM] * len(operands)
    return call(kernel, outs, scalars, *operands, in_specs=specs, **kw)


def lanes(ref, index, size):
    return ref[:, pl.ds(pl.multiple_of(index * size, 128), size)]


def qkv_kernel(*refs):
    rows, (w_ref, b_ref, q_ref, k_ref, v_ref) = refs[:7], refs[7:]
    n = rows[0].shape[0]
    wide = q_ref.shape[1]
    for i, ref in enumerate(rows):
        here = slice(i * n, (i + 1) * n)
        skip = 0 if i < 4 else wide
        full = (mm(ref[...], w_ref[skip:, :], NT) + b_ref[:, skip:]).astype(BF)
        if i < 4:
            q_ref[here, :] = full[:, :wide]
        k_ref[here, :] = full[:, wide - skip : 2 * wide - skip]
        v_ref[here, :] = full[:, 2 * wide - skip :]


def last_kv_kernel(x_ref, w_ref, b_ref, *refs):
    k_ref, v_ref = refs[-2:]
    wide = k_ref.shape[1]
    full = (mm(x_ref[...], w_ref[wide:, :], NT) + b_ref[:, wide:]).astype(BF)
    k_ref[...] = full[:, :wide]
    v_ref[...] = full[:, wide:]


def attend_fwd_kernel(chunk, *refs):
    q_ref, k_ref, v_ref = refs[:3]
    o_ref, p_ref, f_ref, l_ref = refs[-4:]
    outs, logs = [], []
    for h in range(q_ref.shape[1] // HD):
        cols = slice(h * HD, (h + 1) * HD)
        scores = mm(q_ref[:, cols], k_ref[:, cols], NT)
        top = jnp.max(scores, axis=1, keepdims=True)
        expo = jnp.exp2((scores - top) * SCALE_LOG2)
        total = jnp.sum(expo, axis=1, keepdims=True)
        outs.append(mm(expo.astype(BF), v_ref[:, cols]) / total)
        logs.append(top * SCALE_LOG2 + jnp.log2(total))
    mixed = jnp.concatenate(outs, axis=1)
    f_ref[...] = mixed
    l_ref[...] = jnp.concatenate(logs, axis=1).T
    for step, ref in enumerate((o_ref, p_ref)):

        @pl.when(pl.program_id(0) == step)
        def _():
            ref[...] = mixed.astype(BF)


def attend_fwd(chunk, block, q, k, v, *before):
    nq, w = q.shape
    nk = k.shape[0]
    heads = w // HD
    q_spec = pl.BlockSpec((block, w), lambda i: (chunk * 2 + i, 0))
    l_spec = pl.BlockSpec((heads, block), lambda i: (0, chunk * 2 + i))
    o_spec = pl.BlockSpec((block, w), lambda i: (0, 0))
    k_spec = pl.BlockSpec((nk, w), lambda i: (0, 0))
    anywhere = pl.BlockSpec(memory_space=pl.ANY)
    return call(
        functools.partial(attend_fwd_kernel, chunk),
        [shaped((block, w), BF)] * 2 + [shaped((nq, w), F32), shaped((heads, nq), F32)],
        q,
        k,
        v,
        *before,
        name="attend_fwd",
        limit=24,
        grid=(2,),
        in_specs=[q_spec, k_spec, k_spec] + [anywhere] * len(before),
        out_specs=[o_spec, o_spec, q_spec, l_spec],
        input_output_aliases={3: 2, 4: 3} if before else {},
    )


def grad_mixed_kernel(*refs):
    gas, (w_ref, f_ref, g_ref, d_ref) = refs[:4], refs[4:]
    n = gas[0].shape[0]
    heads = w_ref.shape[0] // HD
    for i, ga in enumerate(gas):
        here = slice(i * n, (i + 1) * n)
        g = mm(ga[...], w_ref[...], NT).astype(BF)
        g_ref[here, :] = g
        prod = (g.astype(F32) * f_ref[here, :]).T
        d_ref[:, here] = jnp.concatenate(
            [jnp.sum(prod[h * HD : (h + 1) * HD], axis=0, keepdims=True) for h in range(heads)]
        )


def attend_bwd_kernel(heads, first, last, split, *refs):
    q_ref, k_ref, v_ref, g_ref, l_ref, d_ref = refs[:6]
    add_ref = refs[6] if not first else None
    dq_ref, outs, acc = refs[6 + (not first)], refs[7 + (not first) : -1], refs[-1]
    dqs, dks, dvs = [], [], []
    for h in heads:
        cols = slice(h * HD, (h + 1) * HD)
        q, k, v, g = q_ref[:, cols], k_ref[:, cols], v_ref[:, cols], g_ref[:, cols]
        probs = jnp.exp2(mm(k, q, NT) * SCALE_LOG2 - l_ref[h : h + 1, :])
        grad_scores = (probs * (mm(v, g, NT) - d_ref[h : h + 1, :])).astype(BF)
        dvs.append(mm(probs.astype(BF), g))
        dks.append(mm(grad_scores, q) * SCALE)
        dqs.append(mm(k, grad_scores, TN))
    dq = (dqs[0] if len(dqs) == 1 else jnp.concatenate(dqs, axis=0)).T
    if not first:
        dq = dq + add_ref[...]
    dq_ref[...] = (dq * SCALE).astype(BF) if last else dq
    dkv = jnp.concatenate(dks + dvs, axis=1)
    step = pl.program_id(0)

    @pl.when(step == 0)
    def _():
        acc[...] = dkv

    @pl.when(step > 0)
    def _():
        acc[...] += dkv

    @pl.when(step == pl.num_programs(0) - 1)
    def _():
        n = acc.shape[0] // len(outs)
        for i, ref in enumerate(outs):
            ref[...] = acc[i * n : (i + 1) * n].astype(BF)


def attend_bwd(heads, key_block, key_rows, split, q, k, v, g, logs, inner, *add, last=True, block=256):
    nq, w = q.shape
    n = len(heads) * HD
    q_spec = pl.BlockSpec((block, w), lambda i: (i, 0))
    k_spec = pl.BlockSpec((key_rows, w), lambda i: (key_block, 0))
    n_spec = pl.BlockSpec((block, n), lambda i: (i, 0))
    l_spec = pl.BlockSpec((logs.shape[0], block), lambda i: (0, i))
    whole = pl.BlockSpec((key_rows // split, 2 * n), lambda i: (0, 0))
    return call(
        functools.partial(attend_bwd_kernel, heads, not add, last, split),
        [shaped((nq, n), BF if last else F32)] + [shaped((key_rows // split, 2 * n), BF)] * split,
        q,
        k,
        v,
        g,
        logs,
        inner,
        *add,
        name="attend_bwd",
        limit=36,
        grid=(nq // block,),
        in_specs=[q_spec, k_spec, k_spec, q_spec, l_spec, l_spec] + [n_spec] * len(add),
        out_specs=[n_spec] + [whole] * split,
        scratch_shapes=[pltpu.VMEM((key_rows, 2 * n), F32)],
    )


def normed(x):
    centred = x - jnp.mean(x, axis=-1, keepdims=True)
    inverse = lax.rsqrt(jnp.mean(centred * centred, axis=-1, keepdims=True) + EPS)
    return centred * inverse, inverse


def norm_back(g, norm, inverse):
    return inverse * (
        g
        - jnp.mean(g, axis=-1, keepdims=True)
        - norm * jnp.mean(g * norm, axis=-1, keepdims=True)
    )


def down_rows(*terms):
    return jnp.concatenate([jnp.sum(t, axis=0, keepdims=True) for t in terms], axis=0)


def norm_one_kernel(m0, m1, m2, m3, w0, w1, w2, w3, t_ref, p_ref, y_ref, low_ref, n_ref, i_ref):
    near = mm(m0[...], w0[...]) + mm(m1[...], w1[...])
    far = mm(m2[...], w2[...]) + mm(m3[...], w3[...])
    norm, inverse = normed(t_ref[...].astype(F32) + ((near + far) + p_ref[0:1, :]))
    y = norm * p_ref[1:2, :] + p_ref[2:3, :]
    y_ref[...] = y
    low_ref[...] = y.astype(BF)
    n_ref[...] = norm
    i_ref[...] = inverse


def ffn_kernel(s_ref, y_ref, up_own, up_far, b_ref, down_own, down_far, h_ref, sl_ref, p_ref):
    f = s_ref[0]
    size = up_own.shape[0]
    x = mm(lanes(y_ref, f, size), up_own[...]) + mm(lanes(y_ref, 1 - f, size), up_far[...]) + b_ref[...]
    cdf = 0.5 * (1.0 + lax.erf(x * (1.0 / math.sqrt(2.0))))
    pdf = jnp.exp(-0.5 * x * x) * (1.0 / math.sqrt(2.0 * math.pi))
    sl_ref[...] = cdf + x * pdf
    hidden = (x * cdf).astype(BF)
    h_ref[...] = hidden
    for part, ref in ((f, down_own), (1 - f, down_far)):
        here = pl.ds(pl.multiple_of(part * size, 128), size)
        p_ref[:, here] = mm(hidden, ref[...]).astype(p_ref.dtype)


def norm_two_kernel(near, far, y_ref, g_ref, p_ref, o_ref, gs_ref, gf_ref, sums):
    ffn = near[...].astype(F32) + far[...].astype(F32)
    norm, inverse = normed(y_ref[...] + (ffn + p_ref[0:1, :]))
    o_ref[...] = (norm * p_ref[1:2, :] + p_ref[2:3, :]).astype(BF)
    g = g_ref[...].astype(F32)
    grad = norm_back(g * p_ref[1:2, :], norm, inverse)
    low = grad.astype(BF)
    gs_ref[...] = grad
    gf_ref[...] = low
    sums[...] = down_rows(low.astype(F32), g * norm, g)


def ffn_back_kernel(s_ref, g_ref, down_own, down_far, sl_ref, up_own, up_far, gp_ref, p_ref, sums):
    f = s_ref[0]
    size = up_own.shape[0]
    grad = mm(lanes(g_ref, f, size), down_own[...], NT) + mm(lanes(g_ref, 1 - f, size), down_far[...], NT)
    low = (grad * sl_ref[...]).astype(BF)
    gp_ref[...] = low
    sums[...] = down_rows(low.astype(F32))
    for part, ref in ((f, up_own), (1 - f, up_far)):
        here = pl.ds(pl.multiple_of(part * size, 128), size)
        p_ref[:, here] = mm(low, ref[...], NT).astype(p_ref.dtype)


def norm_one_back_kernel(gs_ref, near, far, n_ref, i_ref, p_ref, g_ref, low_ref, sums):
    grad_y = gs_ref[...] + (near[...].astype(F32) + far[...].astype(F32))
    norm = n_ref[...]
    grad = norm_back(grad_y * p_ref[1:2, :], norm, i_ref[...])
    low = grad.astype(BF)
    g_ref[...] = grad
    low_ref[...] = low
    sums[...] = down_rows(low.astype(F32), grad_y * norm, grad_y)


def by_kind(parts):
    return [x[:, :HD] for x in parts] + [x[:, HD:] for x in parts]


def input_part_kernel(first_row, *refs):
    w_ref, o_ref, p_ref = refs[-3:]
    heads = (len(refs) - 3) // 3
    dqs, dkvs, moved = (refs[i * heads : (i + 1) * heads] for i in range(3))
    n = o_ref.shape[0]
    for part, ref in enumerate((o_ref, p_ref)):
        here = slice(first_row + part * n, first_row + (part + 1) * n)
        lows = [(a[here, :].astype(F32) + b[here, :].astype(F32)).astype(BF) for a, b in zip(dkvs, moved)]
        grads = jnp.concatenate([d[here, :] for d in dqs] + by_kind(lows), axis=1)
        ref[...] = mm(grads, w_ref[...]).astype(ref.dtype)


def near_kernel(a_ref, b_ref, o_ref):
    o_ref[...] = (a_ref[...] + b_ref[...].astype(F32)).astype(BF)


def input_grad_kernel(g_ref, a_ref, b_ref, o_ref):
    o_ref[...] = (g_ref[...] + (a_ref[...].astype(F32) + b_ref[...].astype(F32))).astype(BF)


def place_kernel(s_ref, a, b, c, d, o_ref):
    n = a.shape[0]
    group, core = s_ref[2], s_ref[3]
    for block, half, ref in ((group, core, a), (group, 1 - core, b), (1 - group, core, c), (1 - group, 1 - core, d)):
        o_ref[block, pl.ds(pl.multiple_of(half * n, n), n), :] = ref[...]


def pack_kernel(a0, a1, b0, b1, u0, u1, u2, u3, o_ref):
    o_ref[0:3, :] = a0[...] + a1[...]
    o_ref[3:6, :] = b0[...] + b1[...]
    o_ref[6:7, :] = u0[...] + u1[...] + u2[...] + u3[...]
    o_ref[7:8, :] = jnp.zeros_like(u0)


EXTRA = 16


def two_parts(x):
    high = x.astype(BF).astype(F32)
    return high + (x - high).astype(BF).astype(F32)


def put(ref, main, small):
    n = main.shape[0]
    ref[0:n, :] = main.astype(ref.dtype)
    if small is not None:
        high = small.astype(ref.dtype)
        ref[n : n + EXTRA, :] = high
        if ref.shape[0] > n + EXTRA:
            ref[n + EXTRA :, :] = (small - high.astype(F32)).astype(ref.dtype)


def get(ref, small):
    if not small:
        return ref[...].astype(F32), None
    parts = 1 if ref.dtype == F32 else 2
    n = ref.shape[0] - parts * EXTRA
    rest = ref[n : n + EXTRA, :].astype(F32)
    if parts == 2:
        rest = rest + ref[n + EXTRA :, :].astype(F32)
    return ref[0:n, :].astype(F32), rest


def up_grad_kernel(s_ref, *refs):
    ys, gs, (keep, send) = refs[:4], refs[4:8], refs[8:]
    f = s_ref[0]
    size = ys[0].shape[1] // 2
    for out, part in ((send, 1 - f), (keep, f)):
        put(out, sum(mm(lanes(y, part, size), g[...], TN) for y, g in zip(ys, gs)), None)


def down_grad_kernel(s_ref, *refs):
    hs, gs, (keep, send) = refs[:4], refs[4:8], refs[8:]
    f = s_ref[0]
    size = gs[0].shape[1] // 2
    for out, part in ((send, 1 - f), (keep, f)):
        put(out, sum(mm(h[...], lanes(g, part, size), TN) for h, g in zip(hs, gs)), None)


def qkv_grad_kernel(heads, with_out, s_ref, *refs):
    rows, more, (keep, send) = refs[:8], refs[8 + 3 * heads : -2], refs[-2:]
    dqs, owns, fars = (refs[8 + i * heads : 8 + (i + 1) * heads] for i in range(3))
    f = s_ref[0]
    size = rows[0].shape[1] // 2
    n = rows[0].shape[0]
    m = heads * HD
    own = jnp.concatenate([d[...] for d in dqs] + by_kind([x[...] for x in owns]), axis=1)
    far = jnp.concatenate(by_kind([x[...] for x in fars]), axis=1)
    far_sums = jnp.sum(far.astype(F32), axis=0, keepdims=True)
    sums = jnp.sum(own.astype(F32), axis=0, keepdims=True)
    sums = jnp.concatenate([sums[:, :m], sums[:, m:] + far_sums], axis=1)
    if sums.shape[1] < size:
        sums = jnp.concatenate([sums, jnp.zeros((1, size - sums.shape[1]), F32)], axis=1)
    small = [sums]
    if with_out:
        packed, moved = more[-2:]
        six = packed[0:6, :] + moved[0:6, :]
        ups = packed[6:7, :]
        small = [six[:, :size], ups[:, :size], six[:, size:], ups[:, size:], sums]
    small.append(jnp.zeros((EXTRA - sum(x.shape[0] for x in small), size), F32))
    small = two_parts(jnp.concatenate(small, axis=0))
    for out, part in ((send, 1 - f), (keep, f)):
        one = two = None
        for i in range(4):
            here = slice(i * n, (i + 1) * n)
            a = mm(own[here], lanes(rows[i], part, size), TN)
            b = mm(far[here], lanes(rows[4 + i], part, size), TN)
            one = a if one is None else one + a
            two = b if two is None else two + b
        grad = [one[:m], one[m:] + two]
        if with_out:
            grad.append(sum(mm(a[...], lanes(g, part, size), TN) for a, g in zip(more[:4], more[4:8])))
        put(out, jnp.concatenate(grad, axis=0), small)


def half_of(main, which):
    n = main.shape[0] // 2
    return jnp.where(which == 0, main[:n], main[n:])


def first_sum_kernel(small, s_ref, keep, moved, own, send):
    (a, c), (b, d) = get(keep, small), get(moved, small)
    total = a + b
    rest = two_parts(c + d) if small else None
    put(own, half_of(total, s_ref[1]), rest)
    put(send, half_of(total, 1 - s_ref[1]), rest)


def sum_kernel(small, a_ref, b_ref, out):
    (a, c), (b, d) = get(a_ref, small), get(b_ref, small)
    put(out, a + b, c + d if small else None)


def joined(s_ref, own, moved):
    first = s_ref[1] == 0
    return jnp.concatenate([jnp.where(first, own, moved), jnp.where(first, moved, own)], axis=0)


def owned_kernel(s_ref, own, moved, out):
    out[...] = joined(s_ref, get(own, False)[0], get(moved, False)[0])


def owned_qkv_kernel(s_ref, own1, own2, moved1, moved2, qkv, outw, sums, bias):
    (one, small1), (two, small2) = get(own1, True), get(own2, True)
    one = joined(s_ref, one, get(moved1, True)[0])
    two = joined(s_ref, two, get(moved2, True)[0])
    n = outw.shape[0]
    m1, m2 = (one.shape[0] - n) // 3, two.shape[0] // 3
    for j in range(3):
        qkv[j, 0:m1, :] = one[j * m1 : (j + 1) * m1]
        qkv[j, m1:, :] = two[j * m2 : (j + 1) * m2]
    outw[...] = one[3 * m1 :]
    sums[0:7, :] = jnp.concatenate([small1[0:7], small1[7:14]], axis=1)
    sums[7:8, :] = jnp.zeros_like(sums[7:8, :])
    for i, j in ((0, 0), (1, 2)):
        bias[i : i + 1, :] = jnp.concatenate(
            [small1[14:15, j * m1 : (j + 1) * m1], small2[0:1, j * m2 : (j + 1) * m2]], axis=1
        )


def swap(x, axis, size, mask):
    return lax.ppermute(x, axis, [(i, i ^ mask) for i in range(size)])


def pick(first, second, bit, axis):
    n = first.shape[axis]
    ring = jnp.concatenate([first, second, first], axis=axis)
    return lax.dynamic_slice_in_dim(ring, bit * n, 2 * n, axis)


class Order:
    def __init__(self):
        self.done = None

    def __call__(self, fn, *operands):
        if self.done is not None:
            operands, _ = lax.optimization_barrier((operands, self.done))
        out = fn(*operands)
        self.done = out
        return out


class Reduction:
    def __init__(self, run, name, place, keep, moved, small, over_z1, over_z2):
        self.run, self.name, self.place, self.small = run, name, place, small
        self.own, self.moved, self.stage = keep, moved, 0
        self.over = [over_z1, over_z2, over_z1]
        self.rows, self.cols = keep.shape[0] - small * EXTRA, keep.shape[1]

    def step(self):
        self.stage += 1
        low = shaped((self.rows // 2 + self.small * 2 * EXTRA, self.cols), BF)
        wide = shaped((self.rows // 2 + self.small * EXTRA, self.cols), F32)
        name = f"{self.name}_{self.stage}"
        with jax.named_scope(name):
            if self.stage == 1:
                kernel = functools.partial(first_sum_kernel, self.small)
                fn = lambda *x: scalar_call(kernel, [wide, low], *x, name=name)
                self.own, send = self.run(fn, self.place, self.own, self.moved)
            else:
                kernel = functools.partial(sum_kernel, self.small)
                fn = lambda *x: call(kernel, [low], *x, name=name)
                (self.own,) = self.run(fn, self.own, self.moved)
                send = self.own
            self.moved = self.over[self.stage - 1](send)


def body(sizes, *args):
    (
        tokens,
        cotangent,
        w_qkv,
        qv_bias,
        w_out,
        out_bias,
        gain_one,
        shift_one,
        w_up,
        up_bias,
        w_down,
        down_bias,
        gain_two,
        shift_two,
    ) = args
    n_f, n_c, n_t = sizes
    _, rows, width = tokens.shape
    wide = w_qkv.shape[2]
    heads = wide // HD
    hidden_here = w_up.shape[1]
    half = rows // 2
    f = lax.axis_index("fsdp") if n_f == 2 else 0
    z = lax.axis_index("context")
    core = lax.axis_index("tensor") % 2
    group = z // 2
    over_core = functools.partial(swap, axis="tensor", size=n_t, mask=1)
    over_y = functools.partial(swap, axis="tensor", size=n_t, mask=2)
    over_both = functools.partial(swap, axis="tensor", size=n_t, mask=3)
    over_z1 = functools.partial(swap, axis="context", size=n_c, mask=1)
    over_z2 = functools.partial(swap, axis="context", size=n_c, mask=2)
    over_x = functools.partial(swap, axis="fsdp", size=n_f, mask=1)
    run = Order()

    def whole_f(w, axis):
        return lax.all_gather(w, "fsdp", axis=axis, tiled=True)

    def halves(w, axis):
        if n_f == 2:
            return w, over_x(w)
        w = whole_f(w, axis)
        return jnp.split(w, 2, axis=axis)

    def block_of(x, which, part):
        return lax.dynamic_slice(x, (which, part * half, 0), (1, half, width))[0]

    def touch(*x):
        return run(lambda *a: a, *x)

    def after(x, *others):
        return lax.optimization_barrier((x, others))[0]

    with jax.named_scope("arrive"):
        give = run(lambda t: block_of(t, 1 - group, core), tokens)
        b_own = over_z2(give)
        a_own = run(lambda t: block_of(t, group, core), tokens)
        oa_own = over_z1(a_own)
        qkv_t = after(w_qkv.transpose(1, 2, 0).reshape(3 * wide, -1), a_own)
        qkv_moved = over_x(qkv_t) if n_f == 2 else whole_f(qkv_t, 1)
        w_out_later = after(w_out, a_own)
        out_moved = over_x(w_out_later) if n_f == 2 else whole_f(w_out_later, 1)
        cot_give, cot_a, a_far, place, par_one, par_two, bias_row, up_row = run(
            lambda g, t, qb, ub, p1, p2: (
                block_of(g, 1 - group, core),
                block_of(g, group, core),
                block_of(t, group, 1 - core),
                jnp.stack(
                    [
                        jnp.int32(f),
                        (z % 2).astype(jnp.int32),
                        group.astype(jnp.int32),
                        core.astype(jnp.int32),
                    ]
                ),
                jnp.stack(p1),
                jnp.stack(p2),
                jnp.concatenate([qb[0], jnp.zeros_like(qb[0]), qb[1]])[None],
                ub[None],
            ),
            cotangent,
            tokens,
            qv_bias,
            up_bias,
            (out_bias, gain_one, shift_one),
            (down_bias, gain_two, shift_two),
        )
        qkv_w = run(lambda a, b: pick(a, b, f, 1) if n_f == 2 else b, qkv_t, qkv_moved)
        out_w = run(lambda a, b: pick(a, b, f, 1) if n_f == 2 else b, w_out, out_moved)
        (b_own,) = touch(b_own)
        ob_own = over_z1(b_own)
        (oa_own,) = touch(oa_own)
        b_far, oa_far = over_core(b_own), over_core(oa_own)
        b_far, oa_far, out_later = touch(b_far, oa_far, out_w)
        out_near, out_far = over_core(out_later), over_y(out_later)
        up_two = halves(after(w_up, out_later), 0)
        out_near, out_far = touch(out_near, out_far)
        (ob_own,) = touch(ob_own)
        ob_far = over_core(ob_own)
    with jax.named_scope("cotangent"):
        cot_b = over_z2(after(cot_give, ob_own))
    own = [a_own, a_far, b_own, b_far]
    other = [oa_own, oa_far, ob_own, ob_far]
    total = 8 * half
    n_own = total // 2

    q, k, v = run(
        lambda *x: call(
            qkv_kernel,
            [shaped((n_own, wide), BF), shaped((total, wide), BF), shaped((total, wide), BF)],
            *x,
            name="qkv",
        ),
        *own,
        *other[:3],
        qkv_w,
        bias_row,
    )
    row_spec = pl.BlockSpec((half, wide), lambda i: (7, 0))
    k, v = run(
        lambda *x: call(
            last_kv_kernel,
            [shaped((total, wide), BF), shaped((total, wide), BF)],
            *x,
            name="last_kv",
            grid=(1,),
            in_specs=[pl.BlockSpec(a.shape, lambda i: (0, 0)) for a in x[:3]]
            + [pl.BlockSpec(memory_space=pl.ANY)] * 2,
            out_specs=[row_spec, row_spec],
            input_output_aliases={3: 0, 4: 1},
        ),
        ob_far,
        qkv_w,
        bias_row,
        k,
        v,
    )
    with jax.named_scope("down_weight"):
        down_two = halves(after(w_down, q), 1)
    with jax.named_scope("out_weight"):
        out_both = over_both(after(out_later, q))

    mixed, pieces, shared = [], [], ()
    for c in range(2):
        with jax.named_scope(f"attend{c}"):
            mo, mp, *shared = run(lambda *x: attend_fwd(c, half, *x), q, k, v, *shared)
            mixed += [mo, mp]
            if c == 0:
                (*up_two, out_both) = touch(*up_two, out_both)
            else:
                (*pieces[0], cot_b) = touch(*pieces[0], cot_b)
            mo, mp = touch(mo, mp)
            pieces.append((mo, over_core(mp), over_y(mo), over_both(mp)))
    mixed_f, logs = shared
    tok = (a_own, b_own)
    f_rows = shaped((half, width), F32)
    b_rows = shaped((half, width), BF)
    h_rows = shaped((half, hidden_here), BF)
    state = [dict(), dict()]

    def norm_one(c):
        with jax.named_scope(f"normone{c}"):
            s = state[c]
            outs = [f_rows, b_rows, f_rows, shaped((half, 1), F32)]
            s["y"], s["yo"], s["n1"], s["i1"] = run(
                lambda *x: call(norm_one_kernel, outs, *x, name="norm_one"),
                *pieces[c],
                out_w,
                out_near,
                out_far,
                out_both,
                tok[c],
                par_one,
            )
            s["yp"] = over_core(s["yo"])

    def feed(c, which, dtype):
        with jax.named_scope(f"feed{c}{which}"):
            s = state[c]
            outs = [h_rows, shaped((half, hidden_here), F32), shaped((half, width), dtype)]
            s["h" + which], s["s" + which], s["p" + which] = run(
                lambda *x: scalar_call(ffn_kernel, outs, *x, name="feed"),
                place,
                s["y" + which],
                *up_two,
                up_row,
                *down_two,
            )
            if which == "p":
                s["c2"] = over_core(s["pp"])

    def near_sum(c, name):
        with jax.named_scope(f"near{c}{name}"):
            s = state[c]
            (s["near" + name],) = run(
                lambda *x: call(near_kernel, [b_rows], *x, name="near"), s["po"], s["c" + name]
            )
            s["far" + name] = over_y(s["near" + name])

    def norm_two(c):
        with jax.named_scope(f"normtwo{c}"):
            s = state[c]
            outs = [b_rows, f_rows, b_rows, shaped((3, width), F32)]
            s["out"], s["gs"], s["gfo"], s["sum2"] = run(
                lambda *x: call(norm_two_kernel, outs, *x, name="norm_two"),
                s["near2"],
                s["far2"],
                s["y"],
                cot[c],
                par_two,
            )
            s["gfp"] = over_core(s["gfo"])

    def feed_back(c, which, dtype):
        with jax.named_scope(f"feedback{c}{which}"):
            s = state[c]
            outs = [h_rows, shaped((half, width), dtype), shaped((1, hidden_here), F32)]
            s["gp" + which], s["p" + which], s["sumu" + which] = run(
                lambda *x: scalar_call(ffn_back_kernel, outs, *x, name="feed_back"),
                place,
                s["gf" + which],
                *down_two,
                s["s" + which],
                *up_two,
            )
            if which == "p":
                s["c5"] = over_core(s["pp"])

    def norm_one_back(c):
        with jax.named_scope(f"normoneback{c}"):
            s = state[c]
            s["gfirst"], s["gao"], s["sum1"] = run(
                lambda *x: call(
                    norm_one_back_kernel,
                    [f_rows, b_rows, shaped((3, width), F32)],
                    *x,
                    name="norm_one_back",
                ),
                s["gs"],
                s["near5"],
                s["far5"],
                s["n1"],
                s["i1"],
                par_one,
            )
            s["gap"] = over_core(s["gao"])

    def weight_grad(kernel, operands, rows, cols, name, small=False):
        with jax.named_scope(name):
            outs = [
                shaped((rows + small * EXTRA, cols), F32),
                shaped((rows + small * 2 * EXTRA, cols), BF),
            ]
            keep, send = run(lambda *x: scalar_call(kernel, outs, *x, name=name), place, *operands)
            return Reduction(run, name, place, keep, over_x(send), small, over_z1, over_z2)

    def owned(red, name):
        with jax.named_scope(name):
            return run(
                lambda *x: scalar_call(owned_kernel, [shaped((red.rows, red.cols), F32)], *x, name=name),
                place,
                red.own,
                red.moved,
            )[0]

    four = [(c, w) for c in range(2) for w in "op"]

    def pieces_of(name):
        return [state[c][name + w] for c, w in four]

    cot = (cot_a, cot_b)
    norm_one(0)
    feed(0, "o", F32)
    norm_one(1)
    feed(0, "p", BF)
    feed(1, "p", BF)
    near_sum(0, "2")
    feed(1, "o", F32)
    near_sum(1, "2")
    norm_two(0)
    feed_back(0, "o", F32)
    feed_back(0, "p", BF)
    norm_two(1)
    with jax.named_scope("outback"):
        out_back = over_z2(state[1]["out"])
    near_sum(0, "5")
    feed_back(1, "o", F32)
    feed_back(1, "p", BF)
    if n_f == 2:
        red_down = weight_grad(
            down_grad_kernel, pieces_of("h") + pieces_of("gf"), hidden_here, width // 2, "down_grad"
        )
    near_sum(1, "5")
    norm_one_back(0)
    if n_f == 2:
        red_up = weight_grad(
            up_grad_kernel, pieces_of("y") + pieces_of("gp"), width // 2, hidden_here, "up_grad"
        )
    norm_one_back(1)
    (out_back,) = touch(out_back)
    with jax.named_scope("smallpack"):
        (packed,) = run(
            lambda *x: call(pack_kernel, [shaped((8, width), F32)], *x, name="pack"),
            *[state[c][s] for s in ("sum1", "sum2") for c in range(2)],
            *pieces_of("sumu"),
        )
        packed_moved = over_core(packed)
    def placed(blocks):
        return run(
            lambda *x: scalar_call(place_kernel, [shaped(tokens.shape, BF)], *x, name="place"),
            place,
            *blocks,
        )[0]

    def both_halves(a, b):
        return a, over_core(a), b, over_core(b)

    if n_f == 2:
        red_down.step()
    with jax.named_scope("placeout"):
        out_blocks = both_halves(after(state[0]["out"], out_back), out_back)
    grad_attn = pieces_of("ga")
    grad_mixed, inner = run(
        lambda *x: call(
            grad_mixed_kernel, [shaped((n_own, wide), BF), shaped((heads, n_own), F32)], *x, name="grad_mixed"
        ),
        *grad_attn,
        out_w,
        mixed_f,
    )
    (*out_blocks, packed_moved) = touch(*out_blocks, packed_moved)

    early, late = tuple(range(heads - 1)), (heads - 1,)
    bwd_args = (q, k, v, grad_mixed, logs, inner)
    n_one, n_two = 3 * len(early) * HD, 3 * HD
    dqs, owns, fars, moved = [], [], [], []
    for h in early:
        with jax.named_scope(f"back{h}"):
            dq, mine, far = run(lambda *x: attend_bwd((h,), 0, total, 2, *x), *bwd_args)
            dqs.append(dq)
            owns.append(mine)
            fars.append(far)
            moved.append(over_z1(far))
        if n_f == 2 and h == 0:
            red_down.step()
        if n_f == 2 and h == early[-1]:
            red_up.step()
    with jax.named_scope("backfar"):
        dq, far = run(lambda *x: attend_bwd(late, 1, n_own, 1, *x, last=False), *bwd_args)
        fars.append(far)
        moved.append(over_z1(far))
    with jax.named_scope("backown"):
        dq, mine = run(lambda *x: attend_bwd(late, 0, n_own, 1, *x), *bwd_args, dq)
        dqs.append(dq)
        owns.append(mine)
    moved[:-1] = touch(*moved[:-1])
    if n_f == 2:
        red_one = weight_grad(
            functools.partial(qkv_grad_kernel, len(early), True),
            own + other + dqs[:-1] + owns[:-1] + fars[:-1] + mixed + grad_attn + [packed, packed_moved],
            n_one + wide,
            width // 2,
            "one_grad",
            True,
        )
    if n_f == 2:
        red_up.step()

    item = [dict(), dict()]

    def input_part(c):
        with jax.named_scope(f"inputpart{c}"):
            s = item[c]
            s["po"], pp = run(
                lambda *x: call(
                    functools.partial(input_part_kernel, c * rows), [f_rows, b_rows], *x, name="input_part"
                ),
                *dqs,
                *owns,
                *moved,
                qkv_w,
            )
            s["cp"] = over_core(pp)

    def input_near(c):
        with jax.named_scope(f"inputnear{c}"):
            s = item[c]
            (s["near"],) = run(
                lambda *x: call(near_kernel, [b_rows], *x, name="near"), s["po"], s["cp"]
            )
            s["far"] = over_y(s["near"])

    def input_last(c):
        with jax.named_scope(f"inputlast{c}"):
            s = item[c]
            (s["in"],) = run(
                lambda *x: call(input_grad_kernel, [b_rows], *x, name="input_grad"),
                state[c]["gfirst"],
                s["near"],
                s["far"],
            )

    input_part(1)
    if n_f == 2:
        red_down.step()
        red_two = weight_grad(
            functools.partial(qkv_grad_kernel, 1, False),
            own + other + dqs[-1:] + owns[-1:] + fars[-1:],
            n_two,
            width // 2,
            "two_grad",
            True,
        )
    input_near(1)
    with jax.named_scope("placeout"):
        output = placed(out_blocks)
    if n_f == 2:
        red_one.step()
    input_last(1)
    with jax.named_scope("inputback"):
        in_back = over_z2(item[1]["in"])
    if n_f == 2:
        red_up.step()
        red_two.step()
        (red_down.moved,) = touch(red_down.moved)
    input_part(0)
    if n_f == 2:
        owned_down = owned(red_down, "owned_down")
    input_near(0)
    if n_f == 2:
        red_one.step()
        red_two.step()
    input_last(0)
    with jax.named_scope("placein"):
        in_far = over_core(item[0]["in"])
    if n_f == 2:
        owned_up = owned(red_up, "owned_up")
        red_one.step()
        red_two.step()
    (in_back,) = touch(in_back)
    with jax.named_scope("placein"):
        in_blocks = [item[0]["in"], in_far, in_back, over_core(in_back)]
    with jax.named_scope("finish"):
        if n_f == 2:
            qkv_grad, owned_out, small, bias_grad = run(
                lambda *x: scalar_call(
                    owned_qkv_kernel,
                    [
                        shaped((3, wide, width // 2), F32),
                        shaped((wide, width // 2), F32),
                        shaped((8, width), F32),
                        shaped((2, wide), F32),
                    ],
                    *x,
                    name="owned_qkv",
                ),
                place,
                red_one.own,
                red_two.own,
                red_one.moved,
                red_two.moved,
            )
            owned_qkv = qkv_grad.transpose(2, 0, 1)
        else:

            def reduce_plain(left, right, axis):
                grad = mm(jnp.concatenate(left), jnp.concatenate(right), TN)
                keep = lax.psum_scatter(grad, "fsdp", scatter_dimension=axis, tiled=True)
                return lax.psum(keep, "context").astype(BF).astype(F32)

            zero = jnp.zeros((n_own, wide), BF)
            left = jnp.concatenate(dqs + by_kind(owns), axis=1)
            right = jnp.concatenate([zero] + by_kind(fars), axis=1)
            owned_up = reduce_plain(pieces_of("y"), pieces_of("gp"), 0)
            owned_down = reduce_plain(pieces_of("h"), pieces_of("gf"), 1)
            owned_out = reduce_plain(mixed, grad_attn, 1)
            owned_qkv = reduce_plain(own + other, [left, right], 0).reshape(w_qkv.shape)
            column_sums = jnp.sum((left.astype(F32) + right.astype(F32)), axis=0)
            bias_grad = jnp.stack([column_sums[:wide], column_sums[2 * wide :]])
            small = jnp.concatenate([packed[:6] + packed_moved[:6], packed[6:]])
            small, bias_grad = lax.psum((small, bias_grad), ("fsdp", "context"))
    with jax.named_scope("placein"):
        input_grad = placed(in_blocks)
    return (
        output,
        input_grad,
        owned_qkv,
        bias_grad,
        owned_out,
        small[0],
        small[1],
        small[2],
        owned_up,
        small[6],
        owned_down,
        small[3],
        small[4],
        small[5],
    )


def solution(mesh):
    sizes = tuple(mesh.shape[name] for name in ("fsdp", "context", "tensor"))
    specs = (
        P("fsdp", None, "tensor"),
        P(None, "tensor"),
        P("tensor", "fsdp"),
        P(),
        P(),
        P(),
        P("fsdp", "tensor"),
        P("tensor"),
        P("tensor", "fsdp"),
        P(),
        P(),
        P(),
    )
    rows = P("fsdp", "context", None)
    return jax.shard_map(
        functools.partial(body, sizes),
        mesh=mesh,
        in_specs=(rows, rows) + specs,
        out_specs=(rows, rows) + specs,
        check_vma=False,
    )
```

```python
import functools
import math

import jax
import jax.numpy as jnp
from jax import lax
from jax.experimental import pallas as pl
from jax.experimental.pallas import tpu as pltpu
from jax.sharding import PartitionSpec as P

HD = 64
SCALE = 1.0 / math.sqrt(HD)
SCALE_LOG2 = SCALE * math.log2(math.e)
EPS = 1e-06
BF = jnp.bfloat16
F32 = jnp.float32
NT = (((1,), (1,)), ((), ()))
TN = (((0,), (0,)), ((), ()))
NN = (((1,), (0,)), ((), ()))


def mm(a, b, dims=NN):
    return lax.dot_general(a, b, dims, preferred_element_type=F32)


def shaped(shape, dtype):
    return jax.ShapeDtypeStruct(shape, dtype)


def call(kernel, outs, *operands, name, limit=16, **extra):
    return pl.pallas_call(
        kernel,
        out_shape=list(outs),
        cost_estimate=pl.CostEstimate(flops=int(5e9), bytes_accessed=1, transcendentals=0),
        compiler_params=pltpu.CompilerParams(vmem_limit_bytes=limit << 20),
        name=name,
        **extra,
    )(*operands)


SMEM = pl.BlockSpec(memory_space=pltpu.SMEM)
VMEM = pl.BlockSpec(memory_space=pltpu.VMEM)


def scalar_call(kernel, outs, scalars, *operands, **kw):
    specs = [SMEM] + [VMEM] * len(operands)
    return call(kernel, outs, scalars, *operands, in_specs=specs, **kw)


def lanes(ref, index, size):
    return ref[:, pl.ds(pl.multiple_of(index * size, 128), size)]


def qkv_kernel(*refs):
    rows, (w_ref, b_ref, q_ref, k_ref, v_ref) = refs[:7], refs[7:]
    n = rows[0].shape[0]
    wide = q_ref.shape[1]
    for i, ref in enumerate(rows):
        here = slice(i * n, (i + 1) * n)
        skip = 0 if i < 4 else wide
        full = (mm(ref[...], w_ref[skip:, :], NT) + b_ref[:, skip:]).astype(BF)
        if i < 4:
            q_ref[here, :] = full[:, :wide]
        k_ref[here, :] = full[:, wide - skip : 2 * wide - skip]
        v_ref[here, :] = full[:, 2 * wide - skip :]


def last_kv_kernel(x_ref, w_ref, b_ref, *refs):
    k_ref, v_ref = refs[-2:]
    wide = k_ref.shape[1]
    full = (mm(x_ref[...], w_ref[wide:, :], NT) + b_ref[:, wide:]).astype(BF)
    k_ref[...] = full[:, :wide]
    v_ref[...] = full[:, wide:]


def attend_fwd_kernel(chunk, *refs):
    q_ref, k_ref, v_ref = refs[:3]
    o_ref, p_ref, f_ref, l_ref = refs[-4:]
    outs, logs = [], []
    for h in range(q_ref.shape[1] // HD):
        cols = slice(h * HD, (h + 1) * HD)
        scores = mm(q_ref[:, cols], k_ref[:, cols], NT)
        top = jnp.max(scores, axis=1, keepdims=True)
        expo = jnp.exp2((scores - top) * SCALE_LOG2)
        total = jnp.sum(expo, axis=1, keepdims=True)
        outs.append(mm(expo.astype(BF), v_ref[:, cols]) / total)
        logs.append(top * SCALE_LOG2 + jnp.log2(total))
    mixed = jnp.concatenate(outs, axis=1)
    f_ref[...] = mixed
    l_ref[...] = jnp.concatenate(logs, axis=1).T
    for step, ref in enumerate((o_ref, p_ref)):

        @pl.when(pl.program_id(0) == step)
        def _():
            ref[...] = mixed.astype(BF)


def attend_fwd(chunk, block, q, k, v, *before):
    nq, w = q.shape
    nk = k.shape[0]
    heads = w // HD
    q_spec = pl.BlockSpec((block, w), lambda i: (chunk * 2 + i, 0))
    l_spec = pl.BlockSpec((heads, block), lambda i: (0, chunk * 2 + i))
    o_spec = pl.BlockSpec((block, w), lambda i: (0, 0))
    k_spec = pl.BlockSpec((nk, w), lambda i: (0, 0))
    anywhere = pl.BlockSpec(memory_space=pl.ANY)
    return call(
        functools.partial(attend_fwd_kernel, chunk),
        [shaped((block, w), BF)] * 2 + [shaped((nq, w), F32), shaped((heads, nq), F32)],
        q,
        k,
        v,
        *before,
        name="attend_fwd",
        limit=24,
        grid=(2,),
        in_specs=[q_spec, k_spec, k_spec] + [anywhere] * len(before),
        out_specs=[o_spec, o_spec, q_spec, l_spec],
        input_output_aliases={3: 2, 4: 3} if before else {},
    )


def grad_mixed_kernel(*refs):
    gas, (w_ref, f_ref, g_ref, d_ref) = refs[:4], refs[4:]
    n = gas[0].shape[0]
    heads = w_ref.shape[0] // HD
    for i, ga in enumerate(gas):
        here = slice(i * n, (i + 1) * n)
        g = mm(ga[...], w_ref[...], NT).astype(BF)
        g_ref[here, :] = g
        prod = (g.astype(F32) * f_ref[here, :]).T
        d_ref[:, here] = jnp.concatenate(
            [jnp.sum(prod[h * HD : (h + 1) * HD], axis=0, keepdims=True) for h in range(heads)]
        )


def attend_bwd_kernel(heads, first, last, split, *refs):
    q_ref, k_ref, v_ref, g_ref, l_ref, d_ref = refs[:6]
    add_ref = refs[6] if not first else None
    dq_ref, outs, acc = refs[6 + (not first)], refs[7 + (not first) : -1], refs[-1]
    dqs, dks, dvs = [], [], []
    for h in heads:
        cols = slice(h * HD, (h + 1) * HD)
        q, k, v, g = q_ref[:, cols], k_ref[:, cols], v_ref[:, cols], g_ref[:, cols]
        probs = jnp.exp2(mm(k, q, NT) * SCALE_LOG2 - l_ref[h : h + 1, :])
        grad_scores = (probs * (mm(v, g, NT) - d_ref[h : h + 1, :])).astype(BF)
        dvs.append(mm(probs.astype(BF), g))
        dks.append(mm(grad_scores, q) * SCALE)
        dqs.append(mm(k, grad_scores, TN))
    dq = (dqs[0] if len(dqs) == 1 else jnp.concatenate(dqs, axis=0)).T
    if not first:
        dq = dq + add_ref[...]
    dq_ref[...] = (dq * SCALE).astype(BF) if last else dq
    dkv = jnp.concatenate(dks + dvs, axis=1)
    step = pl.program_id(0)

    @pl.when(step == 0)
    def _():
        acc[...] = dkv

    @pl.when(step > 0)
    def _():
        acc[...] += dkv

    @pl.when(step == pl.num_programs(0) - 1)
    def _():
        n = acc.shape[0] // len(outs)
        for i, ref in enumerate(outs):
            ref[...] = acc[i * n : (i + 1) * n].astype(BF)


def attend_bwd(heads, key_block, key_rows, split, q, k, v, g, logs, inner, *add, last=True, block=256):
    nq, w = q.shape
    n = len(heads) * HD
    q_spec = pl.BlockSpec((block, w), lambda i: (i, 0))
    k_spec = pl.BlockSpec((key_rows, w), lambda i: (key_block, 0))
    n_spec = pl.BlockSpec((block, n), lambda i: (i, 0))
    l_spec = pl.BlockSpec((logs.shape[0], block), lambda i: (0, i))
    whole = pl.BlockSpec((key_rows // split, 2 * n), lambda i: (0, 0))
    return call(
        functools.partial(attend_bwd_kernel, heads, not add, last, split),
        [shaped((nq, n), BF if last else F32)] + [shaped((key_rows // split, 2 * n), BF)] * split,
        q,
        k,
        v,
        g,
        logs,
        inner,
        *add,
        name="attend_bwd",
        limit=36,
        grid=(nq // block,),
        in_specs=[q_spec, k_spec, k_spec, q_spec, l_spec, l_spec] + [n_spec] * len(add),
        out_specs=[n_spec] + [whole] * split,
        scratch_shapes=[pltpu.VMEM((key_rows, 2 * n), F32)],
    )


def normed(x):
    centred = x - jnp.mean(x, axis=-1, keepdims=True)
    inverse = lax.rsqrt(jnp.mean(centred * centred, axis=-1, keepdims=True) + EPS)
    return centred * inverse, inverse


def norm_back(g, norm, inverse):
    return inverse * (
        g
        - jnp.mean(g, axis=-1, keepdims=True)
        - norm * jnp.mean(g * norm, axis=-1, keepdims=True)
    )


def down_rows(*terms):
    return jnp.concatenate([jnp.sum(t, axis=0, keepdims=True) for t in terms], axis=0)


def norm_one_kernel(m0, m1, m2, m3, w0, w1, w2, w3, t_ref, p_ref, y_ref, low_ref, n_ref, i_ref):
    near = mm(m0[...], w0[...]) + mm(m1[...], w1[...])
    far = mm(m2[...], w2[...]) + mm(m3[...], w3[...])
    norm, inverse = normed(t_ref[...].astype(F32) + ((near + far) + p_ref[0:1, :]))
    y = norm * p_ref[1:2, :] + p_ref[2:3, :]
    y_ref[...] = y
    low_ref[...] = y.astype(BF)
    n_ref[...] = norm
    i_ref[...] = inverse


def ffn_kernel(s_ref, y_ref, up_own, up_far, b_ref, down_own, down_far, h_ref, sl_ref, p_ref):
    f = s_ref[0]
    size = up_own.shape[0]
    x = mm(lanes(y_ref, f, size), up_own[...]) + mm(lanes(y_ref, 1 - f, size), up_far[...]) + b_ref[...]
    cdf = 0.5 * (1.0 + lax.erf(x * (1.0 / math.sqrt(2.0))))
    pdf = jnp.exp(-0.5 * x * x) * (1.0 / math.sqrt(2.0 * math.pi))
    sl_ref[...] = cdf + x * pdf
    hidden = (x * cdf).astype(BF)
    h_ref[...] = hidden
    for part, ref in ((f, down_own), (1 - f, down_far)):
        here = pl.ds(pl.multiple_of(part * size, 128), size)
        p_ref[:, here] = mm(hidden, ref[...]).astype(p_ref.dtype)


def norm_two_kernel(near, far, y_ref, g_ref, p_ref, o_ref, gs_ref, gf_ref, sums):
    ffn = near[...].astype(F32) + far[...].astype(F32)
    norm, inverse = normed(y_ref[...] + (ffn + p_ref[0:1, :]))
    o_ref[...] = (norm * p_ref[1:2, :] + p_ref[2:3, :]).astype(BF)
    g = g_ref[...].astype(F32)
    grad = norm_back(g * p_ref[1:2, :], norm, inverse)
    low = grad.astype(BF)
    gs_ref[...] = grad
    gf_ref[...] = low
    sums[...] = down_rows(low.astype(F32), g * norm, g)


def ffn_back_kernel(s_ref, g_ref, down_own, down_far, sl_ref, up_own, up_far, gp_ref, p_ref, sums):
    f = s_ref[0]
    size = up_own.shape[0]
    grad = mm(lanes(g_ref, f, size), down_own[...], NT) + mm(lanes(g_ref, 1 - f, size), down_far[...], NT)
    low = (grad * sl_ref[...]).astype(BF)
    gp_ref[...] = low
    sums[...] = down_rows(low.astype(F32))
    for part, ref in ((f, up_own), (1 - f, up_far)):
        here = pl.ds(pl.multiple_of(part * size, 128), size)
        p_ref[:, here] = mm(low, ref[...], NT).astype(p_ref.dtype)


def norm_one_back_kernel(gs_ref, near, far, n_ref, i_ref, p_ref, g_ref, low_ref, sums):
    grad_y = gs_ref[...] + (near[...].astype(F32) + far[...].astype(F32))
    norm = n_ref[...]
    grad = norm_back(grad_y * p_ref[1:2, :], norm, i_ref[...])
    low = grad.astype(BF)
    g_ref[...] = grad
    low_ref[...] = low
    sums[...] = down_rows(low.astype(F32), grad_y * norm, grad_y)


def by_kind(parts):
    return [x[:, :HD] for x in parts] + [x[:, HD:] for x in parts]


def input_part_kernel(first_row, *refs):
    w_ref, o_ref, p_ref = refs[-3:]
    heads = (len(refs) - 3) // 3
    dqs, dkvs, moved = (refs[i * heads : (i + 1) * heads] for i in range(3))
    n = o_ref.shape[0]
    for part, ref in enumerate((o_ref, p_ref)):
        here = slice(first_row + part * n, first_row + (part + 1) * n)
        lows = [(a[here, :].astype(F32) + b[here, :].astype(F32)).astype(BF) for a, b in zip(dkvs, moved)]
        grads = jnp.concatenate([d[here, :] for d in dqs] + by_kind(lows), axis=1)
        ref[...] = mm(grads, w_ref[...]).astype(ref.dtype)


def near_kernel(a_ref, b_ref, o_ref):
    o_ref[...] = (a_ref[...] + b_ref[...].astype(F32)).astype(BF)


def input_grad_kernel(g_ref, a_ref, b_ref, o_ref):
    o_ref[...] = (g_ref[...] + (a_ref[...].astype(F32) + b_ref[...].astype(F32))).astype(BF)


def place_kernel(s_ref, a, b, c, d, o_ref):
    n = a.shape[0]
    group, core = s_ref[2], s_ref[3]
    for block, half, ref in ((group, core, a), (group, 1 - core, b), (1 - group, core, c), (1 - group, 1 - core, d)):
        o_ref[block, pl.ds(pl.multiple_of(half * n, n), n), :] = ref[...]


def pack_kernel(a0, a1, b0, b1, u0, u1, u2, u3, o_ref):
    o_ref[0:3, :] = a0[...] + a1[...]
    o_ref[3:6, :] = b0[...] + b1[...]
    o_ref[6:7, :] = u0[...] + u1[...] + u2[...] + u3[...]
    o_ref[7:8, :] = jnp.zeros_like(u0)


EXTRA = 16


def two_parts(x):
    high = x.astype(BF).astype(F32)
    return high + (x - high).astype(BF).astype(F32)


def put(ref, main, small):
    n = main.shape[0]
    ref[0:n, :] = main.astype(ref.dtype)
    if small is not None:
        high = small.astype(ref.dtype)
        ref[n : n + EXTRA, :] = high
        if ref.shape[0] > n + EXTRA:
            ref[n + EXTRA :, :] = (small - high.astype(F32)).astype(ref.dtype)


def get(ref, small):
    if not small:
        return ref[...].astype(F32), None
    parts = 1 if ref.dtype == F32 else 2
    n = ref.shape[0] - parts * EXTRA
    rest = ref[n : n + EXTRA, :].astype(F32)
    if parts == 2:
        rest = rest + ref[n + EXTRA :, :].astype(F32)
    return ref[0:n, :].astype(F32), rest


def up_grad_kernel(s_ref, *refs):
    ys, gs, (keep, send) = refs[:4], refs[4:8], refs[8:]
    f = s_ref[0]
    size = ys[0].shape[1] // 2
    for out, part in ((send, 1 - f), (keep, f)):
        put(out, sum(mm(lanes(y, part, size), g[...], TN) for y, g in zip(ys, gs)), None)


def down_grad_kernel(s_ref, *refs):
    hs, gs, (keep, send) = refs[:4], refs[4:8], refs[8:]
    f = s_ref[0]
    size = gs[0].shape[1] // 2
    for out, part in ((send, 1 - f), (keep, f)):
        put(out, sum(mm(h[...], lanes(g, part, size), TN) for h, g in zip(hs, gs)), None)


def qkv_grad_kernel(heads, with_out, s_ref, *refs):
    rows, more, (keep, send) = refs[:8], refs[8 + 3 * heads : -2], refs[-2:]
    dqs, owns, fars = (refs[8 + i * heads : 8 + (i + 1) * heads] for i in range(3))
    f = s_ref[0]
    size = rows[0].shape[1] // 2
    n = rows[0].shape[0]
    m = heads * HD
    own = jnp.concatenate([d[...] for d in dqs] + by_kind([x[...] for x in owns]), axis=1)
    far = jnp.concatenate(by_kind([x[...] for x in fars]), axis=1)
    far_sums = jnp.sum(far.astype(F32), axis=0, keepdims=True)
    sums = jnp.sum(own.astype(F32), axis=0, keepdims=True)
    sums = jnp.concatenate([sums[:, :m], sums[:, m:] + far_sums], axis=1)
    if sums.shape[1] < size:
        sums = jnp.concatenate([sums, jnp.zeros((1, size - sums.shape[1]), F32)], axis=1)
    small = [sums]
    if with_out:
        packed, moved = more[-2:]
        six = packed[0:6, :] + moved[0:6, :]
        ups = packed[6:7, :]
        small = [six[:, :size], ups[:, :size], six[:, size:], ups[:, size:], sums]
    small.append(jnp.zeros((EXTRA - sum(x.shape[0] for x in small), size), F32))
    small = two_parts(jnp.concatenate(small, axis=0))
    for out, part in ((send, 1 - f), (keep, f)):
        one = two = None
        for i in range(4):
            here = slice(i * n, (i + 1) * n)
            a = mm(own[here], lanes(rows[i], part, size), TN)
            b = mm(far[here], lanes(rows[4 + i], part, size), TN)
            one = a if one is None else one + a
            two = b if two is None else two + b
        grad = [one[:m], one[m:] + two]
        if with_out:
            grad.append(sum(mm(a[...], lanes(g, part, size), TN) for a, g in zip(more[:4], more[4:8])))
        put(out, jnp.concatenate(grad, axis=0), small)


def half_of(main, which):
    n = main.shape[0] // 2
    return jnp.where(which == 0, main[:n], main[n:])


def first_sum_kernel(small, s_ref, keep, moved, own, send):
    (a, c), (b, d) = get(keep, small), get(moved, small)
    total = a + b
    rest = two_parts(c + d) if small else None
    put(own, half_of(total, s_ref[1]), rest)
    put(send, half_of(total, 1 - s_ref[1]), rest)


def sum_kernel(small, a_ref, b_ref, out):
    (a, c), (b, d) = get(a_ref, small), get(b_ref, small)
    put(out, a + b, c + d if small else None)


def joined(s_ref, own, moved):
    first = s_ref[1] == 0
    return jnp.concatenate([jnp.where(first, own, moved), jnp.where(first, moved, own)], axis=0)


def owned_kernel(s_ref, own, moved, out):
    out[...] = joined(s_ref, get(own, False)[0], get(moved, False)[0])


def owned_qkv_kernel(s_ref, own1, own2, moved1, moved2, qkv, outw, sums, bias):
    (one, small1), (two, small2) = get(own1, True), get(own2, True)
    one = joined(s_ref, one, get(moved1, True)[0])
    two = joined(s_ref, two, get(moved2, True)[0])
    n = outw.shape[0]
    m1, m2 = (one.shape[0] - n) // 3, two.shape[0] // 3
    for j in range(3):
        qkv[j, 0:m1, :] = one[j * m1 : (j + 1) * m1]
        qkv[j, m1:, :] = two[j * m2 : (j + 1) * m2]
    outw[...] = one[3 * m1 :]
    sums[0:7, :] = jnp.concatenate([small1[0:7], small1[7:14]], axis=1)
    sums[7:8, :] = jnp.zeros_like(sums[7:8, :])
    for i, j in ((0, 0), (1, 2)):
        bias[i : i + 1, :] = jnp.concatenate(
            [small1[14:15, j * m1 : (j + 1) * m1], small2[0:1, j * m2 : (j + 1) * m2]], axis=1
        )


def swap(x, axis, size, mask):
    return lax.ppermute(x, axis, [(i, i ^ mask) for i in range(size)])


def pick(first, second, bit, axis):
    n = first.shape[axis]
    ring = jnp.concatenate([first, second, first], axis=axis)
    return lax.dynamic_slice_in_dim(ring, bit * n, 2 * n, axis)


class Order:
    def __init__(self):
        self.done = None

    def __call__(self, fn, *operands):
        if self.done is not None:
            operands, _ = lax.optimization_barrier((operands, self.done))
        out = fn(*operands)
        self.done = out
        return out


class Reduction:
    def __init__(self, run, name, place, keep, moved, small, over_z1, over_z2):
        self.run, self.name, self.place, self.small = run, name, place, small
        self.own, self.moved, self.stage = keep, moved, 0
        self.over = [over_z1, over_z2, over_z1]
        self.rows, self.cols = keep.shape[0] - small * EXTRA, keep.shape[1]

    def step(self):
        self.stage += 1
        low = shaped((self.rows // 2 + self.small * 2 * EXTRA, self.cols), BF)
        wide = shaped((self.rows // 2 + self.small * EXTRA, self.cols), F32)
        name = f"{self.name}_{self.stage}"
        with jax.named_scope(name):
            if self.stage == 1:
                kernel = functools.partial(first_sum_kernel, self.small)
                fn = lambda *x: scalar_call(kernel, [wide, low], *x, name=name)
                self.own, send = self.run(fn, self.place, self.own, self.moved)
            else:
                kernel = functools.partial(sum_kernel, self.small)
                fn = lambda *x: call(kernel, [low], *x, name=name)
                (self.own,) = self.run(fn, self.own, self.moved)
                send = self.own
            self.moved = self.over[self.stage - 1](send)


def body(sizes, *args):
    (
        tokens,
        cotangent,
        w_qkv,
        qv_bias,
        w_out,
        out_bias,
        gain_one,
        shift_one,
        w_up,
        up_bias,
        w_down,
        down_bias,
        gain_two,
        shift_two,
    ) = args
    n_f, n_c, n_t = sizes
    _, rows, width = tokens.shape
    wide = w_qkv.shape[2]
    heads = wide // HD
    hidden_here = w_up.shape[1]
    half = rows // 2
    f = lax.axis_index("fsdp") if n_f == 2 else 0
    z = lax.axis_index("context")
    core = lax.axis_index("tensor") % 2
    group = z // 2
    over_core = functools.partial(swap, axis="tensor", size=n_t, mask=1)
    over_y = functools.partial(swap, axis="tensor", size=n_t, mask=2)
    over_both = functools.partial(swap, axis="tensor", size=n_t, mask=3)
    over_z1 = functools.partial(swap, axis="context", size=n_c, mask=1)
    over_z2 = functools.partial(swap, axis="context", size=n_c, mask=2)
    over_x = functools.partial(swap, axis="fsdp", size=n_f, mask=1)
    run = Order()

    def whole_f(w, axis):
        return lax.all_gather(w, "fsdp", axis=axis, tiled=True)

    def halves(w, axis):
        if n_f == 2:
            return w, over_x(w)
        w = whole_f(w, axis)
        return jnp.split(w, 2, axis=axis)

    def block_of(x, which, part):
        return lax.dynamic_slice(x, (which, part * half, 0), (1, half, width))[0]

    def touch(*x):
        return run(lambda *a: a, *x)

    def after(x, *others):
        return lax.optimization_barrier((x, others))[0]

    with jax.named_scope("arrive"):
        give = run(lambda t: block_of(t, 1 - group, core), tokens)
        b_own = over_z2(give)
        a_own = run(lambda t: block_of(t, group, core), tokens)
        oa_own = over_z1(a_own)
        qkv_t = after(w_qkv.transpose(1, 2, 0).reshape(3 * wide, -1), a_own)
        qkv_moved = over_x(qkv_t) if n_f == 2 else whole_f(qkv_t, 1)
        w_out_later = after(w_out, a_own)
        out_moved = over_x(w_out_later) if n_f == 2 else whole_f(w_out_later, 1)
        cot_give, cot_a, a_far, place, par_one, par_two, bias_row, up_row = run(
            lambda g, t, qb, ub, p1, p2: (
                block_of(g, 1 - group, core),
                block_of(g, group, core),
                block_of(t, group, 1 - core),
                jnp.stack(
                    [
                        jnp.int32(f),
                        (z % 2).astype(jnp.int32),
                        group.astype(jnp.int32),
                        core.astype(jnp.int32),
                    ]
                ),
                jnp.stack(p1),
                jnp.stack(p2),
                jnp.concatenate([qb[0], jnp.zeros_like(qb[0]), qb[1]])[None],
                ub[None],
            ),
            cotangent,
            tokens,
            qv_bias,
            up_bias,
            (out_bias, gain_one, shift_one),
            (down_bias, gain_two, shift_two),
        )
        qkv_w = run(lambda a, b: pick(a, b, f, 1) if n_f == 2 else b, qkv_t, qkv_moved)
        out_w = run(lambda a, b: pick(a, b, f, 1) if n_f == 2 else b, w_out, out_moved)
        (b_own,) = touch(b_own)
        ob_own = over_z1(b_own)
        (oa_own,) = touch(oa_own)
        b_far, oa_far = over_core(b_own), over_core(oa_own)
        b_far, oa_far, out_later = touch(b_far, oa_far, out_w)
        out_near, out_far = over_core(out_later), over_y(out_later)
        up_two = halves(after(w_up, out_later), 0)
        out_near, out_far = touch(out_near, out_far)
        (ob_own,) = touch(ob_own)
        ob_far = over_core(ob_own)
    with jax.named_scope("cotangent"):
        cot_b = over_z2(after(cot_give, ob_own))
    own = [a_own, a_far, b_own, b_far]
    other = [oa_own, oa_far, ob_own, ob_far]
    total = 8 * half
    n_own = total // 2

    q, k, v = run(
        lambda *x: call(
            qkv_kernel,
            [shaped((n_own, wide), BF), shaped((total, wide), BF), shaped((total, wide), BF)],
            *x,
            name="qkv",
        ),
        *own,
        *other[:3],
        qkv_w,
        bias_row,
    )
    row_spec = pl.BlockSpec((half, wide), lambda i: (7, 0))
    k, v = run(
        lambda *x: call(
            last_kv_kernel,
            [shaped((total, wide), BF), shaped((total, wide), BF)],
            *x,
            name="last_kv",
            grid=(1,),
            in_specs=[pl.BlockSpec(a.shape, lambda i: (0, 0)) for a in x[:3]]
            + [pl.BlockSpec(memory_space=pl.ANY)] * 2,
            out_specs=[row_spec, row_spec],
            input_output_aliases={3: 0, 4: 1},
        ),
        ob_far,
        qkv_w,
        bias_row,
        k,
        v,
    )
    with jax.named_scope("down_weight"):
        down_two = halves(after(w_down, q), 1)
    with jax.named_scope("out_weight"):
        out_both = over_both(after(out_later, q))

    mixed, pieces, shared = [], [], ()
    for c in range(2):
        with jax.named_scope(f"attend{c}"):
            mo, mp, *shared = run(lambda *x: attend_fwd(c, half, *x), q, k, v, *shared)
            mixed += [mo, mp]
            if c == 0:
                (*up_two, out_both) = touch(*up_two, out_both)
            else:
                (*pieces[0], cot_b) = touch(*pieces[0], cot_b)
            mo, mp = touch(mo, mp)
            pieces.append((mo, over_core(mp), over_y(mo), over_both(mp)))
    mixed_f, logs = shared
    tok = (a_own, b_own)
    f_rows = shaped((half, width), F32)
    b_rows = shaped((half, width), BF)
    h_rows = shaped((half, hidden_here), BF)
    state = [dict(), dict()]

    def norm_one(c):
        with jax.named_scope(f"normone{c}"):
            s = state[c]
            outs = [f_rows, b_rows, f_rows, shaped((half, 1), F32)]
            s["y"], s["yo"], s["n1"], s["i1"] = run(
                lambda *x: call(norm_one_kernel, outs, *x, name="norm_one"),
                *pieces[c],
                out_w,
                out_near,
                out_far,
                out_both,
                tok[c],
                par_one,
            )
            s["yp"] = over_core(s["yo"])

    def feed(c, which, dtype):
        with jax.named_scope(f"feed{c}{which}"):
            s = state[c]
            outs = [h_rows, shaped((half, hidden_here), F32), shaped((half, width), dtype)]
            s["h" + which], s["s" + which], s["p" + which] = run(
                lambda *x: scalar_call(ffn_kernel, outs, *x, name="feed"),
                place,
                s["y" + which],
                *up_two,
                up_row,
                *down_two,
            )
            if which == "p":
                s["c2"] = over_core(s["pp"])

    def near_sum(c, name):
        with jax.named_scope(f"near{c}{name}"):
            s = state[c]
            (s["near" + name],) = run(
                lambda *x: call(near_kernel, [b_rows], *x, name="near"), s["po"], s["c" + name]
            )
            s["far" + name] = over_y(s["near" + name])

    def norm_two(c):
        with jax.named_scope(f"normtwo{c}"):
            s = state[c]
            outs = [b_rows, f_rows, b_rows, shaped((3, width), F32)]
            s["out"], s["gs"], s["gfo"], s["sum2"] = run(
                lambda *x: call(norm_two_kernel, outs, *x, name="norm_two"),
                s["near2"],
                s["far2"],
                s["y"],
                cot[c],
                par_two,
            )
            s["gfp"] = over_core(s["gfo"])

    def feed_back(c, which, dtype):
        with jax.named_scope(f"feedback{c}{which}"):
            s = state[c]
            outs = [h_rows, shaped((half, width), dtype), shaped((1, hidden_here), F32)]
            s["gp" + which], s["p" + which], s["sumu" + which] = run(
                lambda *x: scalar_call(ffn_back_kernel, outs, *x, name="feed_back"),
                place,
                s["gf" + which],
                *down_two,
                s["s" + which],
                *up_two,
            )
            if which == "p":
                s["c5"] = over_core(s["pp"])

    def norm_one_back(c):
        with jax.named_scope(f"normoneback{c}"):
            s = state[c]
            s["gfirst"], s["gao"], s["sum1"] = run(
                lambda *x: call(
                    norm_one_back_kernel,
                    [f_rows, b_rows, shaped((3, width), F32)],
                    *x,
                    name="norm_one_back",
                ),
                s["gs"],
                s["near5"],
                s["far5"],
                s["n1"],
                s["i1"],
                par_one,
            )
            s["gap"] = over_core(s["gao"])

    def weight_grad(kernel, operands, rows, cols, name, small=False):
        with jax.named_scope(name):
            outs = [
                shaped((rows + small * EXTRA, cols), F32),
                shaped((rows + small * 2 * EXTRA, cols), BF),
            ]
            keep, send = run(lambda *x: scalar_call(kernel, outs, *x, name=name), place, *operands)
            return Reduction(run, name, place, keep, over_x(send), small, over_z1, over_z2)

    def owned(red, name):
        with jax.named_scope(name):
            return run(
                lambda *x: scalar_call(owned_kernel, [shaped((red.rows, red.cols), F32)], *x, name=name),
                place,
                red.own,
                red.moved,
            )[0]

    four = [(c, w) for c in range(2) for w in "op"]

    def pieces_of(name):
        return [state[c][name + w] for c, w in four]

    cot = (cot_a, cot_b)
    norm_one(0)
    feed(0, "o", F32)
    norm_one(1)
    feed(0, "p", BF)
    feed(1, "p", BF)
    near_sum(0, "2")
    feed(1, "o", F32)
    near_sum(1, "2")
    norm_two(0)
    feed_back(0, "o", F32)
    feed_back(0, "p", BF)
    norm_two(1)
    with jax.named_scope("outback"):
        out_back = over_z2(state[1]["out"])
    near_sum(0, "5")
    feed_back(1, "o", F32)
    feed_back(1, "p", BF)
    if n_f == 2:
        red_down = weight_grad(
            down_grad_kernel, pieces_of("h") + pieces_of("gf"), hidden_here, width // 2, "down_grad"
        )
    near_sum(1, "5")
    norm_one_back(0)
    if n_f == 2:
        red_up = weight_grad(
            up_grad_kernel, pieces_of("y") + pieces_of("gp"), width // 2, hidden_here, "up_grad"
        )
    norm_one_back(1)
    (out_back,) = touch(out_back)
    with jax.named_scope("smallpack"):
        (packed,) = run(
            lambda *x: call(pack_kernel, [shaped((8, width), F32)], *x, name="pack"),
            *[state[c][s] for s in ("sum1", "sum2") for c in range(2)],
            *pieces_of("sumu"),
        )
        packed_moved = over_core(packed)
    def placed(blocks):
        return run(
            lambda *x: scalar_call(place_kernel, [shaped(tokens.shape, BF)], *x, name="place"),
            place,
            *blocks,
        )[0]

    def both_halves(a, b):
        return a, over_core(a), b, over_core(b)

    if n_f == 2:
        red_down.step()
    with jax.named_scope("placeout"):
        out_blocks = both_halves(after(state[0]["out"], out_back), out_back)
    grad_attn = pieces_of("ga")
    grad_mixed, inner = run(
        lambda *x: call(
            grad_mixed_kernel, [shaped((n_own, wide), BF), shaped((heads, n_own), F32)], *x, name="grad_mixed"
        ),
        *grad_attn,
        out_w,
        mixed_f,
    )
    (*out_blocks, packed_moved) = touch(*out_blocks, packed_moved)

    early, late = tuple(range(heads - 1)), (heads - 1,)
    bwd_args = (q, k, v, grad_mixed, logs, inner)
    n_one, n_two = 3 * len(early) * HD, 3 * HD
    dqs, owns, fars, moved = [], [], [], []
    for h in early:
        with jax.named_scope(f"back{h}"):
            dq, mine, far = run(lambda *x: attend_bwd((h,), 0, total, 2, *x), *bwd_args)
            dqs.append(dq)
            owns.append(mine)
            fars.append(far)
            moved.append(over_z1(far))
        if n_f == 2 and h == 0:
            red_down.step()
    with jax.named_scope("backfar"):
        dq, far = run(lambda *x: attend_bwd(late, 1, n_own, 1, *x, last=False), *bwd_args)
        fars.append(far)
        moved.append(over_z1(far))
    with jax.named_scope("backown"):
        dq, mine = run(lambda *x: attend_bwd(late, 0, n_own, 1, *x), *bwd_args, dq)
        dqs.append(dq)
        owns.append(mine)
    if n_f == 2:
        red_up.step()
    (moved[0],) = touch(moved[0])
    if n_f == 2:
        red_one = weight_grad(
            functools.partial(qkv_grad_kernel, len(early), True),
            own + other + dqs[:-1] + owns[:-1] + fars[:-1] + mixed + grad_attn + [packed, packed_moved],
            n_one + wide,
            width // 2,
            "one_grad",
            True,
        )
    moved[1:-1] = touch(*moved[1:-1])

    item = [dict(), dict()]

    def input_part(c):
        with jax.named_scope(f"inputpart{c}"):
            s = item[c]
            s["po"], pp = run(
                lambda *x: call(
                    functools.partial(input_part_kernel, c * rows), [f_rows, b_rows], *x, name="input_part"
                ),
                *dqs,
                *owns,
                *moved,
                qkv_w,
            )
            s["cp"] = over_core(pp)

    def input_near(c):
        with jax.named_scope(f"inputnear{c}"):
            s = item[c]
            (s["near"],) = run(
                lambda *x: call(near_kernel, [b_rows], *x, name="near"), s["po"], s["cp"]
            )
            s["far"] = over_y(s["near"])

    def input_last(c):
        with jax.named_scope(f"inputlast{c}"):
            s = item[c]
            (s["in"],) = run(
                lambda *x: call(input_grad_kernel, [b_rows], *x, name="input_grad"),
                state[c]["gfirst"],
                s["near"],
                s["far"],
            )

    input_part(1)
    if n_f == 2:
        red_two = weight_grad(
            functools.partial(qkv_grad_kernel, 1, False),
            own + other + dqs[-1:] + owns[-1:] + fars[-1:],
            n_two,
            width // 2,
            "two_grad",
            True,
        )
    input_near(1)
    if n_f == 2:
        red_down.step()
        red_up.step()
        red_one.step()
    input_last(1)
    with jax.named_scope("inputback"):
        in_back = over_z2(item[1]["in"])
    with jax.named_scope("placeout"):
        output = placed(out_blocks)
    if n_f == 2:
        red_two.step()
        (red_down.moved,) = touch(red_down.moved)
    input_part(0)
    if n_f == 2:
        owned_down = owned(red_down, "owned_down")
    input_near(0)
    if n_f == 2:
        red_one.step()
        red_up.step()
        red_two.step()
    input_last(0)
    with jax.named_scope("placein"):
        in_far = over_core(item[0]["in"])
    if n_f == 2:
        owned_up = owned(red_up, "owned_up")
        red_one.step()
        red_two.step()
    (in_back,) = touch(in_back)
    with jax.named_scope("placein"):
        in_blocks = [item[0]["in"], in_far, in_back, over_core(in_back)]
    with jax.named_scope("finish"):
        if n_f == 2:
            qkv_grad, owned_out, small, bias_grad = run(
                lambda *x: scalar_call(
                    owned_qkv_kernel,
                    [
                        shaped((3, wide, width // 2), F32),
                        shaped((wide, width // 2), F32),
                        shaped((8, width), F32),
                        shaped((2, wide), F32),
                    ],
                    *x,
                    name="owned_qkv",
                ),
                place,
                red_one.own,
                red_two.own,
                red_one.moved,
                red_two.moved,
            )
            owned_qkv = qkv_grad.transpose(2, 0, 1)
        else:

            def reduce_plain(left, right, axis):
                grad = mm(jnp.concatenate(left), jnp.concatenate(right), TN)
                keep = lax.psum_scatter(grad, "fsdp", scatter_dimension=axis, tiled=True)
                return lax.psum(keep, "context").astype(BF).astype(F32)

            zero = jnp.zeros((n_own, wide), BF)
            left = jnp.concatenate(dqs + by_kind(owns), axis=1)
            right = jnp.concatenate([zero] + by_kind(fars), axis=1)
            owned_up = reduce_plain(pieces_of("y"), pieces_of("gp"), 0)
            owned_down = reduce_plain(pieces_of("h"), pieces_of("gf"), 1)
            owned_out = reduce_plain(mixed, grad_attn, 1)
            owned_qkv = reduce_plain(own + other, [left, right], 0).reshape(w_qkv.shape)
            column_sums = jnp.sum((left.astype(F32) + right.astype(F32)), axis=0)
            bias_grad = jnp.stack([column_sums[:wide], column_sums[2 * wide :]])
            small = jnp.concatenate([packed[:6] + packed_moved[:6], packed[6:]])
            small, bias_grad = lax.psum((small, bias_grad), ("fsdp", "context"))
    with jax.named_scope("placein"):
        input_grad = placed(in_blocks)
    return (
        output,
        input_grad,
        owned_qkv,
        bias_grad,
        owned_out,
        small[0],
        small[1],
        small[2],
        owned_up,
        small[6],
        owned_down,
        small[3],
        small[4],
        small[5],
    )


def solution(mesh):
    sizes = tuple(mesh.shape[name] for name in ("fsdp", "context", "tensor"))
    specs = (
        P("fsdp", None, "tensor"),
        P(None, "tensor"),
        P("tensor", "fsdp"),
        P(),
        P(),
        P(),
        P("fsdp", "tensor"),
        P("tensor"),
        P("tensor", "fsdp"),
        P(),
        P(),
        P(),
    )
    rows = P("fsdp", "context", None)
    return jax.shard_map(
        functools.partial(body, sizes),
        mesh=mesh,
        in_specs=(rows, rows) + specs,
        out_specs=(rows, rows) + specs,
        check_vma=False,
    )
```

```python
import functools
import math

import jax
import jax.numpy as jnp
from jax import lax
from jax.experimental import pallas as pl
from jax.experimental.pallas import tpu as pltpu
from jax.sharding import PartitionSpec as P

HD = 64
SCALE = 1.0 / math.sqrt(HD)
SCALE_LOG2 = SCALE * math.log2(math.e)
EPS = 1e-06
BF = jnp.bfloat16
F32 = jnp.float32
NT = (((1,), (1,)), ((), ()))
TN = (((0,), (0,)), ((), ()))
NN = (((1,), (0,)), ((), ()))


def mm(a, b, dims=NN):
    return lax.dot_general(a, b, dims, preferred_element_type=F32)


def shaped(shape, dtype):
    return jax.ShapeDtypeStruct(shape, dtype)


def call(kernel, outs, *operands, name, limit=16, **extra):
    return pl.pallas_call(
        kernel,
        out_shape=list(outs),
        cost_estimate=pl.CostEstimate(flops=int(5e9), bytes_accessed=1, transcendentals=0),
        compiler_params=pltpu.CompilerParams(vmem_limit_bytes=limit << 20),
        name=name,
        **extra,
    )(*operands)


SMEM = pl.BlockSpec(memory_space=pltpu.SMEM)
VMEM = pl.BlockSpec(memory_space=pltpu.VMEM)


def scalar_call(kernel, outs, scalars, *operands, **kw):
    specs = [SMEM] + [VMEM] * len(operands)
    return call(kernel, outs, scalars, *operands, in_specs=specs, **kw)


def lanes(ref, index, size):
    return ref[:, pl.ds(pl.multiple_of(index * size, 128), size)]


def qkv_kernel(*refs):
    rows, (w_ref, b_ref, q_ref, k_ref, v_ref) = refs[:7], refs[7:]
    n = rows[0].shape[0]
    wide = q_ref.shape[1]
    for i, ref in enumerate(rows):
        here = slice(i * n, (i + 1) * n)
        skip = 0 if i < 4 else wide
        full = (mm(ref[...], w_ref[skip:, :], NT) + b_ref[:, skip:]).astype(BF)
        if i < 4:
            q_ref[here, :] = full[:, :wide]
        k_ref[here, :] = full[:, wide - skip : 2 * wide - skip]
        v_ref[here, :] = full[:, 2 * wide - skip :]


def last_kv_kernel(x_ref, w_ref, b_ref, *refs):
    k_ref, v_ref = refs[-2:]
    wide = k_ref.shape[1]
    full = (mm(x_ref[...], w_ref[wide:, :], NT) + b_ref[:, wide:]).astype(BF)
    k_ref[...] = full[:, :wide]
    v_ref[...] = full[:, wide:]


def attend_fwd_kernel(chunk, *refs):
    q_ref, k_ref, v_ref = refs[:3]
    o_ref, p_ref, f_ref, l_ref = refs[-4:]
    outs, logs = [], []
    for h in range(q_ref.shape[1] // HD):
        cols = slice(h * HD, (h + 1) * HD)
        scores = mm(q_ref[:, cols], k_ref[:, cols], NT)
        top = jnp.max(scores, axis=1, keepdims=True)
        expo = jnp.exp2((scores - top) * SCALE_LOG2)
        total = jnp.sum(expo, axis=1, keepdims=True)
        outs.append(mm(expo.astype(BF), v_ref[:, cols]) / total)
        logs.append(top * SCALE_LOG2 + jnp.log2(total))
    mixed = jnp.concatenate(outs, axis=1)
    f_ref[...] = mixed
    l_ref[...] = jnp.concatenate(logs, axis=1).T
    for step, ref in enumerate((o_ref, p_ref)):

        @pl.when(pl.program_id(0) == step)
        def _():
            ref[...] = mixed.astype(BF)


def attend_fwd(chunk, block, q, k, v, *before):
    nq, w = q.shape
    nk = k.shape[0]
    heads = w // HD
    q_spec = pl.BlockSpec((block, w), lambda i: (chunk * 2 + i, 0))
    l_spec = pl.BlockSpec((heads, block), lambda i: (0, chunk * 2 + i))
    o_spec = pl.BlockSpec((block, w), lambda i: (0, 0))
    k_spec = pl.BlockSpec((nk, w), lambda i: (0, 0))
    anywhere = pl.BlockSpec(memory_space=pl.ANY)
    return call(
        functools.partial(attend_fwd_kernel, chunk),
        [shaped((block, w), BF)] * 2 + [shaped((nq, w), F32), shaped((heads, nq), F32)],
        q,
        k,
        v,
        *before,
        name="attend_fwd",
        limit=24,
        grid=(2,),
        in_specs=[q_spec, k_spec, k_spec] + [anywhere] * len(before),
        out_specs=[o_spec, o_spec, q_spec, l_spec],
        input_output_aliases={3: 2, 4: 3} if before else {},
    )


def grad_mixed_kernel(*refs):
    gas, (w_ref, f_ref, g_ref, d_ref) = refs[:4], refs[4:]
    n = gas[0].shape[0]
    heads = w_ref.shape[0] // HD
    for i, ga in enumerate(gas):
        here = slice(i * n, (i + 1) * n)
        g = mm(ga[...], w_ref[...], NT).astype(BF)
        g_ref[here, :] = g
        prod = (g.astype(F32) * f_ref[here, :]).T
        d_ref[:, here] = jnp.concatenate(
            [jnp.sum(prod[h * HD : (h + 1) * HD], axis=0, keepdims=True) for h in range(heads)]
        )


def attend_bwd_kernel(heads, first, last, split, *refs):
    q_ref, k_ref, v_ref, g_ref, l_ref, d_ref = refs[:6]
    add_ref = refs[6] if not first else None
    dq_ref, outs, acc = refs[6 + (not first)], refs[7 + (not first) : -1], refs[-1]
    dqs, dks, dvs = [], [], []
    for h in heads:
        cols = slice(h * HD, (h + 1) * HD)
        q, k, v, g = q_ref[:, cols], k_ref[:, cols], v_ref[:, cols], g_ref[:, cols]
        probs = jnp.exp2(mm(k, q, NT) * SCALE_LOG2 - l_ref[h : h + 1, :])
        grad_scores = (probs * (mm(v, g, NT) - d_ref[h : h + 1, :])).astype(BF)
        dvs.append(mm(probs.astype(BF), g))
        dks.append(mm(grad_scores, q) * SCALE)
        dqs.append(mm(k, grad_scores, TN))
    dq = (dqs[0] if len(dqs) == 1 else jnp.concatenate(dqs, axis=0)).T
    if not first:
        dq = dq + add_ref[...]
    dq_ref[...] = (dq * SCALE).astype(BF) if last else dq
    dkv = jnp.concatenate(dks + dvs, axis=1)
    step = pl.program_id(0)

    @pl.when(step == 0)
    def _():
        acc[...] = dkv

    @pl.when(step > 0)
    def _():
        acc[...] += dkv

    @pl.when(step == pl.num_programs(0) - 1)
    def _():
        n = acc.shape[0] // len(outs)
        for i, ref in enumerate(outs):
            ref[...] = acc[i * n : (i + 1) * n].astype(BF)


def attend_bwd(heads, key_block, key_rows, split, q, k, v, g, logs, inner, *add, last=True, block=512):
    nq, w = q.shape
    n = len(heads) * HD
    q_spec = pl.BlockSpec((block, w), lambda i: (i, 0))
    k_spec = pl.BlockSpec((key_rows, w), lambda i: (key_block, 0))
    n_spec = pl.BlockSpec((block, n), lambda i: (i, 0))
    l_spec = pl.BlockSpec((logs.shape[0], block), lambda i: (0, i))
    whole = pl.BlockSpec((key_rows // split, 2 * n), lambda i: (0, 0))
    return call(
        functools.partial(attend_bwd_kernel, heads, not add, last, split),
        [shaped((nq, n), BF if last else F32)] + [shaped((key_rows // split, 2 * n), BF)] * split,
        q,
        k,
        v,
        g,
        logs,
        inner,
        *add,
        name="attend_bwd",
        limit=36,
        grid=(nq // block,),
        in_specs=[q_spec, k_spec, k_spec, q_spec, l_spec, l_spec] + [n_spec] * len(add),
        out_specs=[n_spec] + [whole] * split,
        scratch_shapes=[pltpu.VMEM((key_rows, 2 * n), F32)],
    )


def normed(x):
    centred = x - jnp.mean(x, axis=-1, keepdims=True)
    inverse = lax.rsqrt(jnp.mean(centred * centred, axis=-1, keepdims=True) + EPS)
    return centred * inverse, inverse


def norm_back(g, norm, inverse):
    return inverse * (
        g
        - jnp.mean(g, axis=-1, keepdims=True)
        - norm * jnp.mean(g * norm, axis=-1, keepdims=True)
    )


def down_rows(*terms):
    return jnp.concatenate([jnp.sum(t, axis=0, keepdims=True) for t in terms], axis=0)


def norm_one_kernel(m0, m1, m2, m3, w0, w1, w2, w3, t_ref, p_ref, y_ref, low_ref, n_ref, i_ref):
    near = mm(m0[...], w0[...]) + mm(m1[...], w1[...])
    far = mm(m2[...], w2[...]) + mm(m3[...], w3[...])
    norm, inverse = normed(t_ref[...].astype(F32) + ((near + far) + p_ref[0:1, :]))
    y = norm * p_ref[1:2, :] + p_ref[2:3, :]
    y_ref[...] = y
    low_ref[...] = y.astype(BF)
    n_ref[...] = norm
    i_ref[...] = inverse


def ffn_kernel(s_ref, y_ref, up_own, up_far, b_ref, down_own, down_far, h_ref, sl_ref, p_ref):
    f = s_ref[0]
    size = up_own.shape[0]
    x = mm(lanes(y_ref, f, size), up_own[...]) + mm(lanes(y_ref, 1 - f, size), up_far[...]) + b_ref[...]
    cdf = 0.5 * (1.0 + lax.erf(x * (1.0 / math.sqrt(2.0))))
    pdf = jnp.exp(-0.5 * x * x) * (1.0 / math.sqrt(2.0 * math.pi))
    sl_ref[...] = cdf + x * pdf
    hidden = (x * cdf).astype(BF)
    h_ref[...] = hidden
    for part, ref in ((f, down_own), (1 - f, down_far)):
        here = pl.ds(pl.multiple_of(part * size, 128), size)
        p_ref[:, here] = mm(hidden, ref[...]).astype(p_ref.dtype)


def norm_two_kernel(near, far, y_ref, g_ref, p_ref, o_ref, gs_ref, gf_ref, sums):
    ffn = near[...].astype(F32) + far[...].astype(F32)
    norm, inverse = normed(y_ref[...] + (ffn + p_ref[0:1, :]))
    o_ref[...] = (norm * p_ref[1:2, :] + p_ref[2:3, :]).astype(BF)
    g = g_ref[...].astype(F32)
    grad = norm_back(g * p_ref[1:2, :], norm, inverse)
    low = grad.astype(BF)
    gs_ref[...] = grad
    gf_ref[...] = low
    sums[...] = down_rows(low.astype(F32), g * norm, g)


def ffn_back_kernel(s_ref, g_ref, down_own, down_far, sl_ref, up_own, up_far, gp_ref, p_ref, sums):
    f = s_ref[0]
    size = up_own.shape[0]
    grad = mm(lanes(g_ref, f, size), down_own[...], NT) + mm(lanes(g_ref, 1 - f, size), down_far[...], NT)
    low = (grad * sl_ref[...]).astype(BF)
    gp_ref[...] = low
    sums[...] = down_rows(low.astype(F32))
    for part, ref in ((f, up_own), (1 - f, up_far)):
        here = pl.ds(pl.multiple_of(part * size, 128), size)
        p_ref[:, here] = mm(low, ref[...], NT).astype(p_ref.dtype)


def norm_one_back_kernel(gs_ref, near, far, n_ref, i_ref, p_ref, g_ref, low_ref, sums):
    grad_y = gs_ref[...] + (near[...].astype(F32) + far[...].astype(F32))
    norm = n_ref[...]
    grad = norm_back(grad_y * p_ref[1:2, :], norm, i_ref[...])
    low = grad.astype(BF)
    g_ref[...] = grad
    low_ref[...] = low
    sums[...] = down_rows(low.astype(F32), grad_y * norm, grad_y)


def by_kind(parts):
    return [x[:, :HD] for x in parts] + [x[:, HD:] for x in parts]


def input_part_kernel(first_row, *refs):
    w_ref, o_ref, p_ref = refs[-3:]
    heads = (len(refs) - 3) // 3
    dqs, dkvs, moved = (refs[i * heads : (i + 1) * heads] for i in range(3))
    n = o_ref.shape[0]
    for part, ref in enumerate((o_ref, p_ref)):
        here = slice(first_row + part * n, first_row + (part + 1) * n)
        lows = [(a[here, :].astype(F32) + b[here, :].astype(F32)).astype(BF) for a, b in zip(dkvs, moved)]
        grads = jnp.concatenate([d[here, :] for d in dqs] + by_kind(lows), axis=1)
        ref[...] = mm(grads, w_ref[...]).astype(ref.dtype)


def near_kernel(a_ref, b_ref, o_ref):
    o_ref[...] = (a_ref[...] + b_ref[...].astype(F32)).astype(BF)


def input_grad_kernel(g_ref, a_ref, b_ref, o_ref):
    o_ref[...] = (g_ref[...] + (a_ref[...].astype(F32) + b_ref[...].astype(F32))).astype(BF)


def place_kernel(s_ref, a, b, c, d, o_ref):
    n = a.shape[0]
    group, core = s_ref[2], s_ref[3]
    for block, half, ref in ((group, core, a), (group, 1 - core, b), (1 - group, core, c), (1 - group, 1 - core, d)):
        o_ref[block, pl.ds(pl.multiple_of(half * n, n), n), :] = ref[...]


def pack_kernel(a0, a1, b0, b1, u0, u1, u2, u3, o_ref):
    o_ref[0:3, :] = a0[...] + a1[...]
    o_ref[3:6, :] = b0[...] + b1[...]
    o_ref[6:7, :] = u0[...] + u1[...] + u2[...] + u3[...]
    o_ref[7:8, :] = jnp.zeros_like(u0)


EXTRA = 16


def two_parts(x):
    high = x.astype(BF).astype(F32)
    return high + (x - high).astype(BF).astype(F32)


def put(ref, main, small):
    n = main.shape[0]
    ref[0:n, :] = main.astype(ref.dtype)
    if small is not None:
        high = small.astype(ref.dtype)
        ref[n : n + EXTRA, :] = high
        if ref.shape[0] > n + EXTRA:
            ref[n + EXTRA :, :] = (small - high.astype(F32)).astype(ref.dtype)


def get(ref, small):
    if not small:
        return ref[...].astype(F32), None
    parts = 1 if ref.dtype == F32 else 2
    n = ref.shape[0] - parts * EXTRA
    rest = ref[n : n + EXTRA, :].astype(F32)
    if parts == 2:
        rest = rest + ref[n + EXTRA :, :].astype(F32)
    return ref[0:n, :].astype(F32), rest


def up_grad_kernel(s_ref, *refs):
    ys, gs, (keep, send) = refs[:4], refs[4:8], refs[8:]
    f = s_ref[0]
    size = ys[0].shape[1] // 2
    for out, part in ((send, 1 - f), (keep, f)):
        put(out, sum(mm(lanes(y, part, size), g[...], TN) for y, g in zip(ys, gs)), None)


def down_grad_kernel(s_ref, *refs):
    hs, gs, (keep, send) = refs[:4], refs[4:8], refs[8:]
    f = s_ref[0]
    size = gs[0].shape[1] // 2
    for out, part in ((send, 1 - f), (keep, f)):
        put(out, sum(mm(h[...], lanes(g, part, size), TN) for h, g in zip(hs, gs)), None)


def qkv_grad_kernel(heads, with_out, s_ref, *refs):
    rows, more, (keep, send) = refs[:8], refs[8 + 3 * heads : -2], refs[-2:]
    dqs, owns, fars = (refs[8 + i * heads : 8 + (i + 1) * heads] for i in range(3))
    f = s_ref[0]
    size = rows[0].shape[1] // 2
    n = rows[0].shape[0]
    m = heads * HD
    own = jnp.concatenate([d[...] for d in dqs] + by_kind([x[...] for x in owns]), axis=1)
    far = jnp.concatenate(by_kind([x[...] for x in fars]), axis=1)
    far_sums = jnp.sum(far.astype(F32), axis=0, keepdims=True)
    sums = jnp.sum(own.astype(F32), axis=0, keepdims=True)
    sums = jnp.concatenate([sums[:, :m], sums[:, m:] + far_sums], axis=1)
    if sums.shape[1] < size:
        sums = jnp.concatenate([sums, jnp.zeros((1, size - sums.shape[1]), F32)], axis=1)
    small = [sums]
    if with_out:
        packed, moved = more[-2:]
        six = packed[0:6, :] + moved[0:6, :]
        ups = packed[6:7, :]
        small = [six[:, :size], ups[:, :size], six[:, size:], ups[:, size:], sums]
    small.append(jnp.zeros((EXTRA - sum(x.shape[0] for x in small), size), F32))
    small = two_parts(jnp.concatenate(small, axis=0))
    for out, part in ((send, 1 - f), (keep, f)):
        one = two = None
        for i in range(4):
            here = slice(i * n, (i + 1) * n)
            a = mm(own[here], lanes(rows[i], part, size), TN)
            b = mm(far[here], lanes(rows[4 + i], part, size), TN)
            one = a if one is None else one + a
            two = b if two is None else two + b
        grad = [one[:m], one[m:] + two]
        if with_out:
            grad.append(sum(mm(a[...], lanes(g, part, size), TN) for a, g in zip(more[:4], more[4:8])))
        put(out, jnp.concatenate(grad, axis=0), small)


def half_of(main, which):
    n = main.shape[0] // 2
    return jnp.where(which == 0, main[:n], main[n:])


def first_sum_kernel(small, s_ref, keep, moved, own, send):
    (a, c), (b, d) = get(keep, small), get(moved, small)
    total = a + b
    rest = two_parts(c + d) if small else None
    put(own, half_of(total, s_ref[1]), rest)
    put(send, half_of(total, 1 - s_ref[1]), rest)


def sum_kernel(small, a_ref, b_ref, out):
    (a, c), (b, d) = get(a_ref, small), get(b_ref, small)
    put(out, a + b, c + d if small else None)


def joined(s_ref, own, moved):
    first = s_ref[1] == 0
    return jnp.concatenate([jnp.where(first, own, moved), jnp.where(first, moved, own)], axis=0)


def owned_kernel(s_ref, own, moved, out):
    out[...] = joined(s_ref, get(own, False)[0], get(moved, False)[0])


def owned_qkv_kernel(s_ref, own1, own2, moved1, moved2, qkv, outw, sums, bias):
    (one, small1), (two, small2) = get(own1, True), get(own2, True)
    one = joined(s_ref, one, get(moved1, True)[0])
    two = joined(s_ref, two, get(moved2, True)[0])
    n = outw.shape[0]
    m1, m2 = (one.shape[0] - n) // 3, two.shape[0] // 3
    for j in range(3):
        qkv[j, 0:m1, :] = one[j * m1 : (j + 1) * m1]
        qkv[j, m1:, :] = two[j * m2 : (j + 1) * m2]
    outw[...] = one[3 * m1 :]
    sums[0:7, :] = jnp.concatenate([small1[0:7], small1[7:14]], axis=1)
    sums[7:8, :] = jnp.zeros_like(sums[7:8, :])
    for i, j in ((0, 0), (1, 2)):
        bias[i : i + 1, :] = jnp.concatenate(
            [small1[14:15, j * m1 : (j + 1) * m1], small2[0:1, j * m2 : (j + 1) * m2]], axis=1
        )


def swap(x, axis, size, mask):
    return lax.ppermute(x, axis, [(i, i ^ mask) for i in range(size)])


def pick(first, second, bit, axis):
    n = first.shape[axis]
    ring = jnp.concatenate([first, second, first], axis=axis)
    return lax.dynamic_slice_in_dim(ring, bit * n, 2 * n, axis)


class Order:
    def __init__(self):
        self.done = None

    def __call__(self, fn, *operands):
        if self.done is not None:
            operands, _ = lax.optimization_barrier((operands, self.done))
        out = fn(*operands)
        self.done = out
        return out


class Reduction:
    def __init__(self, run, name, place, keep, moved, small, over_z1, over_z2):
        self.run, self.name, self.place, self.small = run, name, place, small
        self.own, self.moved, self.stage = keep, moved, 0
        self.over = [over_z1, over_z2, over_z1]
        self.rows, self.cols = keep.shape[0] - small * EXTRA, keep.shape[1]

    def step(self):
        self.stage += 1
        low = shaped((self.rows // 2 + self.small * 2 * EXTRA, self.cols), BF)
        wide = shaped((self.rows // 2 + self.small * EXTRA, self.cols), F32)
        name = f"{self.name}_{self.stage}"
        with jax.named_scope(name):
            if self.stage == 1:
                kernel = functools.partial(first_sum_kernel, self.small)
                fn = lambda *x: scalar_call(kernel, [wide, low], *x, name=name)
                self.own, send = self.run(fn, self.place, self.own, self.moved)
            else:
                kernel = functools.partial(sum_kernel, self.small)
                fn = lambda *x: call(kernel, [low], *x, name=name)
                (self.own,) = self.run(fn, self.own, self.moved)
                send = self.own
            self.moved = self.over[self.stage - 1](send)


def body(sizes, *args):
    (
        tokens,
        cotangent,
        w_qkv,
        qv_bias,
        w_out,
        out_bias,
        gain_one,
        shift_one,
        w_up,
        up_bias,
        w_down,
        down_bias,
        gain_two,
        shift_two,
    ) = args
    n_f, n_c, n_t = sizes
    _, rows, width = tokens.shape
    wide = w_qkv.shape[2]
    heads = wide // HD
    hidden_here = w_up.shape[1]
    half = rows // 2
    f = lax.axis_index("fsdp") if n_f == 2 else 0
    z = lax.axis_index("context")
    core = lax.axis_index("tensor") % 2
    group = z // 2
    over_core = functools.partial(swap, axis="tensor", size=n_t, mask=1)
    over_y = functools.partial(swap, axis="tensor", size=n_t, mask=2)
    over_both = functools.partial(swap, axis="tensor", size=n_t, mask=3)
    over_z1 = functools.partial(swap, axis="context", size=n_c, mask=1)
    over_z2 = functools.partial(swap, axis="context", size=n_c, mask=2)
    over_x = functools.partial(swap, axis="fsdp", size=n_f, mask=1)
    run = Order()

    def whole_f(w, axis):
        return lax.all_gather(w, "fsdp", axis=axis, tiled=True)

    def halves(w, axis):
        if n_f == 2:
            return w, over_x(w)
        w = whole_f(w, axis)
        return jnp.split(w, 2, axis=axis)

    def block_of(x, which, part):
        return lax.dynamic_slice(x, (which, part * half, 0), (1, half, width))[0]

    def touch(*x):
        return run(lambda *a: a, *x)

    def after(x, *others):
        return lax.optimization_barrier((x, others))[0]

    with jax.named_scope("arrive"):
        give = run(lambda t: block_of(t, 1 - group, core), tokens)
        b_own = over_z2(give)
        a_own = run(lambda t: block_of(t, group, core), tokens)
        oa_own = over_z1(a_own)
        qkv_t = after(w_qkv.transpose(1, 2, 0).reshape(3 * wide, -1), a_own)
        qkv_moved = over_x(qkv_t) if n_f == 2 else whole_f(qkv_t, 1)
        w_out_later = after(w_out, a_own)
        out_moved = over_x(w_out_later) if n_f == 2 else whole_f(w_out_later, 1)
        cot_give, cot_a, a_far, place, par_one, par_two, bias_row, up_row = run(
            lambda g, t, qb, ub, p1, p2: (
                block_of(g, 1 - group, core),
                block_of(g, group, core),
                block_of(t, group, 1 - core),
                jnp.stack(
                    [
                        jnp.int32(f),
                        (z % 2).astype(jnp.int32),
                        group.astype(jnp.int32),
                        core.astype(jnp.int32),
                    ]
                ),
                jnp.stack(p1),
                jnp.stack(p2),
                jnp.concatenate([qb[0], jnp.zeros_like(qb[0]), qb[1]])[None],
                ub[None],
            ),
            cotangent,
            tokens,
            qv_bias,
            up_bias,
            (out_bias, gain_one, shift_one),
            (down_bias, gain_two, shift_two),
        )
        qkv_w = run(lambda a, b: pick(a, b, f, 1) if n_f == 2 else b, qkv_t, qkv_moved)
        out_w = run(lambda a, b: pick(a, b, f, 1) if n_f == 2 else b, w_out, out_moved)
        (b_own,) = touch(b_own)
        ob_own = over_z1(b_own)
        (oa_own,) = touch(oa_own)
        b_far, oa_far = over_core(b_own), over_core(oa_own)
        b_far, oa_far, out_later = touch(b_far, oa_far, out_w)
        out_near, out_far = over_core(out_later), over_y(out_later)
        up_two = halves(after(w_up, out_later), 0)
        out_near, out_far = touch(out_near, out_far)
        (ob_own,) = touch(ob_own)
        ob_far = over_core(ob_own)
    with jax.named_scope("cotangent"):
        cot_b = over_z2(after(cot_give, ob_own))
    own = [a_own, a_far, b_own, b_far]
    other = [oa_own, oa_far, ob_own, ob_far]
    total = 8 * half
    n_own = total // 2

    q, k, v = run(
        lambda *x: call(
            qkv_kernel,
            [shaped((n_own, wide), BF), shaped((total, wide), BF), shaped((total, wide), BF)],
            *x,
            name="qkv",
        ),
        *own,
        *other[:3],
        qkv_w,
        bias_row,
    )
    row_spec = pl.BlockSpec((half, wide), lambda i: (7, 0))
    k, v = run(
        lambda *x: call(
            last_kv_kernel,
            [shaped((total, wide), BF), shaped((total, wide), BF)],
            *x,
            name="last_kv",
            grid=(1,),
            in_specs=[pl.BlockSpec(a.shape, lambda i: (0, 0)) for a in x[:3]]
            + [pl.BlockSpec(memory_space=pl.ANY)] * 2,
            out_specs=[row_spec, row_spec],
            input_output_aliases={3: 0, 4: 1},
        ),
        ob_far,
        qkv_w,
        bias_row,
        k,
        v,
    )
    with jax.named_scope("down_weight"):
        down_two = halves(after(w_down, q), 1)
    with jax.named_scope("out_weight"):
        out_both = over_both(after(out_later, q))

    mixed, pieces, shared = [], [], ()
    for c in range(2):
        with jax.named_scope(f"attend{c}"):
            mo, mp, *shared = run(lambda *x: attend_fwd(c, half, *x), q, k, v, *shared)
            mixed += [mo, mp]
            if c == 0:
                (*up_two, out_both) = touch(*up_two, out_both)
            else:
                (*pieces[0], cot_b) = touch(*pieces[0], cot_b)
            mo, mp = touch(mo, mp)
            pieces.append((mo, over_core(mp), over_y(mo), over_both(mp)))
    mixed_f, logs = shared
    tok = (a_own, b_own)
    f_rows = shaped((half, width), F32)
    b_rows = shaped((half, width), BF)
    h_rows = shaped((half, hidden_here), BF)
    state = [dict(), dict()]

    def norm_one(c):
        with jax.named_scope(f"normone{c}"):
            s = state[c]
            outs = [f_rows, b_rows, f_rows, shaped((half, 1), F32)]
            s["y"], s["yo"], s["n1"], s["i1"] = run(
                lambda *x: call(norm_one_kernel, outs, *x, name="norm_one"),
                *pieces[c],
                out_w,
                out_near,
                out_far,
                out_both,
                tok[c],
                par_one,
            )
            s["yp"] = over_core(s["yo"])

    def feed(c, which, dtype):
        with jax.named_scope(f"feed{c}{which}"):
            s = state[c]
            outs = [h_rows, shaped((half, hidden_here), F32), shaped((half, width), dtype)]
            s["h" + which], s["s" + which], s["p" + which] = run(
                lambda *x: scalar_call(ffn_kernel, outs, *x, name="feed"),
                place,
                s["y" + which],
                *up_two,
                up_row,
                *down_two,
            )
            if which == "p":
                s["c2"] = over_core(s["pp"])

    def near_sum(c, name):
        with jax.named_scope(f"near{c}{name}"):
            s = state[c]
            (s["near" + name],) = run(
                lambda *x: call(near_kernel, [b_rows], *x, name="near"), s["po"], s["c" + name]
            )
            s["far" + name] = over_y(s["near" + name])

    def norm_two(c):
        with jax.named_scope(f"normtwo{c}"):
            s = state[c]
            outs = [b_rows, f_rows, b_rows, shaped((3, width), F32)]
            s["out"], s["gs"], s["gfo"], s["sum2"] = run(
                lambda *x: call(norm_two_kernel, outs, *x, name="norm_two"),
                s["near2"],
                s["far2"],
                s["y"],
                cot[c],
                par_two,
            )
            s["gfp"] = over_core(s["gfo"])

    def feed_back(c, which, dtype):
        with jax.named_scope(f"feedback{c}{which}"):
            s = state[c]
            outs = [h_rows, shaped((half, width), dtype), shaped((1, hidden_here), F32)]
            s["gp" + which], s["p" + which], s["sumu" + which] = run(
                lambda *x: scalar_call(ffn_back_kernel, outs, *x, name="feed_back"),
                place,
                s["gf" + which],
                *down_two,
                s["s" + which],
                *up_two,
            )
            if which == "p":
                s["c5"] = over_core(s["pp"])

    def norm_one_back(c):
        with jax.named_scope(f"normoneback{c}"):
            s = state[c]
            s["gfirst"], s["gao"], s["sum1"] = run(
                lambda *x: call(
                    norm_one_back_kernel,
                    [f_rows, b_rows, shaped((3, width), F32)],
                    *x,
                    name="norm_one_back",
                ),
                s["gs"],
                s["near5"],
                s["far5"],
                s["n1"],
                s["i1"],
                par_one,
            )
            s["gap"] = over_core(s["gao"])

    def weight_grad(kernel, operands, rows, cols, name, small=False):
        with jax.named_scope(name):
            outs = [
                shaped((rows + small * EXTRA, cols), F32),
                shaped((rows + small * 2 * EXTRA, cols), BF),
            ]
            keep, send = run(lambda *x: scalar_call(kernel, outs, *x, name=name), place, *operands)
            return Reduction(run, name, place, keep, over_x(send), small, over_z1, over_z2)

    def owned(red, name):
        with jax.named_scope(name):
            return run(
                lambda *x: scalar_call(owned_kernel, [shaped((red.rows, red.cols), F32)], *x, name=name),
                place,
                red.own,
                red.moved,
            )[0]

    four = [(c, w) for c in range(2) for w in "op"]

    def pieces_of(name):
        return [state[c][name + w] for c, w in four]

    cot = (cot_a, cot_b)
    norm_one(0)
    feed(0, "o", F32)
    norm_one(1)
    feed(0, "p", BF)
    feed(1, "p", BF)
    near_sum(0, "2")
    feed(1, "o", F32)
    near_sum(1, "2")
    norm_two(0)
    feed_back(0, "o", F32)
    feed_back(0, "p", BF)
    norm_two(1)
    with jax.named_scope("outback"):
        out_back = over_z2(state[1]["out"])
    near_sum(0, "5")
    feed_back(1, "o", F32)
    feed_back(1, "p", BF)
    if n_f == 2:
        red_down = weight_grad(
            down_grad_kernel, pieces_of("h") + pieces_of("gf"), hidden_here, width // 2, "down_grad"
        )
    near_sum(1, "5")
    norm_one_back(0)
    if n_f == 2:
        red_up = weight_grad(
            up_grad_kernel, pieces_of("y") + pieces_of("gp"), width // 2, hidden_here, "up_grad"
        )
    norm_one_back(1)
    (out_back,) = touch(out_back)
    with jax.named_scope("smallpack"):
        (packed,) = run(
            lambda *x: call(pack_kernel, [shaped((8, width), F32)], *x, name="pack"),
            *[state[c][s] for s in ("sum1", "sum2") for c in range(2)],
            *pieces_of("sumu"),
        )
        packed_moved = over_core(packed)
    def placed(blocks):
        return run(
            lambda *x: scalar_call(place_kernel, [shaped(tokens.shape, BF)], *x, name="place"),
            place,
            *blocks,
        )[0]

    def both_halves(a, b):
        return a, over_core(a), b, over_core(b)

    if n_f == 2:
        red_down.step()
    with jax.named_scope("placeout"):
        out_blocks = both_halves(after(state[0]["out"], out_back), out_back)
    grad_attn = pieces_of("ga")
    grad_mixed, inner = run(
        lambda *x: call(
            grad_mixed_kernel, [shaped((n_own, wide), BF), shaped((heads, n_own), F32)], *x, name="grad_mixed"
        ),
        *grad_attn,
        out_w,
        mixed_f,
    )
    (*out_blocks, packed_moved) = touch(*out_blocks, packed_moved)

    early, late = tuple(range(heads - 1)), (heads - 1,)
    bwd_args = (q, k, v, grad_mixed, logs, inner)
    n_one, n_two = 3 * len(early) * HD, 3 * HD
    dqs, owns, fars, moved = [], [], [], []
    for h in early:
        with jax.named_scope(f"back{h}"):
            dq, mine, far = run(lambda *x: attend_bwd((h,), 0, total, 2, *x), *bwd_args)
            dqs.append(dq)
            owns.append(mine)
            fars.append(far)
            moved.append(over_z1(far))
        if n_f == 2 and h == 0:
            red_down.step()
    with jax.named_scope("backfar"):
        dq, far = run(lambda *x: attend_bwd(late, 1, n_own, 1, *x, last=False), *bwd_args)
        fars.append(far)
        moved.append(over_z1(far))
    with jax.named_scope("backown"):
        dq, mine = run(lambda *x: attend_bwd(late, 0, n_own, 1, *x), *bwd_args, dq)
        dqs.append(dq)
        owns.append(mine)
    if n_f == 2:
        red_up.step()
    (moved[0],) = touch(moved[0])
    if n_f == 2:
        red_one = weight_grad(
            functools.partial(qkv_grad_kernel, len(early), True),
            own + other + dqs[:-1] + owns[:-1] + fars[:-1] + mixed + grad_attn + [packed, packed_moved],
            n_one + wide,
            width // 2,
            "one_grad",
            True,
        )
    moved[1:-1] = touch(*moved[1:-1])

    item = [dict(), dict()]

    def input_part(c):
        with jax.named_scope(f"inputpart{c}"):
            s = item[c]
            s["po"], pp = run(
                lambda *x: call(
                    functools.partial(input_part_kernel, c * rows), [f_rows, b_rows], *x, name="input_part"
                ),
                *dqs,
                *owns,
                *moved,
                qkv_w,
            )
            s["cp"] = over_core(pp)

    def input_near(c):
        with jax.named_scope(f"inputnear{c}"):
            s = item[c]
            (s["near"],) = run(
                lambda *x: call(near_kernel, [b_rows], *x, name="near"), s["po"], s["cp"]
            )
            s["far"] = over_y(s["near"])

    def input_last(c):
        with jax.named_scope(f"inputlast{c}"):
            s = item[c]
            (s["in"],) = run(
                lambda *x: call(input_grad_kernel, [b_rows], *x, name="input_grad"),
                state[c]["gfirst"],
                s["near"],
                s["far"],
            )

    input_part(1)
    if n_f == 2:
        red_two = weight_grad(
            functools.partial(qkv_grad_kernel, 1, False),
            own + other + dqs[-1:] + owns[-1:] + fars[-1:],
            n_two,
            width // 2,
            "two_grad",
            True,
        )
    input_near(1)
    if n_f == 2:
        red_down.step()
        red_up.step()
        red_one.step()
    input_last(1)
    with jax.named_scope("inputback"):
        in_back = over_z2(item[1]["in"])
    with jax.named_scope("placeout"):
        output = placed(out_blocks)
    if n_f == 2:
        red_two.step()
        (red_down.moved,) = touch(red_down.moved)
    input_part(0)
    if n_f == 2:
        owned_down = owned(red_down, "owned_down")
    input_near(0)
    if n_f == 2:
        red_one.step()
        red_up.step()
        red_two.step()
    input_last(0)
    with jax.named_scope("placein"):
        in_far = over_core(item[0]["in"])
    if n_f == 2:
        owned_up = owned(red_up, "owned_up")
        red_one.step()
        red_two.step()
    (in_back,) = touch(in_back)
    with jax.named_scope("placein"):
        in_blocks = [item[0]["in"], in_far, in_back, over_core(in_back)]
    with jax.named_scope("finish"):
        if n_f == 2:
            qkv_grad, owned_out, small, bias_grad = run(
                lambda *x: scalar_call(
                    owned_qkv_kernel,
                    [
                        shaped((3, wide, width // 2), F32),
                        shaped((wide, width // 2), F32),
                        shaped((8, width), F32),
                        shaped((2, wide), F32),
                    ],
                    *x,
                    name="owned_qkv",
                ),
                place,
                red_one.own,
                red_two.own,
                red_one.moved,
                red_two.moved,
            )
            owned_qkv = qkv_grad.transpose(2, 0, 1)
        else:

            def reduce_plain(left, right, axis):
                grad = mm(jnp.concatenate(left), jnp.concatenate(right), TN)
                keep = lax.psum_scatter(grad, "fsdp", scatter_dimension=axis, tiled=True)
                return lax.psum(keep, "context").astype(BF).astype(F32)

            zero = jnp.zeros((n_own, wide), BF)
            left = jnp.concatenate(dqs + by_kind(owns), axis=1)
            right = jnp.concatenate([zero] + by_kind(fars), axis=1)
            owned_up = reduce_plain(pieces_of("y"), pieces_of("gp"), 0)
            owned_down = reduce_plain(pieces_of("h"), pieces_of("gf"), 1)
            owned_out = reduce_plain(mixed, grad_attn, 1)
            owned_qkv = reduce_plain(own + other, [left, right], 0).reshape(w_qkv.shape)
            column_sums = jnp.sum((left.astype(F32) + right.astype(F32)), axis=0)
            bias_grad = jnp.stack([column_sums[:wide], column_sums[2 * wide :]])
            small = jnp.concatenate([packed[:6] + packed_moved[:6], packed[6:]])
            small, bias_grad = lax.psum((small, bias_grad), ("fsdp", "context"))
    with jax.named_scope("placein"):
        input_grad = placed(in_blocks)
    return (
        output,
        input_grad,
        owned_qkv,
        bias_grad,
        owned_out,
        small[0],
        small[1],
        small[2],
        owned_up,
        small[6],
        owned_down,
        small[3],
        small[4],
        small[5],
    )


def solution(mesh):
    sizes = tuple(mesh.shape[name] for name in ("fsdp", "context", "tensor"))
    specs = (
        P("fsdp", None, "tensor"),
        P(None, "tensor"),
        P("tensor", "fsdp"),
        P(),
        P(),
        P(),
        P("fsdp", "tensor"),
        P("tensor"),
        P("tensor", "fsdp"),
        P(),
        P(),
        P(),
    )
    rows = P("fsdp", "context", None)
    return jax.shard_map(
        functools.partial(body, sizes),
        mesh=mesh,
        in_specs=(rows, rows) + specs,
        out_specs=(rows, rows) + specs,
        check_vma=False,
    )
```
